32 devices in a mesh: fsdp: 4 (over z), context: 2 (over y), tensor: 4 (over x, core).
Axes of the slice: x: 2, y: 2, z: 4, core: 2. Of those that a mesh axis runs over, the one named last changes fastest.
Arguments:
- hidden_in: bfloat16 [4, 1024, 2048], P('fsdp', 'context'), may hold values from -6 to 6
- attn_gain: bfloat16 [2048], P(('fsdp', 'context')), may hold values from 0.5 to 1.5
- w_query: bfloat16 [2048, 4096], P(('fsdp', 'context'), 'tensor'), may hold values from -0.125 to 0.125
- key_weight: bfloat16 [2048, 512], P(('fsdp', 'context'), 'tensor'), may hold values from -0.125 to 0.125
- value_weight: bfloat16 [2048, 512], P(('fsdp', 'context'), 'tensor'), may hold values from -0.125 to 0.125
- w_output: bfloat16 [2048, 4096], P(('fsdp', 'context'), 'tensor'), may hold values from -0.5 to 0.5
- query_gain: bfloat16 [128], P(('fsdp', 'context')), may hold values from 0.796875 to 2
- key_gain: bfloat16 [128], P(('fsdp', 'context')), may hold values from 0.796875 to 2
- ffn_gain: bfloat16 [2048], P(('fsdp', 'context')), may hold values from 0.5 to 1.5
- router: bfloat16 [2048, 32], P(('fsdp', 'context')), may hold values from -0.0625 to 0.0625
- gate_weight: bfloat16 [32, 2048, 768], P(('fsdp', 'context'), None, 'tensor'), may hold values from -0.125 to 0.125
- up_weight: bfloat16 [32, 2048, 768], P(('fsdp', 'context'), None, 'tensor'), may hold values from -0.125 to 0.125
- down_weight: bfloat16 [32, 768, 2048], P(('fsdp', 'context'), 'tensor'), may hold values from -1.25 to 1.25
- routes: int32 [4, 1024, 8], P('fsdp', 'context'), may hold values from 0 to 31, all different within a row
- segments: int32 [4, 1024], P('fsdp', 'context'), may hold values from 0 to 3, never falling along the last dimension, each value on 1 to 512 neighbouring positions
- cotangent: bfloat16 [4, 1024, 2048], P('fsdp', 'context'), may hold values from -6 to 6
Outputs:
- output: bfloat16 [4, 1024, 2048], P('fsdp', 'context')
- input_grad: float32 [4, 1024, 2048], P('fsdp', 'context')
- grad_attn_gain: float32 [2048], P(('fsdp', 'context'))
- grad_w_query: float32 [2048, 4096], P(('fsdp', 'context'), 'tensor')
- grad_w_key: float32 [2048, 512], P(('fsdp', 'context'), 'tensor')
- grad_w_value: float32 [2048, 512], P(('fsdp', 'context'), 'tensor')
- grad_w_output: float32 [2048, 4096], P(('fsdp', 'context'), 'tensor')
- grad_query_gain: float32 [128], P(('fsdp', 'context'))
- grad_key_gain: float32 [128], P(('fsdp', 'context'))
- grad_ffn_gain: float32 [2048], P(('fsdp', 'context'))
- grad_router: float32 [2048, 32], P(('fsdp', 'context'))
- grad_w_gate: float32 [32, 2048, 768], P(('fsdp', 'context'), None, 'tensor')
- grad_w_up: float32 [32, 2048, 768], P(('fsdp', 'context'), None, 'tensor')
- grad_w_down: float32 [32, 768, 2048], P(('fsdp', 'context'), 'tensor')
The draws below stay inside these ranges and needn't reach their ends.
Inputs may be any that keep to these rules, and one draw needn't show every extreme that they name: `routes`: the 8 experts of a token are different. `segments`: segment numbers never fall along a sequence.
All inputs are finite; a program needn't handle non-finite values.
Results may differ from the reference program's by a relative error of at most 0.03.
Values may be sent and summed in bfloat16 or wider, within the bound.
A program may use at most 320 MiB of HBM per device.

```python
import math
import jax
import jax.numpy as jnp
import numpy as np
from jax import lax

MODEL_DIM = 2048
QUERY_HEADS = 32
KEY_HEADS = 4
HEAD_SIZE = 128
FFE = 768
TOPK = 8
TOK_DEV = 512
EXPERTS = 32
SEQUENCE_COUNT = 4
SEQUENCE_TOKENS = 1024
DOCS = 4
CAP = 144
FFE_DEV = 192
N_TENSOR = 4


def strengthened(array, stream_key, source, target, shards_of, factor):
    owner, partner = [(jnp.arange(array.shape[axis_at]) // (array.shape[axis_at] // shards_of)).reshape([-1 if axis == axis_at else 1 for axis in range(array.ndim)]) for axis_at in (source, target)]
    chosen = jax.random.permutation(stream_key, shards_of)[partner]
    strong = (owner == chosen) | (owner == (partner + shards_of // 2) % shards_of)
    return jnp.where(strong, factor * array, array)


def block_scale(own_key, dims, split, low, largest):
    level = 1.0
    for dim, parts in split:
        steps = jax.random.uniform(jax.random.fold_in(jax.random.fold_in(own_key, 6), dim), (parts,), jnp.float32, low / len(split), largest / len(split))
        level = level * jnp.repeat(jnp.exp(steps), dims[dim] // parts).reshape((-1,) + (1,) * (len(dims) - 1 - dim))
    return level


def choose_distinct(own_key, rows, count, top, lift):
    order = jax.random.permutation(jax.random.fold_in(own_key, 1), count)
    boost = order
    for power in range(3):
        boost = boost * boost // count
    boost = boost * lift // count
    tickets = jax.random.randint(jax.random.fold_in(own_key, 2), (rows, count), 0, 4096) + boost
    holders = jax.random.permutation(jax.random.fold_in(own_key, 3), rows)[jnp.arange(count) % rows]
    tickets = jnp.where(jnp.arange(rows)[:, None] == holders[None, :], 1 << 14, tickets)
    priority = tickets * count + jnp.arange(count)
    return lax.top_k(priority.astype(jnp.int32), top)[1].astype(jnp.int32)


def length_profile(count, total, limit, slope):
    loads = [(1 << 20) // math.isqrt(grade ** slope) + 1 for grade in range(2, count + 1)]
    rest, given = total - limit - (count - 1), [1] * (count - 1)
    while rest > 0:
        free = [i for i in range(count - 1) if given[i] < limit]
        mass, remaining = sum([loads[i] for i in free]), rest
        for i in free:
            extra = min(limit - given[i], max(1, remaining * loads[i] // mass), rest)
            given[i] = given[i] + extra
            rest = rest - extra
    return np.array([limit] + given)


def ragged(rng, amount, total, limit, slope):
    if amount == 2:
        one = jax.random.randint(rng, (), max(1, total - limit), min(limit, total - 1) + 1)
        return jnp.stack([one, total - one])
    lengths = jnp.asarray(length_profile(amount, total, limit, slope), jnp.int32)
    pairs = (amount - 1) // 2
    donor, taker = lengths[1:1 + 2 * pairs:2], lengths[2:2 + 2 * pairs:2]
    slack = jnp.minimum(donor - 1, limit - taker)
    moved = jax.random.randint(jax.random.fold_in(rng, 1), (pairs,), 0, 1 << 20) % (slack + 1)
    lengths = lengths.at[1:1 + 2 * pairs:2].set(donor - moved).at[2:2 + 2 * pairs:2].set(taker + moved)
    return lengths[jax.random.permutation(jax.random.fold_in(rng, 2), amount)]


def noise(stream_key, dims, scale, bound, pieces=(), kind=jnp.bfloat16):
    values = jax.random.normal(stream_key, dims, jnp.float32) * scale
    if len(pieces) > 0:
        values = block_scale(stream_key, dims, pieces, -0.22, 0.18) * values
    return jnp.clip(values, min=-bound, max=bound).astype(kind)


def heavy_noise(key, dims, width, most, pieces, heavy, kind=jnp.bfloat16):
    values = width * jax.random.normal(key, dims, jnp.float32)
    if pieces:
        values = values * block_scale(key, dims, pieces, -0.22, 0.18)
    return jnp.clip(strengthened(values, jax.random.fold_in(key, 3), *heavy), -most, most).astype(kind)


def setup_inputs(seed: int = 0) -> dict:
    arg_keys = jax.random.split(jax.random.key(seed), 17)
    hidden_in = noise(arg_keys[0], (SEQUENCE_COUNT, SEQUENCE_TOKENS, MODEL_DIM), 1.0, 6.0, ((0, 4), (1, 2)))
    attn_gain = jnp.clip(1.0 + 0.1 * jax.random.normal(arg_keys[1], (MODEL_DIM,), jnp.float32), 0.5, 1.5).astype(jnp.bfloat16)
    w_query = noise(arg_keys[2], (MODEL_DIM, QUERY_HEADS * HEAD_SIZE), MODEL_DIM ** -0.5, 0.125, ((0, 8), (1, 4)))
    key_weight = noise(arg_keys[3], (MODEL_DIM, KEY_HEADS * HEAD_SIZE), MODEL_DIM ** -0.5, 0.125, ((0, 8), (1, 4)))
    value_weight = noise(arg_keys[4], (MODEL_DIM, KEY_HEADS * HEAD_SIZE), MODEL_DIM ** -0.5, 0.125, ((0, 8), (1, 4)))
    w_output = noise(arg_keys[5], (MODEL_DIM, QUERY_HEADS * HEAD_SIZE), HEAD_SIZE ** -0.5, 0.5, ((0, 8), (1, 4)))
    query_gain = jnp.clip(jnp.exp(math.log(2.0) - 0.92020463 * jax.random.uniform(arg_keys[6], (HEAD_SIZE,), jnp.float32) ** block_scale(arg_keys[6], (HEAD_SIZE,), ((0, 8),), -0.2, 0.2)), 0.796875, 2.0).astype(jnp.bfloat16)
    key_gain = jnp.clip(jnp.exp(math.log(2.0) - 0.92020463 * jax.random.uniform(arg_keys[7], (HEAD_SIZE,), jnp.float32) ** block_scale(arg_keys[7], (HEAD_SIZE,), ((0, 8),), -0.2, 0.2)), 0.796875, 2.0).astype(jnp.bfloat16)
    ffn_gain = jnp.clip(1.0 + 0.1 * jax.random.normal(arg_keys[8], (MODEL_DIM,), jnp.float32), 0.5, 1.5).astype(jnp.bfloat16)
    router = noise(arg_keys[9], (MODEL_DIM, EXPERTS), (4 * MODEL_DIM) ** -0.5, 0.0625, ((0, 8),))
    gate_weight = noise(arg_keys[10], (EXPERTS, MODEL_DIM, FFE), MODEL_DIM ** -0.5, 0.125, ((0, 8), (2, 4)))
    up_weight = noise(arg_keys[11], (EXPERTS, MODEL_DIM, FFE), MODEL_DIM ** -0.5, 0.125, ((0, 8), (2, 4)))
    down_weight = noise(arg_keys[12], (EXPERTS, FFE, MODEL_DIM), (FFE // 32) ** -0.5, 1.25, ((0, 8), (1, 4)))
    routes = choose_distinct(arg_keys[13], SEQUENCE_COUNT * SEQUENCE_TOKENS, EXPERTS, TOPK, 2048).reshape((SEQUENCE_COUNT, SEQUENCE_TOKENS, TOPK))
    segments = jax.vmap(lambda own: jnp.searchsorted(jnp.cumsum(ragged(own, DOCS, SEQUENCE_TOKENS, SEQUENCE_TOKENS // 2, 2)), jnp.arange(SEQUENCE_TOKENS), side="right"))(jax.random.split(arg_keys[14], SEQUENCE_COUNT)).reshape((SEQUENCE_COUNT, SEQUENCE_TOKENS)).astype(jnp.int32)
    cotangent = heavy_noise(arg_keys[15], (SEQUENCE_COUNT, SEQUENCE_TOKENS, MODEL_DIM), 1.0, 6.0, ((0, 4), (1, 2)), (1, 2, 2, 2.0))
    return {"hidden_in": hidden_in, "attn_gain": attn_gain, "w_query": w_query, "key_weight": key_weight, "value_weight": value_weight, "w_output": w_output, "query_gain": query_gain, "key_gain": key_gain, "ffn_gain": ffn_gain, "router": router, "gate_weight": gate_weight, "up_weight": up_weight, "down_weight": down_weight, "routes": routes, "segments": segments, "cotangent": cotangent}


EPSILON = 1e-06
ROPE_BASE = 1000000.0
NEGATIVE = -1e+30
TOP_PRECISION = lax.Precision.HIGHEST

@jax.custom_vjp
def lower_precision(v):
    return lax.optimization_barrier(v.astype(jnp.bfloat16)).astype(jnp.float32)

@jax.custom_vjp
def lower_precision_reverse(v):
    return v

def low_keep(v):
    return (lower_precision(v), None)

def low_pass(kept, grad):
    return (grad,)

def back_keep(v):
    return (v, None)

def back_low(kept, grad):
    return (lower_precision(grad),)
lower_precision.defvjp(low_keep, low_pass)
lower_precision_reverse.defvjp(back_keep, back_low)

def rms_scale(values, gain_vec):
    return values * lax.rsqrt(lax.optimization_barrier(jnp.mean(values * values, axis=-1, keepdims=True)) + EPSILON) * gain_vec

def rotate(values):
    half_width = values.shape[-1] // 2
    return jnp.concatenate([-values[..., half_width:], values[..., :half_width]], axis=-1)

def rope_tables(positions, head_width):
    step_index = jnp.arange(head_width // 2, dtype=jnp.float32)
    inverse = jnp.exp(step_index * (-2.0 * math.log(ROPE_BASE) / head_width))
    angles = positions.astype(jnp.float32)[..., None] * inverse
    cosine_table = jnp.cos(angles)
    sine_table = jnp.sin(angles)
    return (jnp.concatenate([cosine_table, cosine_table], -1), jnp.concatenate([sine_table, sine_table], -1))

def doc_positions(segment):
    length = segment.shape[1]
    token_index = jnp.broadcast_to(jnp.arange(length, dtype=jnp.int32)[None, :], segment.shape)
    starts = jnp.concatenate([jnp.ones((segment.shape[0], 1), bool), segment[:, 1:] != segment[:, :-1]], axis=1)
    first_index = lax.cummax(jnp.where(starts, token_index, 0), axis=1)
    return token_index - first_index

def attend_sequence(query_vectors, keys, values, segment):
    length = query_vectors.shape[0]
    query_tile_block = min(512, length)
    query_group_width = QUERY_HEADS // KEY_HEADS
    score_scale = HEAD_SIZE ** (-0.5)
    key_index = jnp.arange(length, dtype=jnp.int32)

    def one_block(leading_row):
        query_row_set = lax.dynamic_slice_in_dim(query_vectors, leading_row, query_tile_block, 0).reshape(query_tile_block, KEY_HEADS, query_group_width, HEAD_SIZE)
        query_seg = lax.dynamic_slice_in_dim(segment, leading_row, query_tile_block, 0)
        scores = lower_precision_reverse(jnp.einsum('qkgd,tkd->kgqt', query_row_set, keys, precision=TOP_PRECISION) * score_scale)
        query_index = leading_row + jnp.arange(query_tile_block, dtype=jnp.int32)
        allowed = (query_seg[:, None] == segment[None, :]) & (key_index[None, :] <= query_index[:, None])
        probs = jax.nn.softmax(jnp.where(allowed, scores, NEGATIVE), axis=-1)
        result = jnp.einsum('kgqt,tkd->qkgd', lower_precision(probs), values, precision=TOP_PRECISION)
        return result.reshape(query_tile_block, QUERY_HEADS * HEAD_SIZE)
    starts = jnp.arange(length // query_tile_block, dtype=jnp.int32) * query_tile_block
    return lax.map(jax.checkpoint(one_block), starts).reshape(length, QUERY_HEADS * HEAD_SIZE)

def reference(hidden_in, attn_gain, w_query, key_weight, value_weight, w_output, query_gain, key_gain, ffn_gain, router, gate_weight, up_weight, down_weight, routes, segments, cotangent):
    positions = doc_positions(segments)
    cosine_table, sine_table = rope_tables(positions, HEAD_SIZE)
    cosine_table = cosine_table[:, :, None, :]
    sine_table = sine_table[:, :, None, :]
    tokens = SEQUENCE_COUNT * SEQUENCE_TOKENS
    blocks = tokens // TOK_DEV
    route_rows = routes.reshape(blocks, TOK_DEV, TOPK)
    counts = lax.optimization_barrier(jnp.sum((route_rows[..., None] == jnp.arange(EXPERTS, dtype=jnp.int32)).astype(jnp.int32), axis=2))
    before = jnp.cumsum(counts, axis=1) - counts
    slot_index = jnp.take_along_axis(before, route_rows, axis=2)
    slot_rows = blocks * CAP
    block_index = jnp.arange(blocks, dtype=jnp.int32)[:, None, None]
    place = route_rows * slot_rows + block_index * CAP + slot_index
    pair_slot = jnp.where(slot_index < CAP, place, EXPERTS * slot_rows).reshape(tokens * TOPK)
    token_index = jnp.broadcast_to(jnp.arange(tokens, dtype=jnp.int32)[:, None], (tokens, TOPK)).reshape(tokens * TOPK)
    slot_table = jnp.full((EXPERTS * slot_rows,), tokens, jnp.int32).at[pair_slot].set(token_index, mode='drop').reshape(EXPERTS, slot_rows)

    def rope(values):
        return values * cosine_table + rotate(values) * sine_table

    def forward(input_rows, gain_one, query_matrix, key_matrix, value_matrix, output_matrix, gain_query, gain_key, gain_two, router_matrix, gate_w, up_w, down_w):
        attention_normalized = lower_precision(rms_scale(input_rows, gain_one))
        query_unrotated = lower_precision_reverse(jnp.einsum('bio,oa->bia', attention_normalized, query_matrix, precision=TOP_PRECISION)).reshape(SEQUENCE_COUNT, SEQUENCE_TOKENS, QUERY_HEADS, HEAD_SIZE)
        key_unrotated = lower_precision_reverse(jnp.einsum('bio,oa->bia', attention_normalized, key_matrix, precision=TOP_PRECISION)).reshape(SEQUENCE_COUNT, SEQUENCE_TOKENS, KEY_HEADS, HEAD_SIZE)
        value_complete = lower_precision(lower_precision_reverse(jnp.einsum('bio,oa->bia', attention_normalized, value_matrix, precision=TOP_PRECISION))).reshape(SEQUENCE_COUNT, SEQUENCE_TOKENS, KEY_HEADS, HEAD_SIZE)
        query_all = lower_precision(rope(rms_scale(query_unrotated, gain_query)))
        key_all = lower_precision(rope(rms_scale(key_unrotated, gain_key)))
        head_outputs = jnp.stack([attend_sequence(query_all[seq_id], key_all[seq_id], value_complete[seq_id], segments[seq_id]) for seq_id in range(SEQUENCE_COUNT)])
        head_outputs = lower_precision(lower_precision_reverse(head_outputs))
        residual_stream = input_rows + lower_precision_reverse(jnp.einsum('fym,hm->fyh', head_outputs, output_matrix, precision=TOP_PRECISION))
        feedforward_normalized = lower_precision(rms_scale(residual_stream, gain_two))
        router_scores = lower_precision_reverse(jnp.einsum('bio,oa->bia', feedforward_normalized, router_matrix, precision=TOP_PRECISION))
        gate_probs = jax.nn.softmax(jnp.take_along_axis(router_scores, routes, axis=-1), axis=-1)
        flat_rows = jnp.concatenate([feedforward_normalized.reshape(tokens, MODEL_DIM), jnp.zeros((1, MODEL_DIM), jnp.float32)], axis=0)

        def expert_block(item):
            slot_ids, gate_e, up_e, down_e = item
            picked = flat_rows[slot_ids]
            summed = jnp.zeros((slot_rows, MODEL_DIM), jnp.float32)
            for group_id in range(N_TENSOR):
                columns = slice(group_id * FFE_DEV, (group_id + 1) * FFE_DEV)
                group_in = lower_precision_reverse(picked)
                gate_activation_input = lower_precision_reverse(jnp.dot(group_in, gate_e[:, columns], precision=TOP_PRECISION))
                up_activation_input = lower_precision_reverse(jnp.dot(group_in, up_e[:, columns], precision=TOP_PRECISION))
                hidden_middle = lower_precision(jax.nn.silu(gate_activation_input) * up_activation_input)
                summed = summed + lower_precision(jnp.dot(hidden_middle, down_e[columns], precision=TOP_PRECISION))
            return summed
        expert_out = lower_precision_reverse(lax.map(jax.checkpoint(expert_block), (slot_table, gate_w, up_w, down_w)))
        padded = jnp.concatenate([expert_out.reshape(EXPERTS * slot_rows, MODEL_DIM), jnp.zeros((1, MODEL_DIM), jnp.float32)], axis=0)
        pair_out = padded[pair_slot].reshape(SEQUENCE_COUNT, SEQUENCE_TOKENS, TOPK, MODEL_DIM)
        return residual_stream + lax.optimization_barrier(jnp.sum(gate_probs[..., None] * pair_out, axis=2))
    floats = [hidden_in, attn_gain, w_query, key_weight, value_weight, w_output, query_gain, key_gain, ffn_gain, router, gate_weight, up_weight, down_weight]
    floats = [item.astype(jnp.float32) for item in floats]
    output, pull_back = jax.vjp(forward, *floats)
    grads = pull_back(cotangent.astype(jnp.float32))
    return (output.astype(jnp.bfloat16), grads[0], grads[1], grads[2], grads[3], grads[4], grads[5], grads[6], grads[7], grads[8], grads[9], grads[10], grads[11], grads[12])
```

```python
import functools
import math

import jax
import jax.numpy as jnp
from jax import lax
from jax.experimental import pallas as pl
from jax.experimental.pallas import tpu as pltpu
from jax.sharding import PartitionSpec as P

HEAD_SIZE = 128
TOPK = 8
FSDP, CONTEXT, TENSOR = "fsdp", "context", "tensor"
GROUPS = (FSDP, CONTEXT)
EVERYONE = (FSDP, CONTEXT, TENSOR)


EPSILON = 1e-06
ROPE_BASE = 1000000.0
NEGATIVE = -1e30


def rms_scale(values, gain_vec):
    return (
        values * lax.rsqrt(jnp.mean(values * values, axis=-1, keepdims=True) + EPSILON) * gain_vec
    )


def rotate(values):
    half_width = values.shape[-1] // 2
    return jnp.concatenate([-values[..., half_width:], values[..., :half_width]], axis=-1)


def rope_tables(positions, head_width):
    step_index = jnp.arange(head_width // 2, dtype=jnp.float32)
    inverse = jnp.exp(step_index * (-2.0 * math.log(ROPE_BASE) / head_width))
    angles = positions.astype(jnp.float32)[:, None] * inverse[None, :]
    cosine_table = jnp.cos(angles)
    sine_table = jnp.sin(angles)
    return (
        jnp.concatenate([cosine_table, cosine_table], -1),
        jnp.concatenate([sine_table, sine_table], -1),
    )


def doc_positions(segment):
    token_index = jnp.arange(segment.shape[0], dtype=jnp.int32)
    smaller = (segment[None, :] < segment[:, None]).astype(jnp.int32)
    return token_index - jnp.sum(smaller, axis=1)


def earlier_counts(chosen):
    rows = chosen.shape[0]
    row_id = lax.broadcasted_iota(jnp.int32, (rows, rows), 0)
    col_id = lax.broadcasted_iota(jnp.int32, (rows, rows), 1)
    earlier = (col_id < row_id).astype(jnp.bfloat16)
    return matmul(earlier, chosen.astype(jnp.bfloat16))


def qk_finish(raw_values, gain_vec, cosine_table, sine_table):
    normed = rms_scale(raw_values, gain_vec)
    return normed * cosine_table + rotate(normed) * sine_table


def matmul(left_side, right_side):
    return jnp.dot(left_side, right_side, preferred_element_type=jnp.float32)


def matmul_nt(left_side, right_side):
    return lax.dot_general(
        left_side, right_side, (((1,), (1,)), ((), ())), preferred_element_type=jnp.float32
    )


def matmul_tn(left_side, right_side):
    return lax.dot_general(
        left_side, right_side, (((0,), (0,)), ((), ())), preferred_element_type=jnp.float32
    )


def block_scores(query_vectors, keys_all, seg_all, query_seg, query_index, key_ids, block_id, key_block):
    leading_row = block_id * key_block
    keys_part = lax.dynamic_slice_in_dim(keys_all, leading_row, key_block, 0)
    seg_part = lax.dynamic_slice_in_dim(seg_all, leading_row, key_block, 0)
    key_index = lax.dynamic_slice_in_dim(key_ids, leading_row, key_block, 0)
    score_scale = query_vectors.shape[2] ** (-0.5)
    scores = (
        jnp.einsum("qhd,kd->hqk", query_vectors, keys_part, preferred_element_type=jnp.float32)
        * score_scale
    )
    allowed = (query_seg[:, None] == seg_part[None, :]) & (
        key_index[None, :] <= query_index[:, None]
    )
    return (scores, allowed[None, :, :], keys_part)


def attention_forward(
    query_vectors, keys_all, values_all, seg_all, query_seg, query_index, key_ids, key_block
):
    row_count, head_count, head_width = query_vectors.shape
    block_count = keys_all.shape[0] // key_block

    def stats_step(running, block_id):
        run_max, run_sum = running
        scores, allowed, unused = block_scores(
            query_vectors, keys_all, seg_all, query_seg, query_index, key_ids, block_id, key_block
        )
        masked = jnp.where(allowed, scores, NEGATIVE)
        new_max = jnp.maximum(run_max, jnp.max(masked, axis=2))
        weights = jnp.where(allowed, jnp.exp(masked - new_max[:, :, None]), 0.0)
        run_sum = run_sum * jnp.exp(run_max - new_max) + jnp.sum(weights, axis=2)
        return ((new_max, run_sum), None)

    start_state = (
        jnp.full((head_count, row_count), NEGATIVE, jnp.float32),
        jnp.zeros((head_count, row_count), jnp.float32),
    )
    (run_max, run_sum), ignored = lax.scan(
        stats_step, start_state, jnp.arange(block_count, dtype=jnp.int32)
    )
    log_total = run_max + jnp.log(run_sum)

    def value_step(accumulated, block_id):
        scores, allowed, unused = block_scores(
            query_vectors, keys_all, seg_all, query_seg, query_index, key_ids, block_id, key_block
        )
        prob_block = jnp.where(allowed, jnp.exp(scores - log_total[:, :, None]), 0.0).astype(
            jnp.bfloat16
        )
        values_part = lax.dynamic_slice_in_dim(values_all, block_id * key_block, key_block, 0)
        accumulated = accumulated + jnp.einsum(
            "hqk,kd->qhd", prob_block, values_part, preferred_element_type=jnp.float32
        )
        return (accumulated, None)

    heads_full, ignored = lax.scan(
        value_step,
        jnp.zeros((row_count, head_count, head_width), jnp.float32),
        jnp.arange(block_count, dtype=jnp.int32),
    )
    return (heads_full, log_total)


def attention_backward(
    query_vectors,
    keys_all,
    values_all,
    seg_all,
    query_seg,
    query_index,
    key_ids,
    key_block,
    log_total,
    grad_heads,
    row_delta,
):
    row_count, head_count, head_width = query_vectors.shape
    block_count = keys_all.shape[0] // key_block
    score_scale = head_width ** (-0.5)

    def grad_step(grad_query, block_id):
        scores, allowed, keys_part = block_scores(
            query_vectors, keys_all, seg_all, query_seg, query_index, key_ids, block_id, key_block
        )
        values_part = lax.dynamic_slice_in_dim(values_all, block_id * key_block, key_block, 0)
        prob_block = jnp.where(allowed, jnp.exp(scores - log_total[:, :, None]), 0.0)
        grad_prob = jnp.einsum(
            "qhd,kd->hqk", grad_heads, values_part, preferred_element_type=jnp.float32
        )
        grad_score = (prob_block * (grad_prob - row_delta[:, :, None])).astype(jnp.bfloat16)
        grad_query = (
            grad_query
            + jnp.einsum("hqk,kd->qhd", grad_score, keys_part, preferred_element_type=jnp.float32)
            * score_scale
        )
        grad_key = (
            jnp.einsum("hqk,qhd->kd", grad_score, query_vectors, preferred_element_type=jnp.float32)
            * score_scale
        )
        grad_value = jnp.einsum(
            "hqk,qhd->kd",
            prob_block.astype(jnp.bfloat16),
            grad_heads,
            preferred_element_type=jnp.float32,
        )
        return (grad_query, (grad_key, grad_value))

    grad_query, (grad_key, grad_value) = lax.scan(
        grad_step,
        jnp.zeros((row_count, head_count, head_width), jnp.float32),
        jnp.arange(block_count, dtype=jnp.int32),
    )
    return (grad_query, grad_key.reshape(-1, head_width), grad_value.reshape(-1, head_width))


def to_experts(buffer):
    return lax.all_to_all(buffer, GROUPS, split_axis=0, concat_axis=1, tiled=True)


def from_experts(result_rows):
    return lax.all_to_all(result_rows, GROUPS, split_axis=1, concat_axis=0, tiled=True)


def pick_pairs(buffer, target, row_count):
    model_width = buffer.shape[2]
    flat_rows = jnp.concatenate(
        [buffer.reshape(-1, model_width), jnp.zeros((1, model_width), buffer.dtype)], axis=0
    )
    return flat_rows[target].reshape(row_count, TOPK, model_width)


def routed_local(
    hidden_in,
    attn_gain,
    w_query,
    key_weight,
    value_weight,
    w_output,
    query_gain,
    key_gain,
    ffn_gain,
    router,
    gate_weight,
    up_weight,
    down_weight,
    routes,
    segments,
    cotangent,
):
    context_rank = lax.axis_index(CONTEXT)
    input_rows = hidden_in[0].astype(jnp.float32)
    row_count, model_width = input_rows.shape
    gathered = (
        lax.all_gather(w_query, GROUPS, axis=0, tiled=True),
        lax.all_gather(key_weight, GROUPS, axis=0, tiled=True),
        lax.all_gather(value_weight, GROUPS, axis=0, tiled=True),
        lax.all_gather(w_output, GROUPS, axis=0, tiled=True),
        lax.all_gather(router, GROUPS, axis=0, tiled=True),
        lax.all_gather(attn_gain, GROUPS, axis=0, tiled=True),
        lax.all_gather(ffn_gain, GROUPS, axis=0, tiled=True),
        lax.all_gather(query_gain, GROUPS, axis=0, tiled=True),
        lax.all_gather(key_gain, GROUPS, axis=0, tiled=True),
    )
    full_query, full_key, full_value, full_output, full_router = (
        gathered[0],
        gathered[1],
        gathered[2],
        gathered[3],
        gathered[4],
    )
    gain_attn = gathered[5].astype(jnp.float32)
    gain_ffn = gathered[6].astype(jnp.float32)
    gain_query = gathered[7].astype(jnp.float32)
    gain_key = gathered[8].astype(jnp.float32)
    local_heads = full_query.shape[1] // HEAD_SIZE
    seg_all = lax.all_gather(segments, CONTEXT, axis=1, tiled=True)[0]
    length = seg_all.shape[0]
    start_row = context_rank * row_count
    positions = lax.dynamic_slice_in_dim(doc_positions(seg_all), start_row, row_count)
    cosine_table, sine_table = rope_tables(positions, HEAD_SIZE)
    query_seg = segments[0]
    query_index = start_row + jnp.arange(row_count, dtype=jnp.int32)
    key_ids = jnp.arange(length, dtype=jnp.int32)
    key_block = min(512, length)

    def query_finish(raw_values, gain_vec):
        return qk_finish(raw_values, gain_vec, cosine_table[:, None, :], sine_table[:, None, :])

    def key_finish(raw_values, gain_vec):
        return qk_finish(raw_values, gain_vec, cosine_table, sine_table)

    normed_f, first_pull = jax.vjp(rms_scale, input_rows, gain_attn)
    attention_normalized = normed_f.astype(jnp.bfloat16)
    query_unrotated = matmul(attention_normalized, full_query).reshape(
        row_count, local_heads, HEAD_SIZE
    )
    key_unrotated = matmul(attention_normalized, full_key)
    value_raw = matmul(attention_normalized, full_value)
    query_f, query_pull = jax.vjp(query_finish, query_unrotated, gain_query)
    key_f, key_pull = jax.vjp(key_finish, key_unrotated, gain_key)
    query_vectors = query_f.astype(jnp.bfloat16)
    keys_all, values_all = (
        lax.all_gather(key_f.astype(jnp.bfloat16), CONTEXT, axis=0, tiled=True),
        lax.all_gather(value_raw.astype(jnp.bfloat16), CONTEXT, axis=0, tiled=True),
    )
    heads_full, log_total = attention_forward(
        query_vectors, keys_all, values_all, seg_all, query_seg, query_index, key_ids, key_block
    )
    heads_low = heads_full.reshape(row_count, local_heads * HEAD_SIZE).astype(jnp.bfloat16)
    attn_out = lax.psum(matmul_nt(heads_low, full_output).astype(jnp.bfloat16), TENSOR).astype(
        jnp.float32
    )
    residual_stream = input_rows + attn_out
    second_f, second_pull = jax.vjp(rms_scale, residual_stream, gain_ffn)
    feedforward_normalized = second_f.astype(jnp.bfloat16)
    router_scores = matmul(feedforward_normalized, full_router)
    experts_total = full_router.shape[1]
    route_ids = routes[0]
    chosen = route_ids[:, :, None] == jnp.arange(experts_total, dtype=jnp.int32)
    selected = jnp.sum(jnp.where(chosen, router_scores[:, None, :], 0.0), axis=2)
    gate_probs = jax.nn.softmax(selected, axis=-1)
    capacity = 9 * row_count * TOPK // (8 * experts_total)
    before = earlier_counts(jnp.any(chosen, axis=1)).astype(jnp.int32)
    slot_index = jnp.sum(jnp.where(chosen, before[:, None, :], 0), axis=2)
    target = jnp.where(
        slot_index < capacity, route_ids * capacity + slot_index, experts_total * capacity
    ).reshape(-1)
    source = jnp.repeat(jnp.arange(row_count, dtype=jnp.int32), TOPK)
    send_rows = (
        jnp.zeros((experts_total * capacity, model_width), jnp.bfloat16)
        .at[target]
        .set(feedforward_normalized[source], mode="drop")
    )
    expert_input_rows = to_experts(send_rows.reshape(experts_total, capacity, model_width))
    gate_activation_input = jnp.einsum(
        "phu,puo->pho", expert_input_rows, gate_weight, preferred_element_type=jnp.float32
    )
    up_activation_input = jnp.einsum(
        "phu,puo->pho", expert_input_rows, up_weight, preferred_element_type=jnp.float32
    )
    sigmoid_gate = jax.nn.sigmoid(gate_activation_input)
    silu_gate = gate_activation_input * sigmoid_gate
    hidden_middle = (silu_gate * up_activation_input).astype(jnp.bfloat16)
    expert_part = jnp.einsum(
        "pic,pcw->piw", hidden_middle, down_weight, preferred_element_type=jnp.float32
    ).astype(jnp.bfloat16)
    grad_out = cotangent[0].astype(jnp.float32)
    returned = pick_pairs(from_experts(expert_part), target, row_count)
    moe_part = jnp.sum(returned.astype(jnp.float32) * gate_probs[:, :, None], axis=1)
    moe_out = lax.psum(moe_part.astype(jnp.bfloat16), TENSOR).astype(jnp.float32)
    grad_gate_part = jnp.sum(returned.astype(jnp.float32) * grad_out[:, None, :], axis=2)
    output = (residual_stream + moe_out).astype(jnp.bfloat16)
    pair_grad = (
        (gate_probs[:, :, None] * grad_out[:, None, :])
        .astype(jnp.bfloat16)
        .reshape(row_count * TOPK, model_width)
    )
    send_grad = (
        jnp.zeros((experts_total * capacity, model_width), jnp.bfloat16)
        .at[target]
        .set(pair_grad, mode="drop")
    )
    expert_output_gradient = to_experts(send_grad.reshape(experts_total, capacity, model_width))
    grad_mid = jnp.einsum(
        "jtk,jvk->jtv", expert_output_gradient, down_weight, preferred_element_type=jnp.float32
    )
    grad_w_down = jnp.einsum(
        "tce,tci->tei", hidden_middle, expert_output_gradient, preferred_element_type=jnp.float32
    )
    gate_activation_gradient = (
        grad_mid
        * up_activation_input
        * sigmoid_gate
        * (1.0 + gate_activation_input * (1.0 - sigmoid_gate))
    ).astype(jnp.bfloat16)
    up_activation_gradient = (grad_mid * silu_gate).astype(jnp.bfloat16)
    grad_w_gate = jnp.einsum(
        "ahw,ahp->awp",
        expert_input_rows,
        gate_activation_gradient,
        preferred_element_type=jnp.float32,
    )
    grad_w_up = jnp.einsum(
        "ahw,ahp->awp",
        expert_input_rows,
        up_activation_gradient,
        preferred_element_type=jnp.float32,
    )
    grad_expert_in = (
        jnp.einsum(
            "ous,ops->oup",
            gate_activation_gradient,
            gate_weight,
            preferred_element_type=jnp.float32,
        )
        + jnp.einsum(
            "ous,ops->oup", up_activation_gradient, up_weight, preferred_element_type=jnp.float32
        )
    ).astype(jnp.bfloat16)
    grad_pairs = pick_pairs(from_experts(grad_expert_in), target, row_count)
    grad_normed_part = jnp.sum(grad_pairs.astype(jnp.float32), axis=1)
    grad_normed_moe, grad_gates = (
        lax.psum(grad_normed_part.astype(jnp.bfloat16), TENSOR).astype(jnp.float32),
        lax.psum(grad_gate_part.astype(jnp.bfloat16), TENSOR).astype(jnp.float32),
    )
    grad_selected = gate_probs * (
        grad_gates - jnp.sum(gate_probs * grad_gates, axis=1, keepdims=True)
    )
    grad_logits = jnp.sum(jnp.where(chosen, grad_selected[:, :, None], 0.0), axis=1).astype(
        jnp.bfloat16
    )
    grad_router = matmul_tn(feedforward_normalized, grad_logits)
    grad_normed_two = grad_normed_moe + matmul_nt(grad_logits, full_router)
    grad_resid_norm, grad_gain_ffn = second_pull(grad_normed_two)
    grad_resid = grad_out + grad_resid_norm
    grad_attn = grad_resid.astype(jnp.bfloat16)
    grad_w_output = matmul_tn(grad_attn, heads_low)
    grad_heads = (
        matmul(grad_attn, full_output)
        .astype(jnp.bfloat16)
        .reshape(row_count, local_heads, HEAD_SIZE)
    )
    row_delta = jnp.sum(grad_heads.astype(jnp.float32) * heads_full, axis=2).T
    grad_query, grad_key_terms, grad_value_terms = attention_backward(
        query_vectors,
        keys_all,
        values_all,
        seg_all,
        query_seg,
        query_index,
        key_ids,
        key_block,
        log_total,
        grad_heads,
        row_delta,
    )
    grad_key_local, grad_value_local = (
        lax.psum_scatter(
            grad_key_terms.astype(jnp.bfloat16), CONTEXT, scatter_dimension=0, tiled=True
        ).astype(jnp.float32),
        lax.psum_scatter(
            grad_value_terms.astype(jnp.bfloat16), CONTEXT, scatter_dimension=0, tiled=True
        ).astype(jnp.float32),
    )
    grad_query_raw, grad_gain_query = query_pull(grad_query)
    grad_key_raw, grad_gain_key = key_pull(grad_key_local)
    grad_query_low = grad_query_raw.reshape(row_count, local_heads * HEAD_SIZE).astype(jnp.bfloat16)
    grad_key_low = grad_key_raw.astype(jnp.bfloat16)
    grad_value_low = grad_value_local.astype(jnp.bfloat16)
    grad_w_query = matmul_tn(attention_normalized, grad_query_low)
    grad_w_key = matmul_tn(attention_normalized, grad_key_low)
    grad_w_value = matmul_tn(attention_normalized, grad_value_low)
    grad_normed_one = (
        matmul_nt(grad_query_low, full_query)
        + matmul_nt(grad_key_low, full_key)
        + matmul_nt(grad_value_low, full_value)
    )
    grad_normed_one, grad_gain_query, grad_gain_key = (
        lax.psum(grad_normed_one.astype(jnp.bfloat16), TENSOR).astype(jnp.float32),
        lax.psum(grad_gain_query.astype(jnp.bfloat16), TENSOR).astype(jnp.float32),
        lax.psum(grad_gain_key.astype(jnp.bfloat16), TENSOR).astype(jnp.float32),
    )
    grad_inputs_norm, grad_gain_attn = first_pull(grad_normed_one)
    input_grad = grad_resid + grad_inputs_norm
    owned = (
        lax.psum_scatter(
            grad_w_query.astype(jnp.bfloat16), GROUPS, scatter_dimension=0, tiled=True
        ).astype(jnp.float32),
        lax.psum_scatter(
            grad_w_key.astype(jnp.bfloat16), GROUPS, scatter_dimension=0, tiled=True
        ).astype(jnp.float32),
        lax.psum_scatter(
            grad_w_value.astype(jnp.bfloat16), GROUPS, scatter_dimension=0, tiled=True
        ).astype(jnp.float32),
        lax.psum_scatter(
            grad_w_output.astype(jnp.bfloat16), GROUPS, scatter_dimension=0, tiled=True
        ).astype(jnp.float32),
        lax.psum_scatter(
            grad_router.astype(jnp.bfloat16), GROUPS, scatter_dimension=0, tiled=True
        ).astype(jnp.float32),
        lax.psum_scatter(
            grad_gain_attn.astype(jnp.bfloat16),
            GROUPS,
            scatter_dimension=0,
            tiled=True,
        ).astype(jnp.float32),
        lax.psum_scatter(
            grad_gain_ffn.astype(jnp.bfloat16), GROUPS, scatter_dimension=0, tiled=True
        ).astype(jnp.float32),
        lax.psum_scatter(
            grad_gain_query.astype(jnp.bfloat16),
            GROUPS,
            scatter_dimension=0,
            tiled=True,
        ).astype(jnp.float32),
        lax.psum_scatter(
            grad_gain_key.astype(jnp.bfloat16), GROUPS, scatter_dimension=0, tiled=True
        ).astype(jnp.float32),
    )
    return (
        output[None],
        input_grad[None],
        owned[5],
        owned[0],
        owned[1],
        owned[2],
        owned[3],
        owned[7],
        owned[8],
        owned[6],
        owned[4],
        grad_w_gate,
        grad_w_up,
        grad_w_down,
    )


MESH = pl.DeviceIdType.MESH
Z_UP, Z_DOWN, Y_SIDE, X_SIDE, CORE_SIDE = range(5)

def coords():
    z, y, t = lax.axis_index(FSDP), lax.axis_index(CONTEXT), lax.axis_index(TENSOR)
    return z, y, t // 2, t % 2

def partner(z, index):
    return (z, z + 1 - 2 * (z % 2), 2 - z // 2, 3 - 3 * (z // 2))[index]

def greet(neighbours):
    barrier = pltpu.get_barrier_semaphore()
    for condition, device in neighbours:
        def tell(device=device):
            pl.semaphore_signal(barrier, inc=1, device_id=device, device_id_type=MESH)
        if condition is None: tell()
        else: pl.when(condition)(tell)
    count = sum(1 if condition is None else condition.astype(jnp.int32) for condition, device in neighbours)
    pl.semaphore_wait(barrier, count)


def gather_kernel(x_ref, out_ref, own_sem, send_sems, recv_sems):
    rows = x_ref.shape[0]; half = rows // 2
    z, y, x, c = coords()
    side = {Z_UP: (z + 1, y, 2 * x + c), Z_DOWN: (z - 1, y, 2 * x + c), Y_SIDE: (z, 1 - y, 2 * x + c),
            X_SIDE: (z, y, 2 * (1 - x) + c), CORE_SIDE: (z, y, 2 * x + 1 - c)}
    greet([(z < 3, side[Z_UP]), (z > 0, side[Z_DOWN]), (None, side[Y_SIDE]), (None, side[X_SIDE]), (None, side[CORE_SIDE])])
    def device(zz, yy, xx, cc): return (zz * 2 + yy) * 4 + xx * 2 + cc
    def place(owner, h): return out_ref.at[pl.ds(pl.multiple_of(owner * rows + h * half, half), half)]
    def copy(link, owner, h, own=False):
        src = x_ref.at[pl.ds(h * half, half)] if own else place(owner, h)
        return pltpu.make_async_remote_copy(src_ref=src, dst_ref=place(owner, h), send_sem=send_sems.at[link, owner, h],
            recv_sem=recv_sems.at[owner, h], device_id=side[link], device_id_type=MESH)
    sent = []
    def start(link, owner, h, own=False, condition=None):
        one = copy(link, owner, h, own)
        sent.append((one, condition))
        if condition is None: one.start()
        else: pl.when(condition)(one.start)
    def arrived(owner, h): copy(CORE_SIDE, owner, h).wait_recv()
    me = device(z, y, x, c)
    keep = pltpu.make_async_copy(x_ref, out_ref.at[pl.ds(pl.multiple_of(me * rows, rows), rows)], own_sem)
    keep.start()
    def stage1(i):
        zz = partner(z, i); owner = device(zz, y, x, c); own = i == 0
        if not own:
            arrived(owner, 0); arrived(owner, 1)
        for h in range(2):
            start(Z_UP, owner, h, own, (z < 3) if own else (z < 3) & (zz < z))
            start(Z_DOWN, owner, h, own, (z > 0) if own else (z > 0) & (zz > z))
        start(Y_SIDE, owner, 0, own); start(X_SIDE, owner, 1, own)
        start(Y_SIDE, owner, 1, own); start(X_SIDE, owner, 0, own)
        for h in range(2): start(CORE_SIDE, owner, h, own)
    def stage2(i):
        zz = partner(z, i)
        oy, ox = device(zz, 1 - y, x, c), device(zz, y, 1 - x, c)
        arrived(oy, 0); start(X_SIDE, oy, 0); start(CORE_SIDE, oy, 0)
        arrived(ox, 1); start(Y_SIDE, ox, 1); start(CORE_SIDE, ox, 1)
        arrived(oy, 1); start(CORE_SIDE, oy, 1)
        arrived(ox, 0); start(CORE_SIDE, ox, 0)
    def stage3(i):
        o = device(partner(z, i), 1 - y, 1 - x, c)
        for h in range(2):
            arrived(o, h); start(CORE_SIDE, o, h)
    stage1(0); stage1(1); stage2(0); stage1(2); stage2(1); stage3(0); stage1(3); stage2(2); stage3(1); stage2(3); stage3(2); stage3(3)
    for i in range(4):
        for yy in range(2):
            for xx in range(2):
                for h in range(2): arrived(device(i, yy, xx, 1 - c), h)
    keep.wait()
    for one, condition in sent:
        if condition is None: one.wait_send()
        else: pl.when(condition)(one.wait_send)

def gather_everyone(x, collective_id):
    rows, width = x.shape
    return pl.pallas_call(gather_kernel, out_shape=jax.ShapeDtypeStruct((32 * rows, width), x.dtype),
        in_specs=[pl.BlockSpec(memory_space=pl.ANY)], out_specs=pl.BlockSpec(memory_space=pl.ANY),
        scratch_shapes=[pltpu.SemaphoreType.DMA, pltpu.SemaphoreType.DMA((5, 32, 2)), pltpu.SemaphoreType.DMA((32, 2))],
        compiler_params=pltpu.CompilerParams(collective_id=collective_id, has_side_effects=True))(x)

def scatter_kernel(part_ref, out_ref, mine, core_in, first_in, second_in, line_in, load_sem, core_sem, first_sem, second_sem, line_send, line_recv):
    rows = out_ref.shape[0]; half = rows // 2
    z, y, x, c = coords()
    up, down = (z + 1, y, 2 * x + c), (z - 1, y, 2 * x + c)
    y_side, x_side, core_side = (z, 1 - y, 2 * x + c), (z, y, 2 * (1 - x) + c), (z, y, 2 * x + 1 - c)
    greet([(z < 3, up), (z > 0, down), (None, y_side), (None, x_side), (None, core_side)])
    f32 = jnp.float32
    def spot(zz, yy, xx): return (zz * 2 + yy) * 2 + xx
    def rows_of(zz, yy, xx, cc): return part_ref.at[pl.ds(pl.multiple_of((spot(zz, yy, xx) * 2 + cc) * rows, rows), rows)]
    def remote(src, dst, send, recv, device):
        return pltpu.make_async_remote_copy(src_ref=src, dst_ref=dst, send_sem=send, recv_sem=recv, device_id=device, device_id_type=MESH)
    def piece(zz, yy, xx, h): return mine.at[spot(zz, yy, xx), pl.ds(h * half, half)]
    def load(zz, yy, xx):
        s = spot(zz, yy, xx)
        return pltpu.make_async_copy(rows_of(zz, yy, xx, c), mine.at[s], load_sem.at[s])
    def over_core(zz, yy, xx):
        s = spot(zz, yy, xx)
        return remote(rows_of(zz, yy, xx, 1 - c), core_in.at[s], core_sem.at[0, s], core_sem.at[1, s], core_side)
    def first(h, zz, other):
        src = piece(zz, other, 1 - x, 0) if h == 0 else piece(zz, 1 - y, other, 1)
        s = zz * 2 + other
        return remote(src, first_in.at[h, s], first_sem.at[0, h, s], first_sem.at[1, h, s], x_side if h == 0 else y_side)
    def second(h, zz):
        src = piece(zz, 1 - y, x, 0) if h == 0 else piece(zz, y, 1 - x, 1)
        return remote(src, second_in.at[h, zz], second_sem.at[0, h, zz], second_sem.at[1, h, zz], y_side if h == 0 else x_side)
    def line(h, zz, way):
        return remote(piece(zz, y, x, h), line_in.at[way, zz, h], line_send.at[zz, h], line_recv.at[way, zz, h], up if way == 0 else down)
    def add(s, h, arrived):
        at = (s, pl.ds(h * half, half))
        mine[at] = (mine[at].astype(f32) + arrived[...].astype(f32)).astype(mine.dtype)
    sent = []
    order = [(1 - y, 1 - x), (1 - y, x), (y, 1 - x), (y, x)]
    for i in (3, 2, 1, 0):
        for yy, xx in order:
            one = over_core(partner(z, i), yy, xx); one.start(); sent.append(one)
            load(partner(z, i), yy, xx).start()
    def stage_core(i):
        zz = partner(z, i)
        for n, (yy, xx) in enumerate(order):
            load(zz, yy, xx).wait(); over_core(zz, yy, xx).wait_recv()
            s = spot(zz, yy, xx)
            for h in range(2): add(s, h, core_in.at[s, pl.ds(h * half, half)])
            go = []
            if n in (0, 2): go.append(first(0, zz, yy))
            if n in (0, 1): go.append(first(1, zz, xx))
            for one in go: one.start(); sent.append(one)
    def stage_first(i):
        zz = partner(z, i)
        for n in range(2):
            for h, other in ((0, (1 - y, y)[n]), (1, (1 - x, x)[n])):
                first(h, zz, other).wait_recv()
                s = spot(zz, other, x) if h == 0 else spot(zz, y, other)
                add(s, h, first_in.at[h, zz * 2 + other])
                if n == 0:
                    one = second(h, zz); one.start(); sent.append(one)
    def stage_second(i):
        zz = partner(z, i)
        for h in range(2):
            second(h, zz).wait_recv()
            add(spot(zz, y, x), h, second_in.at[h, zz])
    def stage_line(i):
        zz = partner(z, i); s = spot(zz, y, x)
        for h in range(2):
            for way, from_side, toward in ((0, z > 0, zz > z), (1, z < 3, zz < z)):
                @pl.when(from_side & (toward | (zz == z)) if i == 0 else from_side & toward)
                def _(h=h, way=way):
                    line(h, zz, way).wait_recv()
                    add(s, h, line_in.at[way, zz, h])
                if i > 0:
                    @pl.when(toward)
                    def _(h=h, way=way): line(h, zz, way).start()
    stage_core(3); stage_core(2); stage_first(3); stage_core(1); stage_first(2); stage_second(3)
    stage_core(0); stage_first(1); stage_second(2); stage_line(3); stage_first(0); stage_second(1); stage_line(2)
    stage_second(0); stage_line(1); stage_line(0)
    out_ref[...] = mine[spot(z, y, x)].astype(out_ref.dtype)
    for one in sent: one.wait_send()
    for i in (3, 2, 1):
        zz = partner(z, i)
        for h in range(2):
            line(h, zz, 0).wait_send()

def scatter_everyone(part, collective_id):
    total, width = part.shape; rows = total // 32; half = rows // 2
    dt = part.dtype; D = pltpu.SemaphoreType.DMA
    return pl.pallas_call(scatter_kernel, out_shape=jax.ShapeDtypeStruct((rows, width), jnp.float32),
        in_specs=[pl.BlockSpec(memory_space=pl.ANY)], out_specs=pl.BlockSpec(memory_space=pltpu.VMEM),
        scratch_shapes=[pltpu.VMEM((16, rows, width), dt), pltpu.VMEM((16, rows, width), dt), pltpu.VMEM((2, 8, half, width), dt),
            pltpu.VMEM((2, 4, half, width), dt), pltpu.VMEM((2, 4, 2, half, width), dt),
            D((16,)), D((2, 16)), D((2, 2, 8)), D((2, 2, 4)), D((4, 2)), D((2, 4, 2))],
        compiler_params=pltpu.CompilerParams(collective_id=collective_id, has_side_effects=True, vmem_limit_bytes=48 << 20))(part)

def groups_kernel(splits, *refs):
    count = len(splits)
    ins, outs = refs[:count], refs[count:2 * count]
    keep_sems, send_sems, recv_sems = refs[2 * count:]
    z, y, x, c = coords()
    t = 2 * x + c
    side = {Z_UP: (z + 1, y, t), Z_DOWN: (z - 1, y, t), Y_SIDE: (z, 1 - y, t)}
    greet([(z < 3, side[Z_UP]), (z > 0, side[Z_DOWN]), (None, side[Y_SIDE])])
    sent = []
    def place(k, owner, h):
        rows = ins[k].shape[0]
        first, size = (0, splits[k]) if h == 0 else (splits[k], rows - splits[k])
        return outs[k].at[pl.ds(pl.multiple_of(owner * rows + first, 16), size)], ins[k].at[pl.ds(first, size)]
    def copy(link, k, owner, h, own=False):
        dst, src = place(k, owner, h)
        return pltpu.make_async_remote_copy(src_ref=src if own else dst, dst_ref=dst, send_sem=send_sems.at[link, k, owner, h],
            recv_sem=recv_sems.at[k, owner, h], device_id=side[link], device_id_type=MESH)
    def halves(k): return (0, 1) if splits[k] < ins[k].shape[0] else (0,)
    def start(link, k, owner, h, own=False, condition=None):
        if h not in halves(k): return
        one = copy(link, k, owner, h, own)
        sent.append((one, condition))
        if condition is None: one.start()
        else: pl.when(condition)(one.start)
    def arrived(k, owner, h):
        if h in halves(k): copy(Y_SIDE, k, owner, h).wait_recv()
    def along(k, owner, h, zz, own=False):
        start(Z_UP, k, owner, h, own, (z < 3) & (zz <= z)); start(Z_DOWN, k, owner, h, own, (z > 0) & (zz >= z))
    kept = []
    me = z * 2 + y
    for k in range(count):
        along(k, me, 0, z, True); start(Y_SIDE, k, me, 1, True); start(Y_SIDE, k, me, 0, True); along(k, me, 1, z, True)
        rows = ins[k].shape[0]
        one = pltpu.make_async_copy(ins[k], outs[k].at[pl.ds(pl.multiple_of(me * rows, 16), rows)], keep_sems.at[k])
        one.start(); kept.append(one)
    for k in range(count):
        for i in range(4):
            zz = partner(z, i)
            near, far = zz * 2 + y, zz * 2 + 1 - y
            if i > 0:
                arrived(k, near, 0); along(k, near, 0, zz); start(Y_SIDE, k, near, 0)
                arrived(k, near, 1); along(k, near, 1, zz)
            arrived(k, far, 1); along(k, far, 1, zz)
    for k in range(count):
        for i in range(4): arrived(k, partner(z, i) * 2 + 1 - y, 0)
    for one in kept: one.wait()
    for one, condition in sent:
        if condition is None: one.wait_send()
        else: pl.when(condition)(one.wait_send)

def gather_groups(arrays, splits, collective_id):
    count = len(arrays); D = pltpu.SemaphoreType.DMA
    return pl.pallas_call(functools.partial(groups_kernel, splits),
        out_shape=[jax.ShapeDtypeStruct((8 * a.shape[0], a.shape[1]), a.dtype) for a in arrays],
        in_specs=[pl.BlockSpec(memory_space=pl.ANY)] * count, out_specs=[pl.BlockSpec(memory_space=pl.ANY)] * count,
        scratch_shapes=[D((count,)), D((3, count, 8, 2)), D((count, 8, 2))],
        compiler_params=pltpu.CompilerParams(collective_id=collective_id, has_side_effects=True))(*arrays)

def tensor_gather_kernel(x_ref, out_ref, keep_sem, send_sems, recv_sems):
    z, y, x, c = coords()
    x_side, core_side = (z, y, 2 * (1 - x) + c), (z, y, 2 * x + 1 - c)
    greet([(None, x_side), (None, core_side)])
    def copy(n, owner, device, own=False):
        return pltpu.make_async_remote_copy(src_ref=x_ref if own else out_ref.at[owner], dst_ref=out_ref.at[owner], send_sem=send_sems.at[n],
            recv_sem=recv_sems.at[owner], device_id=device, device_id_type=MESH)
    me, across, beside, last = 2 * x + c, 2 * (1 - x) + c, 2 * x + 1 - c, 2 * (1 - x) + 1 - c
    a, b, d = copy(0, me, x_side, True), copy(1, me, core_side, True), copy(2, across, core_side)
    a.start(); b.start()
    keep = pltpu.make_async_copy(x_ref, out_ref.at[me], keep_sem); keep.start()
    copy(0, across, x_side).wait_recv(); d.start()
    copy(0, beside, x_side).wait_recv(); copy(0, last, x_side).wait_recv()
    keep.wait(); a.wait_send(); b.wait_send(); d.wait_send()

def gather_tensor(x, collective_id):
    D = pltpu.SemaphoreType.DMA
    return pl.pallas_call(tensor_gather_kernel, out_shape=jax.ShapeDtypeStruct((4, *x.shape), x.dtype),
        in_specs=[pl.BlockSpec(memory_space=pl.ANY)], out_specs=pl.BlockSpec(memory_space=pl.ANY),
        scratch_shapes=[D, D((3,)), D((4,))],
        compiler_params=pltpu.CompilerParams(collective_id=collective_id, has_side_effects=True))(x)

def tensor_scatter_kernel(part_ref, out_ref, mine, core_in, line_in, sems, recv):
    z, y, x, c = coords()
    x_side, core_side = (z, y, 2 * (1 - x) + c), (z, y, 2 * x + 1 - c)
    greet([(None, x_side), (None, core_side)])
    rows = out_ref.shape[0]; f32 = jnp.float32
    def rows_of(xx, cc): return part_ref.at[pl.ds(pl.multiple_of((2 * xx + cc) * rows, rows), rows)]
    def over_core(n, xx):
        return pltpu.make_async_remote_copy(src_ref=rows_of(xx, 1 - c), dst_ref=core_in.at[n], send_sem=sems.at[n], recv_sem=recv.at[n],
            device_id=core_side, device_id_type=MESH)
    a, b = over_core(0, 1 - x), over_core(1, x)
    a.start(); b.start()
    a.wait_recv()
    mine[...] = (rows_of(1 - x, c)[...].astype(f32) + core_in[0].astype(f32)).astype(mine.dtype)
    d = pltpu.make_async_remote_copy(src_ref=mine, dst_ref=line_in, send_sem=sems.at[2], recv_sem=recv.at[2], device_id=x_side, device_id_type=MESH)
    d.start(); b.wait_recv()
    out_ref[...] = rows_of(x, c)[...].astype(f32) + core_in[1].astype(f32)
    d.wait_recv()
    out_ref[...] += line_in[...].astype(f32)
    a.wait_send(); b.wait_send(); d.wait_send()

def scatter_tensor(part, collective_id):
    D = pltpu.SemaphoreType.DMA; rows = part.shape[0] // 4; width = part.shape[1]
    return pl.pallas_call(tensor_scatter_kernel, out_shape=jax.ShapeDtypeStruct((rows, width), jnp.float32),
        in_specs=[pl.BlockSpec(memory_space=pltpu.VMEM)], out_specs=pl.BlockSpec(memory_space=pltpu.VMEM),
        scratch_shapes=[pltpu.VMEM((rows, width), part.dtype), pltpu.VMEM((2, rows, width), part.dtype), pltpu.VMEM((rows, width), part.dtype), D((3,)), D((3,))],
        compiler_params=pltpu.CompilerParams(collective_id=collective_id, has_side_effects=True, vmem_limit_bytes=24 << 20))(part)


def gathered_local(
    hidden_in,
    attn_gain,
    w_query,
    key_weight,
    value_weight,
    w_output,
    query_gain,
    key_gain,
    ffn_gain,
    router,
    gate_weight,
    up_weight,
    down_weight,
    routes,
    segments,
    cotangent,
):
    bf16, f32 = jnp.bfloat16, jnp.float32
    context_size = lax.axis_size(CONTEXT)
    tensor_size = lax.axis_size(TENSOR)
    group_count = lax.axis_size(FSDP) * context_size
    fsdp_rank = lax.axis_index(FSDP)
    context_rank = lax.axis_index(CONTEXT)
    tensor_rank = lax.axis_index(TENSOR)
    group_rank = fsdp_rank * context_size + context_rank
    row_count, width = hidden_in.shape[1:]
    own_count = row_count // tensor_size
    local_experts, _, hidden_width = gate_weight.shape
    experts_total = router.shape[1]
    capacity = 9 * row_count * TOPK // (8 * experts_total)

    pieces = (router, attn_gain, ffn_gain, query_gain, key_gain, routes, segments)
    small = jnp.concatenate([piece.astype(bf16).reshape(-1) for piece in pieces])
    small = jnp.pad(small, (0, -small.size % 2048)).reshape(-1, 128)
    qkv_weight = jnp.concatenate([w_query, key_weight, value_weight], axis=1)
    small, qkv_full, full_output = gather_groups((small, qkv_weight, w_output), (small.shape[0], 208, 208), 1)
    small = small.reshape(group_count, -1)
    parts, at = [], 0
    for piece in pieces:
        parts.append(small[:, at : at + piece.size])
        at += piece.size
    full_router = parts[0].reshape(width, experts_total)
    gain_attn, gain_ffn, gain_query, gain_key = (
        part.reshape(-1).astype(f32) for part in parts[1:5]
    )
    all_routes = parts[5].astype(jnp.int32).reshape(group_count, row_count, TOPK)
    seg_all = lax.dynamic_slice_in_dim(
        parts[6].astype(jnp.int32), fsdp_rank * context_size, context_size, 0
    ).reshape(-1)

    own_start = tensor_rank * own_count
    grad_out_own = lax.dynamic_slice_in_dim(cotangent[0], own_start, own_count, 0)
    grad_out_all = lax.all_gather(grad_out_own, EVERYONE, axis=0, tiled=True)

    query_width = w_query.shape[1]
    local_heads = query_width // HEAD_SIZE
    input_rows = hidden_in[0].astype(f32)
    start_row = context_rank * row_count
    positions = lax.dynamic_slice_in_dim(doc_positions(seg_all), start_row, row_count)
    cosine_table, sine_table = rope_tables(positions, HEAD_SIZE)
    query_seg = segments[0]
    query_index = start_row + jnp.arange(row_count, dtype=jnp.int32)
    other_start = (1 - context_rank) * row_count
    key_ids = jnp.concatenate([query_index, query_index - start_row + other_start])
    seg_keys = jnp.concatenate([query_seg, lax.dynamic_slice_in_dim(seg_all, other_start, row_count)])
    key_block = row_count

    def query_finish(raw_values, gain_vec):
        return qk_finish(raw_values, gain_vec, cosine_table[:, None, :], sine_table[:, None, :])

    def key_finish(raw_values, gain_vec):
        return qk_finish(raw_values, gain_vec, cosine_table, sine_table)

    normed_one = rms_scale(input_rows, gain_attn).astype(bf16)
    raw = matmul(normed_one, qkv_full)
    query_unrotated = raw[:, :query_width].reshape(row_count, local_heads, HEAD_SIZE)
    key_unrotated = raw[:, query_width : query_width + HEAD_SIZE]
    value_raw = raw[:, query_width + HEAD_SIZE :]
    query_f, query_pull = jax.vjp(query_finish, query_unrotated, gain_query)
    key_f, key_pull = jax.vjp(key_finish, key_unrotated, gain_key)
    query_vectors = query_f.astype(bf16)
    own_kv = jnp.concatenate([key_f, value_raw], axis=1).astype(bf16)
    swap = ((0, 1), (1, 0))
    kv_all = jnp.concatenate([own_kv, lax.ppermute(own_kv, CONTEXT, swap)], axis=0)
    keys_all, values_all = kv_all[:, :HEAD_SIZE], kv_all[:, HEAD_SIZE:]
    heads_full, log_total = attention_forward(
        query_vectors, keys_all, values_all, seg_keys, query_seg, query_index, key_ids, key_block
    )
    heads_low = heads_full.reshape(row_count, query_width).astype(bf16)
    attn_own = scatter_tensor(matmul_nt(heads_low, full_output).astype(bf16), 2)
    input_own = lax.dynamic_slice_in_dim(hidden_in[0], own_start, own_count, 0).astype(f32)
    residual_own = input_own + attn_own
    second_f, second_pull = jax.vjp(rms_scale, residual_own, gain_ffn)
    normed_own = second_f.astype(bf16)
    normed_all = gather_everyone(normed_own, 3)

    expert_ids = jnp.arange(experts_total, dtype=jnp.int32)

    def dense_gates(normed, chosen):
        scores = jnp.where(chosen, matmul(normed, full_router), NEGATIVE)
        return jnp.where(chosen, jax.nn.softmax(scores, axis=-1), 0.0)

    chosen_all = jnp.any(all_routes[..., None] == expert_ids, axis=2)
    first_expert = group_rank * local_experts
    chosen_local = lax.dynamic_slice_in_dim(chosen_all, first_expert, local_experts, 2)
    slots = earlier_counts(
        chosen_local.transpose(1, 0, 2).reshape(row_count, group_count * local_experts)
    )
    slots = slots.reshape(row_count, group_count, local_experts).transpose(1, 0, 2)
    kept = chosen_local & (slots < capacity)
    gates_all = dense_gates(normed_all, chosen_all.reshape(-1, experts_total))
    gates_local = lax.dynamic_slice_in_dim(gates_all, first_expert, local_experts, 1)
    kept = kept.reshape(-1, local_experts)
    gates_kept = jnp.where(kept, gates_local, 0.0)
    chosen_own = lax.dynamic_slice_in_dim(
        jnp.any(routes[0][..., None] == expert_ids, axis=1), own_start, own_count, 0
    )
    gates_own = dense_gates(normed_own, chosen_own)

    token_count = group_count * row_count
    units = local_experts * hidden_width
    gate_flat = gate_weight.transpose(1, 0, 2).reshape(width, units)
    up_flat = up_weight.transpose(1, 0, 2).reshape(width, units)
    down_flat = down_weight.reshape(units, width)
    gate_in = matmul(normed_all, gate_flat)
    up_in = matmul(normed_all, up_flat)
    grad_mid = matmul_nt(grad_out_all, down_flat)

    def per_unit(values):
        return jnp.broadcast_to(values[:, :, None], (token_count, local_experts, hidden_width)).reshape(
            token_count, units
        )

    gate_units = per_unit(gates_kept)
    sigmoid_gate = jax.nn.sigmoid(gate_in)
    silu_gate = gate_in * sigmoid_gate
    hidden_middle = silu_gate * up_in
    hidden_gated = (hidden_middle * gate_units).astype(bf16)
    grad_gates = jnp.sum(
        (hidden_middle * grad_mid).reshape(token_count, local_experts, hidden_width), axis=2
    )
    grad_gates = jnp.where(kept, grad_gates, 0.0).astype(bf16)
    grad_hidden = grad_mid * gate_units
    gate_grad = (
        grad_hidden * up_in * sigmoid_gate * (1.0 + gate_in * (1.0 - sigmoid_gate))
    ).astype(bf16)
    up_grad = (grad_hidden * silu_gate).astype(bf16)
    dn_part = (matmul_nt(gate_grad, gate_flat) + matmul_nt(up_grad, up_flat)).astype(bf16)
    placed = lax.dynamic_update_slice(
        jnp.zeros((token_count, tensor_size * experts_total), bf16),
        grad_gates,
        (0, tensor_rank * experts_total + first_expert),
    )
    scattered = scatter_everyone(jnp.concatenate([dn_part, placed], axis=1), 4)
    moe_part = matmul(hidden_gated, down_flat).astype(bf16)
    moe_own = lax.psum_scatter(moe_part, EVERYONE, scatter_dimension=0, tiled=True).astype(f32)
    grad_w_down = matmul_tn(hidden_gated, grad_out_all).reshape(down_weight.shape)
    grad_w_gate = jnp.einsum(
        "td,tju->jdu",
        normed_all,
        gate_grad.reshape(token_count, local_experts, hidden_width),
        preferred_element_type=f32,
    )
    grad_w_up = jnp.einsum(
        "td,tju->jdu",
        normed_all,
        up_grad.reshape(token_count, local_experts, hidden_width),
        preferred_element_type=f32,
    )

    gates_grad_own = jnp.sum(
        scattered[:, width:].reshape(own_count, tensor_size, experts_total), axis=1
    )
    grad_selected = gates_own * (
        gates_grad_own - jnp.sum(gates_own * gates_grad_own, axis=1, keepdims=True)
    )
    grad_logits = grad_selected.astype(bf16)
    grad_normed_two = scattered[:, :width] + matmul_nt(grad_logits, full_router)
    grad_resid_norm, grad_gain_ffn = second_pull(grad_normed_two)
    grad_resid_own = grad_out_own.astype(f32) + grad_resid_norm
    message = jnp.concatenate(
        [grad_resid_own.astype(bf16), jnp.pad(grad_logits, ((0, 0), (0, 128 - experts_total)))], axis=1
    )
    extra = jnp.pad(grad_gain_ffn.astype(bf16)[None], ((0, 15), (0, 128)))
    message = gather_tensor(jnp.concatenate([message, extra], axis=0), 5)
    grad_attn = message[:, :own_count, :width].reshape(row_count, width)
    group_logits = message[:, :own_count, width:].reshape(row_count, 128)
    grad_gain_ffn = jnp.sum(message[:, own_count, :width].astype(f32), axis=0)
    normed_group = lax.dynamic_slice_in_dim(normed_all, group_rank * row_count, row_count, 0)
    grad_router = matmul_tn(normed_group, group_logits)
    output = lax.all_gather((residual_own + moe_own).astype(bf16), TENSOR, axis=0, tiled=True)
    extra = jnp.where(jnp.arange(128) == experts_total, grad_gain_ffn[:, None], grad_router)
    grad_w_output = jnp.concatenate([matmul_tn(grad_attn, heads_low), extra], axis=1)
    grad_w_output = lax.psum_scatter(
        grad_w_output.astype(bf16), GROUPS, scatter_dimension=0, tiled=True
    ).astype(f32)
    grad_heads = (
        matmul(grad_attn, full_output).astype(bf16).reshape(row_count, local_heads, HEAD_SIZE)
    )
    row_delta = jnp.sum(grad_heads.astype(f32) * heads_full, axis=2).T
    grad_query, grad_key_terms, grad_value_terms = attention_backward(
        query_vectors,
        keys_all,
        values_all,
        seg_keys,
        query_seg,
        query_index,
        key_ids,
        key_block,
        log_total,
        grad_heads,
        row_delta,
    )
    grad_kv = jnp.concatenate([grad_key_terms, grad_value_terms], axis=1)
    grad_kv = grad_kv[:row_count] + lax.ppermute(
        grad_kv[row_count:].astype(bf16), CONTEXT, swap
    ).astype(f32)
    grad_query_raw, grad_gain_query = query_pull(grad_query)
    grad_key_raw, grad_gain_key = key_pull(grad_kv[:, :HEAD_SIZE])
    grad_raw = jnp.concatenate(
        [grad_query_raw.reshape(row_count, query_width), grad_key_raw, grad_kv[:, HEAD_SIZE:]],
        axis=1,
    ).astype(bf16)
    grad_normed_part = matmul_nt(grad_raw, qkv_full)
    ignored, whole_pull = jax.vjp(rms_scale, input_rows, gain_attn)
    gain_rows = jnp.stack(
        [whole_pull(grad_normed_part)[1], jnp.pad(jnp.concatenate([grad_gain_query, grad_gain_key]), (0, width - 256))]
    )
    message = jnp.pad(
        grad_normed_part.astype(bf16).reshape(tensor_size, own_count, width), ((0, 0), (0, 16), (0, 0))
    )
    message = lax.dynamic_update_slice(message, gain_rows.astype(bf16)[None], (0, own_count, 0))
    message = scatter_tensor(message.reshape(-1, width), 6)
    ignored, first_pull = jax.vjp(rms_scale, input_own, gain_attn)
    grad_inputs_norm, ignored = first_pull(message[:own_count])
    message = jnp.concatenate([grad_resid_own + grad_inputs_norm, message[own_count:]], axis=0)
    message = gather_tensor(message.astype(bf16), 7).astype(f32)
    input_grad = message[:, :own_count].reshape(row_count, width)
    gain_rows = message[0, own_count : own_count + 2]
    head_gains = jnp.pad(
        gain_rows[1, :256].reshape(2, group_count, -1),
        ((0, 0), (0, 0), (0, (width - 128) // group_count)),
    ).reshape(2, width)
    extra = jnp.pad(jnp.stack([gain_rows[0], head_gains[0], head_gains[1]], axis=1), ((0, 0), (0, 125)))
    grad_qkv = jnp.concatenate([matmul_tn(normed_one, grad_raw), extra], axis=1)
    grad_qkv = lax.psum_scatter(
        grad_qkv.astype(bf16), GROUPS, scatter_dimension=0, tiled=True
    ).astype(f32)
    value_at, extra_at = query_width + HEAD_SIZE, query_width + 2 * HEAD_SIZE
    return (
        output[None],
        input_grad[None],
        grad_qkv[:, extra_at],
        grad_qkv[:, :query_width],
        grad_qkv[:, query_width:value_at],
        grad_qkv[:, value_at:extra_at],
        grad_w_output[:, :query_width],
        grad_qkv[: query_gain.shape[0], extra_at + 1],
        grad_qkv[: key_gain.shape[0], extra_at + 2],
        grad_w_output[:, query_width + experts_total],
        grad_w_output[:, query_width : query_width + experts_total],
        grad_w_gate,
        grad_w_up,
        grad_w_down,
    )


def local(*arrays):
    sizes = tuple(lax.axis_size(name) for name in EVERYONE)
    return (gathered_local if sizes == (4, 2, 4) else routed_local)(*arrays)


def solution(mesh):
    in_specs = (
        P(FSDP, CONTEXT, None),
        P(GROUPS),
        P(GROUPS, TENSOR),
        P(GROUPS, TENSOR),
        P(GROUPS, TENSOR),
        P(GROUPS, TENSOR),
        P(GROUPS),
        P(GROUPS),
        P(GROUPS),
        P(GROUPS, None),
        P(GROUPS, None, TENSOR),
        P(GROUPS, None, TENSOR),
        P(GROUPS, TENSOR, None),
        P(FSDP, CONTEXT, None),
        P(FSDP, CONTEXT),
        P(FSDP, CONTEXT, None),
    )
    out_specs = (
        P(FSDP, CONTEXT, None),
        P(FSDP, CONTEXT, None),
        P(GROUPS),
        P(GROUPS, TENSOR),
        P(GROUPS, TENSOR),
        P(GROUPS, TENSOR),
        P(GROUPS, TENSOR),
        P(GROUPS),
        P(GROUPS),
        P(GROUPS),
        P(GROUPS, None),
        P(GROUPS, None, TENSOR),
        P(GROUPS, None, TENSOR),
        P(GROUPS, TENSOR, None),
    )
    return jax.shard_map(local, mesh=mesh, in_specs=in_specs, out_specs=out_specs, check_vma=False)
```

```python
import functools
import math

import jax
import jax.numpy as jnp
from jax import lax
from jax.experimental import pallas as pl
from jax.experimental.pallas import tpu as pltpu
from jax.sharding import PartitionSpec as P

HEAD_SIZE = 128
TOPK = 8
FSDP, CONTEXT, TENSOR = "fsdp", "context", "tensor"
GROUPS = (FSDP, CONTEXT)
EVERYONE = (FSDP, CONTEXT, TENSOR)


EPSILON = 1e-06
ROPE_BASE = 1000000.0
NEGATIVE = -1e30


def rms_scale(values, gain_vec):
    return (
        values * lax.rsqrt(jnp.mean(values * values, axis=-1, keepdims=True) + EPSILON) * gain_vec
    )


def rotate(values):
    half_width = values.shape[-1] // 2
    return jnp.concatenate([-values[..., half_width:], values[..., :half_width]], axis=-1)


def rope_tables(positions, head_width):
    step_index = jnp.arange(head_width // 2, dtype=jnp.float32)
    inverse = jnp.exp(step_index * (-2.0 * math.log(ROPE_BASE) / head_width))
    angles = positions.astype(jnp.float32)[:, None] * inverse[None, :]
    cosine_table = jnp.cos(angles)
    sine_table = jnp.sin(angles)
    return (
        jnp.concatenate([cosine_table, cosine_table], -1),
        jnp.concatenate([sine_table, sine_table], -1),
    )


def doc_positions(segment):
    token_index = jnp.arange(segment.shape[0], dtype=jnp.int32)
    smaller = (segment[None, :] < segment[:, None]).astype(jnp.int32)
    return token_index - jnp.sum(smaller, axis=1)


def earlier_counts(chosen):
    rows = chosen.shape[0]
    row_id = lax.broadcasted_iota(jnp.int32, (rows, rows), 0)
    col_id = lax.broadcasted_iota(jnp.int32, (rows, rows), 1)
    earlier = (col_id < row_id).astype(jnp.bfloat16)
    return matmul(earlier, chosen.astype(jnp.bfloat16))


def qk_finish(raw_values, gain_vec, cosine_table, sine_table):
    normed = rms_scale(raw_values, gain_vec)
    return normed * cosine_table + rotate(normed) * sine_table


def matmul(left_side, right_side):
    return jnp.dot(left_side, right_side, preferred_element_type=jnp.float32)


def matmul_nt(left_side, right_side):
    return lax.dot_general(
        left_side, right_side, (((1,), (1,)), ((), ())), preferred_element_type=jnp.float32
    )


def matmul_tn(left_side, right_side):
    return lax.dot_general(
        left_side, right_side, (((0,), (0,)), ((), ())), preferred_element_type=jnp.float32
    )


def block_scores(query_vectors, keys_all, seg_all, query_seg, query_index, key_ids, block_id, key_block):
    leading_row = block_id * key_block
    keys_part = lax.dynamic_slice_in_dim(keys_all, leading_row, key_block, 0)
    seg_part = lax.dynamic_slice_in_dim(seg_all, leading_row, key_block, 0)
    key_index = lax.dynamic_slice_in_dim(key_ids, leading_row, key_block, 0)
    score_scale = query_vectors.shape[2] ** (-0.5)
    scores = (
        jnp.einsum("qhd,kd->hqk", query_vectors, keys_part, preferred_element_type=jnp.float32)
        * score_scale
    )
    allowed = (query_seg[:, None] == seg_part[None, :]) & (
        key_index[None, :] <= query_index[:, None]
    )
    return (scores, allowed[None, :, :], keys_part)


def attention_forward(
    query_vectors, keys_all, values_all, seg_all, query_seg, query_index, key_ids, key_block
):
    row_count, head_count, head_width = query_vectors.shape
    block_count = keys_all.shape[0] // key_block

    def stats_step(running, block_id):
        run_max, run_sum = running
        scores, allowed, unused = block_scores(
            query_vectors, keys_all, seg_all, query_seg, query_index, key_ids, block_id, key_block
        )
        masked = jnp.where(allowed, scores, NEGATIVE)
        new_max = jnp.maximum(run_max, jnp.max(masked, axis=2))
        weights = jnp.where(allowed, jnp.exp(masked - new_max[:, :, None]), 0.0)
        run_sum = run_sum * jnp.exp(run_max - new_max) + jnp.sum(weights, axis=2)
        return ((new_max, run_sum), None)

    start_state = (
        jnp.full((head_count, row_count), NEGATIVE, jnp.float32),
        jnp.zeros((head_count, row_count), jnp.float32),
    )
    (run_max, run_sum), ignored = lax.scan(
        stats_step, start_state, jnp.arange(block_count, dtype=jnp.int32)
    )
    log_total = run_max + jnp.log(run_sum)

    def value_step(accumulated, block_id):
        scores, allowed, unused = block_scores(
            query_vectors, keys_all, seg_all, query_seg, query_index, key_ids, block_id, key_block
        )
        prob_block = jnp.where(allowed, jnp.exp(scores - log_total[:, :, None]), 0.0).astype(
            jnp.bfloat16
        )
        values_part = lax.dynamic_slice_in_dim(values_all, block_id * key_block, key_block, 0)
        accumulated = accumulated + jnp.einsum(
            "hqk,kd->qhd", prob_block, values_part, preferred_element_type=jnp.float32
        )
        return (accumulated, None)

    heads_full, ignored = lax.scan(
        value_step,
        jnp.zeros((row_count, head_count, head_width), jnp.float32),
        jnp.arange(block_count, dtype=jnp.int32),
    )
    return (heads_full, log_total)


def attention_backward(
    query_vectors,
    keys_all,
    values_all,
    seg_all,
    query_seg,
    query_index,
    key_ids,
    key_block,
    log_total,
    grad_heads,
    row_delta,
):
    row_count, head_count, head_width = query_vectors.shape
    block_count = keys_all.shape[0] // key_block
    score_scale = head_width ** (-0.5)

    def grad_step(grad_query, block_id):
        scores, allowed, keys_part = block_scores(
            query_vectors, keys_all, seg_all, query_seg, query_index, key_ids, block_id, key_block
        )
        values_part = lax.dynamic_slice_in_dim(values_all, block_id * key_block, key_block, 0)
        prob_block = jnp.where(allowed, jnp.exp(scores - log_total[:, :, None]), 0.0)
        grad_prob = jnp.einsum(
            "qhd,kd->hqk", grad_heads, values_part, preferred_element_type=jnp.float32
        )
        grad_score = (prob_block * (grad_prob - row_delta[:, :, None])).astype(jnp.bfloat16)
        grad_query = (
            grad_query
            + jnp.einsum("hqk,kd->qhd", grad_score, keys_part, preferred_element_type=jnp.float32)
            * score_scale
        )
        grad_key = (
            jnp.einsum("hqk,qhd->kd", grad_score, query_vectors, preferred_element_type=jnp.float32)
            * score_scale
        )
        grad_value = jnp.einsum(
            "hqk,qhd->kd",
            prob_block.astype(jnp.bfloat16),
            grad_heads,
            preferred_element_type=jnp.float32,
        )
        return (grad_query, (grad_key, grad_value))

    grad_query, (grad_key, grad_value) = lax.scan(
        grad_step,
        jnp.zeros((row_count, head_count, head_width), jnp.float32),
        jnp.arange(block_count, dtype=jnp.int32),
    )
    return (grad_query, grad_key.reshape(-1, head_width), grad_value.reshape(-1, head_width))


def to_experts(buffer):
    return lax.all_to_all(buffer, GROUPS, split_axis=0, concat_axis=1, tiled=True)


def from_experts(result_rows):
    return lax.all_to_all(result_rows, GROUPS, split_axis=1, concat_axis=0, tiled=True)


def pick_pairs(buffer, target, row_count):
    model_width = buffer.shape[2]
    flat_rows = jnp.concatenate(
        [buffer.reshape(-1, model_width), jnp.zeros((1, model_width), buffer.dtype)], axis=0
    )
    return flat_rows[target].reshape(row_count, TOPK, model_width)


def routed_local(
    hidden_in,
    attn_gain,
    w_query,
    key_weight,
    value_weight,
    w_output,
    query_gain,
    key_gain,
    ffn_gain,
    router,
    gate_weight,
    up_weight,
    down_weight,
    routes,
    segments,
    cotangent,
):
    context_rank = lax.axis_index(CONTEXT)
    input_rows = hidden_in[0].astype(jnp.float32)
    row_count, model_width = input_rows.shape
    gathered = (
        lax.all_gather(w_query, GROUPS, axis=0, tiled=True),
        lax.all_gather(key_weight, GROUPS, axis=0, tiled=True),
        lax.all_gather(value_weight, GROUPS, axis=0, tiled=True),
        lax.all_gather(w_output, GROUPS, axis=0, tiled=True),
        lax.all_gather(router, GROUPS, axis=0, tiled=True),
        lax.all_gather(attn_gain, GROUPS, axis=0, tiled=True),
        lax.all_gather(ffn_gain, GROUPS, axis=0, tiled=True),
        lax.all_gather(query_gain, GROUPS, axis=0, tiled=True),
        lax.all_gather(key_gain, GROUPS, axis=0, tiled=True),
    )
    full_query, full_key, full_value, full_output, full_router = (
        gathered[0],
        gathered[1],
        gathered[2],
        gathered[3],
        gathered[4],
    )
    gain_attn = gathered[5].astype(jnp.float32)
    gain_ffn = gathered[6].astype(jnp.float32)
    gain_query = gathered[7].astype(jnp.float32)
    gain_key = gathered[8].astype(jnp.float32)
    local_heads = full_query.shape[1] // HEAD_SIZE
    seg_all = lax.all_gather(segments, CONTEXT, axis=1, tiled=True)[0]
    length = seg_all.shape[0]
    start_row = context_rank * row_count
    positions = lax.dynamic_slice_in_dim(doc_positions(seg_all), start_row, row_count)
    cosine_table, sine_table = rope_tables(positions, HEAD_SIZE)
    query_seg = segments[0]
    query_index = start_row + jnp.arange(row_count, dtype=jnp.int32)
    key_ids = jnp.arange(length, dtype=jnp.int32)
    key_block = min(512, length)

    def query_finish(raw_values, gain_vec):
        return qk_finish(raw_values, gain_vec, cosine_table[:, None, :], sine_table[:, None, :])

    def key_finish(raw_values, gain_vec):
        return qk_finish(raw_values, gain_vec, cosine_table, sine_table)

    normed_f, first_pull = jax.vjp(rms_scale, input_rows, gain_attn)
    attention_normalized = normed_f.astype(jnp.bfloat16)
    query_unrotated = matmul(attention_normalized, full_query).reshape(
        row_count, local_heads, HEAD_SIZE
    )
    key_unrotated = matmul(attention_normalized, full_key)
    value_raw = matmul(attention_normalized, full_value)
    query_f, query_pull = jax.vjp(query_finish, query_unrotated, gain_query)
    key_f, key_pull = jax.vjp(key_finish, key_unrotated, gain_key)
    query_vectors = query_f.astype(jnp.bfloat16)
    keys_all, values_all = (
        lax.all_gather(key_f.astype(jnp.bfloat16), CONTEXT, axis=0, tiled=True),
        lax.all_gather(value_raw.astype(jnp.bfloat16), CONTEXT, axis=0, tiled=True),
    )
    heads_full, log_total = attention_forward(
        query_vectors, keys_all, values_all, seg_all, query_seg, query_index, key_ids, key_block
    )
    heads_low = heads_full.reshape(row_count, local_heads * HEAD_SIZE).astype(jnp.bfloat16)
    attn_out = lax.psum(matmul_nt(heads_low, full_output).astype(jnp.bfloat16), TENSOR).astype(
        jnp.float32
    )
    residual_stream = input_rows + attn_out
    second_f, second_pull = jax.vjp(rms_scale, residual_stream, gain_ffn)
    feedforward_normalized = second_f.astype(jnp.bfloat16)
    router_scores = matmul(feedforward_normalized, full_router)
    experts_total = full_router.shape[1]
    route_ids = routes[0]
    chosen = route_ids[:, :, None] == jnp.arange(experts_total, dtype=jnp.int32)
    selected = jnp.sum(jnp.where(chosen, router_scores[:, None, :], 0.0), axis=2)
    gate_probs = jax.nn.softmax(selected, axis=-1)
    capacity = 9 * row_count * TOPK // (8 * experts_total)
    before = earlier_counts(jnp.any(chosen, axis=1)).astype(jnp.int32)
    slot_index = jnp.sum(jnp.where(chosen, before[:, None, :], 0), axis=2)
    target = jnp.where(
        slot_index < capacity, route_ids * capacity + slot_index, experts_total * capacity
    ).reshape(-1)
    source = jnp.repeat(jnp.arange(row_count, dtype=jnp.int32), TOPK)
    send_rows = (
        jnp.zeros((experts_total * capacity, model_width), jnp.bfloat16)
        .at[target]
        .set(feedforward_normalized[source], mode="drop")
    )
    expert_input_rows = to_experts(send_rows.reshape(experts_total, capacity, model_width))
    gate_activation_input = jnp.einsum(
        "phu,puo->pho", expert_input_rows, gate_weight, preferred_element_type=jnp.float32
    )
    up_activation_input = jnp.einsum(
        "phu,puo->pho", expert_input_rows, up_weight, preferred_element_type=jnp.float32
    )
    sigmoid_gate = jax.nn.sigmoid(gate_activation_input)
    silu_gate = gate_activation_input * sigmoid_gate
    hidden_middle = (silu_gate * up_activation_input).astype(jnp.bfloat16)
    expert_part = jnp.einsum(
        "pic,pcw->piw", hidden_middle, down_weight, preferred_element_type=jnp.float32
    ).astype(jnp.bfloat16)
    grad_out = cotangent[0].astype(jnp.float32)
    returned = pick_pairs(from_experts(expert_part), target, row_count)
    moe_part = jnp.sum(returned.astype(jnp.float32) * gate_probs[:, :, None], axis=1)
    moe_out = lax.psum(moe_part.astype(jnp.bfloat16), TENSOR).astype(jnp.float32)
    grad_gate_part = jnp.sum(returned.astype(jnp.float32) * grad_out[:, None, :], axis=2)
    output = (residual_stream + moe_out).astype(jnp.bfloat16)
    pair_grad = (
        (gate_probs[:, :, None] * grad_out[:, None, :])
        .astype(jnp.bfloat16)
        .reshape(row_count * TOPK, model_width)
    )
    send_grad = (
        jnp.zeros((experts_total * capacity, model_width), jnp.bfloat16)
        .at[target]
        .set(pair_grad, mode="drop")
    )
    expert_output_gradient = to_experts(send_grad.reshape(experts_total, capacity, model_width))
    grad_mid = jnp.einsum(
        "jtk,jvk->jtv", expert_output_gradient, down_weight, preferred_element_type=jnp.float32
    )
    grad_w_down = jnp.einsum(
        "tce,tci->tei", hidden_middle, expert_output_gradient, preferred_element_type=jnp.float32
    )
    gate_activation_gradient = (
        grad_mid
        * up_activation_input
        * sigmoid_gate
        * (1.0 + gate_activation_input * (1.0 - sigmoid_gate))
    ).astype(jnp.bfloat16)
    up_activation_gradient = (grad_mid * silu_gate).astype(jnp.bfloat16)
    grad_w_gate = jnp.einsum(
        "ahw,ahp->awp",
        expert_input_rows,
        gate_activation_gradient,
        preferred_element_type=jnp.float32,
    )
    grad_w_up = jnp.einsum(
        "ahw,ahp->awp",
        expert_input_rows,
        up_activation_gradient,
        preferred_element_type=jnp.float32,
    )
    grad_expert_in = (
        jnp.einsum(
            "ous,ops->oup",
            gate_activation_gradient,
            gate_weight,
            preferred_element_type=jnp.float32,
        )
        + jnp.einsum(
            "ous,ops->oup", up_activation_gradient, up_weight, preferred_element_type=jnp.float32
        )
    ).astype(jnp.bfloat16)
    grad_pairs = pick_pairs(from_experts(grad_expert_in), target, row_count)
    grad_normed_part = jnp.sum(grad_pairs.astype(jnp.float32), axis=1)
    grad_normed_moe, grad_gates = (
        lax.psum(grad_normed_part.astype(jnp.bfloat16), TENSOR).astype(jnp.float32),
        lax.psum(grad_gate_part.astype(jnp.bfloat16), TENSOR).astype(jnp.float32),
    )
    grad_selected = gate_probs * (
        grad_gates - jnp.sum(gate_probs * grad_gates, axis=1, keepdims=True)
    )
    grad_logits = jnp.sum(jnp.where(chosen, grad_selected[:, :, None], 0.0), axis=1).astype(
        jnp.bfloat16
    )
    grad_router = matmul_tn(feedforward_normalized, grad_logits)
    grad_normed_two = grad_normed_moe + matmul_nt(grad_logits, full_router)
    grad_resid_norm, grad_gain_ffn = second_pull(grad_normed_two)
    grad_resid = grad_out + grad_resid_norm
    grad_attn = grad_resid.astype(jnp.bfloat16)
    grad_w_output = matmul_tn(grad_attn, heads_low)
    grad_heads = (
        matmul(grad_attn, full_output)
        .astype(jnp.bfloat16)
        .reshape(row_count, local_heads, HEAD_SIZE)
    )
    row_delta = jnp.sum(grad_heads.astype(jnp.float32) * heads_full, axis=2).T
    grad_query, grad_key_terms, grad_value_terms = attention_backward(
        query_vectors,
        keys_all,
        values_all,
        seg_all,
        query_seg,
        query_index,
        key_ids,
        key_block,
        log_total,
        grad_heads,
        row_delta,
    )
    grad_key_local, grad_value_local = (
        lax.psum_scatter(
            grad_key_terms.astype(jnp.bfloat16), CONTEXT, scatter_dimension=0, tiled=True
        ).astype(jnp.float32),
        lax.psum_scatter(
            grad_value_terms.astype(jnp.bfloat16), CONTEXT, scatter_dimension=0, tiled=True
        ).astype(jnp.float32),
    )
    grad_query_raw, grad_gain_query = query_pull(grad_query)
    grad_key_raw, grad_gain_key = key_pull(grad_key_local)
    grad_query_low = grad_query_raw.reshape(row_count, local_heads * HEAD_SIZE).astype(jnp.bfloat16)
    grad_key_low = grad_key_raw.astype(jnp.bfloat16)
    grad_value_low = grad_value_local.astype(jnp.bfloat16)
    grad_w_query = matmul_tn(attention_normalized, grad_query_low)
    grad_w_key = matmul_tn(attention_normalized, grad_key_low)
    grad_w_value = matmul_tn(attention_normalized, grad_value_low)
    grad_normed_one = (
        matmul_nt(grad_query_low, full_query)
        + matmul_nt(grad_key_low, full_key)
        + matmul_nt(grad_value_low, full_value)
    )
    grad_normed_one, grad_gain_query, grad_gain_key = (
        lax.psum(grad_normed_one.astype(jnp.bfloat16), TENSOR).astype(jnp.float32),
        lax.psum(grad_gain_query.astype(jnp.bfloat16), TENSOR).astype(jnp.float32),
        lax.psum(grad_gain_key.astype(jnp.bfloat16), TENSOR).astype(jnp.float32),
    )
    grad_inputs_norm, grad_gain_attn = first_pull(grad_normed_one)
    input_grad = grad_resid + grad_inputs_norm
    owned = (
        lax.psum_scatter(
            grad_w_query.astype(jnp.bfloat16), GROUPS, scatter_dimension=0, tiled=True
        ).astype(jnp.float32),
        lax.psum_scatter(
            grad_w_key.astype(jnp.bfloat16), GROUPS, scatter_dimension=0, tiled=True
        ).astype(jnp.float32),
        lax.psum_scatter(
            grad_w_value.astype(jnp.bfloat16), GROUPS, scatter_dimension=0, tiled=True
        ).astype(jnp.float32),
        lax.psum_scatter(
            grad_w_output.astype(jnp.bfloat16), GROUPS, scatter_dimension=0, tiled=True
        ).astype(jnp.float32),
        lax.psum_scatter(
            grad_router.astype(jnp.bfloat16), GROUPS, scatter_dimension=0, tiled=True
        ).astype(jnp.float32),
        lax.psum_scatter(
            grad_gain_attn.astype(jnp.bfloat16),
            GROUPS,
            scatter_dimension=0,
            tiled=True,
        ).astype(jnp.float32),
        lax.psum_scatter(
            grad_gain_ffn.astype(jnp.bfloat16), GROUPS, scatter_dimension=0, tiled=True
        ).astype(jnp.float32),
        lax.psum_scatter(
            grad_gain_query.astype(jnp.bfloat16),
            GROUPS,
            scatter_dimension=0,
            tiled=True,
        ).astype(jnp.float32),
        lax.psum_scatter(
            grad_gain_key.astype(jnp.bfloat16), GROUPS, scatter_dimension=0, tiled=True
        ).astype(jnp.float32),
    )
    return (
        output[None],
        input_grad[None],
        owned[5],
        owned[0],
        owned[1],
        owned[2],
        owned[3],
        owned[7],
        owned[8],
        owned[6],
        owned[4],
        grad_w_gate,
        grad_w_up,
        grad_w_down,
    )


MESH = pl.DeviceIdType.MESH
Z_UP, Z_DOWN, Y_SIDE, X_SIDE, CORE_SIDE = range(5)

def coords():
    z, y, t = lax.axis_index(FSDP), lax.axis_index(CONTEXT), lax.axis_index(TENSOR)
    return z, y, t // 2, t % 2

def partner(z, index):
    return (z, z + 1 - 2 * (z % 2), 2 - z // 2, 3 - 3 * (z // 2))[index]

def greet(neighbours):
    barrier = pltpu.get_barrier_semaphore()
    for condition, device in neighbours:
        def tell(device=device):
            pl.semaphore_signal(barrier, inc=1, device_id=device, device_id_type=MESH)
        if condition is None: tell()
        else: pl.when(condition)(tell)
    count = sum(1 if condition is None else condition.astype(jnp.int32) for condition, device in neighbours)
    pl.semaphore_wait(barrier, count)


def gather_kernel(x_ref, out_ref, own_sem, send_sems, recv_sems):
    rows = x_ref.shape[0]; half = rows // 2
    z, y, x, c = coords()
    side = {Z_UP: (z + 1, y, 2 * x + c), Z_DOWN: (z - 1, y, 2 * x + c), Y_SIDE: (z, 1 - y, 2 * x + c),
            X_SIDE: (z, y, 2 * (1 - x) + c), CORE_SIDE: (z, y, 2 * x + 1 - c)}
    greet([(z < 3, side[Z_UP]), (z > 0, side[Z_DOWN]), (None, side[Y_SIDE]), (None, side[X_SIDE]), (None, side[CORE_SIDE])])
    def device(zz, yy, xx, cc): return (zz * 2 + yy) * 4 + xx * 2 + cc
    def place(owner, h): return out_ref.at[pl.ds(pl.multiple_of(owner * rows + h * half, half), half)]
    def copy(link, owner, h, own=False):
        src = x_ref.at[pl.ds(h * half, half)] if own else place(owner, h)
        return pltpu.make_async_remote_copy(src_ref=src, dst_ref=place(owner, h), send_sem=send_sems.at[link, owner, h],
            recv_sem=recv_sems.at[owner, h], device_id=side[link], device_id_type=MESH)
    sent = []
    def start(link, owner, h, own=False, condition=None):
        one = copy(link, owner, h, own)
        sent.append((one, condition))
        if condition is None: one.start()
        else: pl.when(condition)(one.start)
    def arrived(owner, h): copy(CORE_SIDE, owner, h).wait_recv()
    me = device(z, y, x, c)
    keep = pltpu.make_async_copy(x_ref, out_ref.at[pl.ds(pl.multiple_of(me * rows, rows), rows)], own_sem)
    keep.start()
    def stage1(i):
        zz = partner(z, i); owner = device(zz, y, x, c); own = i == 0
        if not own:
            arrived(owner, 0); arrived(owner, 1)
        for h in range(2):
            start(Z_UP, owner, h, own, (z < 3) if own else (z < 3) & (zz < z))
            start(Z_DOWN, owner, h, own, (z > 0) if own else (z > 0) & (zz > z))
        start(Y_SIDE, owner, 0, own); start(X_SIDE, owner, 1, own)
        start(Y_SIDE, owner, 1, own); start(X_SIDE, owner, 0, own)
        for h in range(2): start(CORE_SIDE, owner, h, own)
    def stage2(i):
        zz = partner(z, i)
        oy, ox = device(zz, 1 - y, x, c), device(zz, y, 1 - x, c)
        arrived(oy, 0); start(X_SIDE, oy, 0); start(CORE_SIDE, oy, 0)
        arrived(ox, 1); start(Y_SIDE, ox, 1); start(CORE_SIDE, ox, 1)
        arrived(oy, 1); start(CORE_SIDE, oy, 1)
        arrived(ox, 0); start(CORE_SIDE, ox, 0)
    def stage3(i):
        o = device(partner(z, i), 1 - y, 1 - x, c)
        for h in range(2):
            arrived(o, h); start(CORE_SIDE, o, h)
    stage1(0); stage1(1); stage2(0); stage1(2); stage2(1); stage3(0); stage1(3); stage2(2); stage3(1); stage2(3); stage3(2); stage3(3)
    for i in range(4):
        for yy in range(2):
            for xx in range(2):
                for h in range(2): arrived(device(i, yy, xx, 1 - c), h)
    keep.wait()
    for one, condition in sent:
        if condition is None: one.wait_send()
        else: pl.when(condition)(one.wait_send)

def gather_everyone(x, collective_id):
    rows, width = x.shape
    return pl.pallas_call(gather_kernel, out_shape=jax.ShapeDtypeStruct((32 * rows, width), x.dtype),
        in_specs=[pl.BlockSpec(memory_space=pl.ANY)], out_specs=pl.BlockSpec(memory_space=pl.ANY),
        scratch_shapes=[pltpu.SemaphoreType.DMA, pltpu.SemaphoreType.DMA((5, 32, 2)), pltpu.SemaphoreType.DMA((32, 2))],
        compiler_params=pltpu.CompilerParams(collective_id=collective_id, has_side_effects=True))(x)

def groups_kernel(splits, *refs):
    count = len(splits)
    ins, outs = refs[:count], refs[count:2 * count]
    keep_sems, send_sems, recv_sems = refs[2 * count:]
    z, y, x, c = coords()
    t = 2 * x + c
    side = {Z_UP: (z + 1, y, t), Z_DOWN: (z - 1, y, t), Y_SIDE: (z, 1 - y, t)}
    greet([(z < 3, side[Z_UP]), (z > 0, side[Z_DOWN]), (None, side[Y_SIDE])])
    sent = []
    def place(k, owner, h):
        rows = ins[k].shape[0]
        first, size = (0, splits[k]) if h == 0 else (splits[k], rows - splits[k])
        return outs[k].at[pl.ds(pl.multiple_of(owner * rows + first, 16), size)], ins[k].at[pl.ds(first, size)]
    def copy(link, k, owner, h, own=False):
        dst, src = place(k, owner, h)
        return pltpu.make_async_remote_copy(src_ref=src if own else dst, dst_ref=dst, send_sem=send_sems.at[link, k, owner, h],
            recv_sem=recv_sems.at[k, owner, h], device_id=side[link], device_id_type=MESH)
    def halves(k): return (0, 1) if splits[k] < ins[k].shape[0] else (0,)
    def start(link, k, owner, h, own=False, condition=None):
        if h not in halves(k): return
        one = copy(link, k, owner, h, own)
        sent.append((one, condition))
        if condition is None: one.start()
        else: pl.when(condition)(one.start)
    def arrived(k, owner, h):
        if h in halves(k): copy(Y_SIDE, k, owner, h).wait_recv()
    def along(k, owner, h, zz, own=False):
        start(Z_UP, k, owner, h, own, (z < 3) & (zz <= z)); start(Z_DOWN, k, owner, h, own, (z > 0) & (zz >= z))
    kept = []
    me = z * 2 + y
    for k in range(count):
        along(k, me, 0, z, True); start(Y_SIDE, k, me, 1, True); start(Y_SIDE, k, me, 0, True); along(k, me, 1, z, True)
        rows = ins[k].shape[0]
        one = pltpu.make_async_copy(ins[k], outs[k].at[pl.ds(pl.multiple_of(me * rows, 16), rows)], keep_sems.at[k])
        one.start(); kept.append(one)
    for k in range(count):
        for i in range(4):
            zz = partner(z, i)
            near, far = zz * 2 + y, zz * 2 + 1 - y
            if i > 0:
                arrived(k, near, 0); along(k, near, 0, zz); start(Y_SIDE, k, near, 0)
                arrived(k, near, 1); along(k, near, 1, zz)
            arrived(k, far, 1); along(k, far, 1, zz)
    for k in range(count):
        for i in range(4): arrived(k, partner(z, i) * 2 + 1 - y, 0)
    for one in kept: one.wait()
    for one, condition in sent:
        if condition is None: one.wait_send()
        else: pl.when(condition)(one.wait_send)

def gather_groups(arrays, splits, collective_id):
    count = len(arrays); D = pltpu.SemaphoreType.DMA
    return pl.pallas_call(functools.partial(groups_kernel, splits),
        out_shape=[jax.ShapeDtypeStruct((8 * a.shape[0], a.shape[1]), a.dtype) for a in arrays],
        in_specs=[pl.BlockSpec(memory_space=pl.ANY)] * count, out_specs=[pl.BlockSpec(memory_space=pl.ANY)] * count,
        scratch_shapes=[D((count,)), D((3, count, 8, 2)), D((count, 8, 2))],
        compiler_params=pltpu.CompilerParams(collective_id=collective_id, has_side_effects=True))(*arrays)

def tensor_gather_kernel(x_ref, out_ref, keep_sem, send_sems, recv_sems):
    z, y, x, c = coords()
    x_side, core_side = (z, y, 2 * (1 - x) + c), (z, y, 2 * x + 1 - c)
    greet([(None, x_side), (None, core_side)])
    def copy(n, owner, device, own=False):
        return pltpu.make_async_remote_copy(src_ref=x_ref if own else out_ref.at[owner], dst_ref=out_ref.at[owner], send_sem=send_sems.at[n],
            recv_sem=recv_sems.at[owner], device_id=device, device_id_type=MESH)
    me, across, beside, last = 2 * x + c, 2 * (1 - x) + c, 2 * x + 1 - c, 2 * (1 - x) + 1 - c
    a, b, d = copy(0, me, x_side, True), copy(1, me, core_side, True), copy(2, across, core_side)
    a.start(); b.start()
    keep = pltpu.make_async_copy(x_ref, out_ref.at[me], keep_sem); keep.start()
    copy(0, across, x_side).wait_recv(); d.start()
    copy(0, beside, x_side).wait_recv(); copy(0, last, x_side).wait_recv()
    keep.wait(); a.wait_send(); b.wait_send(); d.wait_send()

def gather_tensor(x, collective_id):
    D = pltpu.SemaphoreType.DMA
    return pl.pallas_call(tensor_gather_kernel, out_shape=jax.ShapeDtypeStruct((4, *x.shape), x.dtype),
        in_specs=[pl.BlockSpec(memory_space=pl.ANY)], out_specs=pl.BlockSpec(memory_space=pl.ANY),
        scratch_shapes=[D, D((3,)), D((4,))],
        compiler_params=pltpu.CompilerParams(collective_id=collective_id, has_side_effects=True))(x)

def tensor_scatter_kernel(part_ref, out_ref, mine, core_in, line_in, sems, recv):
    z, y, x, c = coords()
    x_side, core_side = (z, y, 2 * (1 - x) + c), (z, y, 2 * x + 1 - c)
    greet([(None, x_side), (None, core_side)])
    rows = out_ref.shape[0]; f32 = jnp.float32
    def rows_of(xx, cc): return part_ref.at[pl.ds(pl.multiple_of((2 * xx + cc) * rows, rows), rows)]
    def over_core(n, xx):
        return pltpu.make_async_remote_copy(src_ref=rows_of(xx, 1 - c), dst_ref=core_in.at[n], send_sem=sems.at[n], recv_sem=recv.at[n],
            device_id=core_side, device_id_type=MESH)
    a, b = over_core(0, 1 - x), over_core(1, x)
    a.start(); b.start()
    a.wait_recv()
    mine[...] = (rows_of(1 - x, c)[...].astype(f32) + core_in[0].astype(f32)).astype(mine.dtype)
    d = pltpu.make_async_remote_copy(src_ref=mine, dst_ref=line_in, send_sem=sems.at[2], recv_sem=recv.at[2], device_id=x_side, device_id_type=MESH)
    d.start(); b.wait_recv()
    out_ref[...] = rows_of(x, c)[...].astype(f32) + core_in[1].astype(f32)
    d.wait_recv()
    out_ref[...] += line_in[...].astype(f32)
    a.wait_send(); b.wait_send(); d.wait_send()

def scatter_tensor(part, collective_id):
    D = pltpu.SemaphoreType.DMA; rows = part.shape[0] // 4; width = part.shape[1]
    return pl.pallas_call(tensor_scatter_kernel, out_shape=jax.ShapeDtypeStruct((rows, width), jnp.float32),
        in_specs=[pl.BlockSpec(memory_space=pltpu.VMEM)], out_specs=pl.BlockSpec(memory_space=pltpu.VMEM),
        scratch_shapes=[pltpu.VMEM((rows, width), part.dtype), pltpu.VMEM((2, rows, width), part.dtype), pltpu.VMEM((rows, width), part.dtype), D((3,)), D((3,))],
        compiler_params=pltpu.CompilerParams(collective_id=collective_id, has_side_effects=True, vmem_limit_bytes=24 << 20))(part)

def groups_scatter_kernel(split, part_ref, out_ref, near_in, mine, line_in, tail_in, tail_mine, tail_line, load_sem, side_sem, line_send, line_recv, tail_load, tail_side, tail_send, tail_recv):
    rows = out_ref.shape[0]; rest = rows - split
    z, y, x, c = coords()
    t = 2 * x + c
    up, down, across = (z + 1, y, t), (z - 1, y, t), (z, 1 - y, t)
    greet([(z < 3, up), (z > 0, down), (None, across)])
    f32, dt = jnp.float32, part_ref.dtype
    def rows_of(zz, yy, first, size): return part_ref.at[pl.ds(pl.multiple_of((zz * 2 + yy) * rows + first, 16), size)]
    def remote(src, dst, send, recv, device):
        return pltpu.make_async_remote_copy(src_ref=src, dst_ref=dst, send_sem=send, recv_sem=recv, device_id=device, device_id_type=MESH)
    def over_y(zz): return remote(rows_of(zz, 1 - y, 0, split), near_in.at[zz], side_sem.at[0, zz], side_sem.at[1, zz], across)
    def load(zz): return pltpu.make_async_copy(rows_of(zz, y, 0, split), mine.at[zz], load_sem.at[zz])
    def load_tail(zz, yy): return pltpu.make_async_copy(rows_of(zz, yy, split, rest), tail_mine.at[zz, yy], tail_load.at[zz, yy])
    def line(zz, way): return remote(mine.at[zz], line_in.at[way, zz], line_send.at[zz], line_recv.at[way, zz], up if way == 0 else down)
    def line_tail(zz, yy, way): return remote(tail_mine.at[zz, yy], tail_line.at[way, zz, yy], tail_send.at[zz, yy], tail_recv.at[way, zz, yy], up if way == 0 else down)
    final = remote(tail_mine.at[z, 1 - y], tail_in, tail_side.at[0], tail_side.at[1], across)
    order = (3, 2, 1, 0)
    for i in order:
        zz = partner(z, i)
        over_y(zz).start(); load(zz).start()
        load_tail(zz, 0).start(); load_tail(zz, 1).start()
    def along(zz, i, copy, add):
        for way, from_side, toward in ((0, z > 0, zz > z), (1, z < 3, zz < z)):
            @pl.when(from_side if i == 0 else from_side & toward)
            def _(way=way):
                copy(way).wait_recv()
                add(way)
        for way, toward in ((0, zz > z), (1, zz < z)):
            if i > 0:
                @pl.when(toward)
                def _(way=way): copy(way).start()
    for i in order:
        zz = partner(z, i)
        for n in range(2):
            yy = (1 - y, y)[n]
            load_tail(zz, yy).wait()
            def add(way, yy=yy): tail_mine[zz, yy] = (tail_mine[zz, yy].astype(f32) + tail_line[way, zz, yy].astype(f32)).astype(dt)
            along(zz, i, lambda way, yy=yy: line_tail(zz, yy, way), add)
            if i == 0 and n == 0: final.start()
        load(zz).wait(); over_y(zz).wait_recv()
        mine[zz] = (mine[zz].astype(f32) + near_in[zz].astype(f32)).astype(dt)
        def add(way): mine[zz] = (mine[zz].astype(f32) + line_in[way, zz].astype(f32)).astype(dt)
        along(zz, i, lambda way: line(zz, way), add)
    out_ref[pl.ds(0, split)] = mine[z].astype(f32)
    final.wait_recv()
    out_ref[pl.ds(split, rest)] = tail_mine[z, y].astype(f32) + tail_in[...].astype(f32)
    final.wait_send()
    for zz in range(4):
        over_y(zz).wait_send()
        @pl.when(zz != z)
        def _(zz=zz):
            line(zz, 0).wait_send()
            for yy in range(2): line_tail(zz, yy, 0).wait_send()

def scatter_groups(part, split, collective_id):
    total, width = part.shape; rows = total // 8; rest = rows - split
    dt = part.dtype; D = pltpu.SemaphoreType.DMA; V = pltpu.VMEM
    return pl.pallas_call(functools.partial(groups_scatter_kernel, split), out_shape=jax.ShapeDtypeStruct((rows, width), jnp.float32),
        in_specs=[pl.BlockSpec(memory_space=pl.ANY)], out_specs=pl.BlockSpec(memory_space=V),
        scratch_shapes=[V((4, split, width), dt), V((4, split, width), dt), V((2, 4, split, width), dt), V((rest, width), dt), V((4, 2, rest, width), dt), V((2, 4, 2, rest, width), dt),
            D((4,)), D((2, 4)), D((4,)), D((2, 4)), D((4, 2)), D((2,)), D((4, 2)), D((2, 4, 2))],
        compiler_params=pltpu.CompilerParams(collective_id=collective_id, has_side_effects=True, vmem_limit_bytes=48 << 20))(part)


def nt(a, b):
    return lax.dot_general(a, b, (((1,), (1,)), ((), ())), preferred_element_type=jnp.float32)

def nn(a, b):
    return jnp.dot(a, b, preferred_element_type=jnp.float32)

def expert_kernel(comm, normed_ref, cot_ref, code_ref, router_ref, expand_ref, place_ref, gate_ref, up_ref, down_ref,
                  out_ref, hid_out, gate_out, up_out,
                  normed_in, cot_in, code_in, units, part, mine, core_in, first_in, second_in, line_in,
                  in_sem, units_sem, core_sem, first_sem, second_sem, line_send, line_recv):
    rows = out_ref.shape[0]; half = rows // 2; width = normed_ref.shape[1]
    wide = gate_ref.shape[1]
    z, y, x, c = coords()
    up, down = (z + 1, y, 2 * x + c), (z - 1, y, 2 * x + c)
    y_side, x_side, core_side = (z, 1 - y, 2 * x + c), (z, y, 2 * (1 - x) + c), (z, y, 2 * x + 1 - c)
    if comm:
        greet([(z < 3, up), (z > 0, down), (None, y_side), (None, x_side), (None, core_side)])
    f32, bf16 = jnp.float32, jnp.bfloat16
    def nearest(index):
        choice = [partner(z, n) for n in range(4)]
        return jnp.where(index == 0, choice[0], jnp.where(index == 1, choice[1], jnp.where(index == 2, choice[2], choice[3])))
    def spot(zz, yy, xx): return (zz * 2 + yy) * 2 + xx
    def target(step):
        n = step % 4
        return nearest(3 - step // 4), jnp.where(n < 2, 1 - y, y), jnp.where(n % 2 == 0, 1 - x, x)
    def remote(src, dst, send, recv, device):
        return pltpu.make_async_remote_copy(src_ref=src, dst_ref=dst, send_sem=send, recv_sem=recv, device_id=device, device_id_type=MESH)
    def block(ref, step):
        return ref.at[pl.ds(pl.multiple_of(spot(*target(step)) * 2 * rows, 2 * rows), 2 * rows)]
    stride = code_ref.shape[0] // 8
    def loads(step):
        slot = step % 2
        zz, yy, xx = target(step)
        codes = code_ref.at[pl.ds(pl.multiple_of((zz * 2 + yy) * stride, 16), rows)]
        pairs = ((block(normed_ref, step), normed_in), (block(cot_ref, step), cot_in), (codes, code_in))
        return [pltpu.make_async_copy(src, dst.at[slot], in_sem.at[n, slot]) for n, (src, dst) in enumerate(pairs)]
    def stores(step):
        slot = step % 2
        return [pltpu.make_async_copy(units.at[slot, n], block(dst, step), units_sem.at[n, slot])
                for n, dst in enumerate((hid_out, gate_out, up_out))]
    def over_core(step):
        s = spot(*target(step))
        return remote(part.at[step % 2, 1 - c], core_in.at[s], core_sem.at[0, s], core_sem.at[1, s], core_side)
    def piece(zz, yy, xx, h): return mine.at[spot(zz, yy, xx), pl.ds(h * half, half)]
    def first(h, zz, other):
        src = piece(zz, other, 1 - x, 0) if h == 0 else piece(zz, 1 - y, other, 1)
        s = zz * 2 + other
        return remote(src, first_in.at[h, s], first_sem.at[0, h, s], first_sem.at[1, h, s], x_side if h == 0 else y_side)
    def second(h, zz):
        src = piece(zz, 1 - y, x, 0) if h == 0 else piece(zz, y, 1 - x, 1)
        return remote(src, second_in.at[h, zz], second_sem.at[0, h, zz], second_sem.at[1, h, zz], y_side if h == 0 else x_side)
    def line(h, zz, way):
        return remote(piece(zz, y, x, h), line_in.at[way, zz, h], line_send.at[zz, h], line_recv.at[way, zz, h], up if way == 0 else down)
    def add(s, h, arrived):
        at = (s, pl.ds(h * half, half))
        mine[at] = (mine[at].astype(f32) + arrived[...].astype(f32)).astype(bf16)
    def stage_core(step):
        zz, yy, xx = target(step)
        s = spot(zz, yy, xx)
        over_core(step).wait_recv()
        mine[s] = (part[step % 2, c].astype(f32) + core_in[s].astype(f32)).astype(bf16)
        n = step % 4
        @pl.when(n % 2 == 0)
        def _(): first(0, zz, yy).start()
        @pl.when(n < 2)
        def _(): first(1, zz, xx).start()
    def stage_first(i):
        zz = nearest(i)
        for n in range(2):
            for h, other in ((0, (1 - y, y)[n]), (1, (1 - x, x)[n])):
                first(h, zz, other).wait_recv()
                s = spot(zz, other, x) if h == 0 else spot(zz, y, other)
                add(s, h, first_in.at[h, zz * 2 + other])
                if n == 0: second(h, zz).start()
    def stage_second(i):
        zz = nearest(i)
        for h in range(2):
            second(h, zz).wait_recv()
            add(spot(zz, y, x), h, second_in.at[h, zz])
    def stage_line(i):
        zz = nearest(i); s = spot(zz, y, x)
        for h in range(2):
            for way, from_side, toward in ((0, z > 0, zz > z), (1, z < 3, zz < z)):
                @pl.when(from_side & (toward | (zz == z)))
                def _(h=h, way=way):
                    line(h, zz, way).wait_recv()
                    add(s, h, line_in.at[way, zz, h])
                @pl.when(toward)
                def _(h=h, way=way): line(h, zz, way).start()
    for one in loads(0): one.start()

    def compute(step):
        slot = step % 2
        for one in loads(step): one.wait()
        @pl.when(step < 15)
        def _():
            for one in loads(step + 1): one.start()
        @pl.when(step >= 2)
        def _():
            for one in stores(step - 2): one.wait()
            if comm: over_core(step - 2).wait_send()
        normed, cot = normed_in[slot], cot_in[slot]
        code = code_in[slot].astype(f32)
        quarter = lax.broadcasted_iota(jnp.int32, code.shape, 1) // (128 // 4) - 2 * target(step)[2]
        code = jnp.concatenate([jnp.where(quarter == n, code, 0.0) for n in range(2)], axis=0)
        scores = jnp.where(code > 0.5, nn(normed, router_ref[...]), NEGATIVE)
        scores = jnp.where(code > 0.5, jnp.exp(scores - jnp.max(scores, axis=1, keepdims=True)), 0.0)
        gates = jnp.where(code > 1.5, scores / jnp.sum(scores, axis=1, keepdims=True), 0.0)
        high = gates.astype(bf16)
        low = (gates - high.astype(f32)).astype(bf16)
        grad_gates = jnp.zeros((2 * rows, 128), f32)
        for n in range(wide // 256):
            at = pl.ds(n * 256, 256)
            gate_in = nn(normed, gate_ref[:, at])
            up_in = nn(normed, up_ref[:, at])
            grad_mid = nt(cot, down_ref[at, :])
            gate = nn(high, expand_ref[:, at]) + nn(low, expand_ref[:, at])
            sig = lax.logistic(gate_in)
            silu = gate_in * sig
            hidden = silu * up_in
            grad_gates += nn(jnp.where(gate != 0.0, hidden * grad_mid, 0.0).astype(bf16), place_ref[at, :])
            grad_hidden = grad_mid * gate
            units[slot, 0, :, at] = (hidden * gate).astype(bf16)
            units[slot, 1, :, at] = (grad_hidden * up_in * sig * (1.0 + gate_in * (1.0 - sig))).astype(bf16)
            units[slot, 2, :, at] = (grad_hidden * silu).astype(bf16)
        for one in stores(step): one.start()
        gate_grad, up_grad = units[slot, 1], units[slot, 2]
        for n in range(width // 512):
            at = pl.ds(n * 512, 512)
            grad = (nt(gate_grad, gate_ref[at, :]) + nt(up_grad, up_ref[at, :])).astype(bf16)
            part[slot, 0, :, at] = grad[:rows]
            part[slot, 1, :, at] = grad[rows:]
        grad_gates = grad_gates.astype(bf16)
        part[slot, 0, :, pl.ds(width, 128)] = grad_gates[:rows]
        part[slot, 1, :, pl.ds(width, 128)] = grad_gates[rows:]
        if comm: over_core(step).start()

    @pl.loop(0, 16)
    def _(step):
        compute(step)
        if not comm: return
        @pl.when(step >= 1)
        def _(): stage_core(step - 1)
        q = step // 4
        @pl.when((step % 4 == 1) & (q >= 1))
        def _(): stage_first(4 - q)
        @pl.when((step % 4 == 3) & (q >= 1))
        def _(): stage_second(4 - q)
        @pl.when((step % 4 == 1) & (q >= 2))
        def _(): stage_line(5 - q)
    for step in (14, 15):
        for one in stores(step): one.wait()
    if not comm:
        out_ref[...] = part[0, 0].astype(f32)
        return
    stage_core(15); stage_first(0); stage_second(0); stage_line(1); stage_line(0)
    out_ref[...] = mine[spot(z, y, x)].astype(f32)
    over_core(14).wait_send(); over_core(15).wait_send()
    for zz in range(4):
        for other in range(2):
            for h in range(2): first(h, zz, other).wait_send()
        for h in range(2): second(h, zz).wait_send()
        @pl.when(zz != z)
        def _(zz=zz):
            for h in range(2): line(h, zz, 0).wait_send()

def run_experts(normed_all, cot_all, code, router, expand, place, gate_flat, up_flat, down_flat, collective_id, comm=True):
    total, width = normed_all.shape; rows = total // 32; half = rows // 2; wide = gate_flat.shape[1]
    bf16 = jnp.bfloat16; D = pltpu.SemaphoreType.DMA; V = pltpu.VMEM; W = width + 128
    anyspec, vspec = pl.BlockSpec(memory_space=pl.ANY), pl.BlockSpec(memory_space=pltpu.VMEM)
    unit = jax.ShapeDtypeStruct((total, wide), bf16)
    params = dict(collective_id=collective_id) if comm else {}
    return pl.pallas_call(functools.partial(expert_kernel, comm),
        out_shape=[jax.ShapeDtypeStruct((rows, W), jnp.float32), unit, unit, unit],
        in_specs=[anyspec] * 3 + [vspec] * 6, out_specs=[vspec] + [anyspec] * 3,
        scratch_shapes=[V((2, 2 * rows, width), bf16), V((2, 2 * rows, width), bf16), V((2, rows, 128), bf16),
            V((2, 3, 2 * rows, wide), bf16), V((2, 2, rows, W), bf16),
            V((16, rows, W), bf16), V((16, rows, W), bf16), V((2, 8, half, W), bf16), V((2, 4, half, W), bf16), V((2, 4, 2, half, W), bf16),
            D((3, 2)), D((3, 2)), D((2, 16)), D((2, 2, 8)), D((2, 2, 4)), D((4, 2)), D((2, 4, 2))],
        compiler_params=pltpu.CompilerParams(has_side_effects=True, vmem_limit_bytes=60 << 20, **params))(
            normed_all, cot_all, code, router, expand, place, gate_flat, up_flat, down_flat)


def inverse_rms(values):
    return lax.rsqrt(jnp.mean(values * values, axis=-1, keepdims=True) + EPSILON)

def attend_kernel(x_ref, gain_ref, qkv_ref, cos_ref, sin_ref, head_gain_ref, seg_rows_ref, seg_cols_ref,
                  normed_ref, raw_ref, q_ref, kv_ref, kv_other_ref, full_ref, lse_ref, bias, send_sem, recv_sem):
    z, y, x, c = coords()
    other = (z, 1 - y, 2 * x + c)
    greet([(None, other)])
    f32, bf16 = jnp.float32, jnp.bfloat16
    rows = x_ref.shape[0]; heads = q_ref.shape[1] // HEAD_SIZE; q_width = heads * HEAD_SIZE
    values = x_ref[...].astype(f32)
    normed_ref[...] = (values * inverse_rms(values) * gain_ref[...]).astype(bf16)
    def finish(raw, n):
        normed = raw * inverse_rms(raw) * head_gain_ref[pl.ds(n, 1), :]
        return (normed * cos_ref[...] + pltpu.roll(normed, HEAD_SIZE // 2, 1) * sin_ref[...]).astype(bf16)
    raw_kv = nn(normed_ref[...], qkv_ref[:, pl.ds(q_width, 2 * HEAD_SIZE)])
    raw_ref[:, pl.ds(q_width, HEAD_SIZE)] = raw_kv[:, :HEAD_SIZE]
    kv_ref[:, pl.ds(0, HEAD_SIZE)] = finish(raw_kv[:, :HEAD_SIZE], 1)
    kv_ref[:, pl.ds(HEAD_SIZE, HEAD_SIZE)] = raw_kv[:, HEAD_SIZE:].astype(bf16)
    move = pltpu.make_async_remote_copy(src_ref=kv_ref, dst_ref=kv_other_ref, send_sem=send_sem, recv_sem=recv_sem,
        device_id=other, device_id_type=MESH)
    @pl.when(y == 0)
    def _():
        move.start()
        kv_other_ref[...] = jnp.zeros_like(kv_other_ref)
    @pl.loop(0, heads // 2)
    def _(n):
        at = pl.ds(pl.multiple_of(n * 2 * HEAD_SIZE, 2 * HEAD_SIZE), 2 * HEAD_SIZE)
        raw = nn(normed_ref[...], qkv_ref[:, at])
        raw_ref[:, at] = raw
        for m in range(2):
            one = pl.ds(pl.multiple_of((2 * n + m) * HEAD_SIZE, HEAD_SIZE), HEAD_SIZE)
            q_ref[:, one] = finish(raw[:, m * HEAD_SIZE:(m + 1) * HEAD_SIZE], 0)
    row_id = lax.broadcasted_iota(jnp.int32, (rows, rows), 0)
    col_id = lax.broadcasted_iota(jnp.int32, (rows, rows), 1)
    bias[0] = jnp.where((seg_rows_ref[...] == seg_cols_ref[pl.ds(0, 1), :]) & (col_id <= row_id), 0.0, NEGATIVE)
    bias[1] = jnp.where(seg_rows_ref[...] == seg_cols_ref[pl.ds(1, 1), :], 0.0, NEGATIVE)
    lse_ref[...] = jnp.zeros_like(lse_ref)
    scale = HEAD_SIZE ** -0.5
    lane = lax.broadcasted_iota(jnp.int32, (rows, HEAD_SIZE), 1)
    def head(h, blocks):
        at = pl.ds(pl.multiple_of(h * HEAD_SIZE, HEAD_SIZE), HEAD_SIZE)
        query = q_ref[:, at]
        refs = (kv_ref, kv_other_ref)[:blocks]
        scores = [nt(query, ref[:, pl.ds(0, HEAD_SIZE)]) * scale + bias[n] for n, ref in enumerate(refs)]
        top = functools.reduce(jnp.maximum, [jnp.max(s, axis=1, keepdims=True) for s in scores])
        weights = [jnp.exp(s - top) for s in scores]
        total = sum(jnp.sum(w, axis=1, keepdims=True) for w in weights)
        inverse = 1.0 / total
        full_ref[:, at] = sum(nn((w * inverse).astype(bf16), ref[:, pl.ds(HEAD_SIZE, HEAD_SIZE)]) for w, ref in zip(weights, refs))
        lse_ref[...] = jnp.where(lane == h, top + jnp.log(total), lse_ref[...])
    @pl.when(y == 0)
    def _():
        @pl.loop(0, heads)
        def _(h): head(h, 1)
        move.wait_send()
    @pl.when(y == 1)
    def _():
        move.wait_recv()
        @pl.loop(0, heads)
        def _(h): head(h, 2)

def attend(x, gain, qkv, cos, sin, head_gains, seg_rows, seg_cols, collective_id):
    rows, width = x.shape; q_width = qkv.shape[1] - 2 * HEAD_SIZE
    V = pltpu.VMEM; f32, bf16 = jnp.float32, jnp.bfloat16; S = jax.ShapeDtypeStruct
    vspec = pl.BlockSpec(memory_space=V)
    return pl.pallas_call(attend_kernel,
        out_shape=[S((rows, width), bf16), S((rows, q_width + HEAD_SIZE), f32), S((rows, q_width), bf16), S((rows, 2 * HEAD_SIZE), bf16),
            S((rows, 2 * HEAD_SIZE), bf16), S((rows, q_width), f32), S((rows, HEAD_SIZE), f32)],
        in_specs=[vspec] * 8, out_specs=[vspec] * 7,
        scratch_shapes=[V((2, rows, rows), f32), pltpu.SemaphoreType.DMA, pltpu.SemaphoreType.DMA],
        compiler_params=pltpu.CompilerParams(collective_id=collective_id, has_side_effects=True, vmem_limit_bytes=48 << 20))(
            x, gain, qkv, cos, sin, head_gains, seg_rows, seg_cols)

def attend_back_kernel(cot_ref, out_w_ref, q_ref, kv_ref, kv_other_ref, raw_ref, full_ref, lse_ref, cos_ref, sin_ref, head_gain_ref,
                       seg_rows_ref, seg_cols_ref, grad_ref, gains_ref, grad_heads, delta, stats, bias, grad_q, grad_kv, kv_send, kv_in, send_sem, recv_sem):
    z, y, x, c = coords()
    other = (z, 1 - y, 2 * x + c)
    greet([(None, other)])
    f32, bf16 = jnp.float32, jnp.bfloat16
    rows = q_ref.shape[0]; heads = q_ref.shape[1] // HEAD_SIZE; q_width = heads * HEAD_SIZE
    scale = HEAD_SIZE ** -0.5
    lane = lax.broadcasted_iota(jnp.int32, (rows, HEAD_SIZE), 1)
    delta[...] = jnp.zeros_like(delta)
    @pl.loop(0, heads // 2)
    def _(n):
        at = pl.ds(pl.multiple_of(n * 2 * HEAD_SIZE, 2 * HEAD_SIZE), 2 * HEAD_SIZE)
        grad = nn(cot_ref[...], out_w_ref[:, at]).astype(bf16)
        grad_heads[:, at] = grad
        product = grad.astype(f32) * full_ref[:, at]
        for m in range(2):
            one = jnp.sum(product[:, m * HEAD_SIZE:(m + 1) * HEAD_SIZE], axis=1, keepdims=True)
            delta[...] = jnp.where(lane == 2 * n + m, one, delta[...])
    stats[0] = lse_ref[...].T
    stats[1] = delta[...].T
    key_id = lax.broadcasted_iota(jnp.int32, (rows, rows), 0)
    query_id = lax.broadcasted_iota(jnp.int32, (rows, rows), 1)
    def block(ref, seg_keys, causal):
        same = seg_keys == seg_cols_ref[pl.ds(0, 1), :]
        bias[...] = jnp.where(same & (key_id <= query_id) if causal else same, 0.0, NEGATIVE)
        grad_kv[...] = jnp.zeros_like(grad_kv)
        key, value = ref[:, pl.ds(0, HEAD_SIZE)], ref[:, pl.ds(HEAD_SIZE, HEAD_SIZE)]
        @pl.loop(0, heads)
        def _(h):
            at = pl.ds(pl.multiple_of(h * HEAD_SIZE, HEAD_SIZE), HEAD_SIZE)
            query, grad = q_ref[:, at], grad_heads[:, at]
            probs = jnp.exp(nt(key, query) * scale + bias[...] - stats[0, pl.ds(h, 1), :])
            grad_scores = (probs * (nt(value, grad) - stats[1, pl.ds(h, 1), :])).astype(bf16)
            grad_kv[:, pl.ds(0, HEAD_SIZE)] += nn(grad_scores, query) * scale
            grad_kv[:, pl.ds(HEAD_SIZE, HEAD_SIZE)] += nn(probs.astype(bf16), grad)
            grad_q[:, at] += lax.dot_general(grad_scores, key, (((0,), (0,)), ((), ())), preferred_element_type=f32) * scale
    grad_q[...] = jnp.zeros_like(grad_q)
    move = pltpu.make_async_remote_copy(src_ref=kv_send, dst_ref=kv_in, send_sem=send_sem, recv_sem=recv_sem, device_id=other, device_id_type=MESH)
    @pl.when(y == 1)
    def _():
        block(kv_other_ref, seg_rows_ref[1], False)
        kv_send[...] = grad_kv[...].astype(bf16)
        move.start()
    block(kv_ref, seg_rows_ref[0], True)
    @pl.when(y == 0)
    def _():
        move.wait_recv()
        grad_kv[...] += kv_in[...].astype(f32)
    def pull(grad, raw, n):
        turned = grad * cos_ref[...] - pltpu.roll(grad, HEAD_SIZE // 2, 1) * sin_ref[...]
        inverse = inverse_rms(raw)
        unit = raw * inverse
        gains_ref[pl.ds(n, 1), :] += jnp.sum(turned * unit, axis=0, keepdims=True)
        scaled = turned * head_gain_ref[pl.ds(n, 1), :]
        return (inverse * (scaled - unit * jnp.mean(scaled * unit, axis=1, keepdims=True))).astype(bf16)
    gains_ref[...] = jnp.zeros_like(gains_ref)
    @pl.loop(0, heads)
    def _(h):
        at = pl.ds(pl.multiple_of(h * HEAD_SIZE, HEAD_SIZE), HEAD_SIZE)
        grad_ref[:, at] = pull(grad_q[:, at], raw_ref[:, at], 0)
    at = pl.ds(q_width, HEAD_SIZE)
    grad_ref[:, at] = pull(grad_kv[:, pl.ds(0, HEAD_SIZE)], raw_ref[:, at], 1)
    grad_ref[:, pl.ds(q_width + HEAD_SIZE, HEAD_SIZE)] = grad_kv[:, pl.ds(HEAD_SIZE, HEAD_SIZE)].astype(bf16)
    @pl.when(y == 1)
    def _(): move.wait_send()

def attend_back(cot, out_w, q, kv, kv_other, raw, full, lse, cos, sin, head_gains, seg_rows, seg_cols, collective_id):
    rows, q_width = q.shape
    V = pltpu.VMEM; f32, bf16 = jnp.float32, jnp.bfloat16; S = jax.ShapeDtypeStruct
    vspec = pl.BlockSpec(memory_space=V)
    return pl.pallas_call(attend_back_kernel,
        out_shape=[S((rows, q_width + 2 * HEAD_SIZE), bf16), S((8, HEAD_SIZE), f32)],
        in_specs=[vspec] * 13, out_specs=[vspec] * 2,
        scratch_shapes=[V((rows, q_width), bf16), V((rows, HEAD_SIZE), f32), V((2, HEAD_SIZE, rows), f32), V((rows, rows), f32), V((rows, q_width), f32),
            V((rows, 2 * HEAD_SIZE), f32), V((rows, 2 * HEAD_SIZE), bf16), V((rows, 2 * HEAD_SIZE), bf16), pltpu.SemaphoreType.DMA, pltpu.SemaphoreType.DMA],
        compiler_params=pltpu.CompilerParams(collective_id=collective_id, has_side_effects=True, vmem_limit_bytes=48 << 20))(
            cot, out_w, q, kv, kv_other, raw, full, lse, cos, sin, head_gains, seg_rows, seg_cols)


def gathered_local(
    hidden_in,
    attn_gain,
    w_query,
    key_weight,
    value_weight,
    w_output,
    query_gain,
    key_gain,
    ffn_gain,
    router,
    gate_weight,
    up_weight,
    down_weight,
    routes,
    segments,
    cotangent,
):
    bf16, f32 = jnp.bfloat16, jnp.float32
    context_size = lax.axis_size(CONTEXT)
    tensor_size = lax.axis_size(TENSOR)
    group_count = lax.axis_size(FSDP) * context_size
    fsdp_rank = lax.axis_index(FSDP)
    context_rank = lax.axis_index(CONTEXT)
    tensor_rank = lax.axis_index(TENSOR)
    group_rank = fsdp_rank * context_size + context_rank
    row_count, width = hidden_in.shape[1:]
    own_count = row_count // tensor_size
    own_start = tensor_rank * own_count
    local_experts, _, hidden_width = gate_weight.shape
    experts_total = router.shape[1]
    first_expert = group_rank * local_experts
    capacity = 9 * row_count * TOPK // (8 * experts_total)
    query_width = w_query.shape[1]

    expert_ids = jnp.arange(experts_total, dtype=jnp.int32)
    chosen = jnp.any(routes[0][..., None] == expert_ids, axis=1)
    kept = chosen & (earlier_counts(chosen) < capacity)
    code = chosen.astype(bf16) + kept.astype(bf16)
    chosen_own = lax.dynamic_slice_in_dim(chosen, own_start, own_count, 0)
    code = code.reshape(tensor_size, own_count, experts_total).transpose(1, 0, 2)

    pieces = (code, router, attn_gain, ffn_gain, query_gain, key_gain, segments)
    small = jnp.concatenate([piece.astype(bf16).reshape(-1) for piece in pieces])
    small = jnp.pad(small, (0, -small.size % 2048)).reshape(-1, 128)
    qkv_weight = jnp.concatenate([w_query, key_weight, value_weight], axis=1)
    small, qkv_full, full_output = gather_groups(
        (small, qkv_weight, w_output), (small.shape[0], 208, 208), 1
    )
    grad_out_own = lax.dynamic_slice_in_dim(cotangent[0], own_start, own_count, 0)
    grad_out_own, codes = lax.optimization_barrier((grad_out_own, small))
    grad_out_all = lax.all_gather(grad_out_own, EVERYONE, axis=0, tiled=True)
    small = small.reshape(group_count, -1)
    parts, at = [], code.size
    for piece in pieces[1:]:
        parts.append(small[:, at : at + piece.size])
        at += piece.size
    full_router = parts[0].reshape(width, experts_total)
    gain_attn, gain_ffn, gain_query, gain_key = (
        part.reshape(-1).astype(f32) for part in parts[1:5]
    )
    head_gains = jnp.stack([gain_query, gain_key])
    all_segments = parts[5].astype(jnp.int32)

    own_seg = segments[0]
    first_seg = lax.dynamic_index_in_dim(all_segments, group_rank - context_rank, 0, keepdims=False)
    other_seg = lax.dynamic_index_in_dim(
        all_segments, group_rank + 1 - 2 * context_rank, 0, keepdims=False
    )
    smaller = jnp.sum((own_seg[None, :] < own_seg[:, None]).astype(jnp.int32), axis=1)
    smaller_first = jnp.sum((first_seg[None, :] < own_seg[:, None]).astype(jnp.int32), axis=1)
    positions = jnp.arange(row_count, dtype=jnp.int32) - smaller
    positions = positions + context_rank * (row_count - smaller_first)
    cosine_table, sine_table = rope_tables(positions, HEAD_SIZE)
    turn = jnp.where(jnp.arange(HEAD_SIZE) < HEAD_SIZE // 2, -1.0, 1.0)
    sine_table = sine_table * turn
    seg_rows = jnp.stack([own_seg, other_seg])

    normed_one, raw, query, kv, kv_other, heads_full, log_total = attend(
        hidden_in[0],
        gain_attn[None],
        qkv_full,
        cosine_table,
        sine_table,
        head_gains,
        own_seg[:, None],
        seg_rows,
        8,
    )
    heads_low = heads_full.astype(bf16)
    attn_own = scatter_tensor(matmul_nt(heads_low, full_output).astype(bf16), 2)
    input_own = lax.dynamic_slice_in_dim(hidden_in[0], own_start, own_count, 0).astype(f32)
    residual_own = input_own + attn_own
    second_f, second_pull = jax.vjp(rms_scale, residual_own, gain_ffn)
    normed_own = second_f.astype(bf16)
    normed_all = gather_everyone(normed_own, 3)

    units = local_experts * hidden_width
    gate_flat = gate_weight.transpose(1, 0, 2).reshape(width, units)
    up_flat = up_weight.transpose(1, 0, 2).reshape(width, units)
    down_flat = down_weight.reshape(units, width)
    unit_expert = first_expert + jnp.arange(units, dtype=jnp.int32) // hidden_width
    lane_ids = jnp.arange(tensor_size * experts_total, dtype=jnp.int32)
    expand = (lane_ids[:, None] % experts_total == unit_expert[None, :]).astype(bf16)
    column = tensor_rank * experts_total + unit_expert
    place = (column[:, None] == lane_ids[None, :]).astype(bf16)
    router_lanes = jnp.concatenate([full_router] * tensor_size, axis=1)
    scattered, hidden_gated, gate_grad, up_grad = run_experts(
        normed_all, grad_out_all, codes, router_lanes, expand, place, gate_flat, up_flat, down_flat, 4
    )
    moe_part = matmul(hidden_gated, down_flat).astype(bf16)
    moe_own = lax.psum_scatter(moe_part, EVERYONE, scatter_dimension=0, tiled=True).astype(f32)
    grad_w_down = matmul_tn(hidden_gated, grad_out_all).reshape(down_weight.shape)

    def by_expert(unit_grad):
        unit_grad = unit_grad.reshape(-1, local_experts, hidden_width)
        return jnp.einsum("td,tju->jdu", normed_all, unit_grad, preferred_element_type=f32)

    grad_w_gate, grad_w_up = by_expert(gate_grad), by_expert(up_grad)

    scores = jnp.where(chosen_own, matmul(normed_own, full_router), NEGATIVE)
    gates_own = jnp.where(chosen_own, jax.nn.softmax(scores, axis=-1), 0.0)
    gates_grad_own = jnp.sum(
        scattered[:, width:].reshape(own_count, tensor_size, experts_total), axis=1
    )
    grad_selected = gates_own * (
        gates_grad_own - jnp.sum(gates_own * gates_grad_own, axis=1, keepdims=True)
    )
    grad_logits = jnp.pad(grad_selected.astype(bf16), ((0, 0), (0, 128 - experts_total)))
    grad_normed_two = scattered[:, :width] + matmul_nt(grad_logits[:, :experts_total], full_router)
    grad_resid_norm, grad_gain_ffn = second_pull(grad_normed_two)
    grad_resid_own = grad_out_own.astype(f32) + grad_resid_norm
    message = jnp.concatenate([grad_resid_own.astype(bf16), grad_logits], axis=1)
    extra = jnp.pad(grad_gain_ffn.astype(bf16)[None], ((0, 15), (0, 128)))
    message = gather_tensor(jnp.concatenate([message, extra], axis=0), 5)
    grad_attn = message[:, :own_count, :width].reshape(row_count, width)
    grad_raw, head_gain_grads = attend_back(
        grad_attn,
        full_output,
        query,
        kv,
        kv_other,
        raw,
        heads_full,
        log_total,
        cosine_table,
        sine_table,
        head_gains,
        seg_rows[:, :, None],
        seg_rows,
        9,
    )
    group_logits = message[:, :own_count, width:].reshape(row_count, 128)
    grad_gain_ffn = jnp.sum(message[:, own_count, :width].astype(f32), axis=0)
    normed_group = lax.dynamic_slice_in_dim(normed_all, group_rank * row_count, row_count, 0)
    grad_router = matmul_tn(normed_group, group_logits)
    extra = jnp.where(jnp.arange(128) == experts_total, grad_gain_ffn[:, None], grad_router)
    grad_w_output = jnp.concatenate([matmul_tn(grad_attn, heads_low), extra], axis=1)
    grad_w_output = lax.psum_scatter(
        grad_w_output.astype(bf16), GROUPS, scatter_dimension=0, tiled=True
    )

    grad_normed_part = matmul_nt(grad_raw, qkv_full)
    ignored, whole_pull = jax.vjp(rms_scale, hidden_in[0].astype(f32), gain_attn)
    head_gain_row = jnp.pad(head_gain_grads[:2].reshape(-1), (0, width - 2 * HEAD_SIZE))
    gain_rows = jnp.stack([whole_pull(grad_normed_part)[1], head_gain_row])
    message = jnp.pad(
        grad_normed_part.astype(bf16).reshape(tensor_size, own_count, width),
        ((0, 0), (0, 16), (0, 0)),
    )
    message = lax.dynamic_update_slice(message, gain_rows.astype(bf16)[None], (0, own_count, 0))
    message = scatter_tensor(message.reshape(-1, width), 6)
    ignored, first_pull = jax.vjp(rms_scale, input_own, gain_attn)
    grad_inputs_norm, ignored = first_pull(message[:own_count])
    message = jnp.concatenate([grad_resid_own + grad_inputs_norm, message[own_count:]], axis=0)
    message, moe_own, grad_w_down, grad_w_gate, grad_w_up = lax.optimization_barrier(
        (message.astype(bf16), moe_own, grad_w_down, grad_w_gate, grad_w_up)
    )
    message = jnp.concatenate([message, (residual_own + moe_own).astype(bf16)], axis=0)
    message = gather_tensor(message, 7)
    input_grad = message[:, :own_count].reshape(row_count, width).astype(f32)
    output = message[:, own_count + 16 :].reshape(row_count, width)
    gain_rows = message[0, own_count : own_count + 2].astype(f32)
    head_gains_grad = jnp.pad(
        gain_rows[1, : 2 * HEAD_SIZE].reshape(2, group_count, -1),
        ((0, 0), (0, 0), (0, (width - HEAD_SIZE) // group_count)),
    ).reshape(2, width)
    extra = jnp.pad(
        jnp.stack([gain_rows[0], head_gains_grad[0], head_gains_grad[1]], axis=1),
        ((0, 0), (0, 125)),
    )
    grad_qkv = jnp.concatenate([matmul_tn(normed_one, grad_raw), extra], axis=1)
    grad_qkv = scatter_groups(grad_qkv.astype(bf16), 208, 10)
    grad_qkv, grad_w_output = lax.optimization_barrier((grad_qkv, grad_w_output))
    value_at, extra_at = query_width + HEAD_SIZE, query_width + 2 * HEAD_SIZE
    return (
        output[None],
        input_grad[None],
        grad_qkv[:, extra_at],
        grad_qkv[:, :query_width],
        grad_qkv[:, query_width:value_at],
        grad_qkv[:, value_at:extra_at],
        grad_w_output[:, :query_width].astype(f32),
        grad_qkv[: query_gain.shape[0], extra_at + 1],
        grad_qkv[: key_gain.shape[0], extra_at + 2],
        grad_w_output[:, query_width + experts_total].astype(f32),
        grad_w_output[:, query_width : query_width + experts_total].astype(f32),
        grad_w_gate,
        grad_w_up,
        grad_w_down,
    )


def local(*arrays):
    sizes = tuple(lax.axis_size(name) for name in EVERYONE)
    return (gathered_local if sizes == (4, 2, 4) and arrays[9].shape[1] == 32 else routed_local)(*arrays)


def solution(mesh):
    in_specs = (
        P(FSDP, CONTEXT, None),
        P(GROUPS),
        P(GROUPS, TENSOR),
        P(GROUPS, TENSOR),
        P(GROUPS, TENSOR),
        P(GROUPS, TENSOR),
        P(GROUPS),
        P(GROUPS),
        P(GROUPS),
        P(GROUPS, None),
        P(GROUPS, None, TENSOR),
        P(GROUPS, None, TENSOR),
        P(GROUPS, TENSOR, None),
        P(FSDP, CONTEXT, None),
        P(FSDP, CONTEXT),
        P(FSDP, CONTEXT, None),
    )
    out_specs = (
        P(FSDP, CONTEXT, None),
        P(FSDP, CONTEXT, None),
        P(GROUPS),
        P(GROUPS, TENSOR),
        P(GROUPS, TENSOR),
        P(GROUPS, TENSOR),
        P(GROUPS, TENSOR),
        P(GROUPS),
        P(GROUPS),
        P(GROUPS),
        P(GROUPS, None),
        P(GROUPS, None, TENSOR),
        P(GROUPS, None, TENSOR),
        P(GROUPS, TENSOR, None),
    )
    return jax.shard_map(local, mesh=mesh, in_specs=in_specs, out_specs=out_specs, check_vma=False)
```

```python
import functools
import math

import jax
import jax.numpy as jnp
from jax import lax
from jax.experimental import pallas as pl
from jax.experimental.pallas import tpu as pltpu
from jax.sharding import PartitionSpec as P

HEAD_SIZE = 128
TOPK = 8
FSDP, CONTEXT, TENSOR = "fsdp", "context", "tensor"
GROUPS = (FSDP, CONTEXT)
EVERYONE = (FSDP, CONTEXT, TENSOR)


EPSILON = 1e-06
ROPE_BASE = 1000000.0
NEGATIVE = -1e30


def rms_scale(values, gain_vec):
    return (
        values * lax.rsqrt(jnp.mean(values * values, axis=-1, keepdims=True) + EPSILON) * gain_vec
    )


def rotate(values):
    half_width = values.shape[-1] // 2
    return jnp.concatenate([-values[..., half_width:], values[..., :half_width]], axis=-1)


def rope_tables(positions, head_width):
    step_index = jnp.arange(head_width // 2, dtype=jnp.float32)
    inverse = jnp.exp(step_index * (-2.0 * math.log(ROPE_BASE) / head_width))
    angles = positions.astype(jnp.float32)[:, None] * inverse[None, :]
    cosine_table = jnp.cos(angles)
    sine_table = jnp.sin(angles)
    return (
        jnp.concatenate([cosine_table, cosine_table], -1),
        jnp.concatenate([sine_table, sine_table], -1),
    )


def doc_positions(segment):
    token_index = jnp.arange(segment.shape[0], dtype=jnp.int32)
    smaller = (segment[None, :] < segment[:, None]).astype(jnp.int32)
    return token_index - jnp.sum(smaller, axis=1)


def earlier_counts(chosen):
    rows = chosen.shape[0]
    row_id = lax.broadcasted_iota(jnp.int32, (rows, rows), 0)
    col_id = lax.broadcasted_iota(jnp.int32, (rows, rows), 1)
    earlier = (col_id < row_id).astype(jnp.bfloat16)
    return matmul(earlier, chosen.astype(jnp.bfloat16))


def qk_finish(raw_values, gain_vec, cosine_table, sine_table):
    normed = rms_scale(raw_values, gain_vec)
    return normed * cosine_table + rotate(normed) * sine_table


def matmul(left_side, right_side):
    return jnp.dot(left_side, right_side, preferred_element_type=jnp.float32)


def matmul_nt(left_side, right_side):
    return lax.dot_general(
        left_side, right_side, (((1,), (1,)), ((), ())), preferred_element_type=jnp.float32
    )


def matmul_tn(left_side, right_side):
    return lax.dot_general(
        left_side, right_side, (((0,), (0,)), ((), ())), preferred_element_type=jnp.float32
    )


def block_scores(query_vectors, keys_all, seg_all, query_seg, query_index, key_ids, block_id, key_block):
    leading_row = block_id * key_block
    keys_part = lax.dynamic_slice_in_dim(keys_all, leading_row, key_block, 0)
    seg_part = lax.dynamic_slice_in_dim(seg_all, leading_row, key_block, 0)
    key_index = lax.dynamic_slice_in_dim(key_ids, leading_row, key_block, 0)
    score_scale = query_vectors.shape[2] ** (-0.5)
    scores = (
        jnp.einsum("qhd,kd->hqk", query_vectors, keys_part, preferred_element_type=jnp.float32)
        * score_scale
    )
    allowed = (query_seg[:, None] == seg_part[None, :]) & (
        key_index[None, :] <= query_index[:, None]
    )
    return (scores, allowed[None, :, :], keys_part)


def attention_forward(
    query_vectors, keys_all, values_all, seg_all, query_seg, query_index, key_ids, key_block
):
    row_count, head_count, head_width = query_vectors.shape
    block_count = keys_all.shape[0] // key_block

    def stats_step(running, block_id):
        run_max, run_sum = running
        scores, allowed, unused = block_scores(
            query_vectors, keys_all, seg_all, query_seg, query_index, key_ids, block_id, key_block
        )
        masked = jnp.where(allowed, scores, NEGATIVE)
        new_max = jnp.maximum(run_max, jnp.max(masked, axis=2))
        weights = jnp.where(allowed, jnp.exp(masked - new_max[:, :, None]), 0.0)
        run_sum = run_sum * jnp.exp(run_max - new_max) + jnp.sum(weights, axis=2)
        return ((new_max, run_sum), None)

    start_state = (
        jnp.full((head_count, row_count), NEGATIVE, jnp.float32),
        jnp.zeros((head_count, row_count), jnp.float32),
    )
    (run_max, run_sum), ignored = lax.scan(
        stats_step, start_state, jnp.arange(block_count, dtype=jnp.int32)
    )
    log_total = run_max + jnp.log(run_sum)

    def value_step(accumulated, block_id):
        scores, allowed, unused = block_scores(
            query_vectors, keys_all, seg_all, query_seg, query_index, key_ids, block_id, key_block
        )
        prob_block = jnp.where(allowed, jnp.exp(scores - log_total[:, :, None]), 0.0).astype(
            jnp.bfloat16
        )
        values_part = lax.dynamic_slice_in_dim(values_all, block_id * key_block, key_block, 0)
        accumulated = accumulated + jnp.einsum(
            "hqk,kd->qhd", prob_block, values_part, preferred_element_type=jnp.float32
        )
        return (accumulated, None)

    heads_full, ignored = lax.scan(
        value_step,
        jnp.zeros((row_count, head_count, head_width), jnp.float32),
        jnp.arange(block_count, dtype=jnp.int32),
    )
    return (heads_full, log_total)


def attention_backward(
    query_vectors,
    keys_all,
    values_all,
    seg_all,
    query_seg,
    query_index,
    key_ids,
    key_block,
    log_total,
    grad_heads,
    row_delta,
):
    row_count, head_count, head_width = query_vectors.shape
    block_count = keys_all.shape[0] // key_block
    score_scale = head_width ** (-0.5)

    def grad_step(grad_query, block_id):
        scores, allowed, keys_part = block_scores(
            query_vectors, keys_all, seg_all, query_seg, query_index, key_ids, block_id, key_block
        )
        values_part = lax.dynamic_slice_in_dim(values_all, block_id * key_block, key_block, 0)
        prob_block = jnp.where(allowed, jnp.exp(scores - log_total[:, :, None]), 0.0)
        grad_prob = jnp.einsum(
            "qhd,kd->hqk", grad_heads, values_part, preferred_element_type=jnp.float32
        )
        grad_score = (prob_block * (grad_prob - row_delta[:, :, None])).astype(jnp.bfloat16)
        grad_query = (
            grad_query
            + jnp.einsum("hqk,kd->qhd", grad_score, keys_part, preferred_element_type=jnp.float32)
            * score_scale
        )
        grad_key = (
            jnp.einsum("hqk,qhd->kd", grad_score, query_vectors, preferred_element_type=jnp.float32)
            * score_scale
        )
        grad_value = jnp.einsum(
            "hqk,qhd->kd",
            prob_block.astype(jnp.bfloat16),
            grad_heads,
            preferred_element_type=jnp.float32,
        )
        return (grad_query, (grad_key, grad_value))

    grad_query, (grad_key, grad_value) = lax.scan(
        grad_step,
        jnp.zeros((row_count, head_count, head_width), jnp.float32),
        jnp.arange(block_count, dtype=jnp.int32),
    )
    return (grad_query, grad_key.reshape(-1, head_width), grad_value.reshape(-1, head_width))


def to_experts(buffer):
    return lax.all_to_all(buffer, GROUPS, split_axis=0, concat_axis=1, tiled=True)


def from_experts(result_rows):
    return lax.all_to_all(result_rows, GROUPS, split_axis=1, concat_axis=0, tiled=True)


def pick_pairs(buffer, target, row_count):
    model_width = buffer.shape[2]
    flat_rows = jnp.concatenate(
        [buffer.reshape(-1, model_width), jnp.zeros((1, model_width), buffer.dtype)], axis=0
    )
    return flat_rows[target].reshape(row_count, TOPK, model_width)


def routed_local(
    hidden_in,
    attn_gain,
    w_query,
    key_weight,
    value_weight,
    w_output,
    query_gain,
    key_gain,
    ffn_gain,
    router,
    gate_weight,
    up_weight,
    down_weight,
    routes,
    segments,
    cotangent,
):
    context_rank = lax.axis_index(CONTEXT)
    input_rows = hidden_in[0].astype(jnp.float32)
    row_count, model_width = input_rows.shape
    gathered = (
        lax.all_gather(w_query, GROUPS, axis=0, tiled=True),
        lax.all_gather(key_weight, GROUPS, axis=0, tiled=True),
        lax.all_gather(value_weight, GROUPS, axis=0, tiled=True),
        lax.all_gather(w_output, GROUPS, axis=0, tiled=True),
        lax.all_gather(router, GROUPS, axis=0, tiled=True),
        lax.all_gather(attn_gain, GROUPS, axis=0, tiled=True),
        lax.all_gather(ffn_gain, GROUPS, axis=0, tiled=True),
        lax.all_gather(query_gain, GROUPS, axis=0, tiled=True),
        lax.all_gather(key_gain, GROUPS, axis=0, tiled=True),
    )
    full_query, full_key, full_value, full_output, full_router = (
        gathered[0],
        gathered[1],
        gathered[2],
        gathered[3],
        gathered[4],
    )
    gain_attn = gathered[5].astype(jnp.float32)
    gain_ffn = gathered[6].astype(jnp.float32)
    gain_query = gathered[7].astype(jnp.float32)
    gain_key = gathered[8].astype(jnp.float32)
    local_heads = full_query.shape[1] // HEAD_SIZE
    seg_all = lax.all_gather(segments, CONTEXT, axis=1, tiled=True)[0]
    length = seg_all.shape[0]
    start_row = context_rank * row_count
    positions = lax.dynamic_slice_in_dim(doc_positions(seg_all), start_row, row_count)
    cosine_table, sine_table = rope_tables(positions, HEAD_SIZE)
    query_seg = segments[0]
    query_index = start_row + jnp.arange(row_count, dtype=jnp.int32)
    key_ids = jnp.arange(length, dtype=jnp.int32)
    key_block = min(512, length)

    def query_finish(raw_values, gain_vec):
        return qk_finish(raw_values, gain_vec, cosine_table[:, None, :], sine_table[:, None, :])

    def key_finish(raw_values, gain_vec):
        return qk_finish(raw_values, gain_vec, cosine_table, sine_table)

    normed_f, first_pull = jax.vjp(rms_scale, input_rows, gain_attn)
    attention_normalized = normed_f.astype(jnp.bfloat16)
    query_unrotated = matmul(attention_normalized, full_query).reshape(
        row_count, local_heads, HEAD_SIZE
    )
    key_unrotated = matmul(attention_normalized, full_key)
    value_raw = matmul(attention_normalized, full_value)
    query_f, query_pull = jax.vjp(query_finish, query_unrotated, gain_query)
    key_f, key_pull = jax.vjp(key_finish, key_unrotated, gain_key)
    query_vectors = query_f.astype(jnp.bfloat16)
    keys_all, values_all = (
        lax.all_gather(key_f.astype(jnp.bfloat16), CONTEXT, axis=0, tiled=True),
        lax.all_gather(value_raw.astype(jnp.bfloat16), CONTEXT, axis=0, tiled=True),
    )
    heads_full, log_total = attention_forward(
        query_vectors, keys_all, values_all, seg_all, query_seg, query_index, key_ids, key_block
    )
    heads_low = heads_full.reshape(row_count, local_heads * HEAD_SIZE).astype(jnp.bfloat16)
    attn_out = lax.psum(matmul_nt(heads_low, full_output).astype(jnp.bfloat16), TENSOR).astype(
        jnp.float32
    )
    residual_stream = input_rows + attn_out
    second_f, second_pull = jax.vjp(rms_scale, residual_stream, gain_ffn)
    feedforward_normalized = second_f.astype(jnp.bfloat16)
    router_scores = matmul(feedforward_normalized, full_router)
    experts_total = full_router.shape[1]
    route_ids = routes[0]
    chosen = route_ids[:, :, None] == jnp.arange(experts_total, dtype=jnp.int32)
    selected = jnp.sum(jnp.where(chosen, router_scores[:, None, :], 0.0), axis=2)
    gate_probs = jax.nn.softmax(selected, axis=-1)
    capacity = 9 * row_count * TOPK // (8 * experts_total)
    before = earlier_counts(jnp.any(chosen, axis=1)).astype(jnp.int32)
    slot_index = jnp.sum(jnp.where(chosen, before[:, None, :], 0), axis=2)
    target = jnp.where(
        slot_index < capacity, route_ids * capacity + slot_index, experts_total * capacity
    ).reshape(-1)
    source = jnp.repeat(jnp.arange(row_count, dtype=jnp.int32), TOPK)
    send_rows = (
        jnp.zeros((experts_total * capacity, model_width), jnp.bfloat16)
        .at[target]
        .set(feedforward_normalized[source], mode="drop")
    )
    expert_input_rows = to_experts(send_rows.reshape(experts_total, capacity, model_width))
    gate_activation_input = jnp.einsum(
        "phu,puo->pho", expert_input_rows, gate_weight, preferred_element_type=jnp.float32
    )
    up_activation_input = jnp.einsum(
        "phu,puo->pho", expert_input_rows, up_weight, preferred_element_type=jnp.float32
    )
    sigmoid_gate = jax.nn.sigmoid(gate_activation_input)
    silu_gate = gate_activation_input * sigmoid_gate
    hidden_middle = (silu_gate * up_activation_input).astype(jnp.bfloat16)
    expert_part = jnp.einsum(
        "pic,pcw->piw", hidden_middle, down_weight, preferred_element_type=jnp.float32
    ).astype(jnp.bfloat16)
    grad_out = cotangent[0].astype(jnp.float32)
    returned = pick_pairs(from_experts(expert_part), target, row_count)
    moe_part = jnp.sum(returned.astype(jnp.float32) * gate_probs[:, :, None], axis=1)
    moe_out = lax.psum(moe_part.astype(jnp.bfloat16), TENSOR).astype(jnp.float32)
    grad_gate_part = jnp.sum(returned.astype(jnp.float32) * grad_out[:, None, :], axis=2)
    output = (residual_stream + moe_out).astype(jnp.bfloat16)
    pair_grad = (
        (gate_probs[:, :, None] * grad_out[:, None, :])
        .astype(jnp.bfloat16)
        .reshape(row_count * TOPK, model_width)
    )
    send_grad = (
        jnp.zeros((experts_total * capacity, model_width), jnp.bfloat16)
        .at[target]
        .set(pair_grad, mode="drop")
    )
    expert_output_gradient = to_experts(send_grad.reshape(experts_total, capacity, model_width))
    grad_mid = jnp.einsum(
        "jtk,jvk->jtv", expert_output_gradient, down_weight, preferred_element_type=jnp.float32
    )
    grad_w_down = jnp.einsum(
        "tce,tci->tei", hidden_middle, expert_output_gradient, preferred_element_type=jnp.float32
    )
    gate_activation_gradient = (
        grad_mid
        * up_activation_input
        * sigmoid_gate
        * (1.0 + gate_activation_input * (1.0 - sigmoid_gate))
    ).astype(jnp.bfloat16)
    up_activation_gradient = (grad_mid * silu_gate).astype(jnp.bfloat16)
    grad_w_gate = jnp.einsum(
        "ahw,ahp->awp",
        expert_input_rows,
        gate_activation_gradient,
        preferred_element_type=jnp.float32,
    )
    grad_w_up = jnp.einsum(
        "ahw,ahp->awp",
        expert_input_rows,
        up_activation_gradient,
        preferred_element_type=jnp.float32,
    )
    grad_expert_in = (
        jnp.einsum(
            "ous,ops->oup",
            gate_activation_gradient,
            gate_weight,
            preferred_element_type=jnp.float32,
        )
        + jnp.einsum(
            "ous,ops->oup", up_activation_gradient, up_weight, preferred_element_type=jnp.float32
        )
    ).astype(jnp.bfloat16)
    grad_pairs = pick_pairs(from_experts(grad_expert_in), target, row_count)
    grad_normed_part = jnp.sum(grad_pairs.astype(jnp.float32), axis=1)
    grad_normed_moe, grad_gates = (
        lax.psum(grad_normed_part.astype(jnp.bfloat16), TENSOR).astype(jnp.float32),
        lax.psum(grad_gate_part.astype(jnp.bfloat16), TENSOR).astype(jnp.float32),
    )
    grad_selected = gate_probs * (
        grad_gates - jnp.sum(gate_probs * grad_gates, axis=1, keepdims=True)
    )
    grad_logits = jnp.sum(jnp.where(chosen, grad_selected[:, :, None], 0.0), axis=1).astype(
        jnp.bfloat16
    )
    grad_router = matmul_tn(feedforward_normalized, grad_logits)
    grad_normed_two = grad_normed_moe + matmul_nt(grad_logits, full_router)
    grad_resid_norm, grad_gain_ffn = second_pull(grad_normed_two)
    grad_resid = grad_out + grad_resid_norm
    grad_attn = grad_resid.astype(jnp.bfloat16)
    grad_w_output = matmul_tn(grad_attn, heads_low)
    grad_heads = (
        matmul(grad_attn, full_output)
        .astype(jnp.bfloat16)
        .reshape(row_count, local_heads, HEAD_SIZE)
    )
    row_delta = jnp.sum(grad_heads.astype(jnp.float32) * heads_full, axis=2).T
    grad_query, grad_key_terms, grad_value_terms = attention_backward(
        query_vectors,
        keys_all,
        values_all,
        seg_all,
        query_seg,
        query_index,
        key_ids,
        key_block,
        log_total,
        grad_heads,
        row_delta,
    )
    grad_key_local, grad_value_local = (
        lax.psum_scatter(
            grad_key_terms.astype(jnp.bfloat16), CONTEXT, scatter_dimension=0, tiled=True
        ).astype(jnp.float32),
        lax.psum_scatter(
            grad_value_terms.astype(jnp.bfloat16), CONTEXT, scatter_dimension=0, tiled=True
        ).astype(jnp.float32),
    )
    grad_query_raw, grad_gain_query = query_pull(grad_query)
    grad_key_raw, grad_gain_key = key_pull(grad_key_local)
    grad_query_low = grad_query_raw.reshape(row_count, local_heads * HEAD_SIZE).astype(jnp.bfloat16)
    grad_key_low = grad_key_raw.astype(jnp.bfloat16)
    grad_value_low = grad_value_local.astype(jnp.bfloat16)
    grad_w_query = matmul_tn(attention_normalized, grad_query_low)
    grad_w_key = matmul_tn(attention_normalized, grad_key_low)
    grad_w_value = matmul_tn(attention_normalized, grad_value_low)
    grad_normed_one = (
        matmul_nt(grad_query_low, full_query)
        + matmul_nt(grad_key_low, full_key)
        + matmul_nt(grad_value_low, full_value)
    )
    grad_normed_one, grad_gain_query, grad_gain_key = (
        lax.psum(grad_normed_one.astype(jnp.bfloat16), TENSOR).astype(jnp.float32),
        lax.psum(grad_gain_query.astype(jnp.bfloat16), TENSOR).astype(jnp.float32),
        lax.psum(grad_gain_key.astype(jnp.bfloat16), TENSOR).astype(jnp.float32),
    )
    grad_inputs_norm, grad_gain_attn = first_pull(grad_normed_one)
    input_grad = grad_resid + grad_inputs_norm
    owned = (
        lax.psum_scatter(
            grad_w_query.astype(jnp.bfloat16), GROUPS, scatter_dimension=0, tiled=True
        ).astype(jnp.float32),
        lax.psum_scatter(
            grad_w_key.astype(jnp.bfloat16), GROUPS, scatter_dimension=0, tiled=True
        ).astype(jnp.float32),
        lax.psum_scatter(
            grad_w_value.astype(jnp.bfloat16), GROUPS, scatter_dimension=0, tiled=True
        ).astype(jnp.float32),
        lax.psum_scatter(
            grad_w_output.astype(jnp.bfloat16), GROUPS, scatter_dimension=0, tiled=True
        ).astype(jnp.float32),
        lax.psum_scatter(
            grad_router.astype(jnp.bfloat16), GROUPS, scatter_dimension=0, tiled=True
        ).astype(jnp.float32),
        lax.psum_scatter(
            grad_gain_attn.astype(jnp.bfloat16),
            GROUPS,
            scatter_dimension=0,
            tiled=True,
        ).astype(jnp.float32),
        lax.psum_scatter(
            grad_gain_ffn.astype(jnp.bfloat16), GROUPS, scatter_dimension=0, tiled=True
        ).astype(jnp.float32),
        lax.psum_scatter(
            grad_gain_query.astype(jnp.bfloat16),
            GROUPS,
            scatter_dimension=0,
            tiled=True,
        ).astype(jnp.float32),
        lax.psum_scatter(
            grad_gain_key.astype(jnp.bfloat16), GROUPS, scatter_dimension=0, tiled=True
        ).astype(jnp.float32),
    )
    return (
        output[None],
        input_grad[None],
        owned[5],
        owned[0],
        owned[1],
        owned[2],
        owned[3],
        owned[7],
        owned[8],
        owned[6],
        owned[4],
        grad_w_gate,
        grad_w_up,
        grad_w_down,
    )


MESH = pl.DeviceIdType.MESH
Z_UP, Z_DOWN, Y_SIDE, X_SIDE, CORE_SIDE = range(5)

def coords():
    z, y, t = lax.axis_index(FSDP), lax.axis_index(CONTEXT), lax.axis_index(TENSOR)
    return z, y, t // 2, t % 2

def partner(z, index):
    return (z, z + 1 - 2 * (z % 2), 2 - z // 2, 3 - 3 * (z // 2))[index]

def greet(neighbours):
    barrier = pltpu.get_barrier_semaphore()
    for condition, device in neighbours:
        def tell(device=device):
            pl.semaphore_signal(barrier, inc=1, device_id=device, device_id_type=MESH)
        if condition is None: tell()
        else: pl.when(condition)(tell)
    count = sum(1 if condition is None else condition.astype(jnp.int32) for condition, device in neighbours)
    pl.semaphore_wait(barrier, count)


def gather_kernel(x_ref, out_ref, own_sem, send_sems, recv_sems):
    rows = x_ref.shape[0]; half = rows // 2
    z, y, x, c = coords()
    side = {Z_UP: (z + 1, y, 2 * x + c), Z_DOWN: (z - 1, y, 2 * x + c), Y_SIDE: (z, 1 - y, 2 * x + c),
            X_SIDE: (z, y, 2 * (1 - x) + c), CORE_SIDE: (z, y, 2 * x + 1 - c)}
    greet([(z < 3, side[Z_UP]), (z > 0, side[Z_DOWN]), (None, side[Y_SIDE]), (None, side[X_SIDE]), (None, side[CORE_SIDE])])
    def device(zz, yy, xx, cc): return (zz * 2 + yy) * 4 + xx * 2 + cc
    def place(owner, h): return out_ref.at[pl.ds(pl.multiple_of(owner * rows + h * half, half), half)]
    def copy(link, owner, h, own=False):
        src = x_ref.at[pl.ds(h * half, half)] if own else place(owner, h)
        return pltpu.make_async_remote_copy(src_ref=src, dst_ref=place(owner, h), send_sem=send_sems.at[link, owner, h],
            recv_sem=recv_sems.at[owner, h], device_id=side[link], device_id_type=MESH)
    sent = []
    def start(link, owner, h, own=False, condition=None):
        one = copy(link, owner, h, own)
        sent.append((one, condition))
        if condition is None: one.start()
        else: pl.when(condition)(one.start)
    def arrived(owner, h): copy(CORE_SIDE, owner, h).wait_recv()
    me = device(z, y, x, c)
    keep = pltpu.make_async_copy(x_ref, out_ref.at[pl.ds(pl.multiple_of(me * rows, rows), rows)], own_sem)
    keep.start()
    def stage1(i):
        zz = partner(z, i); owner = device(zz, y, x, c); own = i == 0
        if not own:
            arrived(owner, 0); arrived(owner, 1)
        for h in range(2):
            start(Z_UP, owner, h, own, (z < 3) if own else (z < 3) & (zz < z))
            start(Z_DOWN, owner, h, own, (z > 0) if own else (z > 0) & (zz > z))
        start(Y_SIDE, owner, 0, own); start(X_SIDE, owner, 1, own)
        start(Y_SIDE, owner, 1, own); start(X_SIDE, owner, 0, own)
        for h in range(2): start(CORE_SIDE, owner, h, own)
    def stage2(i):
        zz = partner(z, i)
        oy, ox = device(zz, 1 - y, x, c), device(zz, y, 1 - x, c)
        arrived(oy, 0); start(X_SIDE, oy, 0); start(CORE_SIDE, oy, 0)
        arrived(ox, 1); start(Y_SIDE, ox, 1); start(CORE_SIDE, ox, 1)
        arrived(oy, 1); start(CORE_SIDE, oy, 1)
        arrived(ox, 0); start(CORE_SIDE, ox, 0)
    def stage3(i):
        o = device(partner(z, i), 1 - y, 1 - x, c)
        for h in range(2):
            arrived(o, h); start(CORE_SIDE, o, h)
    stage1(0); stage1(1); stage2(0); stage1(2); stage2(1); stage3(0); stage1(3); stage2(2); stage3(1); stage2(3); stage3(2); stage3(3)
    for i in range(4):
        for yy in range(2):
            for xx in range(2):
                for h in range(2): arrived(device(i, yy, xx, 1 - c), h)
    keep.wait()
    for one, condition in sent:
        if condition is None: one.wait_send()
        else: pl.when(condition)(one.wait_send)

def gather_everyone(x, collective_id):
    rows, width = x.shape
    return pl.pallas_call(gather_kernel, out_shape=jax.ShapeDtypeStruct((32 * rows, width), x.dtype),
        in_specs=[pl.BlockSpec(memory_space=pl.ANY)], out_specs=pl.BlockSpec(memory_space=pl.ANY),
        scratch_shapes=[pltpu.SemaphoreType.DMA, pltpu.SemaphoreType.DMA((5, 32, 2)), pltpu.SemaphoreType.DMA((32, 2))],
        compiler_params=pltpu.CompilerParams(collective_id=collective_id, has_side_effects=True))(x)

def groups_kernel(splits, *refs):
    count = len(splits)
    ins, outs = refs[:count], refs[count:2 * count]
    keep_sems, send_sems, recv_sems = refs[2 * count:]
    z, y, x, c = coords()
    t = 2 * x + c
    side = {Z_UP: (z + 1, y, t), Z_DOWN: (z - 1, y, t), Y_SIDE: (z, 1 - y, t)}
    greet([(z < 3, side[Z_UP]), (z > 0, side[Z_DOWN]), (None, side[Y_SIDE])])
    sent = []
    def place(k, owner, h):
        rows = ins[k].shape[0]
        first, size = (0, splits[k]) if h == 0 else (splits[k], rows - splits[k])
        return outs[k].at[pl.ds(pl.multiple_of(owner * rows + first, 16), size)], ins[k].at[pl.ds(first, size)]
    def copy(link, k, owner, h, own=False):
        dst, src = place(k, owner, h)
        return pltpu.make_async_remote_copy(src_ref=src if own else dst, dst_ref=dst, send_sem=send_sems.at[link, k, owner, h],
            recv_sem=recv_sems.at[k, owner, h], device_id=side[link], device_id_type=MESH)
    def halves(k): return (0, 1) if splits[k] < ins[k].shape[0] else (0,)
    def start(link, k, owner, h, own=False, condition=None):
        if h not in halves(k): return
        one = copy(link, k, owner, h, own)
        sent.append((one, condition))
        if condition is None: one.start()
        else: pl.when(condition)(one.start)
    def arrived(k, owner, h):
        if h in halves(k): copy(Y_SIDE, k, owner, h).wait_recv()
    def along(k, owner, h, zz, own=False):
        start(Z_UP, k, owner, h, own, (z < 3) & (zz <= z)); start(Z_DOWN, k, owner, h, own, (z > 0) & (zz >= z))
    kept = []
    me = z * 2 + y
    for k in range(count):
        along(k, me, 0, z, True); start(Y_SIDE, k, me, 1, True); start(Y_SIDE, k, me, 0, True); along(k, me, 1, z, True)
        rows = ins[k].shape[0]
        one = pltpu.make_async_copy(ins[k], outs[k].at[pl.ds(pl.multiple_of(me * rows, 16), rows)], keep_sems.at[k])
        one.start(); kept.append(one)
    for k in range(count):
        for i in range(4):
            zz = partner(z, i)
            near, far = zz * 2 + y, zz * 2 + 1 - y
            if i > 0:
                arrived(k, near, 0); along(k, near, 0, zz); start(Y_SIDE, k, near, 0)
                arrived(k, near, 1); along(k, near, 1, zz)
            arrived(k, far, 1); along(k, far, 1, zz)
    for k in range(count):
        for i in range(4): arrived(k, partner(z, i) * 2 + 1 - y, 0)
    for one in kept: one.wait()
    for one, condition in sent:
        if condition is None: one.wait_send()
        else: pl.when(condition)(one.wait_send)

def gather_groups(arrays, splits, collective_id):
    count = len(arrays); D = pltpu.SemaphoreType.DMA
    return pl.pallas_call(functools.partial(groups_kernel, splits),
        out_shape=[jax.ShapeDtypeStruct((8 * a.shape[0], a.shape[1]), a.dtype) for a in arrays],
        in_specs=[pl.BlockSpec(memory_space=pl.ANY)] * count, out_specs=[pl.BlockSpec(memory_space=pl.ANY)] * count,
        scratch_shapes=[D((count,)), D((3, count, 8, 2)), D((count, 8, 2))],
        compiler_params=pltpu.CompilerParams(collective_id=collective_id, has_side_effects=True))(*arrays)

def tensor_gather_kernel(x_ref, out_ref, keep_sem, send_sems, recv_sems):
    z, y, x, c = coords()
    x_side, core_side = (z, y, 2 * (1 - x) + c), (z, y, 2 * x + 1 - c)
    greet([(None, x_side), (None, core_side)])
    def copy(n, owner, device, own=False):
        return pltpu.make_async_remote_copy(src_ref=x_ref if own else out_ref.at[owner], dst_ref=out_ref.at[owner], send_sem=send_sems.at[n],
            recv_sem=recv_sems.at[owner], device_id=device, device_id_type=MESH)
    me, across, beside, last = 2 * x + c, 2 * (1 - x) + c, 2 * x + 1 - c, 2 * (1 - x) + 1 - c
    a, b, d = copy(0, me, x_side, True), copy(1, me, core_side, True), copy(2, across, core_side)
    a.start(); b.start()
    keep = pltpu.make_async_copy(x_ref, out_ref.at[me], keep_sem); keep.start()
    copy(0, across, x_side).wait_recv(); d.start()
    copy(0, beside, x_side).wait_recv(); copy(0, last, x_side).wait_recv()
    keep.wait(); a.wait_send(); b.wait_send(); d.wait_send()

def gather_tensor(x, collective_id):
    D = pltpu.SemaphoreType.DMA
    return pl.pallas_call(tensor_gather_kernel, out_shape=jax.ShapeDtypeStruct((4, *x.shape), x.dtype),
        in_specs=[pl.BlockSpec(memory_space=pl.ANY)], out_specs=pl.BlockSpec(memory_space=pl.ANY),
        scratch_shapes=[D, D((3,)), D((4,))],
        compiler_params=pltpu.CompilerParams(collective_id=collective_id, has_side_effects=True))(x)

def tensor_scatter_kernel(part_ref, out_ref, mine, core_in, line_in, sems, recv):
    z, y, x, c = coords()
    x_side, core_side = (z, y, 2 * (1 - x) + c), (z, y, 2 * x + 1 - c)
    greet([(None, x_side), (None, core_side)])
    rows = out_ref.shape[0]; f32 = jnp.float32
    def rows_of(xx, cc): return part_ref.at[pl.ds(pl.multiple_of((2 * xx + cc) * rows, rows), rows)]
    def over_core(n, xx):
        return pltpu.make_async_remote_copy(src_ref=rows_of(xx, 1 - c), dst_ref=core_in.at[n], send_sem=sems.at[n], recv_sem=recv.at[n],
            device_id=core_side, device_id_type=MESH)
    a, b = over_core(0, 1 - x), over_core(1, x)
    a.start(); b.start()
    a.wait_recv()
    mine[...] = (rows_of(1 - x, c)[...].astype(f32) + core_in[0].astype(f32)).astype(mine.dtype)
    d = pltpu.make_async_remote_copy(src_ref=mine, dst_ref=line_in, send_sem=sems.at[2], recv_sem=recv.at[2], device_id=x_side, device_id_type=MESH)
    d.start(); b.wait_recv()
    out_ref[...] = rows_of(x, c)[...].astype(f32) + core_in[1].astype(f32)
    d.wait_recv()
    out_ref[...] += line_in[...].astype(f32)
    a.wait_send(); b.wait_send(); d.wait_send()

def scatter_tensor(part, collective_id):
    D = pltpu.SemaphoreType.DMA; rows = part.shape[0] // 4; width = part.shape[1]
    return pl.pallas_call(tensor_scatter_kernel, out_shape=jax.ShapeDtypeStruct((rows, width), jnp.float32),
        in_specs=[pl.BlockSpec(memory_space=pltpu.VMEM)], out_specs=pl.BlockSpec(memory_space=pltpu.VMEM),
        scratch_shapes=[pltpu.VMEM((rows, width), part.dtype), pltpu.VMEM((2, rows, width), part.dtype), pltpu.VMEM((rows, width), part.dtype), D((3,)), D((3,))],
        compiler_params=pltpu.CompilerParams(collective_id=collective_id, has_side_effects=True, vmem_limit_bytes=24 << 20))(part)


def nt(a, b):
    return lax.dot_general(a, b, (((1,), (1,)), ((), ())), preferred_element_type=jnp.float32)

def nn(a, b):
    return jnp.dot(a, b, preferred_element_type=jnp.float32)

def nearest(z, index):
    choice = [partner(z, n) for n in range(4)]
    return jnp.where(index == 0, choice[0], jnp.where(index == 1, choice[1], jnp.where(index == 2, choice[2], choice[3])))

def spot(zz, yy, xx): return (zz * 2 + yy) * 2 + xx

def step_target(step):
    z, y, x, c = coords()
    n = step % 4
    return nearest(z, 3 - step // 4), jnp.where(n < 2, 1 - y, y), jnp.where(n % 2 == 0, 1 - x, x)

def step_block(ref, step):
    size = ref.shape[0] // 16
    return ref.at[pl.ds(pl.multiple_of(spot(*step_target(step)) * size, size), size)]

class Reduction:
    def __init__(self, part, mine, core_in, first_in, second_in, line_in, core_sem, first_sem, second_sem, line_send, line_recv):
        self.part, self.mine, self.core_in, self.first_in, self.second_in, self.line_in = part, mine, core_in, first_in, second_in, line_in
        self.core_sem, self.first_sem, self.second_sem, self.line_send, self.line_recv = core_sem, first_sem, second_sem, line_send, line_recv
        self.half = part.shape[2] // 2
        z, y, x, c = self.at = coords()
        self.up, self.down = (z + 1, y, 2 * x + c), (z - 1, y, 2 * x + c)
        self.y_side, self.x_side, self.core_side = (z, 1 - y, 2 * x + c), (z, y, 2 * (1 - x) + c), (z, y, 2 * x + 1 - c)

    @staticmethod
    def scratch(rows, width, dtype):
        V, D, half = pltpu.VMEM, pltpu.SemaphoreType.DMA, rows // 2
        return [V((2, 2, rows, width), dtype), V((16, rows, width), dtype), V((16, rows, width), dtype), V((2, 8, half, width), dtype),
            V((2, 4, half, width), dtype), V((2, 4, 2, half, width), dtype), D((2, 16)), D((2, 2, 8)), D((2, 2, 4)), D((4, 2)), D((2, 4, 2))]

    def greet(self):
        z = self.at[0]
        greet([(z < 3, self.up), (z > 0, self.down), (None, self.y_side), (None, self.x_side), (None, self.core_side)])

    @staticmethod
    def remote(src, dst, send, recv, device):
        return pltpu.make_async_remote_copy(src_ref=src, dst_ref=dst, send_sem=send, recv_sem=recv, device_id=device, device_id_type=MESH)

    def over_core(self, step):
        s = spot(*step_target(step))
        return self.remote(self.part.at[step % 2, 1 - self.at[3]], self.core_in.at[s], self.core_sem.at[0, s], self.core_sem.at[1, s], self.core_side)

    def piece(self, zz, yy, xx, h): return self.mine.at[spot(zz, yy, xx), pl.ds(h * self.half, self.half)]

    def first(self, h, zz, other):
        z, y, x, c = self.at
        src = self.piece(zz, other, 1 - x, 0) if h == 0 else self.piece(zz, 1 - y, other, 1)
        s = zz * 2 + other
        return self.remote(src, self.first_in.at[h, s], self.first_sem.at[0, h, s], self.first_sem.at[1, h, s], self.x_side if h == 0 else self.y_side)

    def second(self, h, zz):
        z, y, x, c = self.at
        src = self.piece(zz, 1 - y, x, 0) if h == 0 else self.piece(zz, y, 1 - x, 1)
        return self.remote(src, self.second_in.at[h, zz], self.second_sem.at[0, h, zz], self.second_sem.at[1, h, zz], self.y_side if h == 0 else self.x_side)

    def line(self, h, zz, way):
        z, y, x, c = self.at
        return self.remote(self.piece(zz, y, x, h), self.line_in.at[way, zz, h], self.line_send.at[zz, h], self.line_recv.at[way, zz, h], self.up if way == 0 else self.down)

    def add(self, s, h, arrived):
        at = (s, pl.ds(h * self.half, self.half))
        self.mine[at] = (self.mine[at].astype(jnp.float32) + arrived[...].astype(jnp.float32)).astype(self.mine.dtype)

    def stage_core(self, step):
        zz, yy, xx = step_target(step)
        s = spot(zz, yy, xx)
        self.over_core(step).wait_recv()
        self.mine[s] = (self.part[step % 2, self.at[3]].astype(jnp.float32) + self.core_in[s].astype(jnp.float32)).astype(self.mine.dtype)
        n = step % 4
        @pl.when(n % 2 == 0)
        def _(): self.first(0, zz, yy).start()
        @pl.when(n < 2)
        def _(): self.first(1, zz, xx).start()

    def stage_first(self, i):
        z, y, x, c = self.at
        zz = nearest(z, i)
        for n in range(2):
            for h, other in ((0, (1 - y, y)[n]), (1, (1 - x, x)[n])):
                self.first(h, zz, other).wait_recv()
                self.add(spot(zz, other, x) if h == 0 else spot(zz, y, other), h, self.first_in.at[h, zz * 2 + other])
                if n == 0: self.second(h, zz).start()

    def stage_second(self, i):
        z, y, x, c = self.at
        zz = nearest(z, i)
        for h in range(2):
            self.second(h, zz).wait_recv()
            self.add(spot(zz, y, x), h, self.second_in.at[h, zz])

    def stage_line(self, i):
        z, y, x, c = self.at
        zz = nearest(z, i)
        for h in range(2):
            for way, from_side, toward in ((0, z > 0, zz > z), (1, z < 3, zz < z)):
                @pl.when(from_side & (toward | (zz == z)))
                def _(h=h, way=way):
                    self.line(h, zz, way).wait_recv()
                    self.add(spot(zz, y, x), h, self.line_in.at[way, zz, h])
                @pl.when(toward)
                def _(h=h, way=way): self.line(h, zz, way).start()

    def follow(self, step):
        @pl.when(step >= 1)
        def _(): self.stage_core(step - 1)
        q = step // 4
        @pl.when((step % 4 == 1) & (q >= 1))
        def _(): self.stage_first(4 - q)
        @pl.when((step % 4 == 3) & (q >= 1))
        def _(): self.stage_second(4 - q)
        @pl.when((step % 4 == 1) & (q >= 2))
        def _(): self.stage_line(5 - q)

    def finish(self, out_ref):
        z, y, x, c = self.at
        self.stage_core(15); self.stage_line(1); self.stage_first(0); self.stage_second(0); self.stage_line(0)
        out_ref[...] = self.mine[spot(z, y, x)].astype(jnp.float32)
        self.over_core(14).wait_send(); self.over_core(15).wait_send()
        for zz in range(4):
            for other in range(2):
                for h in range(2): self.first(h, zz, other).wait_send()
            for h in range(2): self.second(h, zz).wait_send()
            @pl.when(zz != z)
            def _(zz=zz):
                for h in range(2): self.line(h, zz, 0).wait_send()

def expert_kernel(normed_ref, cot_ref, code_ref, router_ref, expand_ref, place_ref, gate_ref, up_ref, down_ref,
                  out_ref, hid_out, gate_out, up_out, normed_in, cot_in, code_in, units, in_sem, units_sem, *scratch):
    reduction = Reduction(*scratch)
    reduction.greet()
    part = reduction.part
    rows, width, wide = out_ref.shape[0], normed_ref.shape[1], gate_ref.shape[1]
    f32, bf16 = jnp.float32, jnp.bfloat16
    stride = code_ref.shape[0] // 8
    def loads(step):
        slot = step % 2
        zz, yy, xx = step_target(step)
        codes = code_ref.at[pl.ds(pl.multiple_of((zz * 2 + yy) * stride, 16), rows)]
        pairs = ((step_block(normed_ref, step), normed_in), (step_block(cot_ref, step), cot_in), (codes, code_in))
        return [pltpu.make_async_copy(src, dst.at[slot], in_sem.at[n, slot]) for n, (src, dst) in enumerate(pairs)]
    def stores(step):
        slot = step % 2
        return [pltpu.make_async_copy(units.at[slot, n], step_block(dst, step), units_sem.at[n, slot])
                for n, dst in enumerate((hid_out, gate_out, up_out))]
    for one in loads(0): one.start()

    def compute(step):
        slot = step % 2
        for one in loads(step): one.wait()
        @pl.when(step < 15)
        def _():
            for one in loads(step + 1): one.start()
        @pl.when(step >= 2)
        def _():
            for one in stores(step - 2): one.wait()
            reduction.over_core(step - 2).wait_send()
        normed, cot = normed_in[slot], cot_in[slot]
        code = code_in[slot].astype(f32)
        quarter = lax.broadcasted_iota(jnp.int32, code.shape, 1) // (128 // 4) - 2 * step_target(step)[2]
        code = jnp.concatenate([jnp.where(quarter == n, code, 0.0) for n in range(2)], axis=0)
        scores = jnp.where(code > 0.5, nn(normed, router_ref[...]), NEGATIVE)
        scores = jnp.where(code > 0.5, jnp.exp(scores - jnp.max(scores, axis=1, keepdims=True)), 0.0)
        gates = jnp.where(code > 1.5, scores / jnp.sum(scores, axis=1, keepdims=True), 0.0)
        high = gates.astype(bf16)
        low = (gates - high.astype(f32)).astype(bf16)
        grad_gates = jnp.zeros((2 * rows, 128), f32)
        for n in range(wide // 256):
            at = pl.ds(n * 256, 256)
            gate_in = nn(normed, gate_ref[:, at])
            up_in = nn(normed, up_ref[:, at])
            grad_mid = nt(cot, down_ref[at, :])
            gate = nn(high, expand_ref[:, at]) + nn(low, expand_ref[:, at])
            sig = lax.logistic(gate_in)
            silu = gate_in * sig
            hidden = silu * up_in
            grad_gates += nn(jnp.where(gate != 0.0, hidden * grad_mid, 0.0).astype(bf16), place_ref[at, :])
            grad_hidden = grad_mid * gate
            units[slot, 0, :, at] = (hidden * gate).astype(bf16)
            units[slot, 1, :, at] = (grad_hidden * up_in * sig * (1.0 + gate_in * (1.0 - sig))).astype(bf16)
            units[slot, 2, :, at] = (grad_hidden * silu).astype(bf16)
        for one in stores(step): one.start()
        gate_grad, up_grad = units[slot, 1], units[slot, 2]
        for n in range(width // 512):
            at = pl.ds(n * 512, 512)
            grad = (nt(gate_grad, gate_ref[at, :]) + nt(up_grad, up_ref[at, :])).astype(bf16)
            part[slot, 0, :, at] = grad[:rows]
            part[slot, 1, :, at] = grad[rows:]
        grad_gates = grad_gates.astype(bf16)
        part[slot, 0, :, pl.ds(width, 128)] = grad_gates[:rows]
        part[slot, 1, :, pl.ds(width, 128)] = grad_gates[rows:]
        reduction.over_core(step).start()

    @pl.loop(0, 16)
    def _(step):
        compute(step)
        reduction.follow(step)
    for step in (14, 15):
        for one in stores(step): one.wait()
    reduction.finish(out_ref)

def run_experts(normed_all, cot_all, codes, router, expand, place, gate_flat, up_flat, down_flat, collective_id):
    total, width = normed_all.shape; rows = total // 32; wide = gate_flat.shape[1]
    bf16 = jnp.bfloat16; D = pltpu.SemaphoreType.DMA; V = pltpu.VMEM; W = width + 128
    anyspec, vspec = pl.BlockSpec(memory_space=pl.ANY), pl.BlockSpec(memory_space=V)
    unit = jax.ShapeDtypeStruct((total, wide), bf16)
    return pl.pallas_call(expert_kernel,
        out_shape=[jax.ShapeDtypeStruct((rows, W), jnp.float32), unit, unit, unit],
        in_specs=[anyspec] * 3 + [vspec] * 6, out_specs=[vspec] + [anyspec] * 3,
        scratch_shapes=[V((2, 2 * rows, width), bf16), V((2, 2 * rows, width), bf16), V((2, rows, 128), bf16),
            V((2, 3, 2 * rows, wide), bf16), D((3, 2)), D((3, 2)), *Reduction.scratch(rows, W, bf16)],
        compiler_params=pltpu.CompilerParams(collective_id=collective_id, has_side_effects=True, vmem_limit_bytes=60 << 20))(
            normed_all, cot_all, codes, router, expand, place, gate_flat, up_flat, down_flat)

def output_kernel(normed_ref, cot_ref, hid_ref, gate_ref, up_ref, down_ref, out_ref, gate_out, up_out, down_out,
                  wide_in, thin_in, in_sem, out_sem, *scratch):
    reduction = Reduction(*scratch)
    reduction.greet()
    part = reduction.part
    rows, width, units = out_ref.shape[0], normed_ref.shape[1], hid_ref.shape[1]
    f32, bf16 = jnp.float32, jnp.bfloat16
    def loads(step):
        slot = step % 2
        return ([pltpu.make_async_copy(step_block(src, step), wide_in.at[slot, n], in_sem.at[n, slot]) for n, src in enumerate((normed_ref, cot_ref))]
            + [pltpu.make_async_copy(step_block(src, step), thin_in.at[slot, n], in_sem.at[2 + n, slot]) for n, src in enumerate((hid_ref, gate_ref, up_ref))])
    for one in loads(0): one.start()

    def inner(gate_sum, up_sum, down_sum):
        gate_sum[...] = jnp.zeros_like(gate_sum)
        up_sum[...] = jnp.zeros_like(up_sum)
        down_sum[...] = jnp.zeros_like(down_sum)

        @pl.loop(0, 16)
        def _(step):
            slot = step % 2
            for one in loads(step): one.wait()
            @pl.when(step < 15)
            def _():
                for one in loads(step + 1): one.start()
            @pl.when(step >= 2)
            def _(): reduction.over_core(step - 2).wait_send()
            hid = thin_in[slot, 0]
            for n in range(width // 512):
                at = pl.ds(n * 512, 512)
                value = nn(hid, down_ref[:, at]).astype(bf16)
                part[slot, 0, :, at] = value[:rows]
                part[slot, 1, :, at] = value[rows:]
            reduction.over_core(step).start()
            for n in range(units // 256):
                at = pl.ds(n * 256, 256)
                down_sum[at, :] += nn(thin_in[slot, 0, :, at].T, wide_in[slot, 1])
            for n in range(width // 256):
                at = pl.ds(n * 256, 256)
                turned = wide_in[slot, 0, :, at].T
                gate_sum[at, :] += nn(turned, thin_in[slot, 1])
                up_sum[at, :] += nn(turned, thin_in[slot, 2])
            reduction.follow(step)
        kept = [pltpu.make_async_copy(src, dst, out_sem.at[n])
                for n, (src, dst) in enumerate(((gate_sum, gate_out), (up_sum, up_out), (down_sum, down_out)))]
        for one in kept: one.start()
        reduction.finish(out_ref)
        for one in kept: one.wait()
    pl.run_scoped(inner, pltpu.VMEM((width, units), f32), pltpu.VMEM((width, units), f32), pltpu.VMEM((units, width), f32))

def run_outputs(normed_all, cot_all, hidden_gated, gate_grad, up_grad, down_flat, collective_id):
    total, width = normed_all.shape; rows = total // 32; units = hidden_gated.shape[1]
    f32, bf16 = jnp.float32, jnp.bfloat16; D = pltpu.SemaphoreType.DMA; V = pltpu.VMEM; S = jax.ShapeDtypeStruct
    anyspec, vspec = pl.BlockSpec(memory_space=pl.ANY), pl.BlockSpec(memory_space=V)
    return pl.pallas_call(output_kernel,
        out_shape=[S((rows, width), f32), S((width, units), f32), S((width, units), f32), S((units, width), f32)],
        in_specs=[anyspec] * 5 + [vspec], out_specs=[vspec] + [anyspec] * 3,
        scratch_shapes=[V((2, 2, 2 * rows, width), bf16), V((2, 3, 2 * rows, units), bf16), D((5, 2)), D((3,)),
            *Reduction.scratch(rows, width, bf16)],
        compiler_params=pltpu.CompilerParams(collective_id=collective_id, has_side_effects=True, vmem_limit_bytes=62 << 20))(
            normed_all, cot_all, hidden_gated, gate_grad, up_grad, down_flat)


def inverse_rms(values):
    return lax.rsqrt(jnp.mean(values * values, axis=-1, keepdims=True) + EPSILON)

def attend_kernel(x_ref, gain_ref, qkv_ref, cos_ref, sin_ref, head_gain_ref, seg_rows_ref, seg_cols_ref,
                  normed_ref, raw_ref, q_ref, kv_ref, kv_other_ref, full_ref, lse_ref, bias, send_sem, recv_sem):
    z, y, x, c = coords()
    other = (z, 1 - y, 2 * x + c)
    greet([(None, other)])
    f32, bf16 = jnp.float32, jnp.bfloat16
    rows = x_ref.shape[0]; heads = q_ref.shape[1] // HEAD_SIZE; q_width = heads * HEAD_SIZE
    values = x_ref[...].astype(f32)
    normed_ref[...] = (values * inverse_rms(values) * gain_ref[...]).astype(bf16)
    def finish(raw, n):
        normed = raw * inverse_rms(raw) * head_gain_ref[pl.ds(n, 1), :]
        return (normed * cos_ref[...] + pltpu.roll(normed, HEAD_SIZE // 2, 1) * sin_ref[...]).astype(bf16)
    raw_kv = nn(normed_ref[...], qkv_ref[:, pl.ds(q_width, 2 * HEAD_SIZE)])
    raw_ref[:, pl.ds(q_width, HEAD_SIZE)] = raw_kv[:, :HEAD_SIZE]
    kv_ref[:, pl.ds(0, HEAD_SIZE)] = finish(raw_kv[:, :HEAD_SIZE], 1)
    kv_ref[:, pl.ds(HEAD_SIZE, HEAD_SIZE)] = raw_kv[:, HEAD_SIZE:].astype(bf16)
    move = pltpu.make_async_remote_copy(src_ref=kv_ref, dst_ref=kv_other_ref, send_sem=send_sem, recv_sem=recv_sem,
        device_id=other, device_id_type=MESH)
    @pl.when(y == 0)
    def _():
        move.start()
        kv_other_ref[...] = jnp.zeros_like(kv_other_ref)
    @pl.loop(0, heads // 2)
    def _(n):
        at = pl.ds(pl.multiple_of(n * 2 * HEAD_SIZE, 2 * HEAD_SIZE), 2 * HEAD_SIZE)
        raw = nn(normed_ref[...], qkv_ref[:, at])
        raw_ref[:, at] = raw
        for m in range(2):
            one = pl.ds(pl.multiple_of((2 * n + m) * HEAD_SIZE, HEAD_SIZE), HEAD_SIZE)
            q_ref[:, one] = finish(raw[:, m * HEAD_SIZE:(m + 1) * HEAD_SIZE], 0)
    row_id = lax.broadcasted_iota(jnp.int32, (rows, rows), 0)
    col_id = lax.broadcasted_iota(jnp.int32, (rows, rows), 1)
    bias[0] = jnp.where((seg_rows_ref[...] == seg_cols_ref[pl.ds(0, 1), :]) & (col_id <= row_id), 0.0, NEGATIVE)
    bias[1] = jnp.where(seg_rows_ref[...] == seg_cols_ref[pl.ds(1, 1), :], 0.0, NEGATIVE)
    lse_ref[...] = jnp.zeros_like(lse_ref)
    scale = HEAD_SIZE ** -0.5
    lane = lax.broadcasted_iota(jnp.int32, (rows, HEAD_SIZE), 1)
    def head(h, blocks):
        at = pl.ds(pl.multiple_of(h * HEAD_SIZE, HEAD_SIZE), HEAD_SIZE)
        query = q_ref[:, at]
        refs = (kv_ref, kv_other_ref)[:blocks]
        scores = [nt(query, ref[:, pl.ds(0, HEAD_SIZE)]) * scale + bias[n] for n, ref in enumerate(refs)]
        top = functools.reduce(jnp.maximum, [jnp.max(s, axis=1, keepdims=True) for s in scores])
        weights = [jnp.exp(s - top) for s in scores]
        total = sum(jnp.sum(w, axis=1, keepdims=True) for w in weights)
        inverse = 1.0 / total
        full_ref[:, at] = sum(nn((w * inverse).astype(bf16), ref[:, pl.ds(HEAD_SIZE, HEAD_SIZE)]) for w, ref in zip(weights, refs))
        lse_ref[...] = jnp.where(lane == h, top + jnp.log(total), lse_ref[...])
    @pl.when(y == 0)
    def _():
        @pl.loop(0, heads)
        def _(h): head(h, 1)
        move.wait_send()
    @pl.when(y == 1)
    def _():
        move.wait_recv()
        @pl.loop(0, heads)
        def _(h): head(h, 2)

def attend(x, gain, qkv, cos, sin, head_gains, seg_rows, seg_cols, collective_id):
    rows, width = x.shape; q_width = qkv.shape[1] - 2 * HEAD_SIZE
    V = pltpu.VMEM; f32, bf16 = jnp.float32, jnp.bfloat16; S = jax.ShapeDtypeStruct
    vspec = pl.BlockSpec(memory_space=V)
    return pl.pallas_call(attend_kernel,
        out_shape=[S((rows, width), bf16), S((rows, q_width + HEAD_SIZE), f32), S((rows, q_width), bf16), S((rows, 2 * HEAD_SIZE), bf16),
            S((rows, 2 * HEAD_SIZE), bf16), S((rows, q_width), f32), S((rows, HEAD_SIZE), f32)],
        in_specs=[vspec] * 8, out_specs=[vspec] * 7,
        scratch_shapes=[V((2, rows, rows), f32), pltpu.SemaphoreType.DMA, pltpu.SemaphoreType.DMA],
        compiler_params=pltpu.CompilerParams(collective_id=collective_id, has_side_effects=True, vmem_limit_bytes=48 << 20))(
            x, gain, qkv, cos, sin, head_gains, seg_rows, seg_cols)

def attend_back_kernel(cot_ref, out_w_ref, q_ref, kv_ref, kv_other_ref, raw_ref, full_ref, lse_ref, cos_ref, sin_ref, head_gain_ref,
                       seg_rows_ref, seg_cols_ref, grad_ref, gains_ref, grad_heads, delta, stats, bias, grad_q, grad_kv, kv_send, kv_in, send_sem, recv_sem):
    z, y, x, c = coords()
    other = (z, 1 - y, 2 * x + c)
    greet([(None, other)])
    f32, bf16 = jnp.float32, jnp.bfloat16
    rows = q_ref.shape[0]; heads = q_ref.shape[1] // HEAD_SIZE; q_width = heads * HEAD_SIZE
    scale = HEAD_SIZE ** -0.5
    lane = lax.broadcasted_iota(jnp.int32, (rows, HEAD_SIZE), 1)
    delta[...] = jnp.zeros_like(delta)
    @pl.loop(0, heads // 2)
    def _(n):
        at = pl.ds(pl.multiple_of(n * 2 * HEAD_SIZE, 2 * HEAD_SIZE), 2 * HEAD_SIZE)
        grad = nn(cot_ref[...], out_w_ref[:, at]).astype(bf16)
        grad_heads[:, at] = grad
        product = grad.astype(f32) * full_ref[:, at]
        for m in range(2):
            one = jnp.sum(product[:, m * HEAD_SIZE:(m + 1) * HEAD_SIZE], axis=1, keepdims=True)
            delta[...] = jnp.where(lane == 2 * n + m, one, delta[...])
    stats[0] = lse_ref[...].T
    stats[1] = delta[...].T
    key_id = lax.broadcasted_iota(jnp.int32, (rows, rows), 0)
    query_id = lax.broadcasted_iota(jnp.int32, (rows, rows), 1)
    def block(ref, seg_keys, causal):
        same = seg_keys == seg_cols_ref[pl.ds(0, 1), :]
        bias[...] = jnp.where(same & (key_id <= query_id) if causal else same, 0.0, NEGATIVE)
        grad_kv[...] = jnp.zeros_like(grad_kv)
        key, value = ref[:, pl.ds(0, HEAD_SIZE)], ref[:, pl.ds(HEAD_SIZE, HEAD_SIZE)]
        @pl.loop(0, heads)
        def _(h):
            at = pl.ds(pl.multiple_of(h * HEAD_SIZE, HEAD_SIZE), HEAD_SIZE)
            query, grad = q_ref[:, at], grad_heads[:, at]
            probs = jnp.exp(nt(key, query) * scale + bias[...] - stats[0, pl.ds(h, 1), :])
            grad_scores = (probs * (nt(value, grad) - stats[1, pl.ds(h, 1), :])).astype(bf16)
            grad_kv[:, pl.ds(0, HEAD_SIZE)] += nn(grad_scores, query) * scale
            grad_kv[:, pl.ds(HEAD_SIZE, HEAD_SIZE)] += nn(probs.astype(bf16), grad)
            grad_q[:, at] += lax.dot_general(grad_scores, key, (((0,), (0,)), ((), ())), preferred_element_type=f32) * scale
    grad_q[...] = jnp.zeros_like(grad_q)
    move = pltpu.make_async_remote_copy(src_ref=kv_send, dst_ref=kv_in, send_sem=send_sem, recv_sem=recv_sem, device_id=other, device_id_type=MESH)
    @pl.when(y == 1)
    def _():
        block(kv_other_ref, seg_rows_ref[1], False)
        kv_send[...] = grad_kv[...].astype(bf16)
        move.start()
    block(kv_ref, seg_rows_ref[0], True)
    @pl.when(y == 0)
    def _():
        move.wait_recv()
        grad_kv[...] += kv_in[...].astype(f32)
    def pull(grad, raw, n):
        turned = grad * cos_ref[...] - pltpu.roll(grad, HEAD_SIZE // 2, 1) * sin_ref[...]
        inverse = inverse_rms(raw)
        unit = raw * inverse
        gains_ref[pl.ds(n, 1), :] += jnp.sum(turned * unit, axis=0, keepdims=True)
        scaled = turned * head_gain_ref[pl.ds(n, 1), :]
        return (inverse * (scaled - unit * jnp.mean(scaled * unit, axis=1, keepdims=True))).astype(bf16)
    gains_ref[...] = jnp.zeros_like(gains_ref)
    @pl.loop(0, heads)
    def _(h):
        at = pl.ds(pl.multiple_of(h * HEAD_SIZE, HEAD_SIZE), HEAD_SIZE)
        grad_ref[:, at] = pull(grad_q[:, at], raw_ref[:, at], 0)
    at = pl.ds(q_width, HEAD_SIZE)
    grad_ref[:, at] = pull(grad_kv[:, pl.ds(0, HEAD_SIZE)], raw_ref[:, at], 1)
    grad_ref[:, pl.ds(q_width + HEAD_SIZE, HEAD_SIZE)] = grad_kv[:, pl.ds(HEAD_SIZE, HEAD_SIZE)].astype(bf16)
    @pl.when(y == 1)
    def _(): move.wait_send()

def attend_back(cot, out_w, q, kv, kv_other, raw, full, lse, cos, sin, head_gains, seg_rows, seg_cols, collective_id):
    rows, q_width = q.shape
    V = pltpu.VMEM; f32, bf16 = jnp.float32, jnp.bfloat16; S = jax.ShapeDtypeStruct
    vspec = pl.BlockSpec(memory_space=V)
    return pl.pallas_call(attend_back_kernel,
        out_shape=[S((rows, q_width + 2 * HEAD_SIZE), bf16), S((8, HEAD_SIZE), f32)],
        in_specs=[vspec] * 13, out_specs=[vspec] * 2,
        scratch_shapes=[V((rows, q_width), bf16), V((rows, HEAD_SIZE), f32), V((2, HEAD_SIZE, rows), f32), V((rows, rows), f32), V((rows, q_width), f32),
            V((rows, 2 * HEAD_SIZE), f32), V((rows, 2 * HEAD_SIZE), bf16), V((rows, 2 * HEAD_SIZE), bf16), pltpu.SemaphoreType.DMA, pltpu.SemaphoreType.DMA],
        compiler_params=pltpu.CompilerParams(collective_id=collective_id, has_side_effects=True, vmem_limit_bytes=48 << 20))(
            cot, out_w, q, kv, kv_other, raw, full, lse, cos, sin, head_gains, seg_rows, seg_cols)


def gathered_local(
    hidden_in,
    attn_gain,
    w_query,
    key_weight,
    value_weight,
    w_output,
    query_gain,
    key_gain,
    ffn_gain,
    router,
    gate_weight,
    up_weight,
    down_weight,
    routes,
    segments,
    cotangent,
):
    bf16, f32 = jnp.bfloat16, jnp.float32
    context_size = lax.axis_size(CONTEXT)
    tensor_size = lax.axis_size(TENSOR)
    group_count = lax.axis_size(FSDP) * context_size
    fsdp_rank = lax.axis_index(FSDP)
    context_rank = lax.axis_index(CONTEXT)
    tensor_rank = lax.axis_index(TENSOR)
    group_rank = fsdp_rank * context_size + context_rank
    row_count, width = hidden_in.shape[1:]
    own_count = row_count // tensor_size
    own_start = tensor_rank * own_count
    local_experts, _, hidden_width = gate_weight.shape
    experts_total = router.shape[1]
    first_expert = group_rank * local_experts
    capacity = 9 * row_count * TOPK // (8 * experts_total)
    query_width = w_query.shape[1]

    expert_ids = jnp.arange(experts_total, dtype=jnp.int32)
    chosen = jnp.any(routes[0][..., None] == expert_ids, axis=1)
    kept = chosen & (earlier_counts(chosen) < capacity)
    code = chosen.astype(bf16) + kept.astype(bf16)
    chosen_own = lax.dynamic_slice_in_dim(chosen, own_start, own_count, 0)
    code = code.reshape(tensor_size, own_count, experts_total).transpose(1, 0, 2)

    pieces = (code, router, attn_gain, ffn_gain, query_gain, key_gain, segments)
    small = jnp.concatenate([piece.astype(bf16).reshape(-1) for piece in pieces])
    small = jnp.pad(small, (0, -small.size % 2048)).reshape(-1, 128)
    qkv_weight = jnp.concatenate([w_query, key_weight, value_weight], axis=1)
    small, qkv_full, full_output = gather_groups(
        (small, qkv_weight, w_output), (small.shape[0], 208, 208), 1
    )
    grad_out_own = lax.dynamic_slice_in_dim(cotangent[0], own_start, own_count, 0)
    grad_out_own, codes = lax.optimization_barrier((grad_out_own, small))
    grad_out_all = lax.all_gather(grad_out_own, EVERYONE, axis=0, tiled=True)
    small = small.reshape(group_count, -1)
    parts, at = [], code.size
    for piece in pieces[1:]:
        parts.append(small[:, at : at + piece.size])
        at += piece.size
    full_router = parts[0].reshape(width, experts_total)
    gain_attn, gain_ffn, gain_query, gain_key = (
        part.reshape(-1).astype(f32) for part in parts[1:5]
    )
    head_gains = jnp.stack([gain_query, gain_key])
    all_segments = parts[5].astype(jnp.int32)

    own_seg = segments[0]
    first_seg = lax.dynamic_index_in_dim(all_segments, group_rank - context_rank, 0, keepdims=False)
    other_seg = lax.dynamic_index_in_dim(
        all_segments, group_rank + 1 - 2 * context_rank, 0, keepdims=False
    )
    smaller = jnp.sum((own_seg[None, :] < own_seg[:, None]).astype(jnp.int32), axis=1)
    smaller_first = jnp.sum((first_seg[None, :] < own_seg[:, None]).astype(jnp.int32), axis=1)
    positions = jnp.arange(row_count, dtype=jnp.int32) - smaller
    positions = positions + context_rank * (row_count - smaller_first)
    cosine_table, sine_table = rope_tables(positions, HEAD_SIZE)
    turn = jnp.where(jnp.arange(HEAD_SIZE) < HEAD_SIZE // 2, -1.0, 1.0)
    sine_table = sine_table * turn
    seg_rows = jnp.stack([own_seg, other_seg])

    normed_one, raw, query, kv, kv_other, heads_full, log_total = attend(
        hidden_in[0],
        gain_attn[None],
        qkv_full,
        cosine_table,
        sine_table,
        head_gains,
        own_seg[:, None],
        seg_rows,
        8,
    )
    heads_low = heads_full.astype(bf16)
    attn_own = scatter_tensor(matmul_nt(heads_low, full_output).astype(bf16), 2)
    input_own = lax.dynamic_slice_in_dim(hidden_in[0], own_start, own_count, 0).astype(f32)
    residual_own = input_own + attn_own
    second_f, second_pull = jax.vjp(rms_scale, residual_own, gain_ffn)
    normed_own = second_f.astype(bf16)
    normed_all = gather_everyone(normed_own, 3)

    units = local_experts * hidden_width
    gate_flat = gate_weight.transpose(1, 0, 2).reshape(width, units)
    up_flat = up_weight.transpose(1, 0, 2).reshape(width, units)
    down_flat = down_weight.reshape(units, width)
    unit_expert = first_expert + jnp.arange(units, dtype=jnp.int32) // hidden_width
    lane_ids = jnp.arange(tensor_size * experts_total, dtype=jnp.int32)
    expand = (lane_ids[:, None] % experts_total == unit_expert[None, :]).astype(bf16)
    column = tensor_rank * experts_total + unit_expert
    place = (column[:, None] == lane_ids[None, :]).astype(bf16)
    router_lanes = jnp.concatenate([full_router] * tensor_size, axis=1)
    scattered, hidden_gated, gate_grad, up_grad = run_experts(
        normed_all, grad_out_all, codes, router_lanes, expand, place, gate_flat, up_flat, down_flat, 4
    )
    scores = jnp.where(chosen_own, matmul(normed_own, full_router), NEGATIVE)
    gates_own = jnp.where(chosen_own, jax.nn.softmax(scores, axis=-1), 0.0)
    gates_grad_own = jnp.sum(
        scattered[:, width:].reshape(own_count, tensor_size, experts_total), axis=1
    )
    grad_selected = gates_own * (
        gates_grad_own - jnp.sum(gates_own * gates_grad_own, axis=1, keepdims=True)
    )
    grad_logits = jnp.pad(grad_selected.astype(bf16), ((0, 0), (0, 128 - experts_total)))
    grad_normed_two = scattered[:, :width] + matmul_nt(grad_logits[:, :experts_total], full_router)
    grad_resid_norm, grad_gain_ffn = second_pull(grad_normed_two)
    grad_resid_own = grad_out_own.astype(f32) + grad_resid_norm
    message = jnp.concatenate([grad_resid_own.astype(bf16), grad_logits], axis=1)
    extra = jnp.pad(grad_gain_ffn.astype(bf16)[None], ((0, 15), (0, 128)))
    message = gather_tensor(jnp.concatenate([message, extra], axis=0), 5)
    grad_attn = message[:, :own_count, :width].reshape(row_count, width)
    grad_raw, head_gain_grads = attend_back(
        grad_attn,
        full_output,
        query,
        kv,
        kv_other,
        raw,
        heads_full,
        log_total,
        cosine_table,
        sine_table,
        head_gains,
        seg_rows[:, :, None],
        seg_rows,
        9,
    )
    group_logits = message[:, :own_count, width:].reshape(row_count, 128)
    grad_gain_ffn = jnp.sum(message[:, own_count, :width].astype(f32), axis=0)
    normed_group = lax.dynamic_slice_in_dim(normed_all, group_rank * row_count, row_count, 0)
    grad_router = matmul_tn(normed_group, group_logits)
    extra = jnp.where(jnp.arange(128) == experts_total, grad_gain_ffn[:, None], grad_router)
    grad_w_output = jnp.concatenate([matmul_tn(grad_attn, heads_low), extra], axis=1)
    grad_w_output = lax.psum_scatter(
        grad_w_output.astype(bf16), GROUPS, scatter_dimension=0, tiled=True
    )

    grad_normed_part = matmul_nt(grad_raw, qkv_full)
    ignored, whole_pull = jax.vjp(rms_scale, hidden_in[0].astype(f32), gain_attn)
    head_gain_row = jnp.pad(head_gain_grads[:2].reshape(-1), (0, width - 2 * HEAD_SIZE))
    gain_rows = jnp.stack([whole_pull(grad_normed_part)[1], head_gain_row])
    message = jnp.pad(
        grad_normed_part.astype(bf16).reshape(tensor_size, own_count, width),
        ((0, 0), (0, 16), (0, 0)),
    )
    message = lax.dynamic_update_slice(message, gain_rows.astype(bf16)[None], (0, own_count, 0))
    message = scatter_tensor(message.reshape(-1, width), 6)
    ignored, first_pull = jax.vjp(rms_scale, input_own, gain_attn)
    grad_inputs_norm, ignored = first_pull(message[:own_count])
    message = jnp.concatenate([grad_resid_own + grad_inputs_norm, message[own_count:]], axis=0)
    message = gather_tensor(message.astype(bf16), 7)
    input_grad = message[:, :own_count].reshape(row_count, width).astype(f32)
    gain_rows = message[0, own_count : own_count + 2].astype(f32)
    head_gains_grad = jnp.pad(
        gain_rows[1, : 2 * HEAD_SIZE].reshape(2, group_count, -1),
        ((0, 0), (0, 0), (0, (width - HEAD_SIZE) // group_count)),
    ).reshape(2, width)
    extra = jnp.pad(
        jnp.stack([gain_rows[0], head_gains_grad[0], head_gains_grad[1]], axis=1),
        ((0, 0), (0, 125)),
    )
    grad_qkv = jnp.concatenate([matmul_tn(normed_one, grad_raw), extra], axis=1)
    grad_qkv, hidden_gated = lax.optimization_barrier((grad_qkv.astype(bf16), hidden_gated))
    grad_qkv = lax.psum_scatter(grad_qkv, GROUPS, scatter_dimension=0, tiled=True)
    moe_own, grad_w_gate, grad_w_up, grad_w_down = run_outputs(
        normed_all, grad_out_all, hidden_gated, gate_grad, up_grad, down_flat, 10
    )

    def by_expert(grad):
        return grad.reshape(width, local_experts, hidden_width).transpose(1, 0, 2)

    grad_w_gate, grad_w_up = by_expert(grad_w_gate), by_expert(grad_w_up)
    output = gather_tensor((residual_own + moe_own).astype(bf16), 11).reshape(row_count, width)
    output, grad_qkv, grad_w_output = lax.optimization_barrier((output, grad_qkv, grad_w_output))
    grad_qkv, grad_w_output = grad_qkv.astype(f32), grad_w_output.astype(f32)
    value_at, extra_at = query_width + HEAD_SIZE, query_width + 2 * HEAD_SIZE
    return (
        output[None],
        input_grad[None],
        grad_qkv[:, extra_at],
        grad_qkv[:, :query_width],
        grad_qkv[:, query_width:value_at],
        grad_qkv[:, value_at:extra_at],
        grad_w_output[:, :query_width],
        grad_qkv[: query_gain.shape[0], extra_at + 1],
        grad_qkv[: key_gain.shape[0], extra_at + 2],
        grad_w_output[:, query_width + experts_total],
        grad_w_output[:, query_width : query_width + experts_total],
        grad_w_gate,
        grad_w_up,
        grad_w_down.reshape(down_weight.shape),
    )


def local(*arrays):
    sizes = tuple(lax.axis_size(name) for name in EVERYONE)
    return (gathered_local if sizes == (4, 2, 4) and arrays[9].shape[1] == 32 else routed_local)(*arrays)


def solution(mesh):
    in_specs = (
        P(FSDP, CONTEXT, None),
        P(GROUPS),
        P(GROUPS, TENSOR),
        P(GROUPS, TENSOR),
        P(GROUPS, TENSOR),
        P(GROUPS, TENSOR),
        P(GROUPS),
        P(GROUPS),
        P(GROUPS),
        P(GROUPS, None),
        P(GROUPS, None, TENSOR),
        P(GROUPS, None, TENSOR),
        P(GROUPS, TENSOR, None),
        P(FSDP, CONTEXT, None),
        P(FSDP, CONTEXT),
        P(FSDP, CONTEXT, None),
    )
    out_specs = (
        P(FSDP, CONTEXT, None),
        P(FSDP, CONTEXT, None),
        P(GROUPS),
        P(GROUPS, TENSOR),
        P(GROUPS, TENSOR),
        P(GROUPS, TENSOR),
        P(GROUPS, TENSOR),
        P(GROUPS),
        P(GROUPS),
        P(GROUPS),
        P(GROUPS, None),
        P(GROUPS, None, TENSOR),
        P(GROUPS, None, TENSOR),
        P(GROUPS, TENSOR, None),
    )
    return jax.shard_map(local, mesh=mesh, in_specs=in_specs, out_specs=out_specs, check_vma=False)
```

```python
import functools
import math

import jax
import jax.numpy as jnp
from jax import lax
from jax.experimental import pallas as pl
from jax.experimental.pallas import tpu as pltpu
from jax.sharding import PartitionSpec as P

HEAD_SIZE = 128
TOPK = 8
FSDP, CONTEXT, TENSOR = "fsdp", "context", "tensor"
GROUPS = (FSDP, CONTEXT)
EVERYONE = (FSDP, CONTEXT, TENSOR)


EPSILON = 1e-06
ROPE_BASE = 1000000.0
NEGATIVE = -1e30


def rms_scale(values, gain_vec):
    return (
        values * lax.rsqrt(jnp.mean(values * values, axis=-1, keepdims=True) + EPSILON) * gain_vec
    )


def rotate(values):
    half_width = values.shape[-1] // 2
    return jnp.concatenate([-values[..., half_width:], values[..., :half_width]], axis=-1)


def rope_tables(positions, head_width):
    step_index = jnp.arange(head_width // 2, dtype=jnp.float32)
    inverse = jnp.exp(step_index * (-2.0 * math.log(ROPE_BASE) / head_width))
    angles = positions.astype(jnp.float32)[:, None] * inverse[None, :]
    cosine_table = jnp.cos(angles)
    sine_table = jnp.sin(angles)
    return (
        jnp.concatenate([cosine_table, cosine_table], -1),
        jnp.concatenate([sine_table, sine_table], -1),
    )


def doc_positions(segment):
    token_index = jnp.arange(segment.shape[0], dtype=jnp.int32)
    smaller = (segment[None, :] < segment[:, None]).astype(jnp.int32)
    return token_index - jnp.sum(smaller, axis=1)


def earlier_counts(chosen):
    rows = chosen.shape[0]
    row_id = lax.broadcasted_iota(jnp.int32, (rows, rows), 0)
    col_id = lax.broadcasted_iota(jnp.int32, (rows, rows), 1)
    earlier = (col_id < row_id).astype(jnp.bfloat16)
    return matmul(earlier, chosen.astype(jnp.bfloat16))


def qk_finish(raw_values, gain_vec, cosine_table, sine_table):
    normed = rms_scale(raw_values, gain_vec)
    return normed * cosine_table + rotate(normed) * sine_table


def matmul(left_side, right_side):
    return jnp.dot(left_side, right_side, preferred_element_type=jnp.float32)


def matmul_nt(left_side, right_side):
    return lax.dot_general(
        left_side, right_side, (((1,), (1,)), ((), ())), preferred_element_type=jnp.float32
    )


def matmul_tn(left_side, right_side):
    return lax.dot_general(
        left_side, right_side, (((0,), (0,)), ((), ())), preferred_element_type=jnp.float32
    )


def block_scores(query_vectors, keys_all, seg_all, query_seg, query_index, key_ids, block_id, key_block):
    leading_row = block_id * key_block
    keys_part = lax.dynamic_slice_in_dim(keys_all, leading_row, key_block, 0)
    seg_part = lax.dynamic_slice_in_dim(seg_all, leading_row, key_block, 0)
    key_index = lax.dynamic_slice_in_dim(key_ids, leading_row, key_block, 0)
    score_scale = query_vectors.shape[2] ** (-0.5)
    scores = (
        jnp.einsum("qhd,kd->hqk", query_vectors, keys_part, preferred_element_type=jnp.float32)
        * score_scale
    )
    allowed = (query_seg[:, None] == seg_part[None, :]) & (
        key_index[None, :] <= query_index[:, None]
    )
    return (scores, allowed[None, :, :], keys_part)


def attention_forward(
    query_vectors, keys_all, values_all, seg_all, query_seg, query_index, key_ids, key_block
):
    row_count, head_count, head_width = query_vectors.shape
    block_count = keys_all.shape[0] // key_block

    def stats_step(running, block_id):
        run_max, run_sum = running
        scores, allowed, unused = block_scores(
            query_vectors, keys_all, seg_all, query_seg, query_index, key_ids, block_id, key_block
        )
        masked = jnp.where(allowed, scores, NEGATIVE)
        new_max = jnp.maximum(run_max, jnp.max(masked, axis=2))
        weights = jnp.where(allowed, jnp.exp(masked - new_max[:, :, None]), 0.0)
        run_sum = run_sum * jnp.exp(run_max - new_max) + jnp.sum(weights, axis=2)
        return ((new_max, run_sum), None)

    start_state = (
        jnp.full((head_count, row_count), NEGATIVE, jnp.float32),
        jnp.zeros((head_count, row_count), jnp.float32),
    )
    (run_max, run_sum), ignored = lax.scan(
        stats_step, start_state, jnp.arange(block_count, dtype=jnp.int32)
    )
    log_total = run_max + jnp.log(run_sum)

    def value_step(accumulated, block_id):
        scores, allowed, unused = block_scores(
            query_vectors, keys_all, seg_all, query_seg, query_index, key_ids, block_id, key_block
        )
        prob_block = jnp.where(allowed, jnp.exp(scores - log_total[:, :, None]), 0.0).astype(
            jnp.bfloat16
        )
        values_part = lax.dynamic_slice_in_dim(values_all, block_id * key_block, key_block, 0)
        accumulated = accumulated + jnp.einsum(
            "hqk,kd->qhd", prob_block, values_part, preferred_element_type=jnp.float32
        )
        return (accumulated, None)

    heads_full, ignored = lax.scan(
        value_step,
        jnp.zeros((row_count, head_count, head_width), jnp.float32),
        jnp.arange(block_count, dtype=jnp.int32),
    )
    return (heads_full, log_total)


def attention_backward(
    query_vectors,
    keys_all,
    values_all,
    seg_all,
    query_seg,
    query_index,
    key_ids,
    key_block,
    log_total,
    grad_heads,
    row_delta,
):
    row_count, head_count, head_width = query_vectors.shape
    block_count = keys_all.shape[0] // key_block
    score_scale = head_width ** (-0.5)

    def grad_step(grad_query, block_id):
        scores, allowed, keys_part = block_scores(
            query_vectors, keys_all, seg_all, query_seg, query_index, key_ids, block_id, key_block
        )
        values_part = lax.dynamic_slice_in_dim(values_all, block_id * key_block, key_block, 0)
        prob_block = jnp.where(allowed, jnp.exp(scores - log_total[:, :, None]), 0.0)
        grad_prob = jnp.einsum(
            "qhd,kd->hqk", grad_heads, values_part, preferred_element_type=jnp.float32
        )
        grad_score = (prob_block * (grad_prob - row_delta[:, :, None])).astype(jnp.bfloat16)
        grad_query = (
            grad_query
            + jnp.einsum("hqk,kd->qhd", grad_score, keys_part, preferred_element_type=jnp.float32)
            * score_scale
        )
        grad_key = (
            jnp.einsum("hqk,qhd->kd", grad_score, query_vectors, preferred_element_type=jnp.float32)
            * score_scale
        )
        grad_value = jnp.einsum(
            "hqk,qhd->kd",
            prob_block.astype(jnp.bfloat16),
            grad_heads,
            preferred_element_type=jnp.float32,
        )
        return (grad_query, (grad_key, grad_value))

    grad_query, (grad_key, grad_value) = lax.scan(
        grad_step,
        jnp.zeros((row_count, head_count, head_width), jnp.float32),
        jnp.arange(block_count, dtype=jnp.int32),
    )
    return (grad_query, grad_key.reshape(-1, head_width), grad_value.reshape(-1, head_width))


def to_experts(buffer):
    return lax.all_to_all(buffer, GROUPS, split_axis=0, concat_axis=1, tiled=True)


def from_experts(result_rows):
    return lax.all_to_all(result_rows, GROUPS, split_axis=1, concat_axis=0, tiled=True)


def pick_pairs(buffer, target, row_count):
    model_width = buffer.shape[2]
    flat_rows = jnp.concatenate(
        [buffer.reshape(-1, model_width), jnp.zeros((1, model_width), buffer.dtype)], axis=0
    )
    return flat_rows[target].reshape(row_count, TOPK, model_width)


def routed_local(
    hidden_in,
    attn_gain,
    w_query,
    key_weight,
    value_weight,
    w_output,
    query_gain,
    key_gain,
    ffn_gain,
    router,
    gate_weight,
    up_weight,
    down_weight,
    routes,
    segments,
    cotangent,
):
    context_rank = lax.axis_index(CONTEXT)
    input_rows = hidden_in[0].astype(jnp.float32)
    row_count, model_width = input_rows.shape
    gathered = (
        lax.all_gather(w_query, GROUPS, axis=0, tiled=True),
        lax.all_gather(key_weight, GROUPS, axis=0, tiled=True),
        lax.all_gather(value_weight, GROUPS, axis=0, tiled=True),
        lax.all_gather(w_output, GROUPS, axis=0, tiled=True),
        lax.all_gather(router, GROUPS, axis=0, tiled=True),
        lax.all_gather(attn_gain, GROUPS, axis=0, tiled=True),
        lax.all_gather(ffn_gain, GROUPS, axis=0, tiled=True),
        lax.all_gather(query_gain, GROUPS, axis=0, tiled=True),
        lax.all_gather(key_gain, GROUPS, axis=0, tiled=True),
    )
    full_query, full_key, full_value, full_output, full_router = (
        gathered[0],
        gathered[1],
        gathered[2],
        gathered[3],
        gathered[4],
    )
    gain_attn = gathered[5].astype(jnp.float32)
    gain_ffn = gathered[6].astype(jnp.float32)
    gain_query = gathered[7].astype(jnp.float32)
    gain_key = gathered[8].astype(jnp.float32)
    local_heads = full_query.shape[1] // HEAD_SIZE
    seg_all = lax.all_gather(segments, CONTEXT, axis=1, tiled=True)[0]
    length = seg_all.shape[0]
    start_row = context_rank * row_count
    positions = lax.dynamic_slice_in_dim(doc_positions(seg_all), start_row, row_count)
    cosine_table, sine_table = rope_tables(positions, HEAD_SIZE)
    query_seg = segments[0]
    query_index = start_row + jnp.arange(row_count, dtype=jnp.int32)
    key_ids = jnp.arange(length, dtype=jnp.int32)
    key_block = min(512, length)

    def query_finish(raw_values, gain_vec):
        return qk_finish(raw_values, gain_vec, cosine_table[:, None, :], sine_table[:, None, :])

    def key_finish(raw_values, gain_vec):
        return qk_finish(raw_values, gain_vec, cosine_table, sine_table)

    normed_f, first_pull = jax.vjp(rms_scale, input_rows, gain_attn)
    attention_normalized = normed_f.astype(jnp.bfloat16)
    query_unrotated = matmul(attention_normalized, full_query).reshape(
        row_count, local_heads, HEAD_SIZE
    )
    key_unrotated = matmul(attention_normalized, full_key)
    value_raw = matmul(attention_normalized, full_value)
    query_f, query_pull = jax.vjp(query_finish, query_unrotated, gain_query)
    key_f, key_pull = jax.vjp(key_finish, key_unrotated, gain_key)
    query_vectors = query_f.astype(jnp.bfloat16)
    keys_all, values_all = (
        lax.all_gather(key_f.astype(jnp.bfloat16), CONTEXT, axis=0, tiled=True),
        lax.all_gather(value_raw.astype(jnp.bfloat16), CONTEXT, axis=0, tiled=True),
    )
    heads_full, log_total = attention_forward(
        query_vectors, keys_all, values_all, seg_all, query_seg, query_index, key_ids, key_block
    )
    heads_low = heads_full.reshape(row_count, local_heads * HEAD_SIZE).astype(jnp.bfloat16)
    attn_out = lax.psum(matmul_nt(heads_low, full_output).astype(jnp.bfloat16), TENSOR).astype(
        jnp.float32
    )
    residual_stream = input_rows + attn_out
    second_f, second_pull = jax.vjp(rms_scale, residual_stream, gain_ffn)
    feedforward_normalized = second_f.astype(jnp.bfloat16)
    router_scores = matmul(feedforward_normalized, full_router)
    experts_total = full_router.shape[1]
    route_ids = routes[0]
    chosen = route_ids[:, :, None] == jnp.arange(experts_total, dtype=jnp.int32)
    selected = jnp.sum(jnp.where(chosen, router_scores[:, None, :], 0.0), axis=2)
    gate_probs = jax.nn.softmax(selected, axis=-1)
    capacity = 9 * row_count * TOPK // (8 * experts_total)
    before = earlier_counts(jnp.any(chosen, axis=1)).astype(jnp.int32)
    slot_index = jnp.sum(jnp.where(chosen, before[:, None, :], 0), axis=2)
    target = jnp.where(
        slot_index < capacity, route_ids * capacity + slot_index, experts_total * capacity
    ).reshape(-1)
    source = jnp.repeat(jnp.arange(row_count, dtype=jnp.int32), TOPK)
    send_rows = (
        jnp.zeros((experts_total * capacity, model_width), jnp.bfloat16)
        .at[target]
        .set(feedforward_normalized[source], mode="drop")
    )
    expert_input_rows = to_experts(send_rows.reshape(experts_total, capacity, model_width))
    gate_activation_input = jnp.einsum(
        "phu,puo->pho", expert_input_rows, gate_weight, preferred_element_type=jnp.float32
    )
    up_activation_input = jnp.einsum(
        "phu,puo->pho", expert_input_rows, up_weight, preferred_element_type=jnp.float32
    )
    sigmoid_gate = jax.nn.sigmoid(gate_activation_input)
    silu_gate = gate_activation_input * sigmoid_gate
    hidden_middle = (silu_gate * up_activation_input).astype(jnp.bfloat16)
    expert_part = jnp.einsum(
        "pic,pcw->piw", hidden_middle, down_weight, preferred_element_type=jnp.float32
    ).astype(jnp.bfloat16)
    grad_out = cotangent[0].astype(jnp.float32)
    returned = pick_pairs(from_experts(expert_part), target, row_count)
    moe_part = jnp.sum(returned.astype(jnp.float32) * gate_probs[:, :, None], axis=1)
    moe_out = lax.psum(moe_part.astype(jnp.bfloat16), TENSOR).astype(jnp.float32)
    grad_gate_part = jnp.sum(returned.astype(jnp.float32) * grad_out[:, None, :], axis=2)
    output = (residual_stream + moe_out).astype(jnp.bfloat16)
    pair_grad = (
        (gate_probs[:, :, None] * grad_out[:, None, :])
        .astype(jnp.bfloat16)
        .reshape(row_count * TOPK, model_width)
    )
    send_grad = (
        jnp.zeros((experts_total * capacity, model_width), jnp.bfloat16)
        .at[target]
        .set(pair_grad, mode="drop")
    )
    expert_output_gradient = to_experts(send_grad.reshape(experts_total, capacity, model_width))
    grad_mid = jnp.einsum(
        "jtk,jvk->jtv", expert_output_gradient, down_weight, preferred_element_type=jnp.float32
    )
    grad_w_down = jnp.einsum(
        "tce,tci->tei", hidden_middle, expert_output_gradient, preferred_element_type=jnp.float32
    )
    gate_activation_gradient = (
        grad_mid
        * up_activation_input
        * sigmoid_gate
        * (1.0 + gate_activation_input * (1.0 - sigmoid_gate))
    ).astype(jnp.bfloat16)
    up_activation_gradient = (grad_mid * silu_gate).astype(jnp.bfloat16)
    grad_w_gate = jnp.einsum(
        "ahw,ahp->awp",
        expert_input_rows,
        gate_activation_gradient,
        preferred_element_type=jnp.float32,
    )
    grad_w_up = jnp.einsum(
        "ahw,ahp->awp",
        expert_input_rows,
        up_activation_gradient,
        preferred_element_type=jnp.float32,
    )
    grad_expert_in = (
        jnp.einsum(
            "ous,ops->oup",
            gate_activation_gradient,
            gate_weight,
            preferred_element_type=jnp.float32,
        )
        + jnp.einsum(
            "ous,ops->oup", up_activation_gradient, up_weight, preferred_element_type=jnp.float32
        )
    ).astype(jnp.bfloat16)
    grad_pairs = pick_pairs(from_experts(grad_expert_in), target, row_count)
    grad_normed_part = jnp.sum(grad_pairs.astype(jnp.float32), axis=1)
    grad_normed_moe, grad_gates = (
        lax.psum(grad_normed_part.astype(jnp.bfloat16), TENSOR).astype(jnp.float32),
        lax.psum(grad_gate_part.astype(jnp.bfloat16), TENSOR).astype(jnp.float32),
    )
    grad_selected = gate_probs * (
        grad_gates - jnp.sum(gate_probs * grad_gates, axis=1, keepdims=True)
    )
    grad_logits = jnp.sum(jnp.where(chosen, grad_selected[:, :, None], 0.0), axis=1).astype(
        jnp.bfloat16
    )
    grad_router = matmul_tn(feedforward_normalized, grad_logits)
    grad_normed_two = grad_normed_moe + matmul_nt(grad_logits, full_router)
    grad_resid_norm, grad_gain_ffn = second_pull(grad_normed_two)
    grad_resid = grad_out + grad_resid_norm
    grad_attn = grad_resid.astype(jnp.bfloat16)
    grad_w_output = matmul_tn(grad_attn, heads_low)
    grad_heads = (
        matmul(grad_attn, full_output)
        .astype(jnp.bfloat16)
        .reshape(row_count, local_heads, HEAD_SIZE)
    )
    row_delta = jnp.sum(grad_heads.astype(jnp.float32) * heads_full, axis=2).T
    grad_query, grad_key_terms, grad_value_terms = attention_backward(
        query_vectors,
        keys_all,
        values_all,
        seg_all,
        query_seg,
        query_index,
        key_ids,
        key_block,
        log_total,
        grad_heads,
        row_delta,
    )
    grad_key_local, grad_value_local = (
        lax.psum_scatter(
            grad_key_terms.astype(jnp.bfloat16), CONTEXT, scatter_dimension=0, tiled=True
        ).astype(jnp.float32),
        lax.psum_scatter(
            grad_value_terms.astype(jnp.bfloat16), CONTEXT, scatter_dimension=0, tiled=True
        ).astype(jnp.float32),
    )
    grad_query_raw, grad_gain_query = query_pull(grad_query)
    grad_key_raw, grad_gain_key = key_pull(grad_key_local)
    grad_query_low = grad_query_raw.reshape(row_count, local_heads * HEAD_SIZE).astype(jnp.bfloat16)
    grad_key_low = grad_key_raw.astype(jnp.bfloat16)
    grad_value_low = grad_value_local.astype(jnp.bfloat16)
    grad_w_query = matmul_tn(attention_normalized, grad_query_low)
    grad_w_key = matmul_tn(attention_normalized, grad_key_low)
    grad_w_value = matmul_tn(attention_normalized, grad_value_low)
    grad_normed_one = (
        matmul_nt(grad_query_low, full_query)
        + matmul_nt(grad_key_low, full_key)
        + matmul_nt(grad_value_low, full_value)
    )
    grad_normed_one, grad_gain_query, grad_gain_key = (
        lax.psum(grad_normed_one.astype(jnp.bfloat16), TENSOR).astype(jnp.float32),
        lax.psum(grad_gain_query.astype(jnp.bfloat16), TENSOR).astype(jnp.float32),
        lax.psum(grad_gain_key.astype(jnp.bfloat16), TENSOR).astype(jnp.float32),
    )
    grad_inputs_norm, grad_gain_attn = first_pull(grad_normed_one)
    input_grad = grad_resid + grad_inputs_norm
    owned = (
        lax.psum_scatter(
            grad_w_query.astype(jnp.bfloat16), GROUPS, scatter_dimension=0, tiled=True
        ).astype(jnp.float32),
        lax.psum_scatter(
            grad_w_key.astype(jnp.bfloat16), GROUPS, scatter_dimension=0, tiled=True
        ).astype(jnp.float32),
        lax.psum_scatter(
            grad_w_value.astype(jnp.bfloat16), GROUPS, scatter_dimension=0, tiled=True
        ).astype(jnp.float32),
        lax.psum_scatter(
            grad_w_output.astype(jnp.bfloat16), GROUPS, scatter_dimension=0, tiled=True
        ).astype(jnp.float32),
        lax.psum_scatter(
            grad_router.astype(jnp.bfloat16), GROUPS, scatter_dimension=0, tiled=True
        ).astype(jnp.float32),
        lax.psum_scatter(
            grad_gain_attn.astype(jnp.bfloat16),
            GROUPS,
            scatter_dimension=0,
            tiled=True,
        ).astype(jnp.float32),
        lax.psum_scatter(
            grad_gain_ffn.astype(jnp.bfloat16), GROUPS, scatter_dimension=0, tiled=True
        ).astype(jnp.float32),
        lax.psum_scatter(
            grad_gain_query.astype(jnp.bfloat16),
            GROUPS,
            scatter_dimension=0,
            tiled=True,
        ).astype(jnp.float32),
        lax.psum_scatter(
            grad_gain_key.astype(jnp.bfloat16), GROUPS, scatter_dimension=0, tiled=True
        ).astype(jnp.float32),
    )
    return (
        output[None],
        input_grad[None],
        owned[5],
        owned[0],
        owned[1],
        owned[2],
        owned[3],
        owned[7],
        owned[8],
        owned[6],
        owned[4],
        grad_w_gate,
        grad_w_up,
        grad_w_down,
    )


MESH = pl.DeviceIdType.MESH
Z_UP, Z_DOWN, Y_SIDE, X_SIDE, CORE_SIDE = range(5)

def coords():
    z, y, t = lax.axis_index(FSDP), lax.axis_index(CONTEXT), lax.axis_index(TENSOR)
    return z, y, t // 2, t % 2

def partner(z, index):
    return (z, z + 1 - 2 * (z % 2), 2 - z // 2, 3 - 3 * (z // 2))[index]

def greet(neighbours):
    barrier = pltpu.get_barrier_semaphore()
    for condition, device in neighbours:
        def tell(device=device):
            pl.semaphore_signal(barrier, inc=1, device_id=device, device_id_type=MESH)
        if condition is None: tell()
        else: pl.when(condition)(tell)
    count = sum(1 if condition is None else condition.astype(jnp.int32) for condition, device in neighbours)
    pl.semaphore_wait(barrier, count)


def spread(x_ref, out_ref, own_sem, send_sems, recv_sems):
    rows = x_ref.shape[0]; half = rows // 2
    z, y, x, c = coords()
    side = {Z_UP: (z + 1, y, 2 * x + c), Z_DOWN: (z - 1, y, 2 * x + c), Y_SIDE: (z, 1 - y, 2 * x + c),
            X_SIDE: (z, y, 2 * (1 - x) + c), CORE_SIDE: (z, y, 2 * x + 1 - c)}
    def device(zz, yy, xx, cc): return (zz * 2 + yy) * 4 + xx * 2 + cc
    def place(owner, h): return out_ref.at[pl.ds(pl.multiple_of(owner * rows + h * half, half), half)]
    def copy(link, owner, h, own=False):
        src = x_ref.at[pl.ds(h * half, half)] if own else place(owner, h)
        return pltpu.make_async_remote_copy(src_ref=src, dst_ref=place(owner, h), send_sem=send_sems.at[link, owner, h],
            recv_sem=recv_sems.at[owner, h], device_id=side[link], device_id_type=MESH)
    sent = []
    def start(link, owner, h, own=False, condition=None):
        one = copy(link, owner, h, own)
        sent.append((one, condition))
        if condition is None: one.start()
        else: pl.when(condition)(one.start)
    def arrived(owner, h): copy(CORE_SIDE, owner, h).wait_recv()
    me = device(z, y, x, c)
    keep = pltpu.make_async_copy(x_ref, out_ref.at[pl.ds(pl.multiple_of(me * rows, rows), rows)], own_sem)
    keep.start()
    def stage1(i):
        zz = partner(z, i); owner = device(zz, y, x, c); own = i == 0
        if not own:
            arrived(owner, 0); arrived(owner, 1)
        for h in range(2):
            start(Z_UP, owner, h, own, (z < 3) if own else (z < 3) & (zz < z))
            start(Z_DOWN, owner, h, own, (z > 0) if own else (z > 0) & (zz > z))
        start(Y_SIDE, owner, 0, own); start(X_SIDE, owner, 1, own)
        start(Y_SIDE, owner, 1, own); start(X_SIDE, owner, 0, own)
        for h in range(2): start(CORE_SIDE, owner, h, own)
    def stage2(i):
        zz = partner(z, i)
        oy, ox = device(zz, 1 - y, x, c), device(zz, y, 1 - x, c)
        arrived(oy, 0); start(X_SIDE, oy, 0); start(CORE_SIDE, oy, 0)
        arrived(ox, 1); start(Y_SIDE, ox, 1); start(CORE_SIDE, ox, 1)
        arrived(oy, 1); start(CORE_SIDE, oy, 1)
        arrived(ox, 0); start(CORE_SIDE, ox, 0)
    def stage3(i):
        o = device(partner(z, i), 1 - y, 1 - x, c)
        for h in range(2):
            arrived(o, h); start(CORE_SIDE, o, h)
    stage1(0); stage1(1); stage2(0); stage1(2); stage2(1); stage3(0); stage1(3); stage2(2); stage3(1); stage2(3); stage3(2); stage3(3)
    for i in range(4):
        for yy in range(2):
            for xx in range(2):
                for h in range(2): arrived(device(i, yy, xx, 1 - c), h)
    keep.wait()
    for one, condition in sent:
        if condition is None: one.wait_send()
        else: pl.when(condition)(one.wait_send)

def mix_kernel(heads_ref, weight_ref, input_ref, gain_ref, resid_ref, normed_ref, all_ref, part, mine, core_in, line_in, sems, recv, *gather_sems):
    z, y, x, c = coords()
    x_side, core_side = (z, y, 2 * (1 - x) + c), (z, y, 2 * x + 1 - c)
    greet([(z < 3, (z + 1, y, 2 * x + c)), (z > 0, (z - 1, y, 2 * x + c)), (None, (z, 1 - y, 2 * x + c)), (None, x_side), (None, core_side)])
    rows, width = input_ref.shape; f32, bf16 = jnp.float32, jnp.bfloat16
    def remote(src, dst, n, device):
        return pltpu.make_async_remote_copy(src_ref=src, dst_ref=dst, send_sem=sems.at[n], recv_sem=recv.at[n], device_id=device, device_id_type=MESH)
    over_core = [remote(part.at[n, 1 - c], core_in.at[n], n, core_side) for n in range(2)]
    over_x = remote(mine, line_in, 2, x_side)
    for n, xx in enumerate((1 - x, x)):
        heads = heads_ref[pl.ds(pl.multiple_of(xx * 2 * rows, 2 * rows), 2 * rows), :]
        for m in range(width // 512):
            at = pl.ds(m * 512, 512)
            value = lax.dot_general(heads, weight_ref[at, :], (((1,), (1,)), ((), ())), preferred_element_type=f32).astype(bf16)
            part[n, 0, :, at] = value[:rows]
            part[n, 1, :, at] = value[rows:]
        over_core[n].start()
    over_core[0].wait_recv()
    mine[...] = part[0, c] + core_in[0]
    over_x.start(); over_core[1].wait_recv()
    total = input_ref[...].astype(f32) + part[1, c].astype(f32) + core_in[1].astype(f32)
    over_x.wait_recv()
    total = total + line_in[...].astype(f32)
    resid_ref[...] = total
    normed_ref[...] = (total * lax.rsqrt(jnp.mean(total * total, axis=-1, keepdims=True) + EPSILON) * gain_ref[...]).astype(bf16)
    spread(normed_ref, all_ref, *gather_sems)
    for one in (*over_core, over_x): one.wait_send()

def mix_heads(heads, weight, own_input, gain, collective_id):
    rows, width = own_input.shape; D, V = pltpu.SemaphoreType.DMA, pltpu.VMEM; S = jax.ShapeDtypeStruct
    f32, bf16 = jnp.float32, jnp.bfloat16; vspec = pl.BlockSpec(memory_space=V)
    return pl.pallas_call(mix_kernel, out_shape=[S((rows, width), f32), S((rows, width), bf16), S((32 * rows, width), bf16)],
        in_specs=[vspec] * 4, out_specs=[vspec, vspec, pl.BlockSpec(memory_space=pl.ANY)],
        scratch_shapes=[V((2, 2, rows, width), bf16), V((rows, width), bf16), V((2, rows, width), bf16), V((rows, width), bf16), D((3,)), D((3,)),
            D, D((5, 32, 2)), D((32, 2))],
        compiler_params=pltpu.CompilerParams(collective_id=collective_id, has_side_effects=True, vmem_limit_bytes=32 << 20))(heads, weight, own_input, gain)

def groups_kernel(parts, count, *refs):
    ins, outs = refs[:count], refs[count:2 * count]
    keep_sems, send_sems, recv_sems = refs[2 * count:]
    z, y, x, c = coords()
    t = 2 * x + c
    side = {Z_UP: (z + 1, y, t), Z_DOWN: (z - 1, y, t), Y_SIDE: (z, 1 - y, t)}
    greet([(z < 3, side[Z_UP]), (z > 0, side[Z_DOWN]), (None, side[Y_SIDE])])
    sent = []
    def copy(link, p, owner, own=False):
        k, first, size, way = parts[p]
        dst = outs[k].at[pl.ds(pl.multiple_of(owner * ins[k].shape[0] + first, 16), size)]
        return pltpu.make_async_remote_copy(src_ref=ins[k].at[pl.ds(first, size)] if own else dst, dst_ref=dst, send_sem=send_sems.at[link, p, owner],
            recv_sem=recv_sems.at[p, owner], device_id=side[link], device_id_type=MESH)
    def start(link, p, owner, own=False, condition=None):
        one = copy(link, p, owner, own)
        sent.append((one, condition))
        if condition is None: one.start()
        else: pl.when(condition)(one.start)
    def arrived(p, owner): copy(Y_SIDE, p, owner).wait_recv()
    def along(p, owner, zz, own=False):
        start(Z_UP, p, owner, own, (z < 3) & (zz <= z)); start(Z_DOWN, p, owner, own, (z > 0) & (zz >= z))
    kept = []
    for p in range(len(parts)):
        along(p, z * 2 + y, z, True); start(Y_SIDE, p, z * 2 + y, True)
    for k in range(count):
        rows = ins[k].shape[0]
        one = pltpu.make_async_copy(ins[k], outs[k].at[pl.ds(pl.multiple_of((z * 2 + y) * rows, 16), rows)], keep_sems.at[k])
        one.start(); kept.append(one)
    def forward(p, i):
        zz = partner(z, i)
        near, far = zz * 2 + y, zz * 2 + 1 - y
        if i > 0:
            arrived(p, near); along(p, near, zz)
            if parts[p][3] == 0: start(Y_SIDE, p, near)
        if parts[p][3] == 1:
            arrived(p, far); along(p, far, zz)
    for wave in range(len(parts) + 3):
        for i in range(4):
            if 0 <= wave - i < len(parts): forward(wave - i, i)
    for p in range(len(parts)):
        if parts[p][3] == 0:
            for i in range(4): arrived(p, partner(z, i) * 2 + 1 - y)
    for one in kept: one.wait()
    for one, condition in sent:
        if condition is None: one.wait_send()
        else: pl.when(condition)(one.wait_send)

def gather_groups(arrays, parts, collective_id):
    count = len(arrays); D = pltpu.SemaphoreType.DMA
    return pl.pallas_call(functools.partial(groups_kernel, parts, count),
        out_shape=[jax.ShapeDtypeStruct((8 * a.shape[0], a.shape[1]), a.dtype) for a in arrays],
        in_specs=[pl.BlockSpec(memory_space=pl.ANY)] * count, out_specs=[pl.BlockSpec(memory_space=pl.ANY)] * count,
        scratch_shapes=[D((count,)), D((3, len(parts), 8)), D((len(parts), 8))],
        compiler_params=pltpu.CompilerParams(collective_id=collective_id, has_side_effects=True))(*arrays)

def tensor_gather_kernel(x_ref, out_ref, keep_sem, send_sems, recv_sems):
    z, y, x, c = coords()
    x_side, core_side = (z, y, 2 * (1 - x) + c), (z, y, 2 * x + 1 - c)
    greet([(None, x_side), (None, core_side)])
    def copy(n, owner, device, own=False):
        return pltpu.make_async_remote_copy(src_ref=x_ref if own else out_ref.at[owner], dst_ref=out_ref.at[owner], send_sem=send_sems.at[n],
            recv_sem=recv_sems.at[owner], device_id=device, device_id_type=MESH)
    me, across, beside, last = 2 * x + c, 2 * (1 - x) + c, 2 * x + 1 - c, 2 * (1 - x) + 1 - c
    a, b, d = copy(0, me, x_side, True), copy(1, me, core_side, True), copy(2, across, core_side)
    a.start(); b.start()
    keep = pltpu.make_async_copy(x_ref, out_ref.at[me], keep_sem); keep.start()
    copy(0, across, x_side).wait_recv(); d.start()
    copy(0, beside, x_side).wait_recv(); copy(0, last, x_side).wait_recv()
    keep.wait(); a.wait_send(); b.wait_send(); d.wait_send()

def gather_tensor(x, collective_id):
    D = pltpu.SemaphoreType.DMA
    return pl.pallas_call(tensor_gather_kernel, out_shape=jax.ShapeDtypeStruct((4, *x.shape), x.dtype),
        in_specs=[pl.BlockSpec(memory_space=pl.ANY)], out_specs=pl.BlockSpec(memory_space=pl.ANY),
        scratch_shapes=[D, D((3,)), D((4,))],
        compiler_params=pltpu.CompilerParams(collective_id=collective_id, has_side_effects=True))(x)

def tensor_scatter_kernel(part_ref, out_ref, mine, core_in, line_in, sems, recv):
    z, y, x, c = coords()
    x_side, core_side = (z, y, 2 * (1 - x) + c), (z, y, 2 * x + 1 - c)
    greet([(None, x_side), (None, core_side)])
    rows = out_ref.shape[0]; f32 = jnp.float32
    def rows_of(xx, cc): return part_ref.at[pl.ds(pl.multiple_of((2 * xx + cc) * rows, rows), rows)]
    def over_core(n, xx):
        return pltpu.make_async_remote_copy(src_ref=rows_of(xx, 1 - c), dst_ref=core_in.at[n], send_sem=sems.at[n], recv_sem=recv.at[n],
            device_id=core_side, device_id_type=MESH)
    a, b = over_core(0, 1 - x), over_core(1, x)
    a.start(); b.start()
    a.wait_recv()
    mine[...] = (rows_of(1 - x, c)[...].astype(f32) + core_in[0].astype(f32)).astype(mine.dtype)
    d = pltpu.make_async_remote_copy(src_ref=mine, dst_ref=line_in, send_sem=sems.at[2], recv_sem=recv.at[2], device_id=x_side, device_id_type=MESH)
    d.start(); b.wait_recv()
    out_ref[...] = rows_of(x, c)[...].astype(f32) + core_in[1].astype(f32)
    d.wait_recv()
    out_ref[...] += line_in[...].astype(f32)
    a.wait_send(); b.wait_send(); d.wait_send()

def scatter_tensor(part, collective_id):
    D = pltpu.SemaphoreType.DMA; rows = part.shape[0] // 4; width = part.shape[1]
    return pl.pallas_call(tensor_scatter_kernel, out_shape=jax.ShapeDtypeStruct((rows, width), jnp.float32),
        in_specs=[pl.BlockSpec(memory_space=pltpu.VMEM)], out_specs=pl.BlockSpec(memory_space=pltpu.VMEM),
        scratch_shapes=[pltpu.VMEM((rows, width), part.dtype), pltpu.VMEM((2, rows, width), part.dtype), pltpu.VMEM((rows, width), part.dtype), D((3,)), D((3,))],
        compiler_params=pltpu.CompilerParams(collective_id=collective_id, has_side_effects=True, vmem_limit_bytes=24 << 20))(part)


def nt(a, b):
    return lax.dot_general(a, b, (((1,), (1,)), ((), ())), preferred_element_type=jnp.float32)

def nn(a, b):
    return jnp.dot(a, b, preferred_element_type=jnp.float32)

def nearest(z, index):
    choice = [partner(z, n) for n in range(4)]
    return jnp.where(index == 0, choice[0], jnp.where(index == 1, choice[1], jnp.where(index == 2, choice[2], choice[3])))

def spot(zz, yy, xx): return (zz * 2 + yy) * 2 + xx

def step_target(step):
    z, y, x, c = coords()
    n = step % 4
    return nearest(z, 3 - step // 4), jnp.where(n < 2, 1 - y, y), jnp.where(n % 2 == 0, 1 - x, x)

def step_block(ref, step):
    size = ref.shape[0] // 16
    return ref.at[pl.ds(pl.multiple_of(spot(*step_target(step)) * size, size), size)]

class Reduction:
    def __init__(self, part, mine, first_in, second_in, line_in, core_sem, first_sem, second_sem, line_send, line_recv):
        self.part, self.mine, self.first_in, self.second_in, self.line_in = part, mine, first_in, second_in, line_in
        self.core_sem, self.first_sem, self.second_sem, self.line_send, self.line_recv = core_sem, first_sem, second_sem, line_send, line_recv
        self.half = part.shape[2] // 2
        z, y, x, c = self.at = coords()
        self.up, self.down = (z + 1, y, 2 * x + c), (z - 1, y, 2 * x + c)
        self.y_side, self.x_side, self.core_side = (z, 1 - y, 2 * x + c), (z, y, 2 * (1 - x) + c), (z, y, 2 * x + 1 - c)

    @staticmethod
    def scratch(rows, width, dtype):
        V, D, half = pltpu.VMEM, pltpu.SemaphoreType.DMA, rows // 2
        return [V((2, 2, rows, width), dtype), V((16, rows, width), dtype), V((2, 8, half, width), dtype),
            V((2, 4, half, width), dtype), V((2, 4, 2, half, width), dtype), D((2, 16)), D((2, 2, 8)), D((2, 2, 4)), D((4, 2)), D((2, 4, 2))]

    def greet(self):
        z = self.at[0]
        greet([(z < 3, self.up), (z > 0, self.down), (None, self.y_side), (None, self.x_side), (None, self.core_side)])

    @staticmethod
    def remote(src, dst, send, recv, device):
        return pltpu.make_async_remote_copy(src_ref=src, dst_ref=dst, send_sem=send, recv_sem=recv, device_id=device, device_id_type=MESH)

    def over_core(self, step):
        s = spot(*step_target(step))
        return self.remote(self.part.at[step % 2, 1 - self.at[3]], self.mine.at[s], self.core_sem.at[0, s], self.core_sem.at[1, s], self.core_side)

    def piece(self, zz, yy, xx, h): return self.mine.at[spot(zz, yy, xx), pl.ds(h * self.half, self.half)]

    def first(self, h, zz, other):
        z, y, x, c = self.at
        src = self.piece(zz, other, 1 - x, 0) if h == 0 else self.piece(zz, 1 - y, other, 1)
        s = zz * 2 + other
        return self.remote(src, self.first_in.at[h, s], self.first_sem.at[0, h, s], self.first_sem.at[1, h, s], self.x_side if h == 0 else self.y_side)

    def second(self, h, zz):
        z, y, x, c = self.at
        src = self.piece(zz, 1 - y, x, 0) if h == 0 else self.piece(zz, y, 1 - x, 1)
        return self.remote(src, self.second_in.at[h, zz], self.second_sem.at[0, h, zz], self.second_sem.at[1, h, zz], self.y_side if h == 0 else self.x_side)

    def line(self, h, zz, way):
        z, y, x, c = self.at
        return self.remote(self.piece(zz, y, x, h), self.line_in.at[way, zz, h], self.line_send.at[zz, h], self.line_recv.at[way, zz, h], self.up if way == 0 else self.down)

    def add(self, s, h, arrived):
        at = (s, pl.ds(h * self.half, self.half))
        self.mine[at] = self.mine[at] + arrived[...]

    def stage_core(self, step):
        zz, yy, xx = step_target(step)
        s = spot(zz, yy, xx)
        self.over_core(step).wait_recv()
        self.mine[s] += self.part[step % 2, self.at[3]]
        n = step % 4
        @pl.when(n % 2 == 0)
        def _(): self.first(0, zz, yy).start()
        @pl.when(n < 2)
        def _(): self.first(1, zz, xx).start()

    def stage_first(self, i):
        z, y, x, c = self.at
        zz = nearest(z, i)
        for n in range(2):
            for h, other in ((0, (1 - y, y)[n]), (1, (1 - x, x)[n])):
                self.first(h, zz, other).wait_recv()
                self.add(spot(zz, other, x) if h == 0 else spot(zz, y, other), h, self.first_in.at[h, zz * 2 + other])
                if n == 0: self.second(h, zz).start()

    def stage_second(self, i):
        z, y, x, c = self.at
        zz = nearest(z, i)
        for h in range(2):
            self.second(h, zz).wait_recv()
            self.add(spot(zz, y, x), h, self.second_in.at[h, zz])

    def stage_line(self, i):
        z, y, x, c = self.at
        zz = nearest(z, i)
        for h in range(2):
            for way, from_side, toward in ((0, z > 0, zz > z), (1, z < 3, zz < z)):
                @pl.when(from_side & (toward | (zz == z)))
                def _(h=h, way=way):
                    self.line(h, zz, way).wait_recv()
                    self.add(spot(zz, y, x), h, self.line_in.at[way, zz, h])
                @pl.when(toward)
                def _(h=h, way=way): self.line(h, zz, way).start()

    def follow(self, step):
        @pl.when((step >= 1) & (step <= 16))
        def _(): self.stage_core(step - 1)
        q = step // 4
        @pl.when((step % 4 == 1) & (q >= 2))
        def _(): self.stage_line(5 - q)
        @pl.when((step % 4 == 1) & (q >= 1))
        def _(): self.stage_first(4 - q)
        @pl.when((step % 4 == 3) & (q >= 1))
        def _(): self.stage_second(4 - q)

    def finish(self, out_ref, steps):
        z, y, x, c = self.at
        if steps == 16:
            self.stage_core(15); self.stage_line(1); self.stage_first(0); self.stage_second(0)
        self.stage_line(0)
        out_ref[...] = self.mine[spot(z, y, x)].astype(jnp.float32)
        self.over_core(14).wait_send(); self.over_core(15).wait_send()
        for zz in range(4):
            for other in range(2):
                for h in range(2): self.first(h, zz, other).wait_send()
            for h in range(2): self.second(h, zz).wait_send()
            @pl.when(zz != z)
            def _(zz=zz):
                for h in range(2): self.line(h, zz, 0).wait_send()

def expert_kernel(normed_ref, cot_ref, code_ref, router_ref, expand_ref, place_ref, gate_ref, up_ref, down_ref,
                  out_ref, hid_out, gate_out, up_out, normed_in, cot_in, code_in, units, in_sem, units_sem, *scratch):
    reduction = Reduction(*scratch)
    reduction.greet()
    part = reduction.part
    rows, width, wide = out_ref.shape[0], normed_ref.shape[1], gate_ref.shape[1]
    f32, bf16 = jnp.float32, jnp.bfloat16
    stride = code_ref.shape[0] // 8
    def loads(step):
        slot = step % 2
        zz, yy, xx = step_target(step)
        codes = code_ref.at[pl.ds(pl.multiple_of((zz * 2 + yy) * stride, 16), rows)]
        pairs = ((step_block(normed_ref, step), normed_in), (step_block(cot_ref, step), cot_in), (codes, code_in))
        return [pltpu.make_async_copy(src, dst.at[slot], in_sem.at[n, slot]) for n, (src, dst) in enumerate(pairs)]
    def stores(step):
        slot = step % 2
        return [pltpu.make_async_copy(units.at[slot, n], step_block(dst, step), units_sem.at[n, slot])
                for n, dst in enumerate((hid_out, gate_out, up_out))]
    for one in loads(0): one.start()

    def compute(step):
        slot = step % 2
        for one in loads(step): one.wait()
        @pl.when(step < 15)
        def _():
            for one in loads(step + 1): one.start()
        @pl.when(step >= 2)
        def _():
            for one in stores(step - 2): one.wait()
            reduction.over_core(step - 2).wait_send()
        normed, cot = normed_in[slot], cot_in[slot]
        code = code_in[slot].astype(f32)
        quarter = lax.broadcasted_iota(jnp.int32, code.shape, 1) // (128 // 4) - 2 * step_target(step)[2]
        code = jnp.concatenate([jnp.where(quarter == n, code, 0.0) for n in range(2)], axis=0)
        scores = jnp.where(code > 0.5, nn(normed, router_ref[...]), NEGATIVE)
        scores = jnp.where(code > 0.5, jnp.exp(scores - jnp.max(scores, axis=1, keepdims=True)), 0.0)
        gates = jnp.where(code > 1.5, scores / jnp.sum(scores, axis=1, keepdims=True), 0.0)
        high = gates.astype(bf16)
        low = (gates - high.astype(f32)).astype(bf16)
        grad_gates = jnp.zeros((2 * rows, 128), f32)
        def products(n):
            at = pl.ds(n * 256, 256)
            return (nn(normed, gate_ref[:, at]), nn(normed, up_ref[:, at]), nt(cot, down_ref[at, :]),
                nn(high, expand_ref[:, at]) + nn(low, expand_ref[:, at]))
        ahead = products(0)
        for n in range(wide // 256):
            gate_in, up_in, grad_mid, gate = ahead
            if n + 1 < wide // 256: ahead = products(n + 1)
            at = pl.ds(n * 256, 256)
            sig = lax.logistic(gate_in)
            silu = gate_in * sig
            hidden = silu * up_in
            grad_gates += nn(jnp.where(gate != 0.0, hidden * grad_mid, 0.0).astype(bf16), place_ref[at, :])
            grad_hidden = grad_mid * gate
            units[slot, 0, :, at] = (hidden * gate).astype(bf16)
            units[slot, 1, :, at] = (grad_hidden * up_in * (sig + silu * (1.0 - sig))).astype(bf16)
            units[slot, 2, :, at] = (grad_hidden * silu).astype(bf16)
        for one in stores(step): one.start()
        gate_grad, up_grad = units[slot, 1], units[slot, 2]
        for n in range(width // 512):
            at = pl.ds(n * 512, 512)
            grad = (nt(gate_grad, gate_ref[at, :]) + nt(up_grad, up_ref[at, :])).astype(bf16)
            part[slot, 0, :, at] = grad[:rows]
            part[slot, 1, :, at] = grad[rows:]
        grad_gates = grad_gates.astype(bf16)
        part[slot, 0, :, pl.ds(width, 128)] = grad_gates[:rows]
        part[slot, 1, :, pl.ds(width, 128)] = grad_gates[rows:]
        reduction.over_core(step).start()

    @pl.loop(0, 16)
    def _(step):
        compute(step)
        reduction.follow(step)
    for step in (14, 15):
        for one in stores(step): one.wait()
    reduction.finish(out_ref, 16)

def run_experts(normed_all, cot_all, codes, router, expand, place, gate_flat, up_flat, down_flat, collective_id):
    total, width = normed_all.shape; rows = total // 32; wide = gate_flat.shape[1]
    bf16 = jnp.bfloat16; D = pltpu.SemaphoreType.DMA; V = pltpu.VMEM; W = width + 128
    anyspec, vspec = pl.BlockSpec(memory_space=pl.ANY), pl.BlockSpec(memory_space=V)
    unit = jax.ShapeDtypeStruct((total, wide), bf16)
    return pl.pallas_call(expert_kernel,
        out_shape=[jax.ShapeDtypeStruct((rows, W), jnp.float32), unit, unit, unit],
        in_specs=[anyspec] * 3 + [vspec] * 6, out_specs=[vspec] + [anyspec] * 3,
        scratch_shapes=[V((2, 2 * rows, width), bf16), V((2, 2 * rows, width), bf16), V((2, rows, 128), bf16),
            V((2, 3, 2 * rows, wide), bf16), D((3, 2)), D((3, 2)), *Reduction.scratch(rows, W, bf16)],
        compiler_params=pltpu.CompilerParams(collective_id=collective_id, has_side_effects=True, vmem_limit_bytes=60 << 20))(
            normed_all, cot_all, codes, router, expand, place, gate_flat, up_flat, down_flat)

def output_kernel(normed_ref, cot_ref, hid_ref, gate_ref, up_ref, down_ref, out_ref, gate_out, up_out, down_out,
                  hid_in, wide_in, thin_in, hid_sem, in_sem, out_sem, *scratch):
    reduction = Reduction(*scratch)
    reduction.greet()
    part = reduction.part
    rows, width, units = out_ref.shape[0], normed_ref.shape[1], hid_ref.shape[1]
    f32, bf16 = jnp.float32, jnp.bfloat16
    lag = 2
    def hid_load(step): return pltpu.make_async_copy(step_block(hid_ref, step), hid_in.at[step % 2], hid_sem.at[step % 2])
    def loads(block):
        slot = block % 2
        zz, yy, xx = step_target(2 * block)
        at = pl.ds(pl.multiple_of((zz * 2 + yy) * 4 * rows, 4 * rows), 4 * rows)
        return ([pltpu.make_async_copy(src.at[at], wide_in.at[slot, n], in_sem.at[n, slot]) for n, src in enumerate((normed_ref, cot_ref))]
            + [pltpu.make_async_copy(src.at[at], thin_in.at[slot, n], in_sem.at[2 + n, slot]) for n, src in enumerate((hid_ref, gate_ref, up_ref))])
    for one in loads(0): one.start()
    hid_load(0).start()

    def inner(gate_sum, up_sum, down_sum):
        gate_sum[...] = jnp.zeros_like(gate_sum)
        up_sum[...] = jnp.zeros_like(up_sum)
        down_sum[...] = jnp.zeros_like(down_sum)

        def outputs(step):
            slot = step % 2
            hid_load(step).wait()
            @pl.when(step < 15)
            def _(): hid_load(step + 1).start()
            @pl.when(step >= 2)
            def _(): reduction.over_core(step - 2).wait_send()
            hid = hid_in[slot]
            for n in range(width // 512):
                at = pl.ds(n * 512, 512)
                value = nn(hid, down_ref[:, at]).astype(bf16)
                part[slot, 0, :, at] = value[:rows]
                part[slot, 1, :, at] = value[rows:]
            reduction.over_core(step).start()

        def down_gradient(block):
            slot = block % 2
            for one in loads(block): one.wait()
            @pl.when(block < 7)
            def _():
                for one in loads(block + 1): one.start()
            for n in range(units // 256):
                at = pl.ds(n * 256, 256)
                down_sum[at, :] += nn(thin_in[slot, 0, :, at].T, wide_in[slot, 1])

        def gate_gradients(block):
            slot = block % 2
            for n in range(width // 256):
                at = pl.ds(n * 256, 256)
                turned = wide_in[slot, 0, :, at].T
                gate_sum[at, :] += nn(turned, thin_in[slot, 1])
                up_sum[at, :] += nn(turned, thin_in[slot, 2])

        @pl.loop(0, 8 + lag)
        def _(block):
            for n, gradients in enumerate((down_gradient, gate_gradients)):
                step = 2 * block + n
                @pl.when(block < 8)
                def _(): outputs(step)
                @pl.when(block >= lag)
                def _(): gradients(block - lag)
                reduction.follow(step)
        kept = [pltpu.make_async_copy(src, dst, out_sem.at[n])
                for n, (src, dst) in enumerate(((gate_sum, gate_out), (up_sum, up_out), (down_sum, down_out)))]
        for one in kept: one.start()
        reduction.finish(out_ref, 16 + 2 * lag)
        for one in kept: one.wait()
    pl.run_scoped(inner, pltpu.VMEM((width, units), f32), pltpu.VMEM((width, units), f32), pltpu.VMEM((units, width), f32))

def run_outputs(normed_all, cot_all, hidden_gated, gate_grad, up_grad, down_flat, collective_id):
    total, width = normed_all.shape; rows = total // 32; units = hidden_gated.shape[1]
    f32, bf16 = jnp.float32, jnp.bfloat16; D = pltpu.SemaphoreType.DMA; V = pltpu.VMEM; S = jax.ShapeDtypeStruct
    anyspec, vspec = pl.BlockSpec(memory_space=pl.ANY), pl.BlockSpec(memory_space=V)
    return pl.pallas_call(output_kernel,
        out_shape=[S((rows, width), f32), S((width, units), f32), S((width, units), f32), S((units, width), f32)],
        in_specs=[anyspec] * 5 + [vspec], out_specs=[vspec] + [anyspec] * 3,
        scratch_shapes=[V((2, 2 * rows, units), bf16), V((2, 2, 4 * rows, width), bf16), V((2, 3, 4 * rows, units), bf16), D((2,)), D((5, 2)), D((3,)),
            *Reduction.scratch(rows, width, bf16)],
        compiler_params=pltpu.CompilerParams(collective_id=collective_id, has_side_effects=True, vmem_limit_bytes=62 << 20))(
            normed_all, cot_all, hidden_gated, gate_grad, up_grad, down_flat)


def inverse_rms(values):
    return lax.rsqrt(jnp.mean(values * values, axis=-1, keepdims=True) + EPSILON)

def attend_kernel(x_ref, gain_ref, qkv_ref, cos_ref, sin_ref, head_gain_ref, seg_rows_ref, seg_cols_ref,
                  normed_ref, raw_ref, q_ref, kv_ref, kv_other_ref, full_ref, heads_ref, lse_ref, bias, send_sem, recv_sem):
    z, y, x, c = coords()
    other = (z, 1 - y, 2 * x + c)
    greet([(None, other)])
    f32, bf16 = jnp.float32, jnp.bfloat16
    rows = x_ref.shape[0]; heads = q_ref.shape[1] // HEAD_SIZE; q_width = heads * HEAD_SIZE
    values = x_ref[...].astype(f32)
    normed_ref[...] = (values * inverse_rms(values) * gain_ref[...]).astype(bf16)
    def finish(raw, n):
        normed = raw * inverse_rms(raw) * head_gain_ref[pl.ds(n, 1), :]
        return (normed * cos_ref[...] + pltpu.roll(normed, HEAD_SIZE // 2, 1) * sin_ref[...]).astype(bf16)
    raw_kv = nn(normed_ref[...], qkv_ref[:, pl.ds(q_width, 2 * HEAD_SIZE)])
    raw_ref[:, pl.ds(q_width, HEAD_SIZE)] = raw_kv[:, :HEAD_SIZE]
    kv_ref[:, pl.ds(0, HEAD_SIZE)] = finish(raw_kv[:, :HEAD_SIZE], 1)
    kv_ref[:, pl.ds(HEAD_SIZE, HEAD_SIZE)] = raw_kv[:, HEAD_SIZE:].astype(bf16)
    move = pltpu.make_async_remote_copy(src_ref=kv_ref, dst_ref=kv_other_ref, send_sem=send_sem, recv_sem=recv_sem,
        device_id=other, device_id_type=MESH)
    @pl.when(y == 0)
    def _():
        move.start()
        kv_other_ref[...] = jnp.zeros_like(kv_other_ref)
    @pl.loop(0, heads // 2)
    def _(n):
        at = pl.ds(pl.multiple_of(n * 2 * HEAD_SIZE, 2 * HEAD_SIZE), 2 * HEAD_SIZE)
        raw = nn(normed_ref[...], qkv_ref[:, at])
        raw_ref[:, at] = raw
        for m in range(2):
            one = pl.ds(pl.multiple_of((2 * n + m) * HEAD_SIZE, HEAD_SIZE), HEAD_SIZE)
            q_ref[:, one] = finish(raw[:, m * HEAD_SIZE:(m + 1) * HEAD_SIZE], 0)
    row_id = lax.broadcasted_iota(jnp.int32, (rows, rows), 0)
    col_id = lax.broadcasted_iota(jnp.int32, (rows, rows), 1)
    bias[0] = jnp.where((seg_rows_ref[...] == seg_cols_ref[pl.ds(0, 1), :]) & (col_id <= row_id), 0.0, NEGATIVE)
    bias[1] = jnp.where(seg_rows_ref[...] == seg_cols_ref[pl.ds(1, 1), :], 0.0, NEGATIVE)
    lse_ref[...] = jnp.zeros_like(lse_ref)
    scale = HEAD_SIZE ** -0.5
    lane = lax.broadcasted_iota(jnp.int32, (rows, HEAD_SIZE), 1)
    def head(h, blocks):
        at = pl.ds(pl.multiple_of(h * HEAD_SIZE, HEAD_SIZE), HEAD_SIZE)
        query = q_ref[:, at]
        refs = (kv_ref, kv_other_ref)[:blocks]
        scores = [nt(query, ref[:, pl.ds(0, HEAD_SIZE)]) * scale + bias[n] for n, ref in enumerate(refs)]
        top = functools.reduce(jnp.maximum, [jnp.max(s, axis=1, keepdims=True) for s in scores])
        weights = [jnp.exp(s - top) for s in scores]
        total = sum(jnp.sum(w, axis=1, keepdims=True) for w in weights)
        inverse = 1.0 / total
        full = sum(nn((w * inverse).astype(bf16), ref[:, pl.ds(HEAD_SIZE, HEAD_SIZE)]) for w, ref in zip(weights, refs))
        full_ref[:, at] = full
        heads_ref[:, at] = full.astype(bf16)
        lse_ref[...] = jnp.where(lane == h, top + jnp.log(total), lse_ref[...])
    @pl.when(y == 0)
    def _():
        @pl.loop(0, heads)
        def _(h): head(h, 1)
        move.wait_send()
    @pl.when(y == 1)
    def _():
        move.wait_recv()
        @pl.loop(0, heads)
        def _(h): head(h, 2)

def attend(x, gain, qkv, cos, sin, head_gains, seg_rows, seg_cols, collective_id):
    rows, width = x.shape; q_width = qkv.shape[1] - 2 * HEAD_SIZE
    V = pltpu.VMEM; f32, bf16 = jnp.float32, jnp.bfloat16; S = jax.ShapeDtypeStruct
    vspec = pl.BlockSpec(memory_space=V)
    return pl.pallas_call(attend_kernel,
        out_shape=[S((rows, width), bf16), S((rows, q_width + HEAD_SIZE), f32), S((rows, q_width), bf16), S((rows, 2 * HEAD_SIZE), bf16),
            S((rows, 2 * HEAD_SIZE), bf16), S((rows, q_width), f32), S((rows, q_width), bf16), S((rows, HEAD_SIZE), f32)],
        in_specs=[vspec] * 8, out_specs=[vspec] * 8,
        scratch_shapes=[V((2, rows, rows), f32), pltpu.SemaphoreType.DMA, pltpu.SemaphoreType.DMA],
        compiler_params=pltpu.CompilerParams(collective_id=collective_id, has_side_effects=True, vmem_limit_bytes=48 << 20))(
            x, gain, qkv, cos, sin, head_gains, seg_rows, seg_cols)

def attend_back_kernel(cot_ref, out_w_ref, q_ref, kv_ref, kv_other_ref, raw_ref, full_ref, lse_ref, cos_ref, sin_ref, head_gain_ref,
                       seg_rows_ref, seg_cols_ref, grad_ref, gains_ref, grad_heads, delta, stats, bias, grad_q, grad_kv, kv_send, kv_in, send_sem, recv_sem):
    z, y, x, c = coords()
    other = (z, 1 - y, 2 * x + c)
    greet([(None, other)])
    f32, bf16 = jnp.float32, jnp.bfloat16
    rows = q_ref.shape[0]; heads = q_ref.shape[1] // HEAD_SIZE; q_width = heads * HEAD_SIZE
    scale = HEAD_SIZE ** -0.5
    lane = lax.broadcasted_iota(jnp.int32, (rows, HEAD_SIZE), 1)
    delta[...] = jnp.zeros_like(delta)
    @pl.loop(0, heads // 2)
    def _(n):
        at = pl.ds(pl.multiple_of(n * 2 * HEAD_SIZE, 2 * HEAD_SIZE), 2 * HEAD_SIZE)
        grad = nn(cot_ref[...], out_w_ref[:, at]).astype(bf16)
        grad_heads[:, at] = grad
        product = grad.astype(f32) * full_ref[:, at]
        for m in range(2):
            one = jnp.sum(product[:, m * HEAD_SIZE:(m + 1) * HEAD_SIZE], axis=1, keepdims=True)
            delta[...] = jnp.where(lane == 2 * n + m, one, delta[...])
    stats[0] = lse_ref[...].T
    stats[1] = delta[...].T
    key_id = lax.broadcasted_iota(jnp.int32, (rows, rows), 0)
    query_id = lax.broadcasted_iota(jnp.int32, (rows, rows), 1)
    def block(ref, seg_keys, causal):
        same = seg_keys == seg_cols_ref[pl.ds(0, 1), :]
        bias[...] = jnp.where(same & (key_id <= query_id) if causal else same, 0.0, NEGATIVE)
        grad_kv[...] = jnp.zeros_like(grad_kv)
        key, value = ref[:, pl.ds(0, HEAD_SIZE)], ref[:, pl.ds(HEAD_SIZE, HEAD_SIZE)]
        @pl.loop(0, heads)
        def _(h):
            at = pl.ds(pl.multiple_of(h * HEAD_SIZE, HEAD_SIZE), HEAD_SIZE)
            query, grad = q_ref[:, at], grad_heads[:, at]
            probs = jnp.exp(nt(key, query) * scale + bias[...] - stats[0, pl.ds(h, 1), :])
            grad_scores = (probs * (nt(value, grad) - stats[1, pl.ds(h, 1), :])).astype(bf16)
            grad_kv[:, pl.ds(0, HEAD_SIZE)] += nn(grad_scores, query) * scale
            grad_kv[:, pl.ds(HEAD_SIZE, HEAD_SIZE)] += nn(probs.astype(bf16), grad)
            grad_q[:, at] += lax.dot_general(grad_scores, key, (((0,), (0,)), ((), ())), preferred_element_type=f32) * scale
    grad_q[...] = jnp.zeros_like(grad_q)
    move = pltpu.make_async_remote_copy(src_ref=kv_send, dst_ref=kv_in, send_sem=send_sem, recv_sem=recv_sem, device_id=other, device_id_type=MESH)
    @pl.when(y == 1)
    def _():
        block(kv_other_ref, seg_rows_ref[1], False)
        kv_send[...] = grad_kv[...].astype(bf16)
        move.start()
    block(kv_ref, seg_rows_ref[0], True)
    @pl.when(y == 0)
    def _():
        move.wait_recv()
        grad_kv[...] += kv_in[...].astype(f32)
    def pull(grad, raw, n):
        turned = grad * cos_ref[...] - pltpu.roll(grad, HEAD_SIZE // 2, 1) * sin_ref[...]
        inverse = inverse_rms(raw)
        unit = raw * inverse
        gains_ref[pl.ds(n, 1), :] += jnp.sum(turned * unit, axis=0, keepdims=True)
        scaled = turned * head_gain_ref[pl.ds(n, 1), :]
        return (inverse * (scaled - unit * jnp.mean(scaled * unit, axis=1, keepdims=True))).astype(bf16)
    gains_ref[...] = jnp.zeros_like(gains_ref)
    @pl.loop(0, heads)
    def _(h):
        at = pl.ds(pl.multiple_of(h * HEAD_SIZE, HEAD_SIZE), HEAD_SIZE)
        grad_ref[:, at] = pull(grad_q[:, at], raw_ref[:, at], 0)
    at = pl.ds(q_width, HEAD_SIZE)
    grad_ref[:, at] = pull(grad_kv[:, pl.ds(0, HEAD_SIZE)], raw_ref[:, at], 1)
    grad_ref[:, pl.ds(q_width + HEAD_SIZE, HEAD_SIZE)] = grad_kv[:, pl.ds(HEAD_SIZE, HEAD_SIZE)].astype(bf16)
    @pl.when(y == 1)
    def _(): move.wait_send()

def attend_back(cot, out_w, q, kv, kv_other, raw, full, lse, cos, sin, head_gains, seg_rows, seg_cols, collective_id):
    rows, q_width = q.shape
    V = pltpu.VMEM; f32, bf16 = jnp.float32, jnp.bfloat16; S = jax.ShapeDtypeStruct
    vspec = pl.BlockSpec(memory_space=V)
    return pl.pallas_call(attend_back_kernel,
        out_shape=[S((rows, q_width + 2 * HEAD_SIZE), bf16), S((8, HEAD_SIZE), f32)],
        in_specs=[vspec] * 13, out_specs=[vspec] * 2,
        scratch_shapes=[V((rows, q_width), bf16), V((rows, HEAD_SIZE), f32), V((2, HEAD_SIZE, rows), f32), V((rows, rows), f32), V((rows, q_width), f32),
            V((rows, 2 * HEAD_SIZE), f32), V((rows, 2 * HEAD_SIZE), bf16), V((rows, 2 * HEAD_SIZE), bf16), pltpu.SemaphoreType.DMA, pltpu.SemaphoreType.DMA],
        compiler_params=pltpu.CompilerParams(collective_id=collective_id, has_side_effects=True, vmem_limit_bytes=48 << 20))(
            cot, out_w, q, kv, kv_other, raw, full, lse, cos, sin, head_gains, seg_rows, seg_cols)


def gathered_local(
    hidden_in,
    attn_gain,
    w_query,
    key_weight,
    value_weight,
    w_output,
    query_gain,
    key_gain,
    ffn_gain,
    router,
    gate_weight,
    up_weight,
    down_weight,
    routes,
    segments,
    cotangent,
):
    bf16, f32 = jnp.bfloat16, jnp.float32
    context_size = lax.axis_size(CONTEXT)
    tensor_size = lax.axis_size(TENSOR)
    group_count = lax.axis_size(FSDP) * context_size
    fsdp_rank = lax.axis_index(FSDP)
    context_rank = lax.axis_index(CONTEXT)
    tensor_rank = lax.axis_index(TENSOR)
    group_rank = fsdp_rank * context_size + context_rank
    row_count, width = hidden_in.shape[1:]
    own_count = row_count // tensor_size
    own_start = tensor_rank * own_count
    local_experts, _, hidden_width = gate_weight.shape
    experts_total = router.shape[1]
    first_expert = group_rank * local_experts
    capacity = 9 * row_count * TOPK // (8 * experts_total)
    query_width = w_query.shape[1]

    expert_ids = jnp.arange(experts_total, dtype=jnp.int32)
    chosen = jnp.any(routes[0][..., None] == expert_ids, axis=1)
    kept = chosen & (earlier_counts(chosen) < capacity)
    code = chosen.astype(bf16) + kept.astype(bf16)
    chosen_own = lax.dynamic_slice_in_dim(chosen, own_start, own_count, 0)
    code = code.reshape(tensor_size, own_count, experts_total).transpose(1, 0, 2)

    pieces = (code, router, attn_gain, ffn_gain, query_gain, key_gain, segments)
    small = jnp.concatenate([piece.astype(bf16).reshape(-1) for piece in pieces])
    small = jnp.pad(small, (0, -small.size % 2048)).reshape(-1, 128)
    qkv_weight = jnp.concatenate([w_query, key_weight, value_weight], axis=1)
    pieces_of = [(0, 0, small.shape[0], 0)]
    for array in (1, 2):
        pieces_of += [(array, 0, 112, 0), (array, 112, 96, 0), (array, 208, 48, 1)]
    small, qkv_full, full_output = gather_groups((small, qkv_weight, w_output), tuple(pieces_of), 1)
    grad_out_own = lax.dynamic_slice_in_dim(cotangent[0], own_start, own_count, 0)
    grad_out_own, codes = lax.optimization_barrier((grad_out_own, small))
    grad_out_all = lax.all_gather(grad_out_own, EVERYONE, axis=0, tiled=True)
    small = small.reshape(group_count, -1)
    parts, at = [], code.size
    for piece in pieces[1:]:
        parts.append(small[:, at : at + piece.size])
        at += piece.size
    full_router = parts[0].reshape(width, experts_total)
    gain_attn, gain_ffn, gain_query, gain_key = (
        part.reshape(-1).astype(f32) for part in parts[1:5]
    )
    head_gains = jnp.stack([gain_query, gain_key])
    all_segments = parts[5].astype(jnp.int32)

    own_seg = segments[0]
    first_seg = lax.dynamic_index_in_dim(all_segments, group_rank - context_rank, 0, keepdims=False)
    other_seg = lax.dynamic_index_in_dim(
        all_segments, group_rank + 1 - 2 * context_rank, 0, keepdims=False
    )
    smaller = jnp.sum((own_seg[None, :] < own_seg[:, None]).astype(jnp.int32), axis=1)
    smaller_first = jnp.sum((first_seg[None, :] < own_seg[:, None]).astype(jnp.int32), axis=1)
    positions = jnp.arange(row_count, dtype=jnp.int32) - smaller
    positions = positions + context_rank * (row_count - smaller_first)
    cosine_table, sine_table = rope_tables(positions, HEAD_SIZE)
    turn = jnp.where(jnp.arange(HEAD_SIZE) < HEAD_SIZE // 2, -1.0, 1.0)
    sine_table = sine_table * turn
    seg_rows = jnp.stack([own_seg, other_seg])

    normed_one, raw, query, kv, kv_other, heads_full, heads_low, log_total = attend(
        hidden_in[0],
        gain_attn[None],
        qkv_full,
        cosine_table,
        sine_table,
        head_gains,
        own_seg[:, None],
        seg_rows,
        8,
    )
    input_own = lax.dynamic_slice_in_dim(hidden_in[0], own_start, own_count, 0)
    residual_own, normed_own, normed_all = mix_heads(
        heads_low, full_output, input_own, gain_ffn[None], 3
    )
    input_own = input_own.astype(f32)
    ignored, second_pull = jax.vjp(rms_scale, residual_own, gain_ffn)

    units = local_experts * hidden_width
    gate_flat = gate_weight.transpose(1, 0, 2).reshape(width, units)
    up_flat = up_weight.transpose(1, 0, 2).reshape(width, units)
    down_flat = down_weight.reshape(units, width)
    unit_expert = first_expert + jnp.arange(units, dtype=jnp.int32) // hidden_width
    lane_ids = jnp.arange(tensor_size * experts_total, dtype=jnp.int32)
    expand = (lane_ids[:, None] % experts_total == unit_expert[None, :]).astype(bf16)
    column = tensor_rank * experts_total + unit_expert
    place = (column[:, None] == lane_ids[None, :]).astype(bf16)
    router_lanes = jnp.concatenate([full_router] * tensor_size, axis=1)
    scattered, hidden_gated, gate_grad, up_grad = run_experts(
        normed_all, grad_out_all, codes, router_lanes, expand, place, gate_flat, up_flat, down_flat, 4
    )
    scores = jnp.where(chosen_own, matmul(normed_own, full_router), NEGATIVE)
    gates_own = jnp.where(chosen_own, jax.nn.softmax(scores, axis=-1), 0.0)
    gates_grad_own = jnp.sum(
        scattered[:, width:].reshape(own_count, tensor_size, experts_total), axis=1
    )
    grad_selected = gates_own * (
        gates_grad_own - jnp.sum(gates_own * gates_grad_own, axis=1, keepdims=True)
    )
    grad_logits = jnp.pad(grad_selected.astype(bf16), ((0, 0), (0, 128 - experts_total)))
    grad_normed_two = scattered[:, :width] + matmul_nt(grad_logits[:, :experts_total], full_router)
    grad_resid_norm, grad_gain_ffn = second_pull(grad_normed_two)
    grad_resid_own = grad_out_own.astype(f32) + grad_resid_norm
    message = jnp.concatenate([grad_resid_own.astype(bf16), grad_logits], axis=1)
    extra = jnp.pad(grad_gain_ffn.astype(bf16)[None], ((0, 15), (0, 128)))
    message = gather_tensor(jnp.concatenate([message, extra], axis=0), 5)
    grad_attn = message[:, :own_count, :width].reshape(row_count, width)
    grad_raw, head_gain_grads = attend_back(
        grad_attn,
        full_output,
        query,
        kv,
        kv_other,
        raw,
        heads_full,
        log_total,
        cosine_table,
        sine_table,
        head_gains,
        seg_rows[:, :, None],
        seg_rows,
        9,
    )
    group_logits = message[:, :own_count, width:].reshape(row_count, 128)
    grad_gain_ffn = jnp.sum(message[:, own_count, :width].astype(f32), axis=0)
    normed_group = lax.dynamic_slice_in_dim(normed_all, group_rank * row_count, row_count, 0)
    grad_router = matmul_tn(normed_group, group_logits)
    extra = jnp.where(jnp.arange(128) == experts_total, grad_gain_ffn[:, None], grad_router)
    grad_w_output = jnp.concatenate([matmul_tn(grad_attn, heads_low), extra], axis=1)
    grad_w_output = lax.psum_scatter(
        grad_w_output.astype(bf16), GROUPS, scatter_dimension=0, tiled=True
    )

    grad_normed_part = matmul_nt(grad_raw, qkv_full)
    ignored, whole_pull = jax.vjp(rms_scale, hidden_in[0].astype(f32), gain_attn)
    head_gain_row = jnp.pad(head_gain_grads[:2].reshape(-1), (0, width - 2 * HEAD_SIZE))
    gain_rows = jnp.stack([whole_pull(grad_normed_part)[1], head_gain_row])
    message = jnp.pad(
        grad_normed_part.astype(bf16).reshape(tensor_size, own_count, width),
        ((0, 0), (0, 16), (0, 0)),
    )
    message = lax.dynamic_update_slice(message, gain_rows.astype(bf16)[None], (0, own_count, 0))
    message = scatter_tensor(message.reshape(-1, width), 6)
    ignored, first_pull = jax.vjp(rms_scale, input_own, gain_attn)
    grad_inputs_norm, ignored = first_pull(message[:own_count])
    message = jnp.concatenate([grad_resid_own + grad_inputs_norm, message[own_count:]], axis=0)
    message = gather_tensor(message.astype(bf16), 7)
    input_grad = message[:, :own_count].reshape(row_count, width).astype(f32)
    gain_rows = message[0, own_count : own_count + 2].astype(f32)
    head_gains_grad = jnp.pad(
        gain_rows[1, : 2 * HEAD_SIZE].reshape(2, group_count, -1),
        ((0, 0), (0, 0), (0, (width - HEAD_SIZE) // group_count)),
    ).reshape(2, width)
    extra = jnp.pad(
        jnp.stack([gain_rows[0], head_gains_grad[0], head_gains_grad[1]], axis=1),
        ((0, 0), (0, 125)),
    )
    grad_qkv = jnp.concatenate([matmul_tn(normed_one, grad_raw), extra], axis=1)
    grad_qkv, hidden_gated = lax.optimization_barrier((grad_qkv.astype(bf16), hidden_gated))
    grad_qkv = lax.psum_scatter(grad_qkv, GROUPS, scatter_dimension=0, tiled=True)
    moe_own, grad_w_gate, grad_w_up, grad_w_down = run_outputs(
        normed_all, grad_out_all, hidden_gated, gate_grad, up_grad, down_flat, 10
    )

    def by_expert(grad):
        return grad.reshape(width, local_experts, hidden_width).transpose(1, 0, 2)

    grad_w_gate, grad_w_up = by_expert(grad_w_gate), by_expert(grad_w_up)
    output = gather_tensor((residual_own + moe_own).astype(bf16), 11).reshape(row_count, width)
    output, grad_qkv, grad_w_output = lax.optimization_barrier((output, grad_qkv, grad_w_output))
    value_at, extra_at = query_width + HEAD_SIZE, query_width + 2 * HEAD_SIZE
    return (
        output[None],
        input_grad[None],
        grad_qkv[:, extra_at].astype(f32),
        grad_qkv[:, :query_width].astype(f32),
        grad_qkv[:, query_width:value_at].astype(f32),
        grad_qkv[:, value_at:extra_at].astype(f32),
        grad_w_output[:, :query_width].astype(f32),
        grad_qkv[: query_gain.shape[0], extra_at + 1].astype(f32),
        grad_qkv[: key_gain.shape[0], extra_at + 2].astype(f32),
        grad_w_output[:, query_width + experts_total].astype(f32),
        grad_w_output[:, query_width : query_width + experts_total].astype(f32),
        grad_w_gate,
        grad_w_up,
        grad_w_down.reshape(down_weight.shape),
    )


def local(*arrays):
    sizes = tuple(lax.axis_size(name) for name in EVERYONE)
    return (gathered_local if sizes == (4, 2, 4) and arrays[9].shape[1] == 32 else routed_local)(*arrays)


def solution(mesh):
    in_specs = (
        P(FSDP, CONTEXT, None),
        P(GROUPS),
        P(GROUPS, TENSOR),
        P(GROUPS, TENSOR),
        P(GROUPS, TENSOR),
        P(GROUPS, TENSOR),
        P(GROUPS),
        P(GROUPS),
        P(GROUPS),
        P(GROUPS, None),
        P(GROUPS, None, TENSOR),
        P(GROUPS, None, TENSOR),
        P(GROUPS, TENSOR, None),
        P(FSDP, CONTEXT, None),
        P(FSDP, CONTEXT),
        P(FSDP, CONTEXT, None),
    )
    out_specs = (
        P(FSDP, CONTEXT, None),
        P(FSDP, CONTEXT, None),
        P(GROUPS),
        P(GROUPS, TENSOR),
        P(GROUPS, TENSOR),
        P(GROUPS, TENSOR),
        P(GROUPS, TENSOR),
        P(GROUPS),
        P(GROUPS),
        P(GROUPS),
        P(GROUPS, None),
        P(GROUPS, None, TENSOR),
        P(GROUPS, None, TENSOR),
        P(GROUPS, TENSOR, None),
    )
    return jax.shard_map(local, mesh=mesh, in_specs=in_specs, out_specs=out_specs, check_vma=False)
```

```python
import functools
import math

import jax
import jax.numpy as jnp
from jax import lax
from jax.experimental import pallas as pl
from jax.experimental.pallas import tpu as pltpu
from jax.sharding import PartitionSpec as P

HEAD_SIZE = 128
TOPK = 8
FSDP, CONTEXT, TENSOR = "fsdp", "context", "tensor"
GROUPS = (FSDP, CONTEXT)
EVERYONE = (FSDP, CONTEXT, TENSOR)


EPSILON = 1e-06
ROPE_BASE = 1000000.0
NEGATIVE = -1e30


def rms_scale(values, gain_vec):
    return (
        values * lax.rsqrt(jnp.mean(values * values, axis=-1, keepdims=True) + EPSILON) * gain_vec
    )


def rotate(values):
    half_width = values.shape[-1] // 2
    return jnp.concatenate([-values[..., half_width:], values[..., :half_width]], axis=-1)


def rope_tables(positions, head_width):
    step_index = jnp.arange(head_width // 2, dtype=jnp.float32)
    inverse = jnp.exp(step_index * (-2.0 * math.log(ROPE_BASE) / head_width))
    angles = positions.astype(jnp.float32)[:, None] * inverse[None, :]
    cosine_table = jnp.cos(angles)
    sine_table = jnp.sin(angles)
    return (
        jnp.concatenate([cosine_table, cosine_table], -1),
        jnp.concatenate([sine_table, sine_table], -1),
    )


def doc_positions(segment):
    token_index = jnp.arange(segment.shape[0], dtype=jnp.int32)
    smaller = (segment[None, :] < segment[:, None]).astype(jnp.int32)
    return token_index - jnp.sum(smaller, axis=1)


def earlier_counts(chosen):
    rows = chosen.shape[0]
    row_id = lax.broadcasted_iota(jnp.int32, (rows, rows), 0)
    col_id = lax.broadcasted_iota(jnp.int32, (rows, rows), 1)
    earlier = (col_id < row_id).astype(jnp.bfloat16)
    return matmul(earlier, chosen.astype(jnp.bfloat16))


def qk_finish(raw_values, gain_vec, cosine_table, sine_table):
    normed = rms_scale(raw_values, gain_vec)
    return normed * cosine_table + rotate(normed) * sine_table


def matmul(left_side, right_side):
    return jnp.dot(left_side, right_side, preferred_element_type=jnp.float32)


def matmul_nt(left_side, right_side):
    return lax.dot_general(
        left_side, right_side, (((1,), (1,)), ((), ())), preferred_element_type=jnp.float32
    )


def matmul_tn(left_side, right_side):
    return lax.dot_general(
        left_side, right_side, (((0,), (0,)), ((), ())), preferred_element_type=jnp.float32
    )


def block_scores(query_vectors, keys_all, seg_all, query_seg, query_index, key_ids, block_id, key_block):
    leading_row = block_id * key_block
    keys_part = lax.dynamic_slice_in_dim(keys_all, leading_row, key_block, 0)
    seg_part = lax.dynamic_slice_in_dim(seg_all, leading_row, key_block, 0)
    key_index = lax.dynamic_slice_in_dim(key_ids, leading_row, key_block, 0)
    score_scale = query_vectors.shape[2] ** (-0.5)
    scores = (
        jnp.einsum("qhd,kd->hqk", query_vectors, keys_part, preferred_element_type=jnp.float32)
        * score_scale
    )
    allowed = (query_seg[:, None] == seg_part[None, :]) & (
        key_index[None, :] <= query_index[:, None]
    )
    return (scores, allowed[None, :, :], keys_part)


def attention_forward(
    query_vectors, keys_all, values_all, seg_all, query_seg, query_index, key_ids, key_block
):
    row_count, head_count, head_width = query_vectors.shape
    block_count = keys_all.shape[0] // key_block

    def stats_step(running, block_id):
        run_max, run_sum = running
        scores, allowed, unused = block_scores(
            query_vectors, keys_all, seg_all, query_seg, query_index, key_ids, block_id, key_block
        )
        masked = jnp.where(allowed, scores, NEGATIVE)
        new_max = jnp.maximum(run_max, jnp.max(masked, axis=2))
        weights = jnp.where(allowed, jnp.exp(masked - new_max[:, :, None]), 0.0)
        run_sum = run_sum * jnp.exp(run_max - new_max) + jnp.sum(weights, axis=2)
        return ((new_max, run_sum), None)

    start_state = (
        jnp.full((head_count, row_count), NEGATIVE, jnp.float32),
        jnp.zeros((head_count, row_count), jnp.float32),
    )
    (run_max, run_sum), ignored = lax.scan(
        stats_step, start_state, jnp.arange(block_count, dtype=jnp.int32)
    )
    log_total = run_max + jnp.log(run_sum)

    def value_step(accumulated, block_id):
        scores, allowed, unused = block_scores(
            query_vectors, keys_all, seg_all, query_seg, query_index, key_ids, block_id, key_block
        )
        prob_block = jnp.where(allowed, jnp.exp(scores - log_total[:, :, None]), 0.0).astype(
            jnp.bfloat16
        )
        values_part = lax.dynamic_slice_in_dim(values_all, block_id * key_block, key_block, 0)
        accumulated = accumulated + jnp.einsum(
            "hqk,kd->qhd", prob_block, values_part, preferred_element_type=jnp.float32
        )
        return (accumulated, None)

    heads_full, ignored = lax.scan(
        value_step,
        jnp.zeros((row_count, head_count, head_width), jnp.float32),
        jnp.arange(block_count, dtype=jnp.int32),
    )
    return (heads_full, log_total)


def attention_backward(
    query_vectors,
    keys_all,
    values_all,
    seg_all,
    query_seg,
    query_index,
    key_ids,
    key_block,
    log_total,
    grad_heads,
    row_delta,
):
    row_count, head_count, head_width = query_vectors.shape
    block_count = keys_all.shape[0] // key_block
    score_scale = head_width ** (-0.5)

    def grad_step(grad_query, block_id):
        scores, allowed, keys_part = block_scores(
            query_vectors, keys_all, seg_all, query_seg, query_index, key_ids, block_id, key_block
        )
        values_part = lax.dynamic_slice_in_dim(values_all, block_id * key_block, key_block, 0)
        prob_block = jnp.where(allowed, jnp.exp(scores - log_total[:, :, None]), 0.0)
        grad_prob = jnp.einsum(
            "qhd,kd->hqk", grad_heads, values_part, preferred_element_type=jnp.float32
        )
        grad_score = (prob_block * (grad_prob - row_delta[:, :, None])).astype(jnp.bfloat16)
        grad_query = (
            grad_query
            + jnp.einsum("hqk,kd->qhd", grad_score, keys_part, preferred_element_type=jnp.float32)
            * score_scale
        )
        grad_key = (
            jnp.einsum("hqk,qhd->kd", grad_score, query_vectors, preferred_element_type=jnp.float32)
            * score_scale
        )
        grad_value = jnp.einsum(
            "hqk,qhd->kd",
            prob_block.astype(jnp.bfloat16),
            grad_heads,
            preferred_element_type=jnp.float32,
        )
        return (grad_query, (grad_key, grad_value))

    grad_query, (grad_key, grad_value) = lax.scan(
        grad_step,
        jnp.zeros((row_count, head_count, head_width), jnp.float32),
        jnp.arange(block_count, dtype=jnp.int32),
    )
    return (grad_query, grad_key.reshape(-1, head_width), grad_value.reshape(-1, head_width))


def to_experts(buffer):
    return lax.all_to_all(buffer, GROUPS, split_axis=0, concat_axis=1, tiled=True)


def from_experts(result_rows):
    return lax.all_to_all(result_rows, GROUPS, split_axis=1, concat_axis=0, tiled=True)


def pick_pairs(buffer, target, row_count):
    model_width = buffer.shape[2]
    flat_rows = jnp.concatenate(
        [buffer.reshape(-1, model_width), jnp.zeros((1, model_width), buffer.dtype)], axis=0
    )
    return flat_rows[target].reshape(row_count, TOPK, model_width)


def routed_local(
    hidden_in,
    attn_gain,
    w_query,
    key_weight,
    value_weight,
    w_output,
    query_gain,
    key_gain,
    ffn_gain,
    router,
    gate_weight,
    up_weight,
    down_weight,
    routes,
    segments,
    cotangent,
):
    context_rank = lax.axis_index(CONTEXT)
    input_rows = hidden_in[0].astype(jnp.float32)
    row_count, model_width = input_rows.shape
    gathered = (
        lax.all_gather(w_query, GROUPS, axis=0, tiled=True),
        lax.all_gather(key_weight, GROUPS, axis=0, tiled=True),
        lax.all_gather(value_weight, GROUPS, axis=0, tiled=True),
        lax.all_gather(w_output, GROUPS, axis=0, tiled=True),
        lax.all_gather(router, GROUPS, axis=0, tiled=True),
        lax.all_gather(attn_gain, GROUPS, axis=0, tiled=True),
        lax.all_gather(ffn_gain, GROUPS, axis=0, tiled=True),
        lax.all_gather(query_gain, GROUPS, axis=0, tiled=True),
        lax.all_gather(key_gain, GROUPS, axis=0, tiled=True),
    )
    full_query, full_key, full_value, full_output, full_router = (
        gathered[0],
        gathered[1],
        gathered[2],
        gathered[3],
        gathered[4],
    )
    gain_attn = gathered[5].astype(jnp.float32)
    gain_ffn = gathered[6].astype(jnp.float32)
    gain_query = gathered[7].astype(jnp.float32)
    gain_key = gathered[8].astype(jnp.float32)
    local_heads = full_query.shape[1] // HEAD_SIZE
    seg_all = lax.all_gather(segments, CONTEXT, axis=1, tiled=True)[0]
    length = seg_all.shape[0]
    start_row = context_rank * row_count
    positions = lax.dynamic_slice_in_dim(doc_positions(seg_all), start_row, row_count)
    cosine_table, sine_table = rope_tables(positions, HEAD_SIZE)
    query_seg = segments[0]
    query_index = start_row + jnp.arange(row_count, dtype=jnp.int32)
    key_ids = jnp.arange(length, dtype=jnp.int32)
    key_block = min(512, length)

    def query_finish(raw_values, gain_vec):
        return qk_finish(raw_values, gain_vec, cosine_table[:, None, :], sine_table[:, None, :])

    def key_finish(raw_values, gain_vec):
        return qk_finish(raw_values, gain_vec, cosine_table, sine_table)

    normed_f, first_pull = jax.vjp(rms_scale, input_rows, gain_attn)
    attention_normalized = normed_f.astype(jnp.bfloat16)
    query_unrotated = matmul(attention_normalized, full_query).reshape(
        row_count, local_heads, HEAD_SIZE
    )
    key_unrotated = matmul(attention_normalized, full_key)
    value_raw = matmul(attention_normalized, full_value)
    query_f, query_pull = jax.vjp(query_finish, query_unrotated, gain_query)
    key_f, key_pull = jax.vjp(key_finish, key_unrotated, gain_key)
    query_vectors = query_f.astype(jnp.bfloat16)
    keys_all, values_all = (
        lax.all_gather(key_f.astype(jnp.bfloat16), CONTEXT, axis=0, tiled=True),
        lax.all_gather(value_raw.astype(jnp.bfloat16), CONTEXT, axis=0, tiled=True),
    )
    heads_full, log_total = attention_forward(
        query_vectors, keys_all, values_all, seg_all, query_seg, query_index, key_ids, key_block
    )
    heads_low = heads_full.reshape(row_count, local_heads * HEAD_SIZE).astype(jnp.bfloat16)
    attn_out = lax.psum(matmul_nt(heads_low, full_output).astype(jnp.bfloat16), TENSOR).astype(
        jnp.float32
    )
    residual_stream = input_rows + attn_out
    second_f, second_pull = jax.vjp(rms_scale, residual_stream, gain_ffn)
    feedforward_normalized = second_f.astype(jnp.bfloat16)
    router_scores = matmul(feedforward_normalized, full_router)
    experts_total = full_router.shape[1]
    route_ids = routes[0]
    chosen = route_ids[:, :, None] == jnp.arange(experts_total, dtype=jnp.int32)
    selected = jnp.sum(jnp.where(chosen, router_scores[:, None, :], 0.0), axis=2)
    gate_probs = jax.nn.softmax(selected, axis=-1)
    capacity = 9 * row_count * TOPK // (8 * experts_total)
    before = earlier_counts(jnp.any(chosen, axis=1)).astype(jnp.int32)
    slot_index = jnp.sum(jnp.where(chosen, before[:, None, :], 0), axis=2)
    target = jnp.where(
        slot_index < capacity, route_ids * capacity + slot_index, experts_total * capacity
    ).reshape(-1)
    source = jnp.repeat(jnp.arange(row_count, dtype=jnp.int32), TOPK)
    send_rows = (
        jnp.zeros((experts_total * capacity, model_width), jnp.bfloat16)
        .at[target]
        .set(feedforward_normalized[source], mode="drop")
    )
    expert_input_rows = to_experts(send_rows.reshape(experts_total, capacity, model_width))
    gate_activation_input = jnp.einsum(
        "phu,puo->pho", expert_input_rows, gate_weight, preferred_element_type=jnp.float32
    )
    up_activation_input = jnp.einsum(
        "phu,puo->pho", expert_input_rows, up_weight, preferred_element_type=jnp.float32
    )
    sigmoid_gate = jax.nn.sigmoid(gate_activation_input)
    silu_gate = gate_activation_input * sigmoid_gate
    hidden_middle = (silu_gate * up_activation_input).astype(jnp.bfloat16)
    expert_part = jnp.einsum(
        "pic,pcw->piw", hidden_middle, down_weight, preferred_element_type=jnp.float32
    ).astype(jnp.bfloat16)
    grad_out = cotangent[0].astype(jnp.float32)
    returned = pick_pairs(from_experts(expert_part), target, row_count)
    moe_part = jnp.sum(returned.astype(jnp.float32) * gate_probs[:, :, None], axis=1)
    moe_out = lax.psum(moe_part.astype(jnp.bfloat16), TENSOR).astype(jnp.float32)
    grad_gate_part = jnp.sum(returned.astype(jnp.float32) * grad_out[:, None, :], axis=2)
    output = (residual_stream + moe_out).astype(jnp.bfloat16)
    pair_grad = (
        (gate_probs[:, :, None] * grad_out[:, None, :])
        .astype(jnp.bfloat16)
        .reshape(row_count * TOPK, model_width)
    )
    send_grad = (
        jnp.zeros((experts_total * capacity, model_width), jnp.bfloat16)
        .at[target]
        .set(pair_grad, mode="drop")
    )
    expert_output_gradient = to_experts(send_grad.reshape(experts_total, capacity, model_width))
    grad_mid = jnp.einsum(
        "jtk,jvk->jtv", expert_output_gradient, down_weight, preferred_element_type=jnp.float32
    )
    grad_w_down = jnp.einsum(
        "tce,tci->tei", hidden_middle, expert_output_gradient, preferred_element_type=jnp.float32
    )
    gate_activation_gradient = (
        grad_mid
        * up_activation_input
        * sigmoid_gate
        * (1.0 + gate_activation_input * (1.0 - sigmoid_gate))
    ).astype(jnp.bfloat16)
    up_activation_gradient = (grad_mid * silu_gate).astype(jnp.bfloat16)
    grad_w_gate = jnp.einsum(
        "ahw,ahp->awp",
        expert_input_rows,
        gate_activation_gradient,
        preferred_element_type=jnp.float32,
    )
    grad_w_up = jnp.einsum(
        "ahw,ahp->awp",
        expert_input_rows,
        up_activation_gradient,
        preferred_element_type=jnp.float32,
    )
    grad_expert_in = (
        jnp.einsum(
            "ous,ops->oup",
            gate_activation_gradient,
            gate_weight,
            preferred_element_type=jnp.float32,
        )
        + jnp.einsum(
            "ous,ops->oup", up_activation_gradient, up_weight, preferred_element_type=jnp.float32
        )
    ).astype(jnp.bfloat16)
    grad_pairs = pick_pairs(from_experts(grad_expert_in), target, row_count)
    grad_normed_part = jnp.sum(grad_pairs.astype(jnp.float32), axis=1)
    grad_normed_moe, grad_gates = (
        lax.psum(grad_normed_part.astype(jnp.bfloat16), TENSOR).astype(jnp.float32),
        lax.psum(grad_gate_part.astype(jnp.bfloat16), TENSOR).astype(jnp.float32),
    )
    grad_selected = gate_probs * (
        grad_gates - jnp.sum(gate_probs * grad_gates, axis=1, keepdims=True)
    )
    grad_logits = jnp.sum(jnp.where(chosen, grad_selected[:, :, None], 0.0), axis=1).astype(
        jnp.bfloat16
    )
    grad_router = matmul_tn(feedforward_normalized, grad_logits)
    grad_normed_two = grad_normed_moe + matmul_nt(grad_logits, full_router)
    grad_resid_norm, grad_gain_ffn = second_pull(grad_normed_two)
    grad_resid = grad_out + grad_resid_norm
    grad_attn = grad_resid.astype(jnp.bfloat16)
    grad_w_output = matmul_tn(grad_attn, heads_low)
    grad_heads = (
        matmul(grad_attn, full_output)
        .astype(jnp.bfloat16)
        .reshape(row_count, local_heads, HEAD_SIZE)
    )
    row_delta = jnp.sum(grad_heads.astype(jnp.float32) * heads_full, axis=2).T
    grad_query, grad_key_terms, grad_value_terms = attention_backward(
        query_vectors,
        keys_all,
        values_all,
        seg_all,
        query_seg,
        query_index,
        key_ids,
        key_block,
        log_total,
        grad_heads,
        row_delta,
    )
    grad_key_local, grad_value_local = (
        lax.psum_scatter(
            grad_key_terms.astype(jnp.bfloat16), CONTEXT, scatter_dimension=0, tiled=True
        ).astype(jnp.float32),
        lax.psum_scatter(
            grad_value_terms.astype(jnp.bfloat16), CONTEXT, scatter_dimension=0, tiled=True
        ).astype(jnp.float32),
    )
    grad_query_raw, grad_gain_query = query_pull(grad_query)
    grad_key_raw, grad_gain_key = key_pull(grad_key_local)
    grad_query_low = grad_query_raw.reshape(row_count, local_heads * HEAD_SIZE).astype(jnp.bfloat16)
    grad_key_low = grad_key_raw.astype(jnp.bfloat16)
    grad_value_low = grad_value_local.astype(jnp.bfloat16)
    grad_w_query = matmul_tn(attention_normalized, grad_query_low)
    grad_w_key = matmul_tn(attention_normalized, grad_key_low)
    grad_w_value = matmul_tn(attention_normalized, grad_value_low)
    grad_normed_one = (
        matmul_nt(grad_query_low, full_query)
        + matmul_nt(grad_key_low, full_key)
        + matmul_nt(grad_value_low, full_value)
    )
    grad_normed_one, grad_gain_query, grad_gain_key = (
        lax.psum(grad_normed_one.astype(jnp.bfloat16), TENSOR).astype(jnp.float32),
        lax.psum(grad_gain_query.astype(jnp.bfloat16), TENSOR).astype(jnp.float32),
        lax.psum(grad_gain_key.astype(jnp.bfloat16), TENSOR).astype(jnp.float32),
    )
    grad_inputs_norm, grad_gain_attn = first_pull(grad_normed_one)
    input_grad = grad_resid + grad_inputs_norm
    owned = (
        lax.psum_scatter(
            grad_w_query.astype(jnp.bfloat16), GROUPS, scatter_dimension=0, tiled=True
        ).astype(jnp.float32),
        lax.psum_scatter(
            grad_w_key.astype(jnp.bfloat16), GROUPS, scatter_dimension=0, tiled=True
        ).astype(jnp.float32),
        lax.psum_scatter(
            grad_w_value.astype(jnp.bfloat16), GROUPS, scatter_dimension=0, tiled=True
        ).astype(jnp.float32),
        lax.psum_scatter(
            grad_w_output.astype(jnp.bfloat16), GROUPS, scatter_dimension=0, tiled=True
        ).astype(jnp.float32),
        lax.psum_scatter(
            grad_router.astype(jnp.bfloat16), GROUPS, scatter_dimension=0, tiled=True
        ).astype(jnp.float32),
        lax.psum_scatter(
            grad_gain_attn.astype(jnp.bfloat16),
            GROUPS,
            scatter_dimension=0,
            tiled=True,
        ).astype(jnp.float32),
        lax.psum_scatter(
            grad_gain_ffn.astype(jnp.bfloat16), GROUPS, scatter_dimension=0, tiled=True
        ).astype(jnp.float32),
        lax.psum_scatter(
            grad_gain_query.astype(jnp.bfloat16),
            GROUPS,
            scatter_dimension=0,
            tiled=True,
        ).astype(jnp.float32),
        lax.psum_scatter(
            grad_gain_key.astype(jnp.bfloat16), GROUPS, scatter_dimension=0, tiled=True
        ).astype(jnp.float32),
    )
    return (
        output[None],
        input_grad[None],
        owned[5],
        owned[0],
        owned[1],
        owned[2],
        owned[3],
        owned[7],
        owned[8],
        owned[6],
        owned[4],
        grad_w_gate,
        grad_w_up,
        grad_w_down,
    )


MESH = pl.DeviceIdType.MESH
Z_UP, Z_DOWN, Y_SIDE, X_SIDE, CORE_SIDE = range(5)

def coords():
    z, y, t = lax.axis_index(FSDP), lax.axis_index(CONTEXT), lax.axis_index(TENSOR)
    return z, y, t // 2, t % 2

def partner(z, index):
    return (z, z + 1 - 2 * (z % 2), 2 - z // 2, 3 - 3 * (z // 2))[index]

def greet(neighbours):
    barrier = pltpu.get_barrier_semaphore()
    for condition, device in neighbours:
        def tell(device=device):
            pl.semaphore_signal(barrier, inc=1, device_id=device, device_id_type=MESH)
        if condition is None: tell()
        else: pl.when(condition)(tell)
    count = sum(1 if condition is None else condition.astype(jnp.int32) for condition, device in neighbours)
    pl.semaphore_wait(barrier, count)


def spread(x_ref, out_ref, own_sem, send_sems, recv_sems):
    rows = x_ref.shape[0]; half = rows // 2
    z, y, x, c = coords()
    side = {Z_UP: (z + 1, y, 2 * x + c), Z_DOWN: (z - 1, y, 2 * x + c), Y_SIDE: (z, 1 - y, 2 * x + c),
            X_SIDE: (z, y, 2 * (1 - x) + c), CORE_SIDE: (z, y, 2 * x + 1 - c)}
    def device(zz, yy, xx, cc): return (zz * 2 + yy) * 4 + xx * 2 + cc
    def place(owner, h): return out_ref.at[pl.ds(pl.multiple_of(owner * rows + h * half, half), half)]
    def copy(link, owner, h, own=False):
        src = x_ref.at[pl.ds(h * half, half)] if own else place(owner, h)
        return pltpu.make_async_remote_copy(src_ref=src, dst_ref=place(owner, h), send_sem=send_sems.at[link, owner, h],
            recv_sem=recv_sems.at[owner, h], device_id=side[link], device_id_type=MESH)
    sent = []
    def start(link, owner, h, own=False, condition=None):
        one = copy(link, owner, h, own)
        sent.append((one, condition))
        if condition is None: one.start()
        else: pl.when(condition)(one.start)
    def arrived(owner, h): copy(CORE_SIDE, owner, h).wait_recv()
    me = device(z, y, x, c)
    keep = pltpu.make_async_copy(x_ref, out_ref.at[pl.ds(pl.multiple_of(me * rows, rows), rows)], own_sem)
    keep.start()
    def stage1(i):
        zz = partner(z, i); owner = device(zz, y, x, c); own = i == 0
        if not own:
            arrived(owner, 0); arrived(owner, 1)
        for h in range(2):
            start(Z_UP, owner, h, own, (z < 3) if own else (z < 3) & (zz < z))
            start(Z_DOWN, owner, h, own, (z > 0) if own else (z > 0) & (zz > z))
        start(Y_SIDE, owner, 0, own); start(X_SIDE, owner, 1, own)
        start(Y_SIDE, owner, 1, own); start(X_SIDE, owner, 0, own)
        for h in range(2): start(CORE_SIDE, owner, h, own)
    def stage2(i):
        zz = partner(z, i)
        oy, ox = device(zz, 1 - y, x, c), device(zz, y, 1 - x, c)
        arrived(oy, 0); start(X_SIDE, oy, 0); start(CORE_SIDE, oy, 0)
        arrived(ox, 1); start(Y_SIDE, ox, 1); start(CORE_SIDE, ox, 1)
        arrived(oy, 1); start(CORE_SIDE, oy, 1)
        arrived(ox, 0); start(CORE_SIDE, ox, 0)
    def stage3(i):
        o = device(partner(z, i), 1 - y, 1 - x, c)
        for h in range(2):
            arrived(o, h); start(CORE_SIDE, o, h)
    stage1(0); stage1(1); stage2(0); stage1(2); stage2(1); stage3(0); stage1(3); stage2(2); stage3(1); stage2(3); stage3(2); stage3(3)
    for i in range(4):
        for yy in range(2):
            for xx in range(2):
                for h in range(2): arrived(device(i, yy, xx, 1 - c), h)
    keep.wait()
    for one, condition in sent:
        if condition is None: one.wait_send()
        else: pl.when(condition)(one.wait_send)

def mix_kernel(heads_ref, weight_ref, input_ref, gain_ref, resid_ref, normed_ref, all_ref, part, mine, core_in, line_in, sems, recv, *gather_sems):
    z, y, x, c = coords()
    x_side, core_side = (z, y, 2 * (1 - x) + c), (z, y, 2 * x + 1 - c)
    greet([(z < 3, (z + 1, y, 2 * x + c)), (z > 0, (z - 1, y, 2 * x + c)), (None, (z, 1 - y, 2 * x + c)), (None, x_side), (None, core_side)])
    rows, width = input_ref.shape; f32, bf16 = jnp.float32, jnp.bfloat16
    def remote(src, dst, n, device):
        return pltpu.make_async_remote_copy(src_ref=src, dst_ref=dst, send_sem=sems.at[n], recv_sem=recv.at[n], device_id=device, device_id_type=MESH)
    over_core = [remote(part.at[n, 1 - c], core_in.at[n], n, core_side) for n in range(2)]
    over_x = remote(mine, line_in, 2, x_side)
    for n, xx in enumerate((1 - x, x)):
        heads = heads_ref[pl.ds(pl.multiple_of(xx * 2 * rows, 2 * rows), 2 * rows), :]
        for m in range(width // 512):
            at = pl.ds(m * 512, 512)
            value = lax.dot_general(heads, weight_ref[at, :], (((1,), (1,)), ((), ())), preferred_element_type=f32).astype(bf16)
            part[n, 0, :, at] = value[:rows]
            part[n, 1, :, at] = value[rows:]
        over_core[n].start()
    over_core[0].wait_recv()
    mine[...] = part[0, c] + core_in[0]
    over_x.start(); over_core[1].wait_recv()
    total = input_ref[...].astype(f32) + part[1, c].astype(f32) + core_in[1].astype(f32)
    over_x.wait_recv()
    total = total + line_in[...].astype(f32)
    resid_ref[...] = total
    normed_ref[...] = (total * lax.rsqrt(jnp.mean(total * total, axis=-1, keepdims=True) + EPSILON) * gain_ref[...]).astype(bf16)
    spread(normed_ref, all_ref, *gather_sems)
    for one in (*over_core, over_x): one.wait_send()

def mix_heads(heads, weight, own_input, gain, collective_id):
    rows, width = own_input.shape; D, V = pltpu.SemaphoreType.DMA, pltpu.VMEM; S = jax.ShapeDtypeStruct
    f32, bf16 = jnp.float32, jnp.bfloat16; vspec = pl.BlockSpec(memory_space=V)
    return pl.pallas_call(mix_kernel, out_shape=[S((rows, width), f32), S((rows, width), bf16), S((32 * rows, width), bf16)],
        in_specs=[vspec] * 4, out_specs=[vspec, vspec, pl.BlockSpec(memory_space=pl.ANY)],
        scratch_shapes=[V((2, 2, rows, width), bf16), V((rows, width), bf16), V((2, rows, width), bf16), V((rows, width), bf16), D((3,)), D((3,)),
            D, D((5, 32, 2)), D((32, 2))],
        compiler_params=pltpu.CompilerParams(collective_id=collective_id, has_side_effects=True, vmem_limit_bytes=32 << 20))(heads, weight, own_input, gain)

def groups_kernel(parts, count, *refs):
    ins, outs = refs[:count], refs[count:2 * count]
    keep_sems, send_sems, recv_sems = refs[2 * count:]
    z, y, x, c = coords()
    t = 2 * x + c
    side = {Z_UP: (z + 1, y, t), Z_DOWN: (z - 1, y, t), Y_SIDE: (z, 1 - y, t)}
    greet([(z < 3, side[Z_UP]), (z > 0, side[Z_DOWN]), (None, side[Y_SIDE])])
    sent = []
    def copy(link, p, owner, own=False):
        k, first, size, way = parts[p]
        dst = outs[k].at[pl.ds(pl.multiple_of(owner * ins[k].shape[0] + first, 16), size)]
        return pltpu.make_async_remote_copy(src_ref=ins[k].at[pl.ds(first, size)] if own else dst, dst_ref=dst, send_sem=send_sems.at[link, p, owner],
            recv_sem=recv_sems.at[p, owner], device_id=side[link], device_id_type=MESH)
    def start(link, p, owner, own=False, condition=None):
        one = copy(link, p, owner, own)
        sent.append((one, condition))
        if condition is None: one.start()
        else: pl.when(condition)(one.start)
    def arrived(p, owner): copy(Y_SIDE, p, owner).wait_recv()
    def along(p, owner, zz, own=False):
        start(Z_UP, p, owner, own, (z < 3) & (zz <= z)); start(Z_DOWN, p, owner, own, (z > 0) & (zz >= z))
    kept = []
    for p in range(len(parts)):
        along(p, z * 2 + y, z, True); start(Y_SIDE, p, z * 2 + y, True)
    for k in range(count):
        rows = ins[k].shape[0]
        one = pltpu.make_async_copy(ins[k], outs[k].at[pl.ds(pl.multiple_of((z * 2 + y) * rows, 16), rows)], keep_sems.at[k])
        one.start(); kept.append(one)
    def forward(p, i):
        zz = partner(z, i)
        near, far = zz * 2 + y, zz * 2 + 1 - y
        if i > 0:
            arrived(p, near); along(p, near, zz)
            if parts[p][3] == 0: start(Y_SIDE, p, near)
        if parts[p][3] == 1:
            arrived(p, far); along(p, far, zz)
    for wave in range(len(parts) + 3):
        for i in range(4):
            if 0 <= wave - i < len(parts): forward(wave - i, i)
    for p in range(len(parts)):
        if parts[p][3] == 0:
            for i in range(4): arrived(p, partner(z, i) * 2 + 1 - y)
    for one in kept: one.wait()
    for one, condition in sent:
        if condition is None: one.wait_send()
        else: pl.when(condition)(one.wait_send)

def gather_groups(arrays, parts, collective_id):
    count = len(arrays); D = pltpu.SemaphoreType.DMA
    return pl.pallas_call(functools.partial(groups_kernel, parts, count),
        out_shape=[jax.ShapeDtypeStruct((8 * a.shape[0], a.shape[1]), a.dtype) for a in arrays],
        in_specs=[pl.BlockSpec(memory_space=pl.ANY)] * count, out_specs=[pl.BlockSpec(memory_space=pl.ANY)] * count,
        scratch_shapes=[D((count,)), D((3, len(parts), 8)), D((len(parts), 8))],
        compiler_params=pltpu.CompilerParams(collective_id=collective_id, has_side_effects=True))(*arrays)

class TensorGather:
    def __init__(self, src, out, keep_sem, send_sems, recv_sems):
        self.src, self.out, self.keep_sem, self.send_sems, self.recv_sems = src, out, keep_sem, send_sems, recv_sems
        z, y, x, c = coords()
        self.x_side, self.core_side = (z, y, 2 * (1 - x) + c), (z, y, 2 * x + 1 - c)
        self.me, self.across, self.beside, self.last = 2 * x + c, 2 * (1 - x) + c, 2 * x + 1 - c, 2 * (1 - x) + 1 - c

    @staticmethod
    def scratch():
        D = pltpu.SemaphoreType.DMA
        return [D, D((3,)), D((4,))]

    def copy(self, n, owner, device, own=False):
        return pltpu.make_async_remote_copy(src_ref=self.src if own else self.out.at[owner], dst_ref=self.out.at[owner],
            send_sem=self.send_sems.at[n], recv_sem=self.recv_sems.at[owner], device_id=device, device_id_type=MESH)

    def start(self):
        self.copy(0, self.me, self.x_side, True).start()
        self.copy(1, self.me, self.core_side, True).start()
        self.keep().start()

    def keep(self): return pltpu.make_async_copy(self.src, self.out.at[self.me], self.keep_sem)

    def finish(self):
        self.copy(0, self.across, self.x_side).wait_recv()
        self.copy(2, self.across, self.core_side).start()
        self.copy(0, self.beside, self.x_side).wait_recv()
        self.copy(0, self.last, self.x_side).wait_recv()
        self.keep().wait()
        self.copy(0, self.me, self.x_side, True).wait_send()
        self.copy(1, self.me, self.core_side, True).wait_send()
        self.copy(2, self.across, self.core_side).wait_send()

def rms_pull(grad, values, inverse, gain):
    scaled = grad * gain
    return inverse * scaled - values * (inverse * inverse * inverse * jnp.mean(scaled * values, axis=-1, keepdims=True))

def pull_kernel(grad_ref, weight_ref, input_ref, gain_ref, head_gain_ref, above_ref, out_ref, part, mine, core_in, line_in, message, sems, recv, *gather):
    z, y, x, c = coords()
    x_side, core_side = (z, y, 2 * (1 - x) + c), (z, y, 2 * x + 1 - c)
    greet([(None, x_side), (None, core_side)])
    rows, width = above_ref.shape; f32, bf16 = jnp.float32, jnp.bfloat16
    def remote(src, dst, n, device):
        return pltpu.make_async_remote_copy(src_ref=src, dst_ref=dst, send_sem=sems.at[n], recv_sem=recv.at[n], device_id=device, device_id_type=MESH)
    over_core = [remote(part.at[n, 1 - c], core_in.at[n], n, core_side) for n in range(2)]
    over_x = remote(mine, line_in, 2, x_side)
    message[pl.ds(rows, 16), :] = jnp.zeros((16, width), f32).astype(bf16)
    gain_parts = [0.0] * (width // 512)
    for n, xx in enumerate((1 - x, x)):
        rows_at = pl.ds(pl.multiple_of(xx * 2 * rows, 2 * rows), 2 * rows)
        grad = grad_ref[rows_at, :]
        whole = input_ref[rows_at, :].astype(f32)
        inverse = lax.rsqrt(jnp.mean(whole * whole, axis=-1, keepdims=True) + EPSILON)
        for m in range(width // 512):
            at = pl.ds(m * 512, 512)
            value = lax.dot_general(grad, weight_ref[at, :], (((1,), (1,)), ((), ())), preferred_element_type=f32)
            part[n, 0, :, at] = value[:rows].astype(bf16)
            part[n, 1, :, at] = value[rows:].astype(bf16)
            gain_parts[m] = gain_parts[m] + jnp.sum(value * input_ref[rows_at, at].astype(f32) * inverse, axis=0, keepdims=True)
        over_core[n].start()
    first_row = lax.broadcasted_iota(jnp.int32, (16, 512), 0)
    for m in range(width // 512):
        message[pl.ds(rows, 16), pl.ds(m * 512, 512)] = jnp.where(first_row == 0, gain_parts[m], 0.0).astype(bf16)
    first_row = lax.broadcasted_iota(jnp.int32, (16, 128), 0)
    for n in range(2):
        at = (pl.ds(rows, 16), pl.ds(n * 128, 128))
        message[at] = jnp.where(first_row == 1, head_gain_ref[pl.ds(n, 1), :], message[at].astype(f32)).astype(bf16)
    over_core[0].wait_recv()
    mine[...] = part[0, c] + core_in[0]
    over_x.start(); over_core[1].wait_recv()
    own_at = pl.ds(pl.multiple_of((2 * x + c) * rows, rows), rows)
    own = input_ref[own_at, :].astype(f32)
    inverse = lax.rsqrt(jnp.mean(own * own, axis=-1, keepdims=True) + EPSILON)
    total = part[1, c].astype(f32) + core_in[1].astype(f32)
    over_x.wait_recv()
    total = total + line_in[...].astype(f32)
    message[pl.ds(0, rows), :] = (above_ref[...] + rms_pull(total, own, inverse, gain_ref[...])).astype(bf16)
    gather = TensorGather(message, out_ref, *gather)
    gather.start(); gather.finish()
    for one in (*over_core, over_x): one.wait_send()

def pull_inputs(grad, weight, inputs, gain, head_gain_grads, above, collective_id):
    rows, width = above.shape; D, V = pltpu.SemaphoreType.DMA, pltpu.VMEM
    bf16 = jnp.bfloat16; vspec = pl.BlockSpec(memory_space=V)
    return pl.pallas_call(pull_kernel, out_shape=jax.ShapeDtypeStruct((4, rows + 16, width), bf16),
        in_specs=[vspec] * 6, out_specs=pl.BlockSpec(memory_space=pl.ANY),
        scratch_shapes=[V((2, 2, rows, width), bf16), V((rows, width), bf16), V((2, rows, width), bf16), V((rows, width), bf16), V((rows + 16, width), bf16),
            D((3,)), D((3,)), *TensorGather.scratch()],
        compiler_params=pltpu.CompilerParams(collective_id=collective_id, has_side_effects=True, vmem_limit_bytes=40 << 20))(
            grad, weight, inputs, gain, head_gain_grads, above)


def nt(a, b):
    return lax.dot_general(a, b, (((1,), (1,)), ((), ())), preferred_element_type=jnp.float32)

def nn(a, b):
    return jnp.dot(a, b, preferred_element_type=jnp.float32)

def nearest(z, index):
    choice = [partner(z, n) for n in range(4)]
    return jnp.where(index == 0, choice[0], jnp.where(index == 1, choice[1], jnp.where(index == 2, choice[2], choice[3])))

def spot(zz, yy, xx): return (zz * 2 + yy) * 2 + xx

def step_target(step):
    z, y, x, c = coords()
    n = step % 4
    return nearest(z, 3 - step // 4), jnp.where(n < 2, 1 - y, y), jnp.where(n % 2 == 0, 1 - x, x)

def step_block(ref, step):
    size = ref.shape[0] // 16
    return ref.at[pl.ds(pl.multiple_of(spot(*step_target(step)) * size, size), size)]

class Reduction:
    def __init__(self, part, mine, first_in, second_in, line_in, core_sem, first_sem, second_sem, line_send, line_recv):
        self.part, self.mine, self.first_in, self.second_in, self.line_in = part, mine, first_in, second_in, line_in
        self.core_sem, self.first_sem, self.second_sem, self.line_send, self.line_recv = core_sem, first_sem, second_sem, line_send, line_recv
        self.half = part.shape[2] // 2
        z, y, x, c = self.at = coords()
        self.up, self.down = (z + 1, y, 2 * x + c), (z - 1, y, 2 * x + c)
        self.y_side, self.x_side, self.core_side = (z, 1 - y, 2 * x + c), (z, y, 2 * (1 - x) + c), (z, y, 2 * x + 1 - c)

    @staticmethod
    def scratch(rows, width, dtype):
        V, D, half = pltpu.VMEM, pltpu.SemaphoreType.DMA, rows // 2
        return [V((2, 2, rows, width), dtype), V((16, rows, width), dtype), V((2, 8, half, width), dtype),
            V((2, 4, half, width), dtype), V((2, 4, 2, half, width), dtype), D((2, 16)), D((2, 2, 8)), D((2, 2, 4)), D((4, 2)), D((2, 4, 2))]

    def greet(self):
        z = self.at[0]
        greet([(z < 3, self.up), (z > 0, self.down), (None, self.y_side), (None, self.x_side), (None, self.core_side)])

    @staticmethod
    def remote(src, dst, send, recv, device):
        return pltpu.make_async_remote_copy(src_ref=src, dst_ref=dst, send_sem=send, recv_sem=recv, device_id=device, device_id_type=MESH)

    def over_core(self, step):
        s = spot(*step_target(step))
        return self.remote(self.part.at[step % 2, 1 - self.at[3]], self.mine.at[s], self.core_sem.at[0, s], self.core_sem.at[1, s], self.core_side)

    def piece(self, zz, yy, xx, h): return self.mine.at[spot(zz, yy, xx), pl.ds(h * self.half, self.half)]

    def first(self, h, zz, other):
        z, y, x, c = self.at
        src = self.piece(zz, other, 1 - x, 0) if h == 0 else self.piece(zz, 1 - y, other, 1)
        s = zz * 2 + other
        return self.remote(src, self.first_in.at[h, s], self.first_sem.at[0, h, s], self.first_sem.at[1, h, s], self.x_side if h == 0 else self.y_side)

    def second(self, h, zz):
        z, y, x, c = self.at
        src = self.piece(zz, 1 - y, x, 0) if h == 0 else self.piece(zz, y, 1 - x, 1)
        return self.remote(src, self.second_in.at[h, zz], self.second_sem.at[0, h, zz], self.second_sem.at[1, h, zz], self.y_side if h == 0 else self.x_side)

    def line(self, h, zz, way):
        z, y, x, c = self.at
        return self.remote(self.piece(zz, y, x, h), self.line_in.at[way, zz, h], self.line_send.at[zz, h], self.line_recv.at[way, zz, h], self.up if way == 0 else self.down)

    def add(self, s, h, arrived):
        at = (s, pl.ds(h * self.half, self.half))
        self.mine[at] = self.mine[at] + arrived[...]

    def stage_core(self, step):
        zz, yy, xx = step_target(step)
        s = spot(zz, yy, xx)
        self.over_core(step).wait_recv()
        self.mine[s] += self.part[step % 2, self.at[3]]
        n = step % 4
        @pl.when(n % 2 == 0)
        def _(): self.first(0, zz, yy).start()
        @pl.when(n < 2)
        def _(): self.first(1, zz, xx).start()

    def stage_first(self, i):
        z, y, x, c = self.at
        zz = nearest(z, i)
        for n in range(2):
            for h, other in ((0, (1 - y, y)[n]), (1, (1 - x, x)[n])):
                self.first(h, zz, other).wait_recv()
                self.add(spot(zz, other, x) if h == 0 else spot(zz, y, other), h, self.first_in.at[h, zz * 2 + other])
                if n == 0: self.second(h, zz).start()

    def stage_second(self, i):
        z, y, x, c = self.at
        zz = nearest(z, i)
        for h in range(2):
            self.second(h, zz).wait_recv()
            self.add(spot(zz, y, x), h, self.second_in.at[h, zz])

    def stage_line(self, i):
        z, y, x, c = self.at
        zz = nearest(z, i)
        for h in range(2):
            for way, from_side, toward in ((0, z > 0, zz > z), (1, z < 3, zz < z)):
                @pl.when(from_side & (toward | (zz == z)))
                def _(h=h, way=way):
                    self.line(h, zz, way).wait_recv()
                    self.add(spot(zz, y, x), h, self.line_in.at[way, zz, h])
                @pl.when(toward)
                def _(h=h, way=way): self.line(h, zz, way).start()

    def follow(self, step):
        @pl.when((step >= 1) & (step <= 16))
        def _(): self.stage_core(step - 1)
        q = step // 4
        @pl.when((step % 4 == 1) & (q >= 2))
        def _(): self.stage_line(5 - q)
        @pl.when((step % 4 == 1) & (q >= 1))
        def _(): self.stage_first(4 - q)
        @pl.when((step % 4 == 3) & (q >= 1))
        def _(): self.stage_second(4 - q)

    def finish(self, steps):
        z, y, x, c = self.at
        if steps == 16:
            self.stage_core(15); self.stage_line(1); self.stage_first(0); self.stage_second(0)
        self.stage_line(0)

    @property
    def own(self): return spot(*self.at[:3])

    def drain(self):
        z, y, x, c = self.at
        self.over_core(14).wait_send(); self.over_core(15).wait_send()
        for zz in range(4):
            for other in range(2):
                for h in range(2): self.first(h, zz, other).wait_send()
            for h in range(2): self.second(h, zz).wait_send()
            @pl.when(zz != z)
            def _(zz=zz):
                for h in range(2): self.line(h, zz, 0).wait_send()

def expert_kernel(normed_ref, cot_ref, code_ref, router_ref, expand_ref, place_ref, gate_ref, up_ref, down_ref,
                  resid_ref, own_normed_ref, own_chosen_ref, own_cot_ref, gain_ref,
                  grad_ref, message_ref, hid_out, gate_out, up_out, normed_in, cot_in, code_in, units, message, in_sem, units_sem, *scratch):
    reduction = Reduction(*scratch[:-3])
    gather = TensorGather(message, message_ref, *scratch[-3:])
    reduction.greet()
    part = reduction.part
    rows, width, wide = grad_ref.shape[0], normed_ref.shape[1], gate_ref.shape[1]
    f32, bf16 = jnp.float32, jnp.bfloat16
    stride = code_ref.shape[0] // 8
    def loads(step):
        slot = step % 2
        zz, yy, xx = step_target(step)
        codes = code_ref.at[pl.ds(pl.multiple_of((zz * 2 + yy) * stride, 16), rows)]
        pairs = ((step_block(normed_ref, step), normed_in), (step_block(cot_ref, step), cot_in), (codes, code_in))
        return [pltpu.make_async_copy(src, dst.at[slot], in_sem.at[n, slot]) for n, (src, dst) in enumerate(pairs)]
    def stores(step):
        slot = step % 2
        return [pltpu.make_async_copy(units.at[slot, n], step_block(dst, step), units_sem.at[n, slot])
                for n, dst in enumerate((hid_out, gate_out, up_out))]
    for one in loads(0): one.start()

    def compute(step):
        slot = step % 2
        for one in loads(step): one.wait()
        @pl.when(step < 15)
        def _():
            for one in loads(step + 1): one.start()
        @pl.when(step >= 2)
        def _():
            for one in stores(step - 2): one.wait()
            reduction.over_core(step - 2).wait_send()
        normed, cot = normed_in[slot], cot_in[slot]
        code = code_in[slot].astype(f32)
        quarter = lax.broadcasted_iota(jnp.int32, code.shape, 1) // (128 // 4) - 2 * step_target(step)[2]
        code = jnp.concatenate([jnp.where(quarter == n, code, 0.0) for n in range(2)], axis=0)
        scores = jnp.where(code > 0.5, nn(normed, router_ref[...]), NEGATIVE)
        scores = jnp.where(code > 0.5, jnp.exp(scores - jnp.max(scores, axis=1, keepdims=True)), 0.0)
        gates = jnp.where(code > 1.5, scores / jnp.sum(scores, axis=1, keepdims=True), 0.0)
        high = gates.astype(bf16)
        low = (gates - high.astype(f32)).astype(bf16)
        grad_gates = jnp.zeros((2 * rows, 128), f32)
        def products(n):
            at = pl.ds(n * 256, 256)
            return (nn(normed, gate_ref[:, at]), nn(normed, up_ref[:, at]), nt(cot, down_ref[at, :]),
                nn(high, expand_ref[:, at]) + nn(low, expand_ref[:, at]))
        ahead = products(0)
        for n in range(wide // 256):
            gate_in, up_in, grad_mid, gate = ahead
            if n + 1 < wide // 256: ahead = products(n + 1)
            at = pl.ds(n * 256, 256)
            sig = lax.logistic(gate_in)
            silu = gate_in * sig
            hidden = silu * up_in
            grad_gates += nn(jnp.where(gate != 0.0, hidden * grad_mid, 0.0).astype(bf16), place_ref[at, :])
            grad_hidden = grad_mid * gate
            units[slot, 0, :, at] = (hidden * gate).astype(bf16)
            units[slot, 1, :, at] = (grad_hidden * up_in * (sig + silu * (1.0 - sig))).astype(bf16)
            units[slot, 2, :, at] = (grad_hidden * silu).astype(bf16)
        for one in stores(step): one.start()
        gate_grad, up_grad = units[slot, 1], units[slot, 2]
        for n in range(width // 512):
            at = pl.ds(n * 512, 512)
            grad = (nt(gate_grad, gate_ref[at, :]) + nt(up_grad, up_ref[at, :])).astype(bf16)
            part[slot, 0, :, at] = grad[:rows]
            part[slot, 1, :, at] = grad[rows:]
        grad_gates = grad_gates.astype(bf16)
        part[slot, 0, :, pl.ds(width, 128)] = grad_gates[:rows]
        part[slot, 1, :, pl.ds(width, 128)] = grad_gates[rows:]
        reduction.over_core(step).start()

    @pl.loop(0, 16)
    def _(step):
        compute(step)
        reduction.follow(step)
    for step in (14, 15):
        for one in stores(step): one.wait()
    reduction.finish(16)
    every, own = pl.ds(0, width), reduction.own
    grad_gates = reduction.mine[own, :, pl.ds(width, 128)].astype(f32)
    grad_gates = grad_gates + pltpu.roll(grad_gates, 64, 1)
    grad_gates = grad_gates + pltpu.roll(grad_gates, 32, 1)
    chosen = own_chosen_ref[...].astype(f32) > 0.5
    scores = jnp.where(chosen, nn(own_normed_ref[...], router_ref[...]), NEGATIVE)
    scores = jnp.where(chosen, jnp.exp(scores - jnp.max(scores, axis=1, keepdims=True)), 0.0)
    gates = scores / jnp.sum(scores, axis=1, keepdims=True)
    grad_logits = (gates * (grad_gates - jnp.sum(gates * grad_gates, axis=1, keepdims=True))).astype(bf16)
    grad = reduction.mine[own, :, every].astype(f32) + nt(grad_logits, router_ref[...])
    values = resid_ref[...]
    inverse = lax.rsqrt(jnp.mean(values * values, axis=-1, keepdims=True) + EPSILON)
    total = own_cot_ref[...].astype(f32) + rms_pull(grad, values, inverse, gain_ref[...])
    grad_ref[...] = total
    message[pl.ds(0, rows), every] = total.astype(bf16)
    message[pl.ds(0, rows), pl.ds(width, 128)] = grad_logits
    first_row = lax.broadcasted_iota(jnp.int32, (16, width), 0)
    message[pl.ds(rows, 16), every] = jnp.where(first_row == 0, jnp.sum(grad * values * inverse, axis=0, keepdims=True), 0.0).astype(bf16)
    message[pl.ds(rows, 16), pl.ds(width, 128)] = jnp.zeros((16, 128), f32).astype(bf16)
    gather.start(); gather.finish()
    reduction.drain()

def run_experts(normed_all, cot_all, codes, router, expand, place, gate_flat, up_flat, down_flat,
                resid, own_normed, own_chosen, own_cot, gain, collective_id):
    total, width = normed_all.shape; rows = total // 32; wide = gate_flat.shape[1]
    bf16 = jnp.bfloat16; D = pltpu.SemaphoreType.DMA; V = pltpu.VMEM; W = width + 128
    anyspec, vspec = pl.BlockSpec(memory_space=pl.ANY), pl.BlockSpec(memory_space=V)
    unit = jax.ShapeDtypeStruct((total, wide), bf16)
    return pl.pallas_call(expert_kernel,
        out_shape=[jax.ShapeDtypeStruct((rows, width), jnp.float32), jax.ShapeDtypeStruct((4, rows + 16, W), bf16), unit, unit, unit],
        in_specs=[anyspec] * 3 + [vspec] * 11, out_specs=[vspec] + [anyspec] * 4,
        scratch_shapes=[V((2, 2 * rows, width), bf16), V((2, 2 * rows, width), bf16), V((2, rows, 128), bf16),
            V((2, 3, 2 * rows, wide), bf16), V((rows + 16, W), bf16), D((3, 2)), D((3, 2)),
            *Reduction.scratch(rows, W, bf16), *TensorGather.scratch()],
        compiler_params=pltpu.CompilerParams(collective_id=collective_id, has_side_effects=True, vmem_limit_bytes=60 << 20))(
            normed_all, cot_all, codes, router, expand, place, gate_flat, up_flat, down_flat, resid, own_normed, own_chosen, own_cot, gain)

def output_kernel(normed_ref, cot_ref, hid_ref, gate_ref, up_ref, down_ref, resid_ref, out_ref, gate_out, up_out, down_out,
                  hid_in, wide_in, thin_in, own_out, hid_sem, in_sem, out_sem, *scratch):
    reduction = Reduction(*scratch[:-3])
    gather = TensorGather(own_out, out_ref, *scratch[-3:])
    reduction.greet()
    part = reduction.part
    rows, width, units = resid_ref.shape[0], normed_ref.shape[1], hid_ref.shape[1]
    f32, bf16 = jnp.float32, jnp.bfloat16
    lag = 2
    def hid_load(step): return pltpu.make_async_copy(step_block(hid_ref, step), hid_in.at[step % 2], hid_sem.at[step % 2])
    def loads(block):
        slot = block % 2
        zz, yy, xx = step_target(2 * block)
        at = pl.ds(pl.multiple_of((zz * 2 + yy) * 4 * rows, 4 * rows), 4 * rows)
        return ([pltpu.make_async_copy(src.at[at], wide_in.at[slot, n], in_sem.at[n, slot]) for n, src in enumerate((normed_ref, cot_ref))]
            + [pltpu.make_async_copy(src.at[at], thin_in.at[slot, n], in_sem.at[2 + n, slot]) for n, src in enumerate((hid_ref, gate_ref, up_ref))])
    for one in loads(0): one.start()
    hid_load(0).start()

    def inner(gate_sum, up_sum, down_sum):
        gate_sum[...] = jnp.zeros_like(gate_sum)
        up_sum[...] = jnp.zeros_like(up_sum)
        down_sum[...] = jnp.zeros_like(down_sum)

        def outputs(step):
            slot = step % 2
            hid_load(step).wait()
            @pl.when(step < 15)
            def _(): hid_load(step + 1).start()
            @pl.when(step >= 2)
            def _(): reduction.over_core(step - 2).wait_send()
            hid = hid_in[slot]
            for n in range(width // 512):
                at = pl.ds(n * 512, 512)
                value = nn(hid, down_ref[:, at]).astype(bf16)
                part[slot, 0, :, at] = value[:rows]
                part[slot, 1, :, at] = value[rows:]
            reduction.over_core(step).start()

        def down_gradient(block):
            slot = block % 2
            for one in loads(block): one.wait()
            @pl.when(block < 7)
            def _():
                for one in loads(block + 1): one.start()
            for n in range(units // 256):
                at = pl.ds(n * 256, 256)
                down_sum[at, :] += nn(thin_in[slot, 0, :, at].T, wide_in[slot, 1])

        def gate_gradients(block):
            slot = block % 2
            for n in range(width // 256):
                at = pl.ds(n * 256, 256)
                turned = wide_in[slot, 0, :, at].T
                gate_sum[at, :] += nn(turned, thin_in[slot, 1])
                up_sum[at, :] += nn(turned, thin_in[slot, 2])

        @pl.loop(0, 8 + lag)
        def _(block):
            for n, gradients in enumerate((down_gradient, gate_gradients)):
                step = 2 * block + n
                @pl.when(block < 8)
                def _(): outputs(step)
                @pl.when(block >= lag)
                def _(): gradients(block - lag)
                reduction.follow(step)
        kept = [pltpu.make_async_copy(src, dst, out_sem.at[n])
                for n, (src, dst) in enumerate(((gate_sum, gate_out), (up_sum, up_out), (down_sum, down_out)))]
        for one in kept: one.start()
        reduction.finish(16 + 2 * lag)
        own_out[...] = (resid_ref[...] + reduction.mine[reduction.own].astype(f32)).astype(bf16)
        gather.start(); gather.finish()
        reduction.drain()
        for one in kept: one.wait()
    pl.run_scoped(inner, pltpu.VMEM((width, units), f32), pltpu.VMEM((width, units), f32), pltpu.VMEM((units, width), f32))

def run_outputs(normed_all, cot_all, hidden_gated, gate_grad, up_grad, down_flat, resid, collective_id):
    total, width = normed_all.shape; rows = total // 32; units = hidden_gated.shape[1]
    f32, bf16 = jnp.float32, jnp.bfloat16; D = pltpu.SemaphoreType.DMA; V = pltpu.VMEM; S = jax.ShapeDtypeStruct
    anyspec, vspec = pl.BlockSpec(memory_space=pl.ANY), pl.BlockSpec(memory_space=V)
    return pl.pallas_call(output_kernel,
        out_shape=[S((4, rows, width), bf16), S((width, units), f32), S((width, units), f32), S((units, width), f32)],
        in_specs=[anyspec] * 5 + [vspec] * 2, out_specs=[anyspec] * 4,
        scratch_shapes=[V((2, 2 * rows, units), bf16), V((2, 2, 4 * rows, width), bf16), V((2, 3, 4 * rows, units), bf16), V((rows, width), bf16), D((2,)), D((5, 2)), D((3,)),
            *Reduction.scratch(rows, width, bf16), *TensorGather.scratch()],
        compiler_params=pltpu.CompilerParams(collective_id=collective_id, has_side_effects=True, vmem_limit_bytes=62 << 20))(
            normed_all, cot_all, hidden_gated, gate_grad, up_grad, down_flat, resid)


def inverse_rms(values):
    return lax.rsqrt(jnp.mean(values * values, axis=-1, keepdims=True) + EPSILON)

def attend_kernel(x_ref, gain_ref, qkv_ref, cos_ref, sin_ref, head_gain_ref, seg_rows_ref, seg_cols_ref,
                  normed_ref, raw_ref, q_ref, kv_ref, kv_other_ref, full_ref, heads_ref, lse_ref, bias, send_sem, recv_sem):
    z, y, x, c = coords()
    other = (z, 1 - y, 2 * x + c)
    greet([(None, other)])
    f32, bf16 = jnp.float32, jnp.bfloat16
    rows = x_ref.shape[0]; heads = q_ref.shape[1] // HEAD_SIZE; q_width = heads * HEAD_SIZE
    values = x_ref[...].astype(f32)
    normed_ref[...] = (values * inverse_rms(values) * gain_ref[...]).astype(bf16)
    def finish(raw, n):
        normed = raw * inverse_rms(raw) * head_gain_ref[pl.ds(n, 1), :]
        return (normed * cos_ref[...] + pltpu.roll(normed, HEAD_SIZE // 2, 1) * sin_ref[...]).astype(bf16)
    raw_kv = nn(normed_ref[...], qkv_ref[:, pl.ds(q_width, 2 * HEAD_SIZE)])
    raw_ref[:, pl.ds(q_width, HEAD_SIZE)] = raw_kv[:, :HEAD_SIZE]
    kv_ref[:, pl.ds(0, HEAD_SIZE)] = finish(raw_kv[:, :HEAD_SIZE], 1)
    kv_ref[:, pl.ds(HEAD_SIZE, HEAD_SIZE)] = raw_kv[:, HEAD_SIZE:].astype(bf16)
    move = pltpu.make_async_remote_copy(src_ref=kv_ref, dst_ref=kv_other_ref, send_sem=send_sem, recv_sem=recv_sem,
        device_id=other, device_id_type=MESH)
    @pl.when(y == 0)
    def _():
        move.start()
        kv_other_ref[...] = jnp.zeros_like(kv_other_ref)
    @pl.loop(0, heads // 2)
    def _(n):
        at = pl.ds(pl.multiple_of(n * 2 * HEAD_SIZE, 2 * HEAD_SIZE), 2 * HEAD_SIZE)
        raw = nn(normed_ref[...], qkv_ref[:, at])
        raw_ref[:, at] = raw
        for m in range(2):
            one = pl.ds(pl.multiple_of((2 * n + m) * HEAD_SIZE, HEAD_SIZE), HEAD_SIZE)
            q_ref[:, one] = finish(raw[:, m * HEAD_SIZE:(m + 1) * HEAD_SIZE], 0)
    row_id = lax.broadcasted_iota(jnp.int32, (rows, rows), 0)
    col_id = lax.broadcasted_iota(jnp.int32, (rows, rows), 1)
    bias[0] = jnp.where((seg_rows_ref[...] == seg_cols_ref[pl.ds(0, 1), :]) & (col_id <= row_id), 0.0, NEGATIVE)
    bias[1] = jnp.where(seg_rows_ref[...] == seg_cols_ref[pl.ds(1, 1), :], 0.0, NEGATIVE)
    lse_ref[...] = jnp.zeros_like(lse_ref)
    scale = HEAD_SIZE ** -0.5
    lane = lax.broadcasted_iota(jnp.int32, (rows, HEAD_SIZE), 1)
    def head(h, blocks):
        at = pl.ds(pl.multiple_of(h * HEAD_SIZE, HEAD_SIZE), HEAD_SIZE)
        query = q_ref[:, at]
        refs = (kv_ref, kv_other_ref)[:blocks]
        scores = [nt(query, ref[:, pl.ds(0, HEAD_SIZE)]) * scale + bias[n] for n, ref in enumerate(refs)]
        top = functools.reduce(jnp.maximum, [jnp.max(s, axis=1, keepdims=True) for s in scores])
        weights = [jnp.exp(s - top) for s in scores]
        total = sum(jnp.sum(w, axis=1, keepdims=True) for w in weights)
        inverse = 1.0 / total
        full = sum(nn((w * inverse).astype(bf16), ref[:, pl.ds(HEAD_SIZE, HEAD_SIZE)]) for w, ref in zip(weights, refs))
        full_ref[:, at] = full
        heads_ref[:, at] = full.astype(bf16)
        lse_ref[...] = jnp.where(lane == h, top + jnp.log(total), lse_ref[...])
    @pl.when(y == 0)
    def _():
        @pl.loop(0, heads)
        def _(h): head(h, 1)
        move.wait_send()
    @pl.when(y == 1)
    def _():
        move.wait_recv()
        @pl.loop(0, heads)
        def _(h): head(h, 2)

def attend(x, gain, qkv, cos, sin, head_gains, seg_rows, seg_cols, collective_id):
    rows, width = x.shape; q_width = qkv.shape[1] - 2 * HEAD_SIZE
    V = pltpu.VMEM; f32, bf16 = jnp.float32, jnp.bfloat16; S = jax.ShapeDtypeStruct
    vspec = pl.BlockSpec(memory_space=V)
    return pl.pallas_call(attend_kernel,
        out_shape=[S((rows, width), bf16), S((rows, q_width + HEAD_SIZE), f32), S((rows, q_width), bf16), S((rows, 2 * HEAD_SIZE), bf16),
            S((rows, 2 * HEAD_SIZE), bf16), S((rows, q_width), f32), S((rows, q_width), bf16), S((rows, HEAD_SIZE), f32)],
        in_specs=[vspec] * 8, out_specs=[vspec] * 8,
        scratch_shapes=[V((2, rows, rows), f32), pltpu.SemaphoreType.DMA, pltpu.SemaphoreType.DMA],
        compiler_params=pltpu.CompilerParams(collective_id=collective_id, has_side_effects=True, vmem_limit_bytes=48 << 20))(
            x, gain, qkv, cos, sin, head_gains, seg_rows, seg_cols)

def attend_back_kernel(cot_ref, out_w_ref, q_ref, kv_ref, kv_other_ref, raw_ref, full_ref, lse_ref, cos_ref, sin_ref, head_gain_ref,
                       seg_rows_ref, seg_cols_ref, grad_ref, gains_ref, grad_heads, delta, stats, bias, grad_q, grad_kv, kv_send, kv_in, send_sem, recv_sem):
    z, y, x, c = coords()
    other = (z, 1 - y, 2 * x + c)
    greet([(None, other)])
    f32, bf16 = jnp.float32, jnp.bfloat16
    rows = q_ref.shape[0]; heads = q_ref.shape[1] // HEAD_SIZE; q_width = heads * HEAD_SIZE
    scale = HEAD_SIZE ** -0.5
    lane = lax.broadcasted_iota(jnp.int32, (rows, HEAD_SIZE), 1)
    delta[...] = jnp.zeros_like(delta)
    @pl.loop(0, heads // 2)
    def _(n):
        at = pl.ds(pl.multiple_of(n * 2 * HEAD_SIZE, 2 * HEAD_SIZE), 2 * HEAD_SIZE)
        grad = nn(cot_ref[...], out_w_ref[:, at]).astype(bf16)
        grad_heads[:, at] = grad
        product = grad.astype(f32) * full_ref[:, at]
        for m in range(2):
            one = jnp.sum(product[:, m * HEAD_SIZE:(m + 1) * HEAD_SIZE], axis=1, keepdims=True)
            delta[...] = jnp.where(lane == 2 * n + m, one, delta[...])
    stats[0] = lse_ref[...].T
    stats[1] = delta[...].T
    key_id = lax.broadcasted_iota(jnp.int32, (rows, rows), 0)
    query_id = lax.broadcasted_iota(jnp.int32, (rows, rows), 1)
    def block(ref, seg_keys, causal):
        same = seg_keys == seg_cols_ref[pl.ds(0, 1), :]
        bias[...] = jnp.where(same & (key_id <= query_id) if causal else same, 0.0, NEGATIVE)
        grad_kv[...] = jnp.zeros_like(grad_kv)
        key, value = ref[:, pl.ds(0, HEAD_SIZE)], ref[:, pl.ds(HEAD_SIZE, HEAD_SIZE)]
        @pl.loop(0, heads)
        def _(h):
            at = pl.ds(pl.multiple_of(h * HEAD_SIZE, HEAD_SIZE), HEAD_SIZE)
            query, grad = q_ref[:, at], grad_heads[:, at]
            probs = jnp.exp(nt(key, query) * scale + bias[...] - stats[0, pl.ds(h, 1), :])
            grad_scores = (probs * (nt(value, grad) - stats[1, pl.ds(h, 1), :])).astype(bf16)
            grad_kv[:, pl.ds(0, HEAD_SIZE)] += nn(grad_scores, query) * scale
            grad_kv[:, pl.ds(HEAD_SIZE, HEAD_SIZE)] += nn(probs.astype(bf16), grad)
            grad_q[:, at] += lax.dot_general(grad_scores, key, (((0,), (0,)), ((), ())), preferred_element_type=f32) * scale
    grad_q[...] = jnp.zeros_like(grad_q)
    move = pltpu.make_async_remote_copy(src_ref=kv_send, dst_ref=kv_in, send_sem=send_sem, recv_sem=recv_sem, device_id=other, device_id_type=MESH)
    @pl.when(y == 1)
    def _():
        block(kv_other_ref, seg_rows_ref[1], False)
        kv_send[...] = grad_kv[...].astype(bf16)
        move.start()
    block(kv_ref, seg_rows_ref[0], True)
    @pl.when(y == 0)
    def _():
        move.wait_recv()
        grad_kv[...] += kv_in[...].astype(f32)
    def pull(grad, raw, n):
        turned = grad * cos_ref[...] - pltpu.roll(grad, HEAD_SIZE // 2, 1) * sin_ref[...]
        inverse = inverse_rms(raw)
        unit = raw * inverse
        gains_ref[pl.ds(n, 1), :] += jnp.sum(turned * unit, axis=0, keepdims=True)
        scaled = turned * head_gain_ref[pl.ds(n, 1), :]
        return (inverse * (scaled - unit * jnp.mean(scaled * unit, axis=1, keepdims=True))).astype(bf16)
    gains_ref[...] = jnp.zeros_like(gains_ref)
    @pl.loop(0, heads)
    def _(h):
        at = pl.ds(pl.multiple_of(h * HEAD_SIZE, HEAD_SIZE), HEAD_SIZE)
        grad_ref[:, at] = pull(grad_q[:, at], raw_ref[:, at], 0)
    at = pl.ds(q_width, HEAD_SIZE)
    grad_ref[:, at] = pull(grad_kv[:, pl.ds(0, HEAD_SIZE)], raw_ref[:, at], 1)
    grad_ref[:, pl.ds(q_width + HEAD_SIZE, HEAD_SIZE)] = grad_kv[:, pl.ds(HEAD_SIZE, HEAD_SIZE)].astype(bf16)
    @pl.when(y == 1)
    def _(): move.wait_send()

def attend_back(cot, out_w, q, kv, kv_other, raw, full, lse, cos, sin, head_gains, seg_rows, seg_cols, collective_id):
    rows, q_width = q.shape
    V = pltpu.VMEM; f32, bf16 = jnp.float32, jnp.bfloat16; S = jax.ShapeDtypeStruct
    vspec = pl.BlockSpec(memory_space=V)
    return pl.pallas_call(attend_back_kernel,
        out_shape=[S((rows, q_width + 2 * HEAD_SIZE), bf16), S((8, HEAD_SIZE), f32)],
        in_specs=[vspec] * 13, out_specs=[vspec] * 2,
        scratch_shapes=[V((rows, q_width), bf16), V((rows, HEAD_SIZE), f32), V((2, HEAD_SIZE, rows), f32), V((rows, rows), f32), V((rows, q_width), f32),
            V((rows, 2 * HEAD_SIZE), f32), V((rows, 2 * HEAD_SIZE), bf16), V((rows, 2 * HEAD_SIZE), bf16), pltpu.SemaphoreType.DMA, pltpu.SemaphoreType.DMA],
        compiler_params=pltpu.CompilerParams(collective_id=collective_id, has_side_effects=True, vmem_limit_bytes=48 << 20))(
            cot, out_w, q, kv, kv_other, raw, full, lse, cos, sin, head_gains, seg_rows, seg_cols)


def gathered_local(
    hidden_in,
    attn_gain,
    w_query,
    key_weight,
    value_weight,
    w_output,
    query_gain,
    key_gain,
    ffn_gain,
    router,
    gate_weight,
    up_weight,
    down_weight,
    routes,
    segments,
    cotangent,
):
    bf16, f32 = jnp.bfloat16, jnp.float32
    context_size = lax.axis_size(CONTEXT)
    tensor_size = lax.axis_size(TENSOR)
    group_count = lax.axis_size(FSDP) * context_size
    fsdp_rank = lax.axis_index(FSDP)
    context_rank = lax.axis_index(CONTEXT)
    tensor_rank = lax.axis_index(TENSOR)
    group_rank = fsdp_rank * context_size + context_rank
    row_count, width = hidden_in.shape[1:]
    own_count = row_count // tensor_size
    own_start = tensor_rank * own_count
    local_experts, _, hidden_width = gate_weight.shape
    experts_total = router.shape[1]
    first_expert = group_rank * local_experts
    capacity = 9 * row_count * TOPK // (8 * experts_total)
    query_width = w_query.shape[1]

    expert_ids = jnp.arange(experts_total, dtype=jnp.int32)
    chosen = jnp.any(routes[0][..., None] == expert_ids, axis=1)
    kept = chosen & (earlier_counts(chosen) < capacity)
    code = chosen.astype(bf16) + kept.astype(bf16)
    chosen_own = lax.dynamic_slice_in_dim(chosen, own_start, own_count, 0)
    code = code.reshape(tensor_size, own_count, experts_total).transpose(1, 0, 2)

    pieces = (code, router, attn_gain, ffn_gain, query_gain, key_gain, segments)
    small = jnp.concatenate([piece.astype(bf16).reshape(-1) for piece in pieces])
    small = jnp.pad(small, (0, -small.size % 2048)).reshape(-1, 128)
    qkv_weight = jnp.concatenate([w_query, key_weight, value_weight], axis=1)
    pieces_of = [(0, 0, small.shape[0], 0)]
    for array in (1, 2):
        pieces_of += [(array, 0, 112, 0), (array, 112, 96, 0), (array, 208, 48, 1)]
    small, qkv_full, full_output = gather_groups((small, qkv_weight, w_output), tuple(pieces_of), 1)
    grad_out_own = lax.dynamic_slice_in_dim(cotangent[0], own_start, own_count, 0)
    grad_out_own, codes = lax.optimization_barrier((grad_out_own, small))
    grad_out_all = lax.all_gather(grad_out_own, EVERYONE, axis=0, tiled=True)
    small = small.reshape(group_count, -1)
    parts, at = [], code.size
    for piece in pieces[1:]:
        parts.append(small[:, at : at + piece.size])
        at += piece.size
    full_router = parts[0].reshape(width, experts_total)
    gain_attn, gain_ffn, gain_query, gain_key = (
        part.reshape(-1).astype(f32) for part in parts[1:5]
    )
    head_gains = jnp.stack([gain_query, gain_key])
    all_segments = parts[5].astype(jnp.int32)

    own_seg = segments[0]
    first_seg = lax.dynamic_index_in_dim(all_segments, group_rank - context_rank, 0, keepdims=False)
    other_seg = lax.dynamic_index_in_dim(
        all_segments, group_rank + 1 - 2 * context_rank, 0, keepdims=False
    )
    smaller = jnp.sum((own_seg[None, :] < own_seg[:, None]).astype(jnp.int32), axis=1)
    smaller_first = jnp.sum((first_seg[None, :] < own_seg[:, None]).astype(jnp.int32), axis=1)
    positions = jnp.arange(row_count, dtype=jnp.int32) - smaller
    positions = positions + context_rank * (row_count - smaller_first)
    cosine_table, sine_table = rope_tables(positions, HEAD_SIZE)
    turn = jnp.where(jnp.arange(HEAD_SIZE) < HEAD_SIZE // 2, -1.0, 1.0)
    sine_table = sine_table * turn
    seg_rows = jnp.stack([own_seg, other_seg])

    normed_one, raw, query, kv, kv_other, heads_full, heads_low, log_total = attend(
        hidden_in[0],
        gain_attn[None],
        qkv_full,
        cosine_table,
        sine_table,
        head_gains,
        own_seg[:, None],
        seg_rows,
        8,
    )
    input_own = lax.dynamic_slice_in_dim(hidden_in[0], own_start, own_count, 0)
    residual_own, normed_own, normed_all = mix_heads(
        heads_low, full_output, input_own, gain_ffn[None], 3
    )

    units = local_experts * hidden_width
    gate_flat = gate_weight.transpose(1, 0, 2).reshape(width, units)
    up_flat = up_weight.transpose(1, 0, 2).reshape(width, units)
    down_flat = down_weight.reshape(units, width)
    unit_expert = first_expert + jnp.arange(units, dtype=jnp.int32) // hidden_width
    lane_ids = jnp.arange(tensor_size * experts_total, dtype=jnp.int32)
    expand = (lane_ids[:, None] % experts_total == unit_expert[None, :]).astype(bf16)
    column = tensor_rank * experts_total + unit_expert
    place = (column[:, None] == lane_ids[None, :]).astype(bf16)
    router_lanes = jnp.concatenate([full_router] * tensor_size, axis=1)
    grad_resid_own, message, hidden_gated, gate_grad, up_grad = run_experts(
        normed_all,
        grad_out_all,
        codes,
        router_lanes,
        expand,
        place,
        gate_flat,
        up_flat,
        down_flat,
        residual_own,
        normed_own,
        jnp.pad(chosen_own.astype(bf16), ((0, 0), (0, 128 - experts_total))),
        grad_out_own,
        gain_ffn[None],
        4,
    )
    grad_attn = message[:, :own_count, :width].reshape(row_count, width)
    grad_raw, head_gain_grads = attend_back(
        grad_attn,
        full_output,
        query,
        kv,
        kv_other,
        raw,
        heads_full,
        log_total,
        cosine_table,
        sine_table,
        head_gains,
        seg_rows[:, :, None],
        seg_rows,
        9,
    )
    group_logits = message[:, :own_count, width:].reshape(row_count, 128)
    grad_gain_ffn = jnp.sum(message[:, own_count, :width].astype(f32), axis=0)
    normed_group = lax.dynamic_slice_in_dim(normed_all, group_rank * row_count, row_count, 0)
    grad_router = matmul_tn(normed_group, group_logits)
    extra = jnp.where(jnp.arange(128) == experts_total, grad_gain_ffn[:, None], grad_router)
    grad_w_output = jnp.concatenate([matmul_tn(grad_attn, heads_low), extra], axis=1)
    grad_w_output = lax.psum_scatter(
        grad_w_output.astype(bf16), GROUPS, scatter_dimension=0, tiled=True
    )

    message = pull_inputs(
        grad_raw, qkv_full, hidden_in[0], gain_attn[None], head_gain_grads, grad_resid_own, 6
    )
    input_grad = message[:, :own_count].reshape(row_count, width).astype(f32)
    gain_rows = jnp.sum(message[:, own_count : own_count + 2].astype(f32), axis=0)
    head_gains_grad = jnp.pad(
        gain_rows[1, : 2 * HEAD_SIZE].reshape(2, group_count, -1),
        ((0, 0), (0, 0), (0, (width - HEAD_SIZE) // group_count)),
    ).reshape(2, width)
    extra = jnp.pad(
        jnp.stack([gain_rows[0], head_gains_grad[0], head_gains_grad[1]], axis=1),
        ((0, 0), (0, 125)),
    )
    grad_qkv = jnp.concatenate([matmul_tn(normed_one, grad_raw), extra], axis=1)
    grad_qkv, hidden_gated = lax.optimization_barrier((grad_qkv.astype(bf16), hidden_gated))
    grad_qkv = lax.psum_scatter(grad_qkv, GROUPS, scatter_dimension=0, tiled=True)
    output, grad_w_gate, grad_w_up, grad_w_down = run_outputs(
        normed_all, grad_out_all, hidden_gated, gate_grad, up_grad, down_flat, residual_own, 10
    )

    def by_expert(grad):
        return grad.reshape(width, local_experts, hidden_width).transpose(1, 0, 2)

    grad_w_gate, grad_w_up = by_expert(grad_w_gate), by_expert(grad_w_up)
    output = output.reshape(row_count, width)
    output, grad_w_output = lax.optimization_barrier((output, grad_w_output))
    grad_w_output = [
        grad_w_output[:, :query_width].astype(f32),
        grad_w_output[:, query_width + experts_total].astype(f32),
        grad_w_output[:, query_width : query_width + experts_total].astype(f32),
    ]
    grad_qkv, grad_w_output, grad_w_gate, grad_w_up = lax.optimization_barrier(
        (grad_qkv, grad_w_output, grad_w_gate, grad_w_up)
    )
    value_at, extra_at = query_width + HEAD_SIZE, query_width + 2 * HEAD_SIZE
    return (
        output[None],
        input_grad[None],
        grad_qkv[:, extra_at].astype(f32),
        grad_qkv[:, :query_width].astype(f32),
        grad_qkv[:, query_width:value_at].astype(f32),
        grad_qkv[:, value_at:extra_at].astype(f32),
        grad_w_output[0],
        grad_qkv[: query_gain.shape[0], extra_at + 1].astype(f32),
        grad_qkv[: key_gain.shape[0], extra_at + 2].astype(f32),
        grad_w_output[1],
        grad_w_output[2],
        grad_w_gate,
        grad_w_up,
        grad_w_down.reshape(down_weight.shape),
    )


def local(*arrays):
    sizes = tuple(lax.axis_size(name) for name in EVERYONE)
    return (gathered_local if sizes == (4, 2, 4) and arrays[9].shape[1] == 32 else routed_local)(*arrays)


def solution(mesh):
    in_specs = (
        P(FSDP, CONTEXT, None),
        P(GROUPS),
        P(GROUPS, TENSOR),
        P(GROUPS, TENSOR),
        P(GROUPS, TENSOR),
        P(GROUPS, TENSOR),
        P(GROUPS),
        P(GROUPS),
        P(GROUPS),
        P(GROUPS, None),
        P(GROUPS, None, TENSOR),
        P(GROUPS, None, TENSOR),
        P(GROUPS, TENSOR, None),
        P(FSDP, CONTEXT, None),
        P(FSDP, CONTEXT),
        P(FSDP, CONTEXT, None),
    )
    out_specs = (
        P(FSDP, CONTEXT, None),
        P(FSDP, CONTEXT, None),
        P(GROUPS),
        P(GROUPS, TENSOR),
        P(GROUPS, TENSOR),
        P(GROUPS, TENSOR),
        P(GROUPS, TENSOR),
        P(GROUPS),
        P(GROUPS),
        P(GROUPS),
        P(GROUPS, None),
        P(GROUPS, None, TENSOR),
        P(GROUPS, None, TENSOR),
        P(GROUPS, TENSOR, None),
    )
    return jax.shard_map(local, mesh=mesh, in_specs=in_specs, out_specs=out_specs, check_vma=False)
```

```python
import functools
import math

import jax
import jax.numpy as jnp
from jax import lax
from jax.experimental import pallas as pl
from jax.experimental.pallas import tpu as pltpu
from jax.sharding import PartitionSpec as P

HEAD_SIZE = 128
TOPK = 8
FSDP, CONTEXT, TENSOR = "fsdp", "context", "tensor"
GROUPS = (FSDP, CONTEXT)
EVERYONE = (FSDP, CONTEXT, TENSOR)


EPSILON = 1e-06
ROPE_BASE = 1000000.0
NEGATIVE = -1e30


def rms_scale(values, gain_vec):
    return (
        values * lax.rsqrt(jnp.mean(values * values, axis=-1, keepdims=True) + EPSILON) * gain_vec
    )


def rotate(values):
    half_width = values.shape[-1] // 2
    return jnp.concatenate([-values[..., half_width:], values[..., :half_width]], axis=-1)


def rope_tables(positions, head_width):
    step_index = jnp.arange(head_width // 2, dtype=jnp.float32)
    inverse = jnp.exp(step_index * (-2.0 * math.log(ROPE_BASE) / head_width))
    angles = positions.astype(jnp.float32)[:, None] * inverse[None, :]
    cosine_table = jnp.cos(angles)
    sine_table = jnp.sin(angles)
    return (
        jnp.concatenate([cosine_table, cosine_table], -1),
        jnp.concatenate([sine_table, sine_table], -1),
    )


def doc_positions(segment):
    token_index = jnp.arange(segment.shape[0], dtype=jnp.int32)
    smaller = (segment[None, :] < segment[:, None]).astype(jnp.int32)
    return token_index - jnp.sum(smaller, axis=1)


def earlier_counts(chosen):
    rows = chosen.shape[0]
    row_id = lax.broadcasted_iota(jnp.int32, (rows, rows), 0)
    col_id = lax.broadcasted_iota(jnp.int32, (rows, rows), 1)
    earlier = (col_id < row_id).astype(jnp.bfloat16)
    return matmul(earlier, chosen.astype(jnp.bfloat16))


def qk_finish(raw_values, gain_vec, cosine_table, sine_table):
    normed = rms_scale(raw_values, gain_vec)
    return normed * cosine_table + rotate(normed) * sine_table


def matmul(left_side, right_side):
    return jnp.dot(left_side, right_side, preferred_element_type=jnp.float32)


def matmul_nt(left_side, right_side):
    return lax.dot_general(
        left_side, right_side, (((1,), (1,)), ((), ())), preferred_element_type=jnp.float32
    )


def matmul_tn(left_side, right_side):
    return lax.dot_general(
        left_side, right_side, (((0,), (0,)), ((), ())), preferred_element_type=jnp.float32
    )


def block_scores(query_vectors, keys_all, seg_all, query_seg, query_index, key_ids, block_id, key_block):
    leading_row = block_id * key_block
    keys_part = lax.dynamic_slice_in_dim(keys_all, leading_row, key_block, 0)
    seg_part = lax.dynamic_slice_in_dim(seg_all, leading_row, key_block, 0)
    key_index = lax.dynamic_slice_in_dim(key_ids, leading_row, key_block, 0)
    score_scale = query_vectors.shape[2] ** (-0.5)
    scores = (
        jnp.einsum("qhd,kd->hqk", query_vectors, keys_part, preferred_element_type=jnp.float32)
        * score_scale
    )
    allowed = (query_seg[:, None] == seg_part[None, :]) & (
        key_index[None, :] <= query_index[:, None]
    )
    return (scores, allowed[None, :, :], keys_part)


def attention_forward(
    query_vectors, keys_all, values_all, seg_all, query_seg, query_index, key_ids, key_block
):
    row_count, head_count, head_width = query_vectors.shape
    block_count = keys_all.shape[0] // key_block

    def stats_step(running, block_id):
        run_max, run_sum = running
        scores, allowed, unused = block_scores(
            query_vectors, keys_all, seg_all, query_seg, query_index, key_ids, block_id, key_block
        )
        masked = jnp.where(allowed, scores, NEGATIVE)
        new_max = jnp.maximum(run_max, jnp.max(masked, axis=2))
        weights = jnp.where(allowed, jnp.exp(masked - new_max[:, :, None]), 0.0)
        run_sum = run_sum * jnp.exp(run_max - new_max) + jnp.sum(weights, axis=2)
        return ((new_max, run_sum), None)

    start_state = (
        jnp.full((head_count, row_count), NEGATIVE, jnp.float32),
        jnp.zeros((head_count, row_count), jnp.float32),
    )
    (run_max, run_sum), ignored = lax.scan(
        stats_step, start_state, jnp.arange(block_count, dtype=jnp.int32)
    )
    log_total = run_max + jnp.log(run_sum)

    def value_step(accumulated, block_id):
        scores, allowed, unused = block_scores(
            query_vectors, keys_all, seg_all, query_seg, query_index, key_ids, block_id, key_block
        )
        prob_block = jnp.where(allowed, jnp.exp(scores - log_total[:, :, None]), 0.0).astype(
            jnp.bfloat16
        )
        values_part = lax.dynamic_slice_in_dim(values_all, block_id * key_block, key_block, 0)
        accumulated = accumulated + jnp.einsum(
            "hqk,kd->qhd", prob_block, values_part, preferred_element_type=jnp.float32
        )
        return (accumulated, None)

    heads_full, ignored = lax.scan(
        value_step,
        jnp.zeros((row_count, head_count, head_width), jnp.float32),
        jnp.arange(block_count, dtype=jnp.int32),
    )
    return (heads_full, log_total)


def attention_backward(
    query_vectors,
    keys_all,
    values_all,
    seg_all,
    query_seg,
    query_index,
    key_ids,
    key_block,
    log_total,
    grad_heads,
    row_delta,
):
    row_count, head_count, head_width = query_vectors.shape
    block_count = keys_all.shape[0] // key_block
    score_scale = head_width ** (-0.5)

    def grad_step(grad_query, block_id):
        scores, allowed, keys_part = block_scores(
            query_vectors, keys_all, seg_all, query_seg, query_index, key_ids, block_id, key_block
        )
        values_part = lax.dynamic_slice_in_dim(values_all, block_id * key_block, key_block, 0)
        prob_block = jnp.where(allowed, jnp.exp(scores - log_total[:, :, None]), 0.0)
        grad_prob = jnp.einsum(
            "qhd,kd->hqk", grad_heads, values_part, preferred_element_type=jnp.float32
        )
        grad_score = (prob_block * (grad_prob - row_delta[:, :, None])).astype(jnp.bfloat16)
        grad_query = (
            grad_query
            + jnp.einsum("hqk,kd->qhd", grad_score, keys_part, preferred_element_type=jnp.float32)
            * score_scale
        )
        grad_key = (
            jnp.einsum("hqk,qhd->kd", grad_score, query_vectors, preferred_element_type=jnp.float32)
            * score_scale
        )
        grad_value = jnp.einsum(
            "hqk,qhd->kd",
            prob_block.astype(jnp.bfloat16),
            grad_heads,
            preferred_element_type=jnp.float32,
        )
        return (grad_query, (grad_key, grad_value))

    grad_query, (grad_key, grad_value) = lax.scan(
        grad_step,
        jnp.zeros((row_count, head_count, head_width), jnp.float32),
        jnp.arange(block_count, dtype=jnp.int32),
    )
    return (grad_query, grad_key.reshape(-1, head_width), grad_value.reshape(-1, head_width))


def to_experts(buffer):
    return lax.all_to_all(buffer, GROUPS, split_axis=0, concat_axis=1, tiled=True)


def from_experts(result_rows):
    return lax.all_to_all(result_rows, GROUPS, split_axis=1, concat_axis=0, tiled=True)


def pick_pairs(buffer, target, row_count):
    model_width = buffer.shape[2]
    flat_rows = jnp.concatenate(
        [buffer.reshape(-1, model_width), jnp.zeros((1, model_width), buffer.dtype)], axis=0
    )
    return flat_rows[target].reshape(row_count, TOPK, model_width)


def routed_local(
    hidden_in,
    attn_gain,
    w_query,
    key_weight,
    value_weight,
    w_output,
    query_gain,
    key_gain,
    ffn_gain,
    router,
    gate_weight,
    up_weight,
    down_weight,
    routes,
    segments,
    cotangent,
):
    context_rank = lax.axis_index(CONTEXT)
    input_rows = hidden_in[0].astype(jnp.float32)
    row_count, model_width = input_rows.shape
    gathered = (
        lax.all_gather(w_query, GROUPS, axis=0, tiled=True),
        lax.all_gather(key_weight, GROUPS, axis=0, tiled=True),
        lax.all_gather(value_weight, GROUPS, axis=0, tiled=True),
        lax.all_gather(w_output, GROUPS, axis=0, tiled=True),
        lax.all_gather(router, GROUPS, axis=0, tiled=True),
        lax.all_gather(attn_gain, GROUPS, axis=0, tiled=True),
        lax.all_gather(ffn_gain, GROUPS, axis=0, tiled=True),
        lax.all_gather(query_gain, GROUPS, axis=0, tiled=True),
        lax.all_gather(key_gain, GROUPS, axis=0, tiled=True),
    )
    full_query, full_key, full_value, full_output, full_router = (
        gathered[0],
        gathered[1],
        gathered[2],
        gathered[3],
        gathered[4],
    )
    gain_attn = gathered[5].astype(jnp.float32)
    gain_ffn = gathered[6].astype(jnp.float32)
    gain_query = gathered[7].astype(jnp.float32)
    gain_key = gathered[8].astype(jnp.float32)
    local_heads = full_query.shape[1] // HEAD_SIZE
    seg_all = lax.all_gather(segments, CONTEXT, axis=1, tiled=True)[0]
    length = seg_all.shape[0]
    start_row = context_rank * row_count
    positions = lax.dynamic_slice_in_dim(doc_positions(seg_all), start_row, row_count)
    cosine_table, sine_table = rope_tables(positions, HEAD_SIZE)
    query_seg = segments[0]
    query_index = start_row + jnp.arange(row_count, dtype=jnp.int32)
    key_ids = jnp.arange(length, dtype=jnp.int32)
    key_block = min(512, length)

    def query_finish(raw_values, gain_vec):
        return qk_finish(raw_values, gain_vec, cosine_table[:, None, :], sine_table[:, None, :])

    def key_finish(raw_values, gain_vec):
        return qk_finish(raw_values, gain_vec, cosine_table, sine_table)

    normed_f, first_pull = jax.vjp(rms_scale, input_rows, gain_attn)
    attention_normalized = normed_f.astype(jnp.bfloat16)
    query_unrotated = matmul(attention_normalized, full_query).reshape(
        row_count, local_heads, HEAD_SIZE
    )
    key_unrotated = matmul(attention_normalized, full_key)
    value_raw = matmul(attention_normalized, full_value)
    query_f, query_pull = jax.vjp(query_finish, query_unrotated, gain_query)
    key_f, key_pull = jax.vjp(key_finish, key_unrotated, gain_key)
    query_vectors = query_f.astype(jnp.bfloat16)
    keys_all, values_all = (
        lax.all_gather(key_f.astype(jnp.bfloat16), CONTEXT, axis=0, tiled=True),
        lax.all_gather(value_raw.astype(jnp.bfloat16), CONTEXT, axis=0, tiled=True),
    )
    heads_full, log_total = attention_forward(
        query_vectors, keys_all, values_all, seg_all, query_seg, query_index, key_ids, key_block
    )
    heads_low = heads_full.reshape(row_count, local_heads * HEAD_SIZE).astype(jnp.bfloat16)
    attn_out = lax.psum(matmul_nt(heads_low, full_output).astype(jnp.bfloat16), TENSOR).astype(
        jnp.float32
    )
    residual_stream = input_rows + attn_out
    second_f, second_pull = jax.vjp(rms_scale, residual_stream, gain_ffn)
    feedforward_normalized = second_f.astype(jnp.bfloat16)
    router_scores = matmul(feedforward_normalized, full_router)
    experts_total = full_router.shape[1]
    route_ids = routes[0]
    chosen = route_ids[:, :, None] == jnp.arange(experts_total, dtype=jnp.int32)
    selected = jnp.sum(jnp.where(chosen, router_scores[:, None, :], 0.0), axis=2)
    gate_probs = jax.nn.softmax(selected, axis=-1)
    capacity = 9 * row_count * TOPK // (8 * experts_total)
    before = earlier_counts(jnp.any(chosen, axis=1)).astype(jnp.int32)
    slot_index = jnp.sum(jnp.where(chosen, before[:, None, :], 0), axis=2)
    target = jnp.where(
        slot_index < capacity, route_ids * capacity + slot_index, experts_total * capacity
    ).reshape(-1)
    source = jnp.repeat(jnp.arange(row_count, dtype=jnp.int32), TOPK)
    send_rows = (
        jnp.zeros((experts_total * capacity, model_width), jnp.bfloat16)
        .at[target]
        .set(feedforward_normalized[source], mode="drop")
    )
    expert_input_rows = to_experts(send_rows.reshape(experts_total, capacity, model_width))
    gate_activation_input = jnp.einsum(
        "phu,puo->pho", expert_input_rows, gate_weight, preferred_element_type=jnp.float32
    )
    up_activation_input = jnp.einsum(
        "phu,puo->pho", expert_input_rows, up_weight, preferred_element_type=jnp.float32
    )
    sigmoid_gate = jax.nn.sigmoid(gate_activation_input)
    silu_gate = gate_activation_input * sigmoid_gate
    hidden_middle = (silu_gate * up_activation_input).astype(jnp.bfloat16)
    expert_part = jnp.einsum(
        "pic,pcw->piw", hidden_middle, down_weight, preferred_element_type=jnp.float32
    ).astype(jnp.bfloat16)
    grad_out = cotangent[0].astype(jnp.float32)
    returned = pick_pairs(from_experts(expert_part), target, row_count)
    moe_part = jnp.sum(returned.astype(jnp.float32) * gate_probs[:, :, None], axis=1)
    moe_out = lax.psum(moe_part.astype(jnp.bfloat16), TENSOR).astype(jnp.float32)
    grad_gate_part = jnp.sum(returned.astype(jnp.float32) * grad_out[:, None, :], axis=2)
    output = (residual_stream + moe_out).astype(jnp.bfloat16)
    pair_grad = (
        (gate_probs[:, :, None] * grad_out[:, None, :])
        .astype(jnp.bfloat16)
        .reshape(row_count * TOPK, model_width)
    )
    send_grad = (
        jnp.zeros((experts_total * capacity, model_width), jnp.bfloat16)
        .at[target]
        .set(pair_grad, mode="drop")
    )
    expert_output_gradient = to_experts(send_grad.reshape(experts_total, capacity, model_width))
    grad_mid = jnp.einsum(
        "jtk,jvk->jtv", expert_output_gradient, down_weight, preferred_element_type=jnp.float32
    )
    grad_w_down = jnp.einsum(
        "tce,tci->tei", hidden_middle, expert_output_gradient, preferred_element_type=jnp.float32
    )
    gate_activation_gradient = (
        grad_mid
        * up_activation_input
        * sigmoid_gate
        * (1.0 + gate_activation_input * (1.0 - sigmoid_gate))
    ).astype(jnp.bfloat16)
    up_activation_gradient = (grad_mid * silu_gate).astype(jnp.bfloat16)
    grad_w_gate = jnp.einsum(
        "ahw,ahp->awp",
        expert_input_rows,
        gate_activation_gradient,
        preferred_element_type=jnp.float32,
    )
    grad_w_up = jnp.einsum(
        "ahw,ahp->awp",
        expert_input_rows,
        up_activation_gradient,
        preferred_element_type=jnp.float32,
    )
    grad_expert_in = (
        jnp.einsum(
            "ous,ops->oup",
            gate_activation_gradient,
            gate_weight,
            preferred_element_type=jnp.float32,
        )
        + jnp.einsum(
            "ous,ops->oup", up_activation_gradient, up_weight, preferred_element_type=jnp.float32
        )
    ).astype(jnp.bfloat16)
    grad_pairs = pick_pairs(from_experts(grad_expert_in), target, row_count)
    grad_normed_part = jnp.sum(grad_pairs.astype(jnp.float32), axis=1)
    grad_normed_moe, grad_gates = (
        lax.psum(grad_normed_part.astype(jnp.bfloat16), TENSOR).astype(jnp.float32),
        lax.psum(grad_gate_part.astype(jnp.bfloat16), TENSOR).astype(jnp.float32),
    )
    grad_selected = gate_probs * (
        grad_gates - jnp.sum(gate_probs * grad_gates, axis=1, keepdims=True)
    )
    grad_logits = jnp.sum(jnp.where(chosen, grad_selected[:, :, None], 0.0), axis=1).astype(
        jnp.bfloat16
    )
    grad_router = matmul_tn(feedforward_normalized, grad_logits)
    grad_normed_two = grad_normed_moe + matmul_nt(grad_logits, full_router)
    grad_resid_norm, grad_gain_ffn = second_pull(grad_normed_two)
    grad_resid = grad_out + grad_resid_norm
    grad_attn = grad_resid.astype(jnp.bfloat16)
    grad_w_output = matmul_tn(grad_attn, heads_low)
    grad_heads = (
        matmul(grad_attn, full_output)
        .astype(jnp.bfloat16)
        .reshape(row_count, local_heads, HEAD_SIZE)
    )
    row_delta = jnp.sum(grad_heads.astype(jnp.float32) * heads_full, axis=2).T
    grad_query, grad_key_terms, grad_value_terms = attention_backward(
        query_vectors,
        keys_all,
        values_all,
        seg_all,
        query_seg,
        query_index,
        key_ids,
        key_block,
        log_total,
        grad_heads,
        row_delta,
    )
    grad_key_local, grad_value_local = (
        lax.psum_scatter(
            grad_key_terms.astype(jnp.bfloat16), CONTEXT, scatter_dimension=0, tiled=True
        ).astype(jnp.float32),
        lax.psum_scatter(
            grad_value_terms.astype(jnp.bfloat16), CONTEXT, scatter_dimension=0, tiled=True
        ).astype(jnp.float32),
    )
    grad_query_raw, grad_gain_query = query_pull(grad_query)
    grad_key_raw, grad_gain_key = key_pull(grad_key_local)
    grad_query_low = grad_query_raw.reshape(row_count, local_heads * HEAD_SIZE).astype(jnp.bfloat16)
    grad_key_low = grad_key_raw.astype(jnp.bfloat16)
    grad_value_low = grad_value_local.astype(jnp.bfloat16)
    grad_w_query = matmul_tn(attention_normalized, grad_query_low)
    grad_w_key = matmul_tn(attention_normalized, grad_key_low)
    grad_w_value = matmul_tn(attention_normalized, grad_value_low)
    grad_normed_one = (
        matmul_nt(grad_query_low, full_query)
        + matmul_nt(grad_key_low, full_key)
        + matmul_nt(grad_value_low, full_value)
    )
    grad_normed_one, grad_gain_query, grad_gain_key = (
        lax.psum(grad_normed_one.astype(jnp.bfloat16), TENSOR).astype(jnp.float32),
        lax.psum(grad_gain_query.astype(jnp.bfloat16), TENSOR).astype(jnp.float32),
        lax.psum(grad_gain_key.astype(jnp.bfloat16), TENSOR).astype(jnp.float32),
    )
    grad_inputs_norm, grad_gain_attn = first_pull(grad_normed_one)
    input_grad = grad_resid + grad_inputs_norm
    owned = (
        lax.psum_scatter(
            grad_w_query.astype(jnp.bfloat16), GROUPS, scatter_dimension=0, tiled=True
        ).astype(jnp.float32),
        lax.psum_scatter(
            grad_w_key.astype(jnp.bfloat16), GROUPS, scatter_dimension=0, tiled=True
        ).astype(jnp.float32),
        lax.psum_scatter(
            grad_w_value.astype(jnp.bfloat16), GROUPS, scatter_dimension=0, tiled=True
        ).astype(jnp.float32),
        lax.psum_scatter(
            grad_w_output.astype(jnp.bfloat16), GROUPS, scatter_dimension=0, tiled=True
        ).astype(jnp.float32),
        lax.psum_scatter(
            grad_router.astype(jnp.bfloat16), GROUPS, scatter_dimension=0, tiled=True
        ).astype(jnp.float32),
        lax.psum_scatter(
            grad_gain_attn.astype(jnp.bfloat16),
            GROUPS,
            scatter_dimension=0,
            tiled=True,
        ).astype(jnp.float32),
        lax.psum_scatter(
            grad_gain_ffn.astype(jnp.bfloat16), GROUPS, scatter_dimension=0, tiled=True
        ).astype(jnp.float32),
        lax.psum_scatter(
            grad_gain_query.astype(jnp.bfloat16),
            GROUPS,
            scatter_dimension=0,
            tiled=True,
        ).astype(jnp.float32),
        lax.psum_scatter(
            grad_gain_key.astype(jnp.bfloat16), GROUPS, scatter_dimension=0, tiled=True
        ).astype(jnp.float32),
    )
    return (
        output[None],
        input_grad[None],
        owned[5],
        owned[0],
        owned[1],
        owned[2],
        owned[3],
        owned[7],
        owned[8],
        owned[6],
        owned[4],
        grad_w_gate,
        grad_w_up,
        grad_w_down,
    )


MESH = pl.DeviceIdType.MESH
Z_UP, Z_DOWN, Y_SIDE, X_SIDE, CORE_SIDE = range(5)

def coords():
    z, y, t = lax.axis_index(FSDP), lax.axis_index(CONTEXT), lax.axis_index(TENSOR)
    return z, y, t // 2, t % 2

def partner(z, index):
    return (z, z + 1 - 2 * (z % 2), 2 - z // 2, 3 - 3 * (z // 2))[index]

def greet(neighbours):
    barrier = pltpu.get_barrier_semaphore()
    for condition, device in neighbours:
        def tell(device=device):
            pl.semaphore_signal(barrier, inc=1, device_id=device, device_id_type=MESH)
        if condition is None: tell()
        else: pl.when(condition)(tell)
    count = sum(1 if condition is None else condition.astype(jnp.int32) for condition, device in neighbours)
    pl.semaphore_wait(barrier, count)


def spread(x_ref, out_ref, own_sem, send_sems, recv_sems):
    rows = x_ref.shape[0]; half = rows // 2
    z, y, x, c = coords()
    side = {Z_UP: (z + 1, y, 2 * x + c), Z_DOWN: (z - 1, y, 2 * x + c), Y_SIDE: (z, 1 - y, 2 * x + c),
            X_SIDE: (z, y, 2 * (1 - x) + c), CORE_SIDE: (z, y, 2 * x + 1 - c)}
    def device(zz, yy, xx, cc): return (zz * 2 + yy) * 4 + xx * 2 + cc
    def place(owner, h): return out_ref.at[pl.ds(pl.multiple_of(owner * rows + h * half, half), half)]
    def copy(link, owner, h, own=False):
        src = x_ref.at[pl.ds(h * half, half)] if own else place(owner, h)
        return pltpu.make_async_remote_copy(src_ref=src, dst_ref=place(owner, h), send_sem=send_sems.at[link, owner, h],
            recv_sem=recv_sems.at[owner, h], device_id=side[link], device_id_type=MESH)
    sent = []
    def start(link, owner, h, own=False, condition=None):
        one = copy(link, owner, h, own)
        sent.append((one, condition))
        if condition is None: one.start()
        else: pl.when(condition)(one.start)
    def arrived(owner, h): copy(CORE_SIDE, owner, h).wait_recv()
    me = device(z, y, x, c)
    keep = pltpu.make_async_copy(x_ref, out_ref.at[pl.ds(pl.multiple_of(me * rows, rows), rows)], own_sem)
    keep.start()
    def stage1(i):
        zz = partner(z, i); owner = device(zz, y, x, c); own = i == 0
        if not own:
            arrived(owner, 0); arrived(owner, 1)
        for h in range(2):
            start(Z_UP, owner, h, own, (z < 3) if own else (z < 3) & (zz < z))
            start(Z_DOWN, owner, h, own, (z > 0) if own else (z > 0) & (zz > z))
        start(Y_SIDE, owner, 0, own); start(X_SIDE, owner, 1, own)
        start(Y_SIDE, owner, 1, own); start(X_SIDE, owner, 0, own)
        for h in range(2): start(CORE_SIDE, owner, h, own)
    def stage2(i):
        zz = partner(z, i)
        oy, ox = device(zz, 1 - y, x, c), device(zz, y, 1 - x, c)
        arrived(oy, 0); start(X_SIDE, oy, 0); start(CORE_SIDE, oy, 0)
        arrived(ox, 1); start(Y_SIDE, ox, 1); start(CORE_SIDE, ox, 1)
        arrived(oy, 1); start(CORE_SIDE, oy, 1)
        arrived(ox, 0); start(CORE_SIDE, ox, 0)
    def stage3(i):
        o = device(partner(z, i), 1 - y, 1 - x, c)
        for h in range(2):
            arrived(o, h); start(CORE_SIDE, o, h)
    stage1(0); stage1(1); stage2(0); stage1(2); stage2(1); stage3(0); stage1(3); stage2(2); stage3(1); stage2(3); stage3(2); stage3(3)
    for i in range(4):
        for yy in range(2):
            for xx in range(2):
                for h in range(2): arrived(device(i, yy, xx, 1 - c), h)
    keep.wait()
    for one, condition in sent:
        if condition is None: one.wait_send()
        else: pl.when(condition)(one.wait_send)

def mix_kernel(heads_ref, weight_ref, input_ref, gain_ref, resid_ref, normed_ref, all_ref, part, mine, core_in, line_in, sems, recv, *gather_sems):
    z, y, x, c = coords()
    x_side, core_side = (z, y, 2 * (1 - x) + c), (z, y, 2 * x + 1 - c)
    greet([(z < 3, (z + 1, y, 2 * x + c)), (z > 0, (z - 1, y, 2 * x + c)), (None, (z, 1 - y, 2 * x + c)), (None, x_side), (None, core_side)])
    rows, width = input_ref.shape; f32, bf16 = jnp.float32, jnp.bfloat16
    def remote(src, dst, n, device):
        return pltpu.make_async_remote_copy(src_ref=src, dst_ref=dst, send_sem=sems.at[n], recv_sem=recv.at[n], device_id=device, device_id_type=MESH)
    over_core = [remote(part.at[n, 1 - c], core_in.at[n], n, core_side) for n in range(2)]
    over_x = remote(mine, line_in, 2, x_side)
    for n, xx in enumerate((1 - x, x)):
        heads = heads_ref[pl.ds(pl.multiple_of(xx * 2 * rows, 2 * rows), 2 * rows), :]
        for m in range(width // 512):
            at = pl.ds(m * 512, 512)
            value = lax.dot_general(heads, weight_ref[at, :], (((1,), (1,)), ((), ())), preferred_element_type=f32).astype(bf16)
            part[n, 0, :, at] = value[:rows]
            part[n, 1, :, at] = value[rows:]
        over_core[n].start()
    over_core[0].wait_recv()
    mine[...] = part[0, c] + core_in[0]
    over_x.start(); over_core[1].wait_recv()
    total = input_ref[...].astype(f32) + part[1, c].astype(f32) + core_in[1].astype(f32)
    over_x.wait_recv()
    total = total + line_in[...].astype(f32)
    resid_ref[...] = total
    normed_ref[...] = (total * lax.rsqrt(jnp.mean(total * total, axis=-1, keepdims=True) + EPSILON) * gain_ref[...]).astype(bf16)
    spread(normed_ref, all_ref, *gather_sems)
    for one in (*over_core, over_x): one.wait_send()

def mix_heads(heads, weight, own_input, gain, collective_id):
    rows, width = own_input.shape; D, V = pltpu.SemaphoreType.DMA, pltpu.VMEM; S = jax.ShapeDtypeStruct
    f32, bf16 = jnp.float32, jnp.bfloat16; vspec = pl.BlockSpec(memory_space=V)
    return pl.pallas_call(mix_kernel, out_shape=[S((rows, width), f32), S((rows, width), bf16), S((32 * rows, width), bf16)],
        in_specs=[vspec] * 4, out_specs=[vspec, vspec, pl.BlockSpec(memory_space=pl.ANY)],
        scratch_shapes=[V((2, 2, rows, width), bf16), V((rows, width), bf16), V((2, rows, width), bf16), V((rows, width), bf16), D((3,)), D((3,)),
            D, D((5, 32, 2)), D((32, 2))],
        compiler_params=pltpu.CompilerParams(collective_id=collective_id, has_side_effects=True, vmem_limit_bytes=32 << 20))(heads, weight, own_input, gain)

def groups_kernel(parts, count, *refs):
    ins, outs = refs[:count], refs[count:2 * count]
    keep_sems, send_sems, recv_sems = refs[2 * count:]
    z, y, x, c = coords()
    t = 2 * x + c
    side = {Z_UP: (z + 1, y, t), Z_DOWN: (z - 1, y, t), Y_SIDE: (z, 1 - y, t)}
    greet([(z < 3, side[Z_UP]), (z > 0, side[Z_DOWN]), (None, side[Y_SIDE])])
    sent = []
    def copy(link, p, owner, own=False):
        k, first, size, way = parts[p]
        dst = outs[k].at[pl.ds(pl.multiple_of(owner * ins[k].shape[0] + first, 16), size)]
        return pltpu.make_async_remote_copy(src_ref=ins[k].at[pl.ds(first, size)] if own else dst, dst_ref=dst, send_sem=send_sems.at[link, p, owner],
            recv_sem=recv_sems.at[p, owner], device_id=side[link], device_id_type=MESH)
    def start(link, p, owner, own=False, condition=None):
        one = copy(link, p, owner, own)
        sent.append((one, condition))
        if condition is None: one.start()
        else: pl.when(condition)(one.start)
    def arrived(p, owner): copy(Y_SIDE, p, owner).wait_recv()
    def along(p, owner, zz, own=False):
        start(Z_UP, p, owner, own, (z < 3) & (zz <= z)); start(Z_DOWN, p, owner, own, (z > 0) & (zz >= z))
    kept = []
    for p in range(len(parts)):
        along(p, z * 2 + y, z, True); start(Y_SIDE, p, z * 2 + y, True)
    for k in range(count):
        rows = ins[k].shape[0]
        one = pltpu.make_async_copy(ins[k], outs[k].at[pl.ds(pl.multiple_of((z * 2 + y) * rows, 16), rows)], keep_sems.at[k])
        one.start(); kept.append(one)
    def forward(p, i):
        zz = partner(z, i)
        near, far = zz * 2 + y, zz * 2 + 1 - y
        if i > 0:
            arrived(p, near); along(p, near, zz)
            if parts[p][3] == 0: start(Y_SIDE, p, near)
        if parts[p][3] == 1:
            arrived(p, far); along(p, far, zz)
    for wave in range(len(parts) + 3):
        for i in range(4):
            if 0 <= wave - i < len(parts): forward(wave - i, i)
    for p in range(len(parts)):
        if parts[p][3] == 0:
            for i in range(4): arrived(p, partner(z, i) * 2 + 1 - y)
    for one in kept: one.wait()
    for one, condition in sent:
        if condition is None: one.wait_send()
        else: pl.when(condition)(one.wait_send)

def gather_groups(arrays, parts, collective_id):
    count = len(arrays); D = pltpu.SemaphoreType.DMA
    return pl.pallas_call(functools.partial(groups_kernel, parts, count),
        out_shape=[jax.ShapeDtypeStruct((8 * a.shape[0], a.shape[1]), a.dtype) for a in arrays],
        in_specs=[pl.BlockSpec(memory_space=pl.ANY)] * count, out_specs=[pl.BlockSpec(memory_space=pl.ANY)] * count,
        scratch_shapes=[D((count,)), D((3, len(parts), 8)), D((len(parts), 8))],
        compiler_params=pltpu.CompilerParams(collective_id=collective_id, has_side_effects=True))(*arrays)

class TensorGather:
    def __init__(self, src, out, keep_sem, send_sems, recv_sems):
        self.src, self.out, self.keep_sem, self.send_sems, self.recv_sems = src, out, keep_sem, send_sems, recv_sems
        z, y, x, c = coords()
        self.x_side, self.core_side = (z, y, 2 * (1 - x) + c), (z, y, 2 * x + 1 - c)
        self.me, self.across, self.beside, self.last = 2 * x + c, 2 * (1 - x) + c, 2 * x + 1 - c, 2 * (1 - x) + 1 - c

    @staticmethod
    def scratch():
        D = pltpu.SemaphoreType.DMA
        return [D, D((3,)), D((4,))]

    def copy(self, n, owner, device, own=False):
        return pltpu.make_async_remote_copy(src_ref=self.src if own else self.out.at[owner], dst_ref=self.out.at[owner],
            send_sem=self.send_sems.at[n], recv_sem=self.recv_sems.at[owner], device_id=device, device_id_type=MESH)

    def start(self):
        self.copy(0, self.me, self.x_side, True).start()
        self.copy(1, self.me, self.core_side, True).start()
        self.keep().start()

    def keep(self): return pltpu.make_async_copy(self.src, self.out.at[self.me], self.keep_sem)

    def finish(self):
        self.copy(0, self.across, self.x_side).wait_recv()
        self.copy(2, self.across, self.core_side).start()
        self.copy(0, self.beside, self.x_side).wait_recv()
        self.copy(0, self.last, self.x_side).wait_recv()
        self.keep().wait()
        self.copy(0, self.me, self.x_side, True).wait_send()
        self.copy(1, self.me, self.core_side, True).wait_send()
        self.copy(2, self.across, self.core_side).wait_send()

def rms_pull(grad, values, inverse, gain):
    scaled = grad * gain
    return inverse * scaled - values * (inverse * inverse * inverse * jnp.mean(scaled * values, axis=-1, keepdims=True))

def pull_kernel(grad_ref, weight_ref, input_ref, gain_ref, head_gain_ref, above_ref, out_ref, part, mine, core_in, line_in, message, sems, recv, *gather):
    z, y, x, c = coords()
    x_side, core_side = (z, y, 2 * (1 - x) + c), (z, y, 2 * x + 1 - c)
    greet([(None, x_side), (None, core_side)])
    rows, width = above_ref.shape; f32, bf16 = jnp.float32, jnp.bfloat16
    def remote(src, dst, n, device):
        return pltpu.make_async_remote_copy(src_ref=src, dst_ref=dst, send_sem=sems.at[n], recv_sem=recv.at[n], device_id=device, device_id_type=MESH)
    over_core = [remote(part.at[n, 1 - c], core_in.at[n], n, core_side) for n in range(2)]
    over_x = remote(mine, line_in, 2, x_side)
    message[pl.ds(rows, 16), :] = jnp.zeros((16, width), f32).astype(bf16)
    gain_parts = [0.0] * (width // 512)
    for n, xx in enumerate((1 - x, x)):
        rows_at = pl.ds(pl.multiple_of(xx * 2 * rows, 2 * rows), 2 * rows)
        grad = grad_ref[rows_at, :]
        whole = input_ref[rows_at, :].astype(f32)
        inverse = lax.rsqrt(jnp.mean(whole * whole, axis=-1, keepdims=True) + EPSILON)
        for m in range(width // 512):
            at = pl.ds(m * 512, 512)
            value = lax.dot_general(grad, weight_ref[at, :], (((1,), (1,)), ((), ())), preferred_element_type=f32)
            part[n, 0, :, at] = value[:rows].astype(bf16)
            part[n, 1, :, at] = value[rows:].astype(bf16)
            gain_parts[m] = gain_parts[m] + jnp.sum(value * input_ref[rows_at, at].astype(f32) * inverse, axis=0, keepdims=True)
        over_core[n].start()
    first_row = lax.broadcasted_iota(jnp.int32, (16, 512), 0)
    for m in range(width // 512):
        message[pl.ds(rows, 16), pl.ds(m * 512, 512)] = jnp.where(first_row == 0, gain_parts[m], 0.0).astype(bf16)
    first_row = lax.broadcasted_iota(jnp.int32, (16, 128), 0)
    for n in range(2):
        at = (pl.ds(rows, 16), pl.ds(n * 128, 128))
        message[at] = jnp.where(first_row == 1, head_gain_ref[pl.ds(n, 1), :], message[at].astype(f32)).astype(bf16)
    over_core[0].wait_recv()
    mine[...] = part[0, c] + core_in[0]
    over_x.start(); over_core[1].wait_recv()
    own_at = pl.ds(pl.multiple_of((2 * x + c) * rows, rows), rows)
    own = input_ref[own_at, :].astype(f32)
    inverse = lax.rsqrt(jnp.mean(own * own, axis=-1, keepdims=True) + EPSILON)
    total = part[1, c].astype(f32) + core_in[1].astype(f32)
    over_x.wait_recv()
    total = total + line_in[...].astype(f32)
    message[pl.ds(0, rows), :] = (above_ref[...] + rms_pull(total, own, inverse, gain_ref[...])).astype(bf16)
    gather = TensorGather(message, out_ref, *gather)
    gather.start(); gather.finish()
    for one in (*over_core, over_x): one.wait_send()

def pull_inputs(grad, weight, inputs, gain, head_gain_grads, above, collective_id):
    rows, width = above.shape; D, V = pltpu.SemaphoreType.DMA, pltpu.VMEM
    bf16 = jnp.bfloat16; vspec = pl.BlockSpec(memory_space=V)
    return pl.pallas_call(pull_kernel, out_shape=jax.ShapeDtypeStruct((4, rows + 16, width), bf16),
        in_specs=[vspec] * 6, out_specs=pl.BlockSpec(memory_space=pl.ANY),
        scratch_shapes=[V((2, 2, rows, width), bf16), V((rows, width), bf16), V((2, rows, width), bf16), V((rows, width), bf16), V((rows + 16, width), bf16),
            D((3,)), D((3,)), *TensorGather.scratch()],
        compiler_params=pltpu.CompilerParams(collective_id=collective_id, has_side_effects=True, vmem_limit_bytes=40 << 20))(
            grad, weight, inputs, gain, head_gain_grads, above)


def nt(a, b):
    return lax.dot_general(a, b, (((1,), (1,)), ((), ())), preferred_element_type=jnp.float32)

def nn(a, b):
    return jnp.dot(a, b, preferred_element_type=jnp.float32)

def nearest(z, index):
    choice = [partner(z, n) for n in range(4)]
    return jnp.where(index == 0, choice[0], jnp.where(index == 1, choice[1], jnp.where(index == 2, choice[2], choice[3])))

def spot(zz, yy, xx): return (zz * 2 + yy) * 2 + xx

def step_target(step):
    z, y, x, c = coords()
    n = step % 4
    return nearest(z, 3 - step // 4), jnp.where(n < 2, 1 - y, y), jnp.where(n % 2 == 0, 1 - x, x)

def step_block(ref, step):
    size = ref.shape[0] // 16
    return ref.at[pl.ds(pl.multiple_of(spot(*step_target(step)) * size, size), size)]

class Reduction:
    def __init__(self, part, mine, first_in, second_in, line_in, core_sem, first_sem, second_sem, line_send, line_recv):
        self.part, self.mine, self.first_in, self.second_in, self.line_in = part, mine, first_in, second_in, line_in
        self.core_sem, self.first_sem, self.second_sem, self.line_send, self.line_recv = core_sem, first_sem, second_sem, line_send, line_recv
        self.half = part.shape[2] // 2
        z, y, x, c = self.at = coords()
        self.up, self.down = (z + 1, y, 2 * x + c), (z - 1, y, 2 * x + c)
        self.y_side, self.x_side, self.core_side = (z, 1 - y, 2 * x + c), (z, y, 2 * (1 - x) + c), (z, y, 2 * x + 1 - c)

    @staticmethod
    def scratch(rows, width, dtype):
        V, D, half = pltpu.VMEM, pltpu.SemaphoreType.DMA, rows // 2
        return [V((2, 2, rows, width), dtype), V((16, rows, width), dtype), V((2, 8, half, width), dtype),
            V((2, 4, half, width), dtype), V((2, 4, 2, half, width), dtype), D((2, 16)), D((2, 2, 8)), D((2, 2, 4)), D((4, 2)), D((2, 4, 2))]

    def greet(self):
        z = self.at[0]
        greet([(z < 3, self.up), (z > 0, self.down), (None, self.y_side), (None, self.x_side), (None, self.core_side)])

    @staticmethod
    def remote(src, dst, send, recv, device):
        return pltpu.make_async_remote_copy(src_ref=src, dst_ref=dst, send_sem=send, recv_sem=recv, device_id=device, device_id_type=MESH)

    def over_core(self, step):
        s = spot(*step_target(step))
        return self.remote(self.part.at[step % 2, 1 - self.at[3]], self.mine.at[s], self.core_sem.at[0, s], self.core_sem.at[1, s], self.core_side)

    def piece(self, zz, yy, xx, h): return self.mine.at[spot(zz, yy, xx), pl.ds(h * self.half, self.half)]

    def first(self, h, zz, other):
        z, y, x, c = self.at
        src = self.piece(zz, other, 1 - x, 0) if h == 0 else self.piece(zz, 1 - y, other, 1)
        s = zz * 2 + other
        return self.remote(src, self.first_in.at[h, s], self.first_sem.at[0, h, s], self.first_sem.at[1, h, s], self.x_side if h == 0 else self.y_side)

    def second(self, h, zz):
        z, y, x, c = self.at
        src = self.piece(zz, 1 - y, x, 0) if h == 0 else self.piece(zz, y, 1 - x, 1)
        return self.remote(src, self.second_in.at[h, zz], self.second_sem.at[0, h, zz], self.second_sem.at[1, h, zz], self.y_side if h == 0 else self.x_side)

    def line(self, h, zz, way):
        z, y, x, c = self.at
        return self.remote(self.piece(zz, y, x, h), self.line_in.at[way, zz, h], self.line_send.at[zz, h], self.line_recv.at[way, zz, h], self.up if way == 0 else self.down)

    def add(self, s, h, arrived):
        at = (s, pl.ds(h * self.half, self.half))
        self.mine[at] = self.mine[at] + arrived[...]

    def stage_core(self, step):
        zz, yy, xx = step_target(step)
        s = spot(zz, yy, xx)
        self.over_core(step).wait_recv()
        self.mine[s] += self.part[step % 2, self.at[3]]
        n = step % 4
        @pl.when(n % 2 == 0)
        def _(): self.first(0, zz, yy).start()
        @pl.when(n < 2)
        def _(): self.first(1, zz, xx).start()

    def stage_first(self, i):
        z, y, x, c = self.at
        zz = nearest(z, i)
        for n in range(2):
            for h, other in ((0, (1 - y, y)[n]), (1, (1 - x, x)[n])):
                self.first(h, zz, other).wait_recv()
                self.add(spot(zz, other, x) if h == 0 else spot(zz, y, other), h, self.first_in.at[h, zz * 2 + other])
                if n == 0: self.second(h, zz).start()

    def stage_second(self, i):
        z, y, x, c = self.at
        zz = nearest(z, i)
        for h in range(2):
            self.second(h, zz).wait_recv()
            self.add(spot(zz, y, x), h, self.second_in.at[h, zz])

    def stage_line(self, i):
        z, y, x, c = self.at
        zz = nearest(z, i)
        for h in range(2):
            for way, from_side, toward in ((0, z > 0, zz > z), (1, z < 3, zz < z)):
                @pl.when(from_side & (toward | (zz == z)))
                def _(h=h, way=way):
                    self.line(h, zz, way).wait_recv()
                    self.add(spot(zz, y, x), h, self.line_in.at[way, zz, h])
                @pl.when(toward)
                def _(h=h, way=way): self.line(h, zz, way).start()

    def follow(self, step):
        @pl.when((step >= 1) & (step <= 16))
        def _(): self.stage_core(step - 1)
        q = step // 4
        @pl.when((step % 4 == 1) & (q >= 2))
        def _(): self.stage_line(5 - q)
        @pl.when((step % 4 == 1) & (q >= 1))
        def _(): self.stage_first(4 - q)
        @pl.when((step % 4 == 3) & (q >= 1))
        def _(): self.stage_second(4 - q)

    def finish(self, steps):
        z, y, x, c = self.at
        if steps == 16:
            self.stage_core(15); self.stage_line(1); self.stage_first(0); self.stage_second(0)
        self.stage_line(0)

    @property
    def own(self): return spot(*self.at[:3])

    def drain(self):
        z, y, x, c = self.at
        self.over_core(14).wait_send(); self.over_core(15).wait_send()
        for zz in range(4):
            for other in range(2):
                for h in range(2): self.first(h, zz, other).wait_send()
            for h in range(2): self.second(h, zz).wait_send()
            @pl.when(zz != z)
            def _(zz=zz):
                for h in range(2): self.line(h, zz, 0).wait_send()

def expert_kernel(normed_ref, cot_ref, code_ref, router_ref, expand_ref, place_ref, gate_ref, up_ref, down_ref,
                  resid_ref, own_normed_ref, own_chosen_ref, own_cot_ref, gain_ref,
                  grad_ref, message_ref, hid_out, gate_out, up_out, normed_in, cot_in, code_in, units, message, in_sem, units_sem, *scratch):
    reduction = Reduction(*scratch[:-3])
    gather = TensorGather(message, message_ref, *scratch[-3:])
    reduction.greet()
    part = reduction.part
    rows, width, wide = grad_ref.shape[0], normed_ref.shape[1], gate_ref.shape[1]
    f32, bf16 = jnp.float32, jnp.bfloat16
    stride = code_ref.shape[0] // 8
    def loads(step):
        slot = step % 2
        zz, yy, xx = step_target(step)
        codes = code_ref.at[pl.ds(pl.multiple_of((zz * 2 + yy) * stride, 16), rows)]
        pairs = ((step_block(normed_ref, step), normed_in), (step_block(cot_ref, step), cot_in), (codes, code_in))
        return [pltpu.make_async_copy(src, dst.at[slot], in_sem.at[n, slot]) for n, (src, dst) in enumerate(pairs)]
    def stores(step):
        slot = step % 2
        return [pltpu.make_async_copy(units.at[slot, n], step_block(dst, step), units_sem.at[n, slot])
                for n, dst in enumerate((hid_out, gate_out, up_out))]
    for one in loads(0): one.start()

    def compute(step):
        slot = step % 2
        for one in loads(step): one.wait()
        @pl.when(step < 15)
        def _():
            for one in loads(step + 1): one.start()
        @pl.when(step >= 2)
        def _():
            for one in stores(step - 2): one.wait()
            reduction.over_core(step - 2).wait_send()
        normed, cot = normed_in[slot], cot_in[slot]
        code = code_in[slot].astype(f32)
        quarter = lax.broadcasted_iota(jnp.int32, code.shape, 1) // (128 // 4) - 2 * step_target(step)[2]
        code = jnp.concatenate([jnp.where(quarter == n, code, 0.0) for n in range(2)], axis=0)
        scores = jnp.where(code > 0.5, nn(normed, router_ref[...]), NEGATIVE)
        scores = jnp.where(code > 0.5, jnp.exp(scores - jnp.max(scores, axis=1, keepdims=True)), 0.0)
        gates = jnp.where(code > 1.5, scores / jnp.sum(scores, axis=1, keepdims=True), 0.0)
        high = gates.astype(bf16)
        low = (gates - high.astype(f32)).astype(bf16)
        grad_gates = jnp.zeros((2 * rows, 128), f32)
        def products(n):
            at = pl.ds(n * 256, 256)
            return (nn(normed, gate_ref[:, at]), nn(normed, up_ref[:, at]), nt(cot, down_ref[at, :]),
                nn(high, expand_ref[:, at]) + nn(low, expand_ref[:, at]))
        ahead = products(0)
        for n in range(wide // 256):
            gate_in, up_in, grad_mid, gate = ahead
            if n + 1 < wide // 256: ahead = products(n + 1)
            at = pl.ds(n * 256, 256)
            sig = lax.logistic(gate_in)
            silu = gate_in * sig
            hidden = silu * up_in
            grad_gates += nn(jnp.where(gate != 0.0, hidden * grad_mid, 0.0).astype(bf16), place_ref[at, :])
            grad_hidden = grad_mid * gate
            units[slot, 0, :, at] = (hidden * gate).astype(bf16)
            units[slot, 1, :, at] = (grad_hidden * up_in * (sig + silu * (1.0 - sig))).astype(bf16)
            units[slot, 2, :, at] = (grad_hidden * silu).astype(bf16)
        for one in stores(step): one.start()
        gate_grad, up_grad = units[slot, 1], units[slot, 2]
        for n in range(width // 512):
            at = pl.ds(n * 512, 512)
            grad = (nt(gate_grad, gate_ref[at, :]) + nt(up_grad, up_ref[at, :])).astype(bf16)
            part[slot, 0, :, at] = grad[:rows]
            part[slot, 1, :, at] = grad[rows:]
        grad_gates = grad_gates.astype(bf16)
        part[slot, 0, :, pl.ds(width, 128)] = grad_gates[:rows]
        part[slot, 1, :, pl.ds(width, 128)] = grad_gates[rows:]
        reduction.over_core(step).start()

    @pl.loop(0, 16)
    def _(step):
        compute(step)
        reduction.follow(step)
    for step in (14, 15):
        for one in stores(step): one.wait()
    reduction.finish(16)
    every, own = pl.ds(0, width), reduction.own
    grad_gates = reduction.mine[own, :, pl.ds(width, 128)].astype(f32)
    grad_gates = grad_gates + pltpu.roll(grad_gates, 64, 1)
    grad_gates = grad_gates + pltpu.roll(grad_gates, 32, 1)
    chosen = own_chosen_ref[...].astype(f32) > 0.5
    scores = jnp.where(chosen, nn(own_normed_ref[...], router_ref[...]), NEGATIVE)
    scores = jnp.where(chosen, jnp.exp(scores - jnp.max(scores, axis=1, keepdims=True)), 0.0)
    gates = scores / jnp.sum(scores, axis=1, keepdims=True)
    grad_logits = (gates * (grad_gates - jnp.sum(gates * grad_gates, axis=1, keepdims=True))).astype(bf16)
    grad = reduction.mine[own, :, every].astype(f32) + nt(grad_logits, router_ref[...])
    values = resid_ref[...]
    inverse = lax.rsqrt(jnp.mean(values * values, axis=-1, keepdims=True) + EPSILON)
    total = own_cot_ref[...].astype(f32) + rms_pull(grad, values, inverse, gain_ref[...])
    grad_ref[...] = total
    message[pl.ds(0, rows), every] = total.astype(bf16)
    message[pl.ds(0, rows), pl.ds(width, 128)] = grad_logits
    first_row = lax.broadcasted_iota(jnp.int32, (16, width), 0)
    message[pl.ds(rows, 16), every] = jnp.where(first_row == 0, jnp.sum(grad * values * inverse, axis=0, keepdims=True), 0.0).astype(bf16)
    message[pl.ds(rows, 16), pl.ds(width, 128)] = jnp.zeros((16, 128), f32).astype(bf16)
    gather.start(); gather.finish()
    reduction.drain()

def run_experts(normed_all, cot_all, codes, router, expand, place, gate_flat, up_flat, down_flat,
                resid, own_normed, own_chosen, own_cot, gain, collective_id):
    total, width = normed_all.shape; rows = total // 32; wide = gate_flat.shape[1]
    bf16 = jnp.bfloat16; D = pltpu.SemaphoreType.DMA; V = pltpu.VMEM; W = width + 128
    anyspec, vspec = pl.BlockSpec(memory_space=pl.ANY), pl.BlockSpec(memory_space=V)
    unit = jax.ShapeDtypeStruct((total, wide), bf16)
    return pl.pallas_call(expert_kernel,
        out_shape=[jax.ShapeDtypeStruct((rows, width), jnp.float32), jax.ShapeDtypeStruct((4, rows + 16, W), bf16), unit, unit, unit],
        in_specs=[anyspec] * 3 + [vspec] * 11, out_specs=[vspec] + [anyspec] * 4,
        scratch_shapes=[V((2, 2 * rows, width), bf16), V((2, 2 * rows, width), bf16), V((2, rows, 128), bf16),
            V((2, 3, 2 * rows, wide), bf16), V((rows + 16, W), bf16), D((3, 2)), D((3, 2)),
            *Reduction.scratch(rows, W, bf16), *TensorGather.scratch()],
        compiler_params=pltpu.CompilerParams(collective_id=collective_id, has_side_effects=True, vmem_limit_bytes=60 << 20))(
            normed_all, cot_all, codes, router, expand, place, gate_flat, up_flat, down_flat, resid, own_normed, own_chosen, own_cot, gain)

def output_kernel(normed_ref, cot_ref, hid_ref, gate_ref, up_ref, down_ref, resid_ref, out_ref, gate_out, up_out, down_out,
                  hid_in, wide_in, thin_in, own_out, hid_sem, in_sem, out_sem, *scratch):
    reduction = Reduction(*scratch[:-3])
    gather = TensorGather(own_out, out_ref, *scratch[-3:])
    reduction.greet()
    part = reduction.part
    rows, width, units = resid_ref.shape[0], normed_ref.shape[1], hid_ref.shape[1]
    f32, bf16 = jnp.float32, jnp.bfloat16
    lag = 2
    def hid_load(step): return pltpu.make_async_copy(step_block(hid_ref, step), hid_in.at[step % 2], hid_sem.at[step % 2])
    def loads(block):
        slot = block % 2
        zz, yy, xx = step_target(2 * block)
        at = pl.ds(pl.multiple_of((zz * 2 + yy) * 4 * rows, 4 * rows), 4 * rows)
        return ([pltpu.make_async_copy(src.at[at], wide_in.at[slot, n], in_sem.at[n, slot]) for n, src in enumerate((normed_ref, cot_ref))]
            + [pltpu.make_async_copy(src.at[at], thin_in.at[slot, n], in_sem.at[2 + n, slot]) for n, src in enumerate((hid_ref, gate_ref, up_ref))])
    for one in loads(0): one.start()
    hid_load(0).start()

    def inner(gate_sum, up_sum, down_sum):
        gate_sum[...] = jnp.zeros_like(gate_sum)
        up_sum[...] = jnp.zeros_like(up_sum)
        down_sum[...] = jnp.zeros_like(down_sum)

        def outputs(step):
            slot = step % 2
            hid_load(step).wait()
            @pl.when(step < 15)
            def _(): hid_load(step + 1).start()
            @pl.when(step >= 2)
            def _(): reduction.over_core(step - 2).wait_send()
            hid = hid_in[slot]
            for n in range(width // 512):
                at = pl.ds(n * 512, 512)
                value = nn(hid, down_ref[:, at]).astype(bf16)
                part[slot, 0, :, at] = value[:rows]
                part[slot, 1, :, at] = value[rows:]
            reduction.over_core(step).start()

        def down_gradient(block):
            slot = block % 2
            for one in loads(block): one.wait()
            @pl.when(block < 7)
            def _():
                for one in loads(block + 1): one.start()
            @pl.when(block < 7)
            def _():
                for n in range(units // 256):
                    at = pl.ds(n * 256, 256)
                    down_sum[at, :] += nn(thin_in[slot, 0, :, at].T, wide_in[slot, 1])

        def gate_gradients(block):
            slot = block % 2
            for n in range(width // 256):
                at = pl.ds(n * 256, 256)
                turned = wide_in[slot, 0, :, at].T
                gate_sum[at, :] += nn(turned, thin_in[slot, 1])
                up_sum[at, :] += nn(turned, thin_in[slot, 2])

        @pl.loop(0, 8 + lag)
        def _(block):
            for n, gradients in enumerate((down_gradient, gate_gradients)):
                step = 2 * block + n
                @pl.when(block < 8)
                def _(): outputs(step)
                @pl.when(block >= lag)
                def _(): gradients(block - lag)
                reduction.follow(step)
        kept = [pltpu.make_async_copy(src, dst, out_sem.at[n])
                for n, (src, dst) in enumerate(((gate_sum, gate_out), (up_sum, up_out), (down_sum, down_out)))]
        for one in kept: one.start()
        reduction.finish(16 + 2 * lag)
        own_out[...] = (resid_ref[...] + reduction.mine[reduction.own].astype(f32)).astype(bf16)
        gather.start(); gather.finish()
        reduction.drain()
        for one in kept: one.wait()
    pl.run_scoped(inner, pltpu.VMEM((width, units), f32), pltpu.VMEM((width, units), f32), pltpu.VMEM((units, width), f32))

def run_outputs(normed_all, cot_all, hidden_gated, gate_grad, up_grad, down_flat, resid, collective_id):
    total, width = normed_all.shape; rows = total // 32; units = hidden_gated.shape[1]
    f32, bf16 = jnp.float32, jnp.bfloat16; D = pltpu.SemaphoreType.DMA; V = pltpu.VMEM; S = jax.ShapeDtypeStruct
    anyspec, vspec = pl.BlockSpec(memory_space=pl.ANY), pl.BlockSpec(memory_space=V)
    return pl.pallas_call(output_kernel,
        out_shape=[S((4, rows, width), bf16), S((width, units), f32), S((width, units), f32), S((units, width), f32)],
        in_specs=[anyspec] * 5 + [vspec] * 2, out_specs=[anyspec] * 4,
        scratch_shapes=[V((2, 2 * rows, units), bf16), V((2, 2, 4 * rows, width), bf16), V((2, 3, 4 * rows, units), bf16), V((rows, width), bf16), D((2,)), D((5, 2)), D((3,)),
            *Reduction.scratch(rows, width, bf16), *TensorGather.scratch()],
        compiler_params=pltpu.CompilerParams(collective_id=collective_id, has_side_effects=True, vmem_limit_bytes=62 << 20))(
            normed_all, cot_all, hidden_gated, gate_grad, up_grad, down_flat, resid)


def inverse_rms(values):
    return lax.rsqrt(jnp.mean(values * values, axis=-1, keepdims=True) + EPSILON)

def attend_kernel(x_ref, gain_ref, qkv_ref, cos_ref, sin_ref, head_gain_ref, seg_rows_ref, seg_cols_ref,
                  normed_ref, raw_ref, q_ref, kv_ref, kv_other_ref, full_ref, heads_ref, lse_ref, bias, send_sem, recv_sem):
    z, y, x, c = coords()
    other = (z, 1 - y, 2 * x + c)
    greet([(None, other)])
    f32, bf16 = jnp.float32, jnp.bfloat16
    rows = x_ref.shape[0]; heads = q_ref.shape[1] // HEAD_SIZE; q_width = heads * HEAD_SIZE
    values = x_ref[...].astype(f32)
    normed_ref[...] = (values * inverse_rms(values) * gain_ref[...]).astype(bf16)
    def finish(raw, n):
        normed = raw * inverse_rms(raw) * head_gain_ref[pl.ds(n, 1), :]
        return (normed * cos_ref[...] + pltpu.roll(normed, HEAD_SIZE // 2, 1) * sin_ref[...]).astype(bf16)
    raw_kv = nn(normed_ref[...], qkv_ref[:, pl.ds(q_width, 2 * HEAD_SIZE)])
    raw_ref[:, pl.ds(q_width, HEAD_SIZE)] = raw_kv[:, :HEAD_SIZE]
    kv_ref[:, pl.ds(0, HEAD_SIZE)] = finish(raw_kv[:, :HEAD_SIZE], 1)
    kv_ref[:, pl.ds(HEAD_SIZE, HEAD_SIZE)] = raw_kv[:, HEAD_SIZE:].astype(bf16)
    move = pltpu.make_async_remote_copy(src_ref=kv_ref, dst_ref=kv_other_ref, send_sem=send_sem, recv_sem=recv_sem,
        device_id=other, device_id_type=MESH)
    @pl.when(y == 0)
    def _():
        move.start()
        kv_other_ref[...] = jnp.zeros_like(kv_other_ref)
    @pl.loop(0, heads // 2)
    def _(n):
        at = pl.ds(pl.multiple_of(n * 2 * HEAD_SIZE, 2 * HEAD_SIZE), 2 * HEAD_SIZE)
        raw = nn(normed_ref[...], qkv_ref[:, at])
        raw_ref[:, at] = raw
        for m in range(2):
            one = pl.ds(pl.multiple_of((2 * n + m) * HEAD_SIZE, HEAD_SIZE), HEAD_SIZE)
            q_ref[:, one] = finish(raw[:, m * HEAD_SIZE:(m + 1) * HEAD_SIZE], 0)
    row_id = lax.broadcasted_iota(jnp.int32, (rows, rows), 0)
    col_id = lax.broadcasted_iota(jnp.int32, (rows, rows), 1)
    bias[0] = jnp.where((seg_rows_ref[...] == seg_cols_ref[pl.ds(0, 1), :]) & (col_id <= row_id), 0.0, NEGATIVE)
    bias[1] = jnp.where(seg_rows_ref[...] == seg_cols_ref[pl.ds(1, 1), :], 0.0, NEGATIVE)
    lse_ref[...] = jnp.zeros_like(lse_ref)
    scale = HEAD_SIZE ** -0.5
    lane = lax.broadcasted_iota(jnp.int32, (rows, HEAD_SIZE), 1)
    def head(h, blocks):
        at = pl.ds(pl.multiple_of(h * HEAD_SIZE, HEAD_SIZE), HEAD_SIZE)
        query = q_ref[:, at]
        refs = (kv_ref, kv_other_ref)[:blocks]
        scores = [nt(query, ref[:, pl.ds(0, HEAD_SIZE)]) * scale + bias[n] for n, ref in enumerate(refs)]
        top = functools.reduce(jnp.maximum, [jnp.max(s, axis=1, keepdims=True) for s in scores])
        weights = [jnp.exp(s - top) for s in scores]
        total = sum(jnp.sum(w, axis=1, keepdims=True) for w in weights)
        inverse = 1.0 / total
        full = sum(nn((w * inverse).astype(bf16), ref[:, pl.ds(HEAD_SIZE, HEAD_SIZE)]) for w, ref in zip(weights, refs))
        full_ref[:, at] = full
        heads_ref[:, at] = full.astype(bf16)
        lse_ref[...] = jnp.where(lane == h, top + jnp.log(total), lse_ref[...])
    @pl.when(y == 0)
    def _():
        @pl.loop(0, heads)
        def _(h): head(h, 1)
        move.wait_send()
    @pl.when(y == 1)
    def _():
        move.wait_recv()
        @pl.loop(0, heads)
        def _(h): head(h, 2)

def attend(x, gain, qkv, cos, sin, head_gains, seg_rows, seg_cols, collective_id):
    rows, width = x.shape; q_width = qkv.shape[1] - 2 * HEAD_SIZE
    V = pltpu.VMEM; f32, bf16 = jnp.float32, jnp.bfloat16; S = jax.ShapeDtypeStruct
    vspec = pl.BlockSpec(memory_space=V)
    return pl.pallas_call(attend_kernel,
        out_shape=[S((rows, width), bf16), S((rows, q_width + HEAD_SIZE), f32), S((rows, q_width), bf16), S((rows, 2 * HEAD_SIZE), bf16),
            S((rows, 2 * HEAD_SIZE), bf16), S((rows, q_width), f32), S((rows, q_width), bf16), S((rows, HEAD_SIZE), f32)],
        in_specs=[vspec] * 8, out_specs=[vspec] * 8,
        scratch_shapes=[V((2, rows, rows), f32), pltpu.SemaphoreType.DMA, pltpu.SemaphoreType.DMA],
        compiler_params=pltpu.CompilerParams(collective_id=collective_id, has_side_effects=True, vmem_limit_bytes=48 << 20))(
            x, gain, qkv, cos, sin, head_gains, seg_rows, seg_cols)

def attend_back_kernel(cot_ref, out_w_ref, q_ref, kv_ref, kv_other_ref, raw_ref, full_ref, lse_ref, cos_ref, sin_ref, head_gain_ref,
                       seg_rows_ref, seg_cols_ref, grad_ref, gains_ref, grad_heads, delta, stats, bias, grad_q, grad_kv, kv_send, kv_in, send_sem, recv_sem):
    z, y, x, c = coords()
    other = (z, 1 - y, 2 * x + c)
    greet([(None, other)])
    f32, bf16 = jnp.float32, jnp.bfloat16
    rows = q_ref.shape[0]; heads = q_ref.shape[1] // HEAD_SIZE; q_width = heads * HEAD_SIZE
    scale = HEAD_SIZE ** -0.5
    lane = lax.broadcasted_iota(jnp.int32, (rows, HEAD_SIZE), 1)
    delta[...] = jnp.zeros_like(delta)
    @pl.loop(0, heads // 2)
    def _(n):
        at = pl.ds(pl.multiple_of(n * 2 * HEAD_SIZE, 2 * HEAD_SIZE), 2 * HEAD_SIZE)
        grad = nn(cot_ref[...], out_w_ref[:, at]).astype(bf16)
        grad_heads[:, at] = grad
        product = grad.astype(f32) * full_ref[:, at]
        for m in range(2):
            one = jnp.sum(product[:, m * HEAD_SIZE:(m + 1) * HEAD_SIZE], axis=1, keepdims=True)
            delta[...] = jnp.where(lane == 2 * n + m, one, delta[...])
    stats[0] = lse_ref[...].T
    stats[1] = delta[...].T
    key_id = lax.broadcasted_iota(jnp.int32, (rows, rows), 0)
    query_id = lax.broadcasted_iota(jnp.int32, (rows, rows), 1)
    def block(ref, seg_keys, causal):
        same = seg_keys == seg_cols_ref[pl.ds(0, 1), :]
        bias[...] = jnp.where(same & (key_id <= query_id) if causal else same, 0.0, NEGATIVE)
        grad_kv[...] = jnp.zeros_like(grad_kv)
        key, value = ref[:, pl.ds(0, HEAD_SIZE)], ref[:, pl.ds(HEAD_SIZE, HEAD_SIZE)]
        @pl.loop(0, heads)
        def _(h):
            at = pl.ds(pl.multiple_of(h * HEAD_SIZE, HEAD_SIZE), HEAD_SIZE)
            query, grad = q_ref[:, at], grad_heads[:, at]
            probs = jnp.exp(nt(key, query) * scale + bias[...] - stats[0, pl.ds(h, 1), :])
            grad_scores = (probs * (nt(value, grad) - stats[1, pl.ds(h, 1), :])).astype(bf16)
            grad_kv[:, pl.ds(0, HEAD_SIZE)] += nn(grad_scores, query) * scale
            grad_kv[:, pl.ds(HEAD_SIZE, HEAD_SIZE)] += nn(probs.astype(bf16), grad)
            grad_q[:, at] += lax.dot_general(grad_scores, key, (((0,), (0,)), ((), ())), preferred_element_type=f32) * scale
    grad_q[...] = jnp.zeros_like(grad_q)
    move = pltpu.make_async_remote_copy(src_ref=kv_send, dst_ref=kv_in, send_sem=send_sem, recv_sem=recv_sem, device_id=other, device_id_type=MESH)
    @pl.when(y == 1)
    def _():
        block(kv_other_ref, seg_rows_ref[1], False)
        kv_send[...] = grad_kv[...].astype(bf16)
        move.start()
    block(kv_ref, seg_rows_ref[0], True)
    @pl.when(y == 0)
    def _():
        move.wait_recv()
        grad_kv[...] += kv_in[...].astype(f32)
    def pull(grad, raw, n):
        turned = grad * cos_ref[...] - pltpu.roll(grad, HEAD_SIZE // 2, 1) * sin_ref[...]
        inverse = inverse_rms(raw)
        unit = raw * inverse
        gains_ref[pl.ds(n, 1), :] += jnp.sum(turned * unit, axis=0, keepdims=True)
        scaled = turned * head_gain_ref[pl.ds(n, 1), :]
        return (inverse * (scaled - unit * jnp.mean(scaled * unit, axis=1, keepdims=True))).astype(bf16)
    gains_ref[...] = jnp.zeros_like(gains_ref)
    @pl.loop(0, heads)
    def _(h):
        at = pl.ds(pl.multiple_of(h * HEAD_SIZE, HEAD_SIZE), HEAD_SIZE)
        grad_ref[:, at] = pull(grad_q[:, at], raw_ref[:, at], 0)
    at = pl.ds(q_width, HEAD_SIZE)
    grad_ref[:, at] = pull(grad_kv[:, pl.ds(0, HEAD_SIZE)], raw_ref[:, at], 1)
    grad_ref[:, pl.ds(q_width + HEAD_SIZE, HEAD_SIZE)] = grad_kv[:, pl.ds(HEAD_SIZE, HEAD_SIZE)].astype(bf16)
    @pl.when(y == 1)
    def _(): move.wait_send()

def attend_back(cot, out_w, q, kv, kv_other, raw, full, lse, cos, sin, head_gains, seg_rows, seg_cols, collective_id):
    rows, q_width = q.shape
    V = pltpu.VMEM; f32, bf16 = jnp.float32, jnp.bfloat16; S = jax.ShapeDtypeStruct
    vspec = pl.BlockSpec(memory_space=V)
    return pl.pallas_call(attend_back_kernel,
        out_shape=[S((rows, q_width + 2 * HEAD_SIZE), bf16), S((8, HEAD_SIZE), f32)],
        in_specs=[vspec] * 13, out_specs=[vspec] * 2,
        scratch_shapes=[V((rows, q_width), bf16), V((rows, HEAD_SIZE), f32), V((2, HEAD_SIZE, rows), f32), V((rows, rows), f32), V((rows, q_width), f32),
            V((rows, 2 * HEAD_SIZE), f32), V((rows, 2 * HEAD_SIZE), bf16), V((rows, 2 * HEAD_SIZE), bf16), pltpu.SemaphoreType.DMA, pltpu.SemaphoreType.DMA],
        compiler_params=pltpu.CompilerParams(collective_id=collective_id, has_side_effects=True, vmem_limit_bytes=48 << 20))(
            cot, out_w, q, kv, kv_other, raw, full, lse, cos, sin, head_gains, seg_rows, seg_cols)


def gathered_local(
    hidden_in,
    attn_gain,
    w_query,
    key_weight,
    value_weight,
    w_output,
    query_gain,
    key_gain,
    ffn_gain,
    router,
    gate_weight,
    up_weight,
    down_weight,
    routes,
    segments,
    cotangent,
):
    bf16, f32 = jnp.bfloat16, jnp.float32
    context_size = lax.axis_size(CONTEXT)
    tensor_size = lax.axis_size(TENSOR)
    group_count = lax.axis_size(FSDP) * context_size
    fsdp_rank = lax.axis_index(FSDP)
    context_rank = lax.axis_index(CONTEXT)
    tensor_rank = lax.axis_index(TENSOR)
    group_rank = fsdp_rank * context_size + context_rank
    row_count, width = hidden_in.shape[1:]
    own_count = row_count // tensor_size
    own_start = tensor_rank * own_count
    local_experts, _, hidden_width = gate_weight.shape
    experts_total = router.shape[1]
    first_expert = group_rank * local_experts
    capacity = 9 * row_count * TOPK // (8 * experts_total)
    query_width = w_query.shape[1]

    expert_ids = jnp.arange(experts_total, dtype=jnp.int32)
    chosen = jnp.any(routes[0][..., None] == expert_ids, axis=1)
    kept = chosen & (earlier_counts(chosen) < capacity)
    code = chosen.astype(bf16) + kept.astype(bf16)
    chosen_own = lax.dynamic_slice_in_dim(chosen, own_start, own_count, 0)
    code = code.reshape(tensor_size, own_count, experts_total).transpose(1, 0, 2)

    pieces = (code, router, attn_gain, ffn_gain, query_gain, key_gain, segments)
    small = jnp.concatenate([piece.astype(bf16).reshape(-1) for piece in pieces])
    small = jnp.pad(small, (0, -small.size % 2048)).reshape(-1, 128)
    qkv_weight = jnp.concatenate([w_query, key_weight, value_weight], axis=1)
    pieces_of = [(0, 0, small.shape[0], 0)]
    for array in (1, 2):
        pieces_of += [(array, 0, 112, 0), (array, 112, 96, 0), (array, 208, 48, 1)]
    small, qkv_full, full_output = gather_groups((small, qkv_weight, w_output), tuple(pieces_of), 1)
    grad_out_own = lax.dynamic_slice_in_dim(cotangent[0], own_start, own_count, 0)
    grad_out_own, codes = lax.optimization_barrier((grad_out_own, small))
    grad_out_all = lax.all_gather(grad_out_own, EVERYONE, axis=0, tiled=True)
    small = small.reshape(group_count, -1)
    parts, at = [], code.size
    for piece in pieces[1:]:
        parts.append(small[:, at : at + piece.size])
        at += piece.size
    full_router = parts[0].reshape(width, experts_total)
    gain_attn, gain_ffn, gain_query, gain_key = (
        part.reshape(-1).astype(f32) for part in parts[1:5]
    )
    head_gains = jnp.stack([gain_query, gain_key])
    all_segments = parts[5].astype(jnp.int32)

    own_seg = segments[0]
    first_seg = lax.dynamic_index_in_dim(all_segments, group_rank - context_rank, 0, keepdims=False)
    other_seg = lax.dynamic_index_in_dim(
        all_segments, group_rank + 1 - 2 * context_rank, 0, keepdims=False
    )
    smaller = jnp.sum((own_seg[None, :] < own_seg[:, None]).astype(jnp.int32), axis=1)
    smaller_first = jnp.sum((first_seg[None, :] < own_seg[:, None]).astype(jnp.int32), axis=1)
    positions = jnp.arange(row_count, dtype=jnp.int32) - smaller
    positions = positions + context_rank * (row_count - smaller_first)
    cosine_table, sine_table = rope_tables(positions, HEAD_SIZE)
    turn = jnp.where(jnp.arange(HEAD_SIZE) < HEAD_SIZE // 2, -1.0, 1.0)
    sine_table = sine_table * turn
    seg_rows = jnp.stack([own_seg, other_seg])

    normed_one, raw, query, kv, kv_other, heads_full, heads_low, log_total = attend(
        hidden_in[0],
        gain_attn[None],
        qkv_full,
        cosine_table,
        sine_table,
        head_gains,
        own_seg[:, None],
        seg_rows,
        8,
    )
    input_own = lax.dynamic_slice_in_dim(hidden_in[0], own_start, own_count, 0)
    residual_own, normed_own, normed_all = mix_heads(
        heads_low, full_output, input_own, gain_ffn[None], 3
    )

    units = local_experts * hidden_width
    gate_flat = gate_weight.transpose(1, 0, 2).reshape(width, units)
    up_flat = up_weight.transpose(1, 0, 2).reshape(width, units)
    down_flat = down_weight.reshape(units, width)
    unit_expert = first_expert + jnp.arange(units, dtype=jnp.int32) // hidden_width
    lane_ids = jnp.arange(tensor_size * experts_total, dtype=jnp.int32)
    expand = (lane_ids[:, None] % experts_total == unit_expert[None, :]).astype(bf16)
    column = tensor_rank * experts_total + unit_expert
    place = (column[:, None] == lane_ids[None, :]).astype(bf16)
    router_lanes = jnp.concatenate([full_router] * tensor_size, axis=1)
    grad_resid_own, message, hidden_gated, gate_grad, up_grad = run_experts(
        normed_all,
        grad_out_all,
        codes,
        router_lanes,
        expand,
        place,
        gate_flat,
        up_flat,
        down_flat,
        residual_own,
        normed_own,
        jnp.pad(chosen_own.astype(bf16), ((0, 0), (0, 128 - experts_total))),
        grad_out_own,
        gain_ffn[None],
        4,
    )
    grad_attn = message[:, :own_count, :width].reshape(row_count, width)
    grad_raw, head_gain_grads = attend_back(
        grad_attn,
        full_output,
        query,
        kv,
        kv_other,
        raw,
        heads_full,
        log_total,
        cosine_table,
        sine_table,
        head_gains,
        seg_rows[:, :, None],
        seg_rows,
        9,
    )
    group_logits = message[:, :own_count, width:].reshape(row_count, 128)
    grad_gain_ffn = jnp.sum(message[:, own_count, :width].astype(f32), axis=0)
    normed_group = lax.dynamic_slice_in_dim(normed_all, group_rank * row_count, row_count, 0)
    grad_router = matmul_tn(normed_group, group_logits)
    extra = jnp.where(jnp.arange(128) == experts_total, grad_gain_ffn[:, None], grad_router)
    grad_w_output = jnp.concatenate([matmul_tn(grad_attn, heads_low), extra], axis=1)
    grad_w_output = lax.psum_scatter(
        grad_w_output.astype(bf16), GROUPS, scatter_dimension=0, tiled=True
    )

    message = pull_inputs(
        grad_raw, qkv_full, hidden_in[0], gain_attn[None], head_gain_grads, grad_resid_own, 6
    )
    input_grad = message[:, :own_count].reshape(row_count, width).astype(f32)
    gain_rows = jnp.sum(message[:, own_count : own_count + 2].astype(f32), axis=0)
    head_gains_grad = jnp.pad(
        gain_rows[1, : 2 * HEAD_SIZE].reshape(2, group_count, -1),
        ((0, 0), (0, 0), (0, (width - HEAD_SIZE) // group_count)),
    ).reshape(2, width)
    extra = jnp.pad(
        jnp.stack([gain_rows[0], head_gains_grad[0], head_gains_grad[1]], axis=1),
        ((0, 0), (0, 125)),
    )
    grad_qkv = jnp.concatenate([matmul_tn(normed_one, grad_raw), extra], axis=1)
    grad_qkv, hidden_gated = lax.optimization_barrier((grad_qkv.astype(bf16), hidden_gated))
    grad_qkv = lax.psum_scatter(grad_qkv, GROUPS, scatter_dimension=0, tiled=True)
    output, grad_w_gate, grad_w_up, grad_w_down = run_outputs(
        normed_all, grad_out_all, hidden_gated, gate_grad, up_grad, down_flat, residual_own, 10
    )
    own_hidden = lax.dynamic_slice_in_dim(hidden_gated, group_rank * row_count, row_count, 0)
    grad_w_down = grad_w_down + matmul_tn(own_hidden, cotangent[0])

    def by_expert(grad):
        return grad.reshape(width, local_experts, hidden_width).transpose(1, 0, 2)

    grad_w_gate, grad_w_up = by_expert(grad_w_gate), by_expert(grad_w_up)
    output = output.reshape(row_count, width)
    output, grad_w_output = lax.optimization_barrier((output, grad_w_output))
    grad_w_output = [
        grad_w_output[:, :query_width].astype(f32),
        grad_w_output[:, query_width + experts_total].astype(f32),
        grad_w_output[:, query_width : query_width + experts_total].astype(f32),
    ]
    grad_qkv, grad_w_output, grad_w_gate, grad_w_up, grad_w_down = lax.optimization_barrier(
        (grad_qkv, grad_w_output, grad_w_gate, grad_w_up, grad_w_down)
    )
    value_at, extra_at = query_width + HEAD_SIZE, query_width + 2 * HEAD_SIZE
    return (
        output[None],
        input_grad[None],
        grad_qkv[:, extra_at].astype(f32),
        grad_qkv[:, :query_width].astype(f32),
        grad_qkv[:, query_width:value_at].astype(f32),
        grad_qkv[:, value_at:extra_at].astype(f32),
        grad_w_output[0],
        grad_qkv[: query_gain.shape[0], extra_at + 1].astype(f32),
        grad_qkv[: key_gain.shape[0], extra_at + 2].astype(f32),
        grad_w_output[1],
        grad_w_output[2],
        grad_w_gate,
        grad_w_up,
        grad_w_down.reshape(down_weight.shape),
    )


def local(*arrays):
    sizes = tuple(lax.axis_size(name) for name in EVERYONE)
    return (gathered_local if sizes == (4, 2, 4) and arrays[9].shape[1] == 32 else routed_local)(*arrays)


def solution(mesh):
    in_specs = (
        P(FSDP, CONTEXT, None),
        P(GROUPS),
        P(GROUPS, TENSOR),
        P(GROUPS, TENSOR),
        P(GROUPS, TENSOR),
        P(GROUPS, TENSOR),
        P(GROUPS),
        P(GROUPS),
        P(GROUPS),
        P(GROUPS, None),
        P(GROUPS, None, TENSOR),
        P(GROUPS, None, TENSOR),
        P(GROUPS, TENSOR, None),
        P(FSDP, CONTEXT, None),
        P(FSDP, CONTEXT),
        P(FSDP, CONTEXT, None),
    )
    out_specs = (
        P(FSDP, CONTEXT, None),
        P(FSDP, CONTEXT, None),
        P(GROUPS),
        P(GROUPS, TENSOR),
        P(GROUPS, TENSOR),
        P(GROUPS, TENSOR),
        P(GROUPS, TENSOR),
        P(GROUPS),
        P(GROUPS),
        P(GROUPS),
        P(GROUPS, None),
        P(GROUPS, None, TENSOR),
        P(GROUPS, None, TENSOR),
        P(GROUPS, TENSOR, None),
    )
    return jax.shard_map(local, mesh=mesh, in_specs=in_specs, out_specs=out_specs, check_vma=False)
```

```python
import functools
import math

import jax
import jax.numpy as jnp
from jax import lax
from jax.experimental import pallas as pl
from jax.experimental.pallas import tpu as pltpu
from jax.sharding import PartitionSpec as P

HEAD_SIZE = 128
TOPK = 8
FSDP, CONTEXT, TENSOR = "fsdp", "context", "tensor"
GROUPS = (FSDP, CONTEXT)
EVERYONE = (FSDP, CONTEXT, TENSOR)


EPSILON = 1e-06
ROPE_BASE = 1000000.0
NEGATIVE = -1e30


def rms_scale(values, gain_vec):
    return (
        values * lax.rsqrt(jnp.mean(values * values, axis=-1, keepdims=True) + EPSILON) * gain_vec
    )


def rotate(values):
    half_width = values.shape[-1] // 2
    return jnp.concatenate([-values[..., half_width:], values[..., :half_width]], axis=-1)


def rope_tables(positions, head_width):
    step_index = jnp.arange(head_width // 2, dtype=jnp.float32)
    inverse = jnp.exp(step_index * (-2.0 * math.log(ROPE_BASE) / head_width))
    angles = positions.astype(jnp.float32)[:, None] * inverse[None, :]
    cosine_table = jnp.cos(angles)
    sine_table = jnp.sin(angles)
    return (
        jnp.concatenate([cosine_table, cosine_table], -1),
        jnp.concatenate([sine_table, sine_table], -1),
    )


def doc_positions(segment):
    token_index = jnp.arange(segment.shape[0], dtype=jnp.int32)
    smaller = (segment[None, :] < segment[:, None]).astype(jnp.int32)
    return token_index - jnp.sum(smaller, axis=1)


def earlier_counts(chosen):
    rows = chosen.shape[0]
    row_id = lax.broadcasted_iota(jnp.int32, (rows, rows), 0)
    col_id = lax.broadcasted_iota(jnp.int32, (rows, rows), 1)
    earlier = (col_id < row_id).astype(jnp.bfloat16)
    return matmul(earlier, chosen.astype(jnp.bfloat16))


def qk_finish(raw_values, gain_vec, cosine_table, sine_table):
    normed = rms_scale(raw_values, gain_vec)
    return normed * cosine_table + rotate(normed) * sine_table


def matmul(left_side, right_side):
    return jnp.dot(left_side, right_side, preferred_element_type=jnp.float32)


def matmul_nt(left_side, right_side):
    return lax.dot_general(
        left_side, right_side, (((1,), (1,)), ((), ())), preferred_element_type=jnp.float32
    )


def matmul_tn(left_side, right_side):
    return lax.dot_general(
        left_side, right_side, (((0,), (0,)), ((), ())), preferred_element_type=jnp.float32
    )


def block_scores(query_vectors, keys_all, seg_all, query_seg, query_index, key_ids, block_id, key_block):
    leading_row = block_id * key_block
    keys_part = lax.dynamic_slice_in_dim(keys_all, leading_row, key_block, 0)
    seg_part = lax.dynamic_slice_in_dim(seg_all, leading_row, key_block, 0)
    key_index = lax.dynamic_slice_in_dim(key_ids, leading_row, key_block, 0)
    score_scale = query_vectors.shape[2] ** (-0.5)
    scores = (
        jnp.einsum("qhd,kd->hqk", query_vectors, keys_part, preferred_element_type=jnp.float32)
        * score_scale
    )
    allowed = (query_seg[:, None] == seg_part[None, :]) & (
        key_index[None, :] <= query_index[:, None]
    )
    return (scores, allowed[None, :, :], keys_part)


def attention_forward(
    query_vectors, keys_all, values_all, seg_all, query_seg, query_index, key_ids, key_block
):
    row_count, head_count, head_width = query_vectors.shape
    block_count = keys_all.shape[0] // key_block

    def stats_step(running, block_id):
        run_max, run_sum = running
        scores, allowed, unused = block_scores(
            query_vectors, keys_all, seg_all, query_seg, query_index, key_ids, block_id, key_block
        )
        masked = jnp.where(allowed, scores, NEGATIVE)
        new_max = jnp.maximum(run_max, jnp.max(masked, axis=2))
        weights = jnp.where(allowed, jnp.exp(masked - new_max[:, :, None]), 0.0)
        run_sum = run_sum * jnp.exp(run_max - new_max) + jnp.sum(weights, axis=2)
        return ((new_max, run_sum), None)

    start_state = (
        jnp.full((head_count, row_count), NEGATIVE, jnp.float32),
        jnp.zeros((head_count, row_count), jnp.float32),
    )
    (run_max, run_sum), ignored = lax.scan(
        stats_step, start_state, jnp.arange(block_count, dtype=jnp.int32)
    )
    log_total = run_max + jnp.log(run_sum)

    def value_step(accumulated, block_id):
        scores, allowed, unused = block_scores(
            query_vectors, keys_all, seg_all, query_seg, query_index, key_ids, block_id, key_block
        )
        prob_block = jnp.where(allowed, jnp.exp(scores - log_total[:, :, None]), 0.0).astype(
            jnp.bfloat16
        )
        values_part = lax.dynamic_slice_in_dim(values_all, block_id * key_block, key_block, 0)
        accumulated = accumulated + jnp.einsum(
            "hqk,kd->qhd", prob_block, values_part, preferred_element_type=jnp.float32
        )
        return (accumulated, None)

    heads_full, ignored = lax.scan(
        value_step,
        jnp.zeros((row_count, head_count, head_width), jnp.float32),
        jnp.arange(block_count, dtype=jnp.int32),
    )
    return (heads_full, log_total)


def attention_backward(
    query_vectors,
    keys_all,
    values_all,
    seg_all,
    query_seg,
    query_index,
    key_ids,
    key_block,
    log_total,
    grad_heads,
    row_delta,
):
    row_count, head_count, head_width = query_vectors.shape
    block_count = keys_all.shape[0] // key_block
    score_scale = head_width ** (-0.5)

    def grad_step(grad_query, block_id):
        scores, allowed, keys_part = block_scores(
            query_vectors, keys_all, seg_all, query_seg, query_index, key_ids, block_id, key_block
        )
        values_part = lax.dynamic_slice_in_dim(values_all, block_id * key_block, key_block, 0)
        prob_block = jnp.where(allowed, jnp.exp(scores - log_total[:, :, None]), 0.0)
        grad_prob = jnp.einsum(
            "qhd,kd->hqk", grad_heads, values_part, preferred_element_type=jnp.float32
        )
        grad_score = (prob_block * (grad_prob - row_delta[:, :, None])).astype(jnp.bfloat16)
        grad_query = (
            grad_query
            + jnp.einsum("hqk,kd->qhd", grad_score, keys_part, preferred_element_type=jnp.float32)
            * score_scale
        )
        grad_key = (
            jnp.einsum("hqk,qhd->kd", grad_score, query_vectors, preferred_element_type=jnp.float32)
            * score_scale
        )
        grad_value = jnp.einsum(
            "hqk,qhd->kd",
            prob_block.astype(jnp.bfloat16),
            grad_heads,
            preferred_element_type=jnp.float32,
        )
        return (grad_query, (grad_key, grad_value))

    grad_query, (grad_key, grad_value) = lax.scan(
        grad_step,
        jnp.zeros((row_count, head_count, head_width), jnp.float32),
        jnp.arange(block_count, dtype=jnp.int32),
    )
    return (grad_query, grad_key.reshape(-1, head_width), grad_value.reshape(-1, head_width))


def to_experts(buffer):
    return lax.all_to_all(buffer, GROUPS, split_axis=0, concat_axis=1, tiled=True)


def from_experts(result_rows):
    return lax.all_to_all(result_rows, GROUPS, split_axis=1, concat_axis=0, tiled=True)


def pick_pairs(buffer, target, row_count):
    model_width = buffer.shape[2]
    flat_rows = jnp.concatenate(
        [buffer.reshape(-1, model_width), jnp.zeros((1, model_width), buffer.dtype)], axis=0
    )
    return flat_rows[target].reshape(row_count, TOPK, model_width)


def routed_local(
    hidden_in,
    attn_gain,
    w_query,
    key_weight,
    value_weight,
    w_output,
    query_gain,
    key_gain,
    ffn_gain,
    router,
    gate_weight,
    up_weight,
    down_weight,
    routes,
    segments,
    cotangent,
):
    context_rank = lax.axis_index(CONTEXT)
    input_rows = hidden_in[0].astype(jnp.float32)
    row_count, model_width = input_rows.shape
    gathered = (
        lax.all_gather(w_query, GROUPS, axis=0, tiled=True),
        lax.all_gather(key_weight, GROUPS, axis=0, tiled=True),
        lax.all_gather(value_weight, GROUPS, axis=0, tiled=True),
        lax.all_gather(w_output, GROUPS, axis=0, tiled=True),
        lax.all_gather(router, GROUPS, axis=0, tiled=True),
        lax.all_gather(attn_gain, GROUPS, axis=0, tiled=True),
        lax.all_gather(ffn_gain, GROUPS, axis=0, tiled=True),
        lax.all_gather(query_gain, GROUPS, axis=0, tiled=True),
        lax.all_gather(key_gain, GROUPS, axis=0, tiled=True),
    )
    full_query, full_key, full_value, full_output, full_router = (
        gathered[0],
        gathered[1],
        gathered[2],
        gathered[3],
        gathered[4],
    )
    gain_attn = gathered[5].astype(jnp.float32)
    gain_ffn = gathered[6].astype(jnp.float32)
    gain_query = gathered[7].astype(jnp.float32)
    gain_key = gathered[8].astype(jnp.float32)
    local_heads = full_query.shape[1] // HEAD_SIZE
    seg_all = lax.all_gather(segments, CONTEXT, axis=1, tiled=True)[0]
    length = seg_all.shape[0]
    start_row = context_rank * row_count
    positions = lax.dynamic_slice_in_dim(doc_positions(seg_all), start_row, row_count)
    cosine_table, sine_table = rope_tables(positions, HEAD_SIZE)
    query_seg = segments[0]
    query_index = start_row + jnp.arange(row_count, dtype=jnp.int32)
    key_ids = jnp.arange(length, dtype=jnp.int32)
    key_block = min(512, length)

    def query_finish(raw_values, gain_vec):
        return qk_finish(raw_values, gain_vec, cosine_table[:, None, :], sine_table[:, None, :])

    def key_finish(raw_values, gain_vec):
        return qk_finish(raw_values, gain_vec, cosine_table, sine_table)

    normed_f, first_pull = jax.vjp(rms_scale, input_rows, gain_attn)
    attention_normalized = normed_f.astype(jnp.bfloat16)
    query_unrotated = matmul(attention_normalized, full_query).reshape(
        row_count, local_heads, HEAD_SIZE
    )
    key_unrotated = matmul(attention_normalized, full_key)
    value_raw = matmul(attention_normalized, full_value)
    query_f, query_pull = jax.vjp(query_finish, query_unrotated, gain_query)
    key_f, key_pull = jax.vjp(key_finish, key_unrotated, gain_key)
    query_vectors = query_f.astype(jnp.bfloat16)
    keys_all, values_all = (
        lax.all_gather(key_f.astype(jnp.bfloat16), CONTEXT, axis=0, tiled=True),
        lax.all_gather(value_raw.astype(jnp.bfloat16), CONTEXT, axis=0, tiled=True),
    )
    heads_full, log_total = attention_forward(
        query_vectors, keys_all, values_all, seg_all, query_seg, query_index, key_ids, key_block
    )
    heads_low = heads_full.reshape(row_count, local_heads * HEAD_SIZE).astype(jnp.bfloat16)
    attn_out = lax.psum(matmul_nt(heads_low, full_output).astype(jnp.bfloat16), TENSOR).astype(
        jnp.float32
    )
    residual_stream = input_rows + attn_out
    second_f, second_pull = jax.vjp(rms_scale, residual_stream, gain_ffn)
    feedforward_normalized = second_f.astype(jnp.bfloat16)
    router_scores = matmul(feedforward_normalized, full_router)
    experts_total = full_router.shape[1]
    route_ids = routes[0]
    chosen = route_ids[:, :, None] == jnp.arange(experts_total, dtype=jnp.int32)
    selected = jnp.sum(jnp.where(chosen, router_scores[:, None, :], 0.0), axis=2)
    gate_probs = jax.nn.softmax(selected, axis=-1)
    capacity = 9 * row_count * TOPK // (8 * experts_total)
    before = earlier_counts(jnp.any(chosen, axis=1)).astype(jnp.int32)
    slot_index = jnp.sum(jnp.where(chosen, before[:, None, :], 0), axis=2)
    target = jnp.where(
        slot_index < capacity, route_ids * capacity + slot_index, experts_total * capacity
    ).reshape(-1)
    source = jnp.repeat(jnp.arange(row_count, dtype=jnp.int32), TOPK)
    send_rows = (
        jnp.zeros((experts_total * capacity, model_width), jnp.bfloat16)
        .at[target]
        .set(feedforward_normalized[source], mode="drop")
    )
    expert_input_rows = to_experts(send_rows.reshape(experts_total, capacity, model_width))
    gate_activation_input = jnp.einsum(
        "phu,puo->pho", expert_input_rows, gate_weight, preferred_element_type=jnp.float32
    )
    up_activation_input = jnp.einsum(
        "phu,puo->pho", expert_input_rows, up_weight, preferred_element_type=jnp.float32
    )
    sigmoid_gate = jax.nn.sigmoid(gate_activation_input)
    silu_gate = gate_activation_input * sigmoid_gate
    hidden_middle = (silu_gate * up_activation_input).astype(jnp.bfloat16)
    expert_part = jnp.einsum(
        "pic,pcw->piw", hidden_middle, down_weight, preferred_element_type=jnp.float32
    ).astype(jnp.bfloat16)
    grad_out = cotangent[0].astype(jnp.float32)
    returned = pick_pairs(from_experts(expert_part), target, row_count)
    moe_part = jnp.sum(returned.astype(jnp.float32) * gate_probs[:, :, None], axis=1)
    moe_out = lax.psum(moe_part.astype(jnp.bfloat16), TENSOR).astype(jnp.float32)
    grad_gate_part = jnp.sum(returned.astype(jnp.float32) * grad_out[:, None, :], axis=2)
    output = (residual_stream + moe_out).astype(jnp.bfloat16)
    pair_grad = (
        (gate_probs[:, :, None] * grad_out[:, None, :])
        .astype(jnp.bfloat16)
        .reshape(row_count * TOPK, model_width)
    )
    send_grad = (
        jnp.zeros((experts_total * capacity, model_width), jnp.bfloat16)
        .at[target]
        .set(pair_grad, mode="drop")
    )
    expert_output_gradient = to_experts(send_grad.reshape(experts_total, capacity, model_width))
    grad_mid = jnp.einsum(
        "jtk,jvk->jtv", expert_output_gradient, down_weight, preferred_element_type=jnp.float32
    )
    grad_w_down = jnp.einsum(
        "tce,tci->tei", hidden_middle, expert_output_gradient, preferred_element_type=jnp.float32
    )
    gate_activation_gradient = (
        grad_mid
        * up_activation_input
        * sigmoid_gate
        * (1.0 + gate_activation_input * (1.0 - sigmoid_gate))
    ).astype(jnp.bfloat16)
    up_activation_gradient = (grad_mid * silu_gate).astype(jnp.bfloat16)
    grad_w_gate = jnp.einsum(
        "ahw,ahp->awp",
        expert_input_rows,
        gate_activation_gradient,
        preferred_element_type=jnp.float32,
    )
    grad_w_up = jnp.einsum(
        "ahw,ahp->awp",
        expert_input_rows,
        up_activation_gradient,
        preferred_element_type=jnp.float32,
    )
    grad_expert_in = (
        jnp.einsum(
            "ous,ops->oup",
            gate_activation_gradient,
            gate_weight,
            preferred_element_type=jnp.float32,
        )
        + jnp.einsum(
            "ous,ops->oup", up_activation_gradient, up_weight, preferred_element_type=jnp.float32
        )
    ).astype(jnp.bfloat16)
    grad_pairs = pick_pairs(from_experts(grad_expert_in), target, row_count)
    grad_normed_part = jnp.sum(grad_pairs.astype(jnp.float32), axis=1)
    grad_normed_moe, grad_gates = (
        lax.psum(grad_normed_part.astype(jnp.bfloat16), TENSOR).astype(jnp.float32),
        lax.psum(grad_gate_part.astype(jnp.bfloat16), TENSOR).astype(jnp.float32),
    )
    grad_selected = gate_probs * (
        grad_gates - jnp.sum(gate_probs * grad_gates, axis=1, keepdims=True)
    )
    grad_logits = jnp.sum(jnp.where(chosen, grad_selected[:, :, None], 0.0), axis=1).astype(
        jnp.bfloat16
    )
    grad_router = matmul_tn(feedforward_normalized, grad_logits)
    grad_normed_two = grad_normed_moe + matmul_nt(grad_logits, full_router)
    grad_resid_norm, grad_gain_ffn = second_pull(grad_normed_two)
    grad_resid = grad_out + grad_resid_norm
    grad_attn = grad_resid.astype(jnp.bfloat16)
    grad_w_output = matmul_tn(grad_attn, heads_low)
    grad_heads = (
        matmul(grad_attn, full_output)
        .astype(jnp.bfloat16)
        .reshape(row_count, local_heads, HEAD_SIZE)
    )
    row_delta = jnp.sum(grad_heads.astype(jnp.float32) * heads_full, axis=2).T
    grad_query, grad_key_terms, grad_value_terms = attention_backward(
        query_vectors,
        keys_all,
        values_all,
        seg_all,
        query_seg,
        query_index,
        key_ids,
        key_block,
        log_total,
        grad_heads,
        row_delta,
    )
    grad_key_local, grad_value_local = (
        lax.psum_scatter(
            grad_key_terms.astype(jnp.bfloat16), CONTEXT, scatter_dimension=0, tiled=True
        ).astype(jnp.float32),
        lax.psum_scatter(
            grad_value_terms.astype(jnp.bfloat16), CONTEXT, scatter_dimension=0, tiled=True
        ).astype(jnp.float32),
    )
    grad_query_raw, grad_gain_query = query_pull(grad_query)
    grad_key_raw, grad_gain_key = key_pull(grad_key_local)
    grad_query_low = grad_query_raw.reshape(row_count, local_heads * HEAD_SIZE).astype(jnp.bfloat16)
    grad_key_low = grad_key_raw.astype(jnp.bfloat16)
    grad_value_low = grad_value_local.astype(jnp.bfloat16)
    grad_w_query = matmul_tn(attention_normalized, grad_query_low)
    grad_w_key = matmul_tn(attention_normalized, grad_key_low)
    grad_w_value = matmul_tn(attention_normalized, grad_value_low)
    grad_normed_one = (
        matmul_nt(grad_query_low, full_query)
        + matmul_nt(grad_key_low, full_key)
        + matmul_nt(grad_value_low, full_value)
    )
    grad_normed_one, grad_gain_query, grad_gain_key = (
        lax.psum(grad_normed_one.astype(jnp.bfloat16), TENSOR).astype(jnp.float32),
        lax.psum(grad_gain_query.astype(jnp.bfloat16), TENSOR).astype(jnp.float32),
        lax.psum(grad_gain_key.astype(jnp.bfloat16), TENSOR).astype(jnp.float32),
    )
    grad_inputs_norm, grad_gain_attn = first_pull(grad_normed_one)
    input_grad = grad_resid + grad_inputs_norm
    owned = (
        lax.psum_scatter(
            grad_w_query.astype(jnp.bfloat16), GROUPS, scatter_dimension=0, tiled=True
        ).astype(jnp.float32),
        lax.psum_scatter(
            grad_w_key.astype(jnp.bfloat16), GROUPS, scatter_dimension=0, tiled=True
        ).astype(jnp.float32),
        lax.psum_scatter(
            grad_w_value.astype(jnp.bfloat16), GROUPS, scatter_dimension=0, tiled=True
        ).astype(jnp.float32),
        lax.psum_scatter(
            grad_w_output.astype(jnp.bfloat16), GROUPS, scatter_dimension=0, tiled=True
        ).astype(jnp.float32),
        lax.psum_scatter(
            grad_router.astype(jnp.bfloat16), GROUPS, scatter_dimension=0, tiled=True
        ).astype(jnp.float32),
        lax.psum_scatter(
            grad_gain_attn.astype(jnp.bfloat16),
            GROUPS,
            scatter_dimension=0,
            tiled=True,
        ).astype(jnp.float32),
        lax.psum_scatter(
            grad_gain_ffn.astype(jnp.bfloat16), GROUPS, scatter_dimension=0, tiled=True
        ).astype(jnp.float32),
        lax.psum_scatter(
            grad_gain_query.astype(jnp.bfloat16),
            GROUPS,
            scatter_dimension=0,
            tiled=True,
        ).astype(jnp.float32),
        lax.psum_scatter(
            grad_gain_key.astype(jnp.bfloat16), GROUPS, scatter_dimension=0, tiled=True
        ).astype(jnp.float32),
    )
    return (
        output[None],
        input_grad[None],
        owned[5],
        owned[0],
        owned[1],
        owned[2],
        owned[3],
        owned[7],
        owned[8],
        owned[6],
        owned[4],
        grad_w_gate,
        grad_w_up,
        grad_w_down,
    )


MESH = pl.DeviceIdType.MESH
Z_UP, Z_DOWN, Y_SIDE, X_SIDE, CORE_SIDE = range(5)

def coords():
    z, y, t = lax.axis_index(FSDP), lax.axis_index(CONTEXT), lax.axis_index(TENSOR)
    return z, y, t // 2, t % 2

def partner(z, index):
    return (z, z + 1 - 2 * (z % 2), 2 - z // 2, 3 - 3 * (z // 2))[index]

def greet(neighbours):
    barrier = pltpu.get_barrier_semaphore()
    for condition, device in neighbours:
        def tell(device=device):
            pl.semaphore_signal(barrier, inc=1, device_id=device, device_id_type=MESH)
        if condition is None: tell()
        else: pl.when(condition)(tell)
    count = sum(1 if condition is None else condition.astype(jnp.int32) for condition, device in neighbours)
    pl.semaphore_wait(barrier, count)


def spread(x_ref, out_ref, own_sem, send_sems, recv_sems):
    rows = x_ref.shape[0]; half = rows // 2
    z, y, x, c = coords()
    side = {Z_UP: (z + 1, y, 2 * x + c), Z_DOWN: (z - 1, y, 2 * x + c), Y_SIDE: (z, 1 - y, 2 * x + c),
            X_SIDE: (z, y, 2 * (1 - x) + c), CORE_SIDE: (z, y, 2 * x + 1 - c)}
    def device(zz, yy, xx, cc): return (zz * 2 + yy) * 4 + xx * 2 + cc
    def place(owner, h): return out_ref.at[pl.ds(pl.multiple_of(owner * rows + h * half, half), half)]
    def copy(link, owner, h, own=False):
        src = x_ref.at[pl.ds(h * half, half)] if own else place(owner, h)
        return pltpu.make_async_remote_copy(src_ref=src, dst_ref=place(owner, h), send_sem=send_sems.at[link, owner, h],
            recv_sem=recv_sems.at[owner, h], device_id=side[link], device_id_type=MESH)
    sent = []
    def start(link, owner, h, own=False, condition=None):
        one = copy(link, owner, h, own)
        sent.append((one, condition))
        if condition is None: one.start()
        else: pl.when(condition)(one.start)
    def arrived(owner, h): copy(CORE_SIDE, owner, h).wait_recv()
    me = device(z, y, x, c)
    keep = pltpu.make_async_copy(x_ref, out_ref.at[pl.ds(pl.multiple_of(me * rows, rows), rows)], own_sem)
    keep.start()
    def stage1(i):
        zz = partner(z, i); owner = device(zz, y, x, c); own = i == 0
        if not own:
            arrived(owner, 0); arrived(owner, 1)
        for h in range(2):
            start(Z_UP, owner, h, own, (z < 3) if own else (z < 3) & (zz < z))
            start(Z_DOWN, owner, h, own, (z > 0) if own else (z > 0) & (zz > z))
        start(Y_SIDE, owner, 0, own); start(X_SIDE, owner, 1, own)
        start(Y_SIDE, owner, 1, own); start(X_SIDE, owner, 0, own)
        for h in range(2): start(CORE_SIDE, owner, h, own)
    def stage2(i):
        zz = partner(z, i)
        oy, ox = device(zz, 1 - y, x, c), device(zz, y, 1 - x, c)
        arrived(oy, 0); start(X_SIDE, oy, 0); start(CORE_SIDE, oy, 0)
        arrived(ox, 1); start(Y_SIDE, ox, 1); start(CORE_SIDE, ox, 1)
        arrived(oy, 1); start(CORE_SIDE, oy, 1)
        arrived(ox, 0); start(CORE_SIDE, ox, 0)
    def stage3(i):
        o = device(partner(z, i), 1 - y, 1 - x, c)
        for h in range(2):
            arrived(o, h); start(CORE_SIDE, o, h)
    stage1(0); stage1(1); stage2(0); stage1(2); stage2(1); stage3(0); stage1(3); stage2(2); stage3(1); stage2(3); stage3(2); stage3(3)
    for i in range(4):
        for yy in range(2):
            for xx in range(2):
                for h in range(2): arrived(device(i, yy, xx, 1 - c), h)
    keep.wait()
    for one, condition in sent:
        if condition is None: one.wait_send()
        else: pl.when(condition)(one.wait_send)

def mix_kernel(heads_ref, weight_ref, input_ref, gain_ref, resid_ref, normed_ref, all_ref, part, mine, core_in, line_in, sems, recv, *gather_sems):
    z, y, x, c = coords()
    x_side, core_side = (z, y, 2 * (1 - x) + c), (z, y, 2 * x + 1 - c)
    greet([(z < 3, (z + 1, y, 2 * x + c)), (z > 0, (z - 1, y, 2 * x + c)), (None, (z, 1 - y, 2 * x + c)), (None, x_side), (None, core_side)])
    rows, width = input_ref.shape; f32, bf16 = jnp.float32, jnp.bfloat16
    def remote(src, dst, n, device):
        return pltpu.make_async_remote_copy(src_ref=src, dst_ref=dst, send_sem=sems.at[n], recv_sem=recv.at[n], device_id=device, device_id_type=MESH)
    over_core = [remote(part.at[n, 1 - c], core_in.at[n], n, core_side) for n in range(2)]
    over_x = remote(mine, line_in, 2, x_side)
    for n, xx in enumerate((1 - x, x)):
        heads = heads_ref[pl.ds(pl.multiple_of(xx * 2 * rows, 2 * rows), 2 * rows), :]
        for m in range(width // 512):
            at = pl.ds(m * 512, 512)
            value = lax.dot_general(heads, weight_ref[at, :], (((1,), (1,)), ((), ())), preferred_element_type=f32).astype(bf16)
            part[n, 0, :, at] = value[:rows]
            part[n, 1, :, at] = value[rows:]
        over_core[n].start()
    over_core[0].wait_recv()
    mine[...] = part[0, c] + core_in[0]
    over_x.start(); over_core[1].wait_recv()
    total = input_ref[...].astype(f32) + part[1, c].astype(f32) + core_in[1].astype(f32)
    over_x.wait_recv()
    total = total + line_in[...].astype(f32)
    resid_ref[...] = total
    normed_ref[...] = (total * lax.rsqrt(jnp.mean(total * total, axis=-1, keepdims=True) + EPSILON) * gain_ref[...]).astype(bf16)
    spread(normed_ref, all_ref, *gather_sems)
    for one in (*over_core, over_x): one.wait_send()

def mix_heads(heads, weight, own_input, gain, collective_id):
    rows, width = own_input.shape; D, V = pltpu.SemaphoreType.DMA, pltpu.VMEM; S = jax.ShapeDtypeStruct
    f32, bf16 = jnp.float32, jnp.bfloat16; vspec = pl.BlockSpec(memory_space=V)
    return pl.pallas_call(mix_kernel, out_shape=[S((rows, width), f32), S((rows, width), bf16), S((32 * rows, width), bf16)],
        in_specs=[vspec] * 4, out_specs=[vspec, vspec, pl.BlockSpec(memory_space=pl.ANY)],
        scratch_shapes=[V((2, 2, rows, width), bf16), V((rows, width), bf16), V((2, rows, width), bf16), V((rows, width), bf16), D((3,)), D((3,)),
            D, D((5, 32, 2)), D((32, 2))],
        compiler_params=pltpu.CompilerParams(collective_id=collective_id, has_side_effects=True, vmem_limit_bytes=32 << 20))(heads, weight, own_input, gain)

def groups_kernel(parts, count, *refs):
    ins, outs = refs[:count], refs[count:2 * count]
    keep_sems, send_sems, recv_sems = refs[2 * count:]
    z, y, x, c = coords()
    t = 2 * x + c
    side = {Z_UP: (z + 1, y, t), Z_DOWN: (z - 1, y, t), Y_SIDE: (z, 1 - y, t)}
    greet([(z < 3, side[Z_UP]), (z > 0, side[Z_DOWN]), (None, side[Y_SIDE])])
    sent = []
    def copy(link, p, owner, own=False):
        k, first, size, way = parts[p]
        dst = outs[k].at[pl.ds(pl.multiple_of(owner * ins[k].shape[0] + first, 16), size)]
        return pltpu.make_async_remote_copy(src_ref=ins[k].at[pl.ds(first, size)] if own else dst, dst_ref=dst, send_sem=send_sems.at[link, p, owner],
            recv_sem=recv_sems.at[p, owner], device_id=side[link], device_id_type=MESH)
    def start(link, p, owner, own=False, condition=None):
        one = copy(link, p, owner, own)
        sent.append((one, condition))
        if condition is None: one.start()
        else: pl.when(condition)(one.start)
    def arrived(p, owner): copy(Y_SIDE, p, owner).wait_recv()
    def along(p, owner, zz, own=False):
        start(Z_UP, p, owner, own, (z < 3) & (zz <= z)); start(Z_DOWN, p, owner, own, (z > 0) & (zz >= z))
    kept = []
    for p in range(len(parts)):
        along(p, z * 2 + y, z, True); start(Y_SIDE, p, z * 2 + y, True)
    for k in range(count):
        rows = ins[k].shape[0]
        one = pltpu.make_async_copy(ins[k], outs[k].at[pl.ds(pl.multiple_of((z * 2 + y) * rows, 16), rows)], keep_sems.at[k])
        one.start(); kept.append(one)
    def forward(p, i):
        zz = partner(z, i)
        near, far = zz * 2 + y, zz * 2 + 1 - y
        if i > 0:
            arrived(p, near); along(p, near, zz)
            if parts[p][3] == 0: start(Y_SIDE, p, near)
        if parts[p][3] == 1:
            arrived(p, far); along(p, far, zz)
    for wave in range(len(parts) + 3):
        for i in range(4):
            if 0 <= wave - i < len(parts): forward(wave - i, i)
    for p in range(len(parts)):
        if parts[p][3] == 0:
            for i in range(4): arrived(p, partner(z, i) * 2 + 1 - y)
    for one in kept: one.wait()
    for one, condition in sent:
        if condition is None: one.wait_send()
        else: pl.when(condition)(one.wait_send)

def gather_groups(arrays, parts, collective_id):
    count = len(arrays); D = pltpu.SemaphoreType.DMA
    return pl.pallas_call(functools.partial(groups_kernel, parts, count),
        out_shape=[jax.ShapeDtypeStruct((8 * a.shape[0], a.shape[1]), a.dtype) for a in arrays],
        in_specs=[pl.BlockSpec(memory_space=pl.ANY)] * count, out_specs=[pl.BlockSpec(memory_space=pl.ANY)] * count,
        scratch_shapes=[D((count,)), D((3, len(parts), 8)), D((len(parts), 8))],
        compiler_params=pltpu.CompilerParams(collective_id=collective_id, has_side_effects=True))(*arrays)

class TensorGather:
    def __init__(self, src, out, keep_sem, send_sems, recv_sems):
        self.src, self.out, self.keep_sem, self.send_sems, self.recv_sems = src, out, keep_sem, send_sems, recv_sems
        z, y, x, c = coords()
        self.x_side, self.core_side = (z, y, 2 * (1 - x) + c), (z, y, 2 * x + 1 - c)
        self.me, self.across, self.beside, self.last = 2 * x + c, 2 * (1 - x) + c, 2 * x + 1 - c, 2 * (1 - x) + 1 - c

    @staticmethod
    def scratch():
        D = pltpu.SemaphoreType.DMA
        return [D, D((3,)), D((4,))]

    def copy(self, n, owner, device, own=False):
        return pltpu.make_async_remote_copy(src_ref=self.src if own else self.out.at[owner], dst_ref=self.out.at[owner],
            send_sem=self.send_sems.at[n], recv_sem=self.recv_sems.at[owner], device_id=device, device_id_type=MESH)

    def start(self):
        self.copy(0, self.me, self.x_side, True).start()
        self.copy(1, self.me, self.core_side, True).start()
        self.keep().start()

    def keep(self): return pltpu.make_async_copy(self.src, self.out.at[self.me], self.keep_sem)

    def finish(self):
        self.copy(0, self.across, self.x_side).wait_recv()
        self.copy(2, self.across, self.core_side).start()
        self.copy(0, self.beside, self.x_side).wait_recv()
        self.copy(0, self.last, self.x_side).wait_recv()
        self.keep().wait()
        self.copy(0, self.me, self.x_side, True).wait_send()
        self.copy(1, self.me, self.core_side, True).wait_send()
        self.copy(2, self.across, self.core_side).wait_send()

def rms_pull(grad, values, inverse, gain):
    scaled = grad * gain
    return inverse * scaled - values * (inverse * inverse * inverse * jnp.mean(scaled * values, axis=-1, keepdims=True))

def pull_kernel(grad_ref, weight_ref, input_ref, gain_ref, head_gain_ref, above_ref, out_ref, part, mine, core_in, line_in, message, sems, recv, *gather):
    z, y, x, c = coords()
    x_side, core_side = (z, y, 2 * (1 - x) + c), (z, y, 2 * x + 1 - c)
    greet([(None, x_side), (None, core_side)])
    rows, width = above_ref.shape; f32, bf16 = jnp.float32, jnp.bfloat16
    def remote(src, dst, n, device):
        return pltpu.make_async_remote_copy(src_ref=src, dst_ref=dst, send_sem=sems.at[n], recv_sem=recv.at[n], device_id=device, device_id_type=MESH)
    over_core = [remote(part.at[n, 1 - c], core_in.at[n], n, core_side) for n in range(2)]
    over_x = remote(mine, line_in, 2, x_side)
    message[pl.ds(rows, 16), :] = jnp.zeros((16, width), f32).astype(bf16)
    gain_parts = [0.0] * (width // 512)
    for n, xx in enumerate((1 - x, x)):
        rows_at = pl.ds(pl.multiple_of(xx * 2 * rows, 2 * rows), 2 * rows)
        grad = grad_ref[rows_at, :]
        whole = input_ref[rows_at, :].astype(f32)
        inverse = lax.rsqrt(jnp.mean(whole * whole, axis=-1, keepdims=True) + EPSILON)
        for m in range(width // 512):
            at = pl.ds(m * 512, 512)
            value = lax.dot_general(grad, weight_ref[at, :], (((1,), (1,)), ((), ())), preferred_element_type=f32)
            part[n, 0, :, at] = value[:rows].astype(bf16)
            part[n, 1, :, at] = value[rows:].astype(bf16)
            gain_parts[m] = gain_parts[m] + jnp.sum(value * input_ref[rows_at, at].astype(f32) * inverse, axis=0, keepdims=True)
        over_core[n].start()
    first_row = lax.broadcasted_iota(jnp.int32, (16, 512), 0)
    for m in range(width // 512):
        message[pl.ds(rows, 16), pl.ds(m * 512, 512)] = jnp.where(first_row == 0, gain_parts[m], 0.0).astype(bf16)
    first_row = lax.broadcasted_iota(jnp.int32, (16, 128), 0)
    for n in range(2):
        at = (pl.ds(rows, 16), pl.ds(n * 128, 128))
        message[at] = jnp.where(first_row == 1, head_gain_ref[pl.ds(n, 1), :], message[at].astype(f32)).astype(bf16)
    over_core[0].wait_recv()
    mine[...] = part[0, c] + core_in[0]
    over_x.start(); over_core[1].wait_recv()
    own_at = pl.ds(pl.multiple_of((2 * x + c) * rows, rows), rows)
    own = input_ref[own_at, :].astype(f32)
    inverse = lax.rsqrt(jnp.mean(own * own, axis=-1, keepdims=True) + EPSILON)
    total = part[1, c].astype(f32) + core_in[1].astype(f32)
    over_x.wait_recv()
    total = total + line_in[...].astype(f32)
    message[pl.ds(0, rows), :] = (above_ref[...] + rms_pull(total, own, inverse, gain_ref[...])).astype(bf16)
    gather = TensorGather(message, out_ref, *gather)
    gather.start(); gather.finish()
    for one in (*over_core, over_x): one.wait_send()

def pull_inputs(grad, weight, inputs, gain, head_gain_grads, above, collective_id):
    rows, width = above.shape; D, V = pltpu.SemaphoreType.DMA, pltpu.VMEM
    bf16 = jnp.bfloat16; vspec = pl.BlockSpec(memory_space=V)
    return pl.pallas_call(pull_kernel, out_shape=jax.ShapeDtypeStruct((4, rows + 16, width), bf16),
        in_specs=[vspec] * 6, out_specs=pl.BlockSpec(memory_space=pl.ANY),
        scratch_shapes=[V((2, 2, rows, width), bf16), V((rows, width), bf16), V((2, rows, width), bf16), V((rows, width), bf16), V((rows + 16, width), bf16),
            D((3,)), D((3,)), *TensorGather.scratch()],
        compiler_params=pltpu.CompilerParams(collective_id=collective_id, has_side_effects=True, vmem_limit_bytes=40 << 20))(
            grad, weight, inputs, gain, head_gain_grads, above)


def nt(a, b):
    return lax.dot_general(a, b, (((1,), (1,)), ((), ())), preferred_element_type=jnp.float32)

def nn(a, b):
    return jnp.dot(a, b, preferred_element_type=jnp.float32)

def nearest(z, index):
    choice = [partner(z, n) for n in range(4)]
    return jnp.where(index == 0, choice[0], jnp.where(index == 1, choice[1], jnp.where(index == 2, choice[2], choice[3])))

def spot(zz, yy, xx): return (zz * 2 + yy) * 2 + xx

def step_target(step):
    z, y, x, c = coords()
    n = step % 4
    return nearest(z, 3 - step // 4), jnp.where(n < 2, 1 - y, y), jnp.where(n % 2 == 0, 1 - x, x)

def step_block(ref, step):
    size = ref.shape[0] // 16
    return ref.at[pl.ds(pl.multiple_of(spot(*step_target(step)) * size, size), size)]

class Reduction:
    def __init__(self, part, mine, first_in, second_in, line_in, core_sem, first_sem, second_sem, line_send, line_recv, split):
        self.part, self.mine, self.first_in, self.second_in, self.line_in = part, mine, first_in, second_in, line_in
        self.core_sem, self.first_sem, self.second_sem, self.line_send, self.line_recv = core_sem, first_sem, second_sem, line_send, line_recv
        self.pieces = (pl.ds(0, split), pl.ds(split, part.shape[2] - split))
        self.sizes = (pl.ds(0, split), pl.ds(0, part.shape[2] - split))
        z, y, x, c = self.at = coords()
        self.up, self.down = (z + 1, y, 2 * x + c), (z - 1, y, 2 * x + c)
        self.y_side, self.x_side, self.core_side = (z, 1 - y, 2 * x + c), (z, y, 2 * (1 - x) + c), (z, y, 2 * x + 1 - c)

    @staticmethod
    def scratch(rows, width, dtype, split):
        V, D, half = pltpu.VMEM, pltpu.SemaphoreType.DMA, max(split, rows - split)
        return [V((2, 2, rows, width), dtype), V((16, rows, width), dtype), V((2, 8, half, width), dtype),
            V((2, 4, half, width), dtype), V((2, 4, 2, half, width), dtype), D((2, 16)), D((2, 2, 8)), D((2, 2, 4)), D((4, 2)), D((2, 4, 2))]

    def greet(self):
        z = self.at[0]
        greet([(z < 3, self.up), (z > 0, self.down), (None, self.y_side), (None, self.x_side), (None, self.core_side)])

    @staticmethod
    def remote(src, dst, send, recv, device):
        return pltpu.make_async_remote_copy(src_ref=src, dst_ref=dst, send_sem=send, recv_sem=recv, device_id=device, device_id_type=MESH)

    def over_core(self, step):
        s = spot(*step_target(step))
        return self.remote(self.part.at[step % 2, 1 - self.at[3]], self.mine.at[s], self.core_sem.at[0, s], self.core_sem.at[1, s], self.core_side)

    def piece(self, zz, yy, xx, h): return self.mine.at[spot(zz, yy, xx), self.pieces[h]]

    def first(self, h, zz, other):
        z, y, x, c = self.at
        src = self.piece(zz, other, 1 - x, 0) if h == 0 else self.piece(zz, 1 - y, other, 1)
        s = zz * 2 + other
        return self.remote(src, self.first_in.at[h, s, self.sizes[h]], self.first_sem.at[0, h, s], self.first_sem.at[1, h, s], self.x_side if h == 0 else self.y_side)

    def second(self, h, zz):
        z, y, x, c = self.at
        src = self.piece(zz, 1 - y, x, 0) if h == 0 else self.piece(zz, y, 1 - x, 1)
        return self.remote(src, self.second_in.at[h, zz, self.sizes[h]], self.second_sem.at[0, h, zz], self.second_sem.at[1, h, zz], self.y_side if h == 0 else self.x_side)

    def line(self, h, zz, way):
        z, y, x, c = self.at
        return self.remote(self.piece(zz, y, x, h), self.line_in.at[way, zz, h, self.sizes[h]], self.line_send.at[zz, h], self.line_recv.at[way, zz, h], self.up if way == 0 else self.down)

    def add(self, s, h, arrived):
        at = (s, self.pieces[h])
        self.mine[at] = self.mine[at] + arrived[...]

    def stage_core(self, step):
        zz, yy, xx = step_target(step)
        s = spot(zz, yy, xx)
        self.over_core(step).wait_recv()
        self.mine[s] += self.part[step % 2, self.at[3]]
        n = step % 4
        @pl.when(n % 2 == 0)
        def _(): self.first(0, zz, yy).start()
        @pl.when(n < 2)
        def _(): self.first(1, zz, xx).start()

    def stage_first(self, i):
        z, y, x, c = self.at
        zz = nearest(z, i)
        for n in range(2):
            for h, other in ((0, (1 - y, y)[n]), (1, (1 - x, x)[n])):
                self.first(h, zz, other).wait_recv()
                self.add(spot(zz, other, x) if h == 0 else spot(zz, y, other), h, self.first_in.at[h, zz * 2 + other, self.sizes[h]])
                if n == 0: self.second(h, zz).start()

    def stage_second(self, i):
        z, y, x, c = self.at
        zz = nearest(z, i)
        for h in range(2):
            self.second(h, zz).wait_recv()
            self.add(spot(zz, y, x), h, self.second_in.at[h, zz, self.sizes[h]])

    def stage_line(self, i):
        z, y, x, c = self.at
        zz = nearest(z, i)
        for h in range(2):
            for way, from_side, toward in ((0, z > 0, zz > z), (1, z < 3, zz < z)):
                @pl.when(from_side & (toward | (zz == z)))
                def _(h=h, way=way):
                    self.line(h, zz, way).wait_recv()
                    self.add(spot(zz, y, x), h, self.line_in.at[way, zz, h, self.sizes[h]])
                @pl.when(toward)
                def _(h=h, way=way): self.line(h, zz, way).start()

    def follow(self, step):
        @pl.when((step >= 1) & (step <= 16))
        def _(): self.stage_core(step - 1)
        q = step // 4
        @pl.when((step % 4 == 1) & (q >= 2))
        def _(): self.stage_line(5 - q)
        @pl.when((step % 4 == 1) & (q >= 1))
        def _(): self.stage_first(4 - q)
        @pl.when((step % 4 == 3) & (q >= 1))
        def _(): self.stage_second(4 - q)

    def finish(self, steps):
        z, y, x, c = self.at
        if steps == 16:
            self.stage_core(15); self.stage_line(1); self.stage_first(0); self.stage_second(0)
        self.stage_line(0)

    @property
    def own(self): return spot(*self.at[:3])

    def drain(self):
        z, y, x, c = self.at
        self.over_core(14).wait_send(); self.over_core(15).wait_send()
        for zz in range(4):
            for other in range(2):
                for h in range(2): self.first(h, zz, other).wait_send()
            for h in range(2): self.second(h, zz).wait_send()
            @pl.when(zz != z)
            def _(zz=zz):
                for h in range(2): self.line(h, zz, 0).wait_send()

def expert_kernel(normed_ref, cot_ref, code_ref, router_ref, expand_ref, place_ref, gate_ref, up_ref, down_ref,
                  resid_ref, own_normed_ref, own_chosen_ref, own_cot_ref, gain_ref,
                  grad_ref, message_ref, hid_out, gate_out, up_out, normed_in, cot_in, code_in, units, message, in_sem, units_sem, *scratch):
    reduction = Reduction(*scratch[:-3], split=64)
    gather = TensorGather(message, message_ref, *scratch[-3:])
    reduction.greet()
    part = reduction.part
    rows, width, wide = grad_ref.shape[0], normed_ref.shape[1], gate_ref.shape[1]
    f32, bf16 = jnp.float32, jnp.bfloat16
    stride = code_ref.shape[0] // 8
    def loads(step):
        slot = step % 2
        zz, yy, xx = step_target(step)
        codes = code_ref.at[pl.ds(pl.multiple_of((zz * 2 + yy) * stride, 16), rows)]
        pairs = ((step_block(normed_ref, step), normed_in), (step_block(cot_ref, step), cot_in), (codes, code_in))
        return [pltpu.make_async_copy(src, dst.at[slot], in_sem.at[n, slot]) for n, (src, dst) in enumerate(pairs)]
    def stores(step):
        slot = step % 2
        return [pltpu.make_async_copy(units.at[slot, n], step_block(dst, step), units_sem.at[n, slot])
                for n, dst in enumerate((hid_out, gate_out, up_out))]
    for one in loads(0): one.start()

    def compute(step):
        slot = step % 2
        for one in loads(step): one.wait()
        @pl.when(step < 15)
        def _():
            for one in loads(step + 1): one.start()
        @pl.when(step >= 2)
        def _():
            for one in stores(step - 2): one.wait()
            reduction.over_core(step - 2).wait_send()
        normed, cot = normed_in[slot], cot_in[slot]
        code = code_in[slot].astype(f32)
        quarter = lax.broadcasted_iota(jnp.int32, code.shape, 1) // (128 // 4) - 2 * step_target(step)[2]
        code = jnp.concatenate([jnp.where(quarter == n, code, 0.0) for n in range(2)], axis=0)
        scores = jnp.where(code > 0.5, nn(normed, router_ref[...]), NEGATIVE)
        scores = jnp.where(code > 0.5, jnp.exp(scores - jnp.max(scores, axis=1, keepdims=True)), 0.0)
        gates = jnp.where(code > 1.5, scores / jnp.sum(scores, axis=1, keepdims=True), 0.0)
        high = gates.astype(bf16)
        low = (gates - high.astype(f32)).astype(bf16)
        grad_gates = jnp.zeros((2 * rows, 128), f32)
        def products(n):
            at = pl.ds(n * 256, 256)
            return (nn(normed, gate_ref[:, at]), nn(normed, up_ref[:, at]), nt(cot, down_ref[at, :]),
                nn(high, expand_ref[:, at]) + nn(low, expand_ref[:, at]))
        ahead = products(0)
        for n in range(wide // 256):
            gate_in, up_in, grad_mid, gate = ahead
            if n + 1 < wide // 256: ahead = products(n + 1)
            at = pl.ds(n * 256, 256)
            sig = lax.logistic(gate_in)
            silu = gate_in * sig
            hidden = silu * up_in
            grad_gates += nn(jnp.where(gate != 0.0, hidden * grad_mid, 0.0).astype(bf16), place_ref[at, :])
            grad_hidden = grad_mid * gate
            units[slot, 0, :, at] = (hidden * gate).astype(bf16)
            units[slot, 1, :, at] = (grad_hidden * up_in * (sig + silu * (1.0 - sig))).astype(bf16)
            units[slot, 2, :, at] = (grad_hidden * silu).astype(bf16)
        for one in stores(step): one.start()
        gate_grad, up_grad = units[slot, 1], units[slot, 2]
        for n in range(width // 512):
            at = pl.ds(n * 512, 512)
            grad = (nt(gate_grad, gate_ref[at, :]) + nt(up_grad, up_ref[at, :])).astype(bf16)
            part[slot, 0, :, at] = grad[:rows]
            part[slot, 1, :, at] = grad[rows:]
        grad_gates = grad_gates.astype(bf16)
        part[slot, 0, :, pl.ds(width, 128)] = grad_gates[:rows]
        part[slot, 1, :, pl.ds(width, 128)] = grad_gates[rows:]
        reduction.over_core(step).start()

    @pl.loop(0, 16)
    def _(step):
        compute(step)
        reduction.follow(step)
    for step in (14, 15):
        for one in stores(step): one.wait()
    reduction.finish(16)
    every, own = pl.ds(0, width), reduction.own
    grad_gates = reduction.mine[own, :, pl.ds(width, 128)].astype(f32)
    grad_gates = grad_gates + pltpu.roll(grad_gates, 64, 1)
    grad_gates = grad_gates + pltpu.roll(grad_gates, 32, 1)
    chosen = own_chosen_ref[...].astype(f32) > 0.5
    scores = jnp.where(chosen, nn(own_normed_ref[...], router_ref[...]), NEGATIVE)
    scores = jnp.where(chosen, jnp.exp(scores - jnp.max(scores, axis=1, keepdims=True)), 0.0)
    gates = scores / jnp.sum(scores, axis=1, keepdims=True)
    grad_logits = (gates * (grad_gates - jnp.sum(gates * grad_gates, axis=1, keepdims=True))).astype(bf16)
    grad = reduction.mine[own, :, every].astype(f32) + nt(grad_logits, router_ref[...])
    values = resid_ref[...]
    inverse = lax.rsqrt(jnp.mean(values * values, axis=-1, keepdims=True) + EPSILON)
    total = own_cot_ref[...].astype(f32) + rms_pull(grad, values, inverse, gain_ref[...])
    grad_ref[...] = total
    message[pl.ds(0, rows), every] = total.astype(bf16)
    message[pl.ds(0, rows), pl.ds(width, 128)] = grad_logits
    first_row = lax.broadcasted_iota(jnp.int32, (16, width), 0)
    message[pl.ds(rows, 16), every] = jnp.where(first_row == 0, jnp.sum(grad * values * inverse, axis=0, keepdims=True), 0.0).astype(bf16)
    message[pl.ds(rows, 16), pl.ds(width, 128)] = jnp.zeros((16, 128), f32).astype(bf16)
    gather.start(); gather.finish()
    reduction.drain()

def run_experts(normed_all, cot_all, codes, router, expand, place, gate_flat, up_flat, down_flat,
                resid, own_normed, own_chosen, own_cot, gain, collective_id):
    total, width = normed_all.shape; rows = total // 32; wide = gate_flat.shape[1]
    bf16 = jnp.bfloat16; D = pltpu.SemaphoreType.DMA; V = pltpu.VMEM; W = width + 128
    anyspec, vspec = pl.BlockSpec(memory_space=pl.ANY), pl.BlockSpec(memory_space=V)
    unit = jax.ShapeDtypeStruct((total, wide), bf16)
    return pl.pallas_call(expert_kernel,
        out_shape=[jax.ShapeDtypeStruct((rows, width), jnp.float32), jax.ShapeDtypeStruct((4, rows + 16, W), bf16), unit, unit, unit],
        in_specs=[anyspec] * 3 + [vspec] * 11, out_specs=[vspec] + [anyspec] * 4,
        scratch_shapes=[V((2, 2 * rows, width), bf16), V((2, 2 * rows, width), bf16), V((2, rows, 128), bf16),
            V((2, 3, 2 * rows, wide), bf16), V((rows + 16, W), bf16), D((3, 2)), D((3, 2)),
            *Reduction.scratch(rows, W, bf16, 64), *TensorGather.scratch()],
        compiler_params=pltpu.CompilerParams(collective_id=collective_id, has_side_effects=True, vmem_limit_bytes=60 << 20))(
            normed_all, cot_all, codes, router, expand, place, gate_flat, up_flat, down_flat, resid, own_normed, own_chosen, own_cot, gain)

def output_kernel(normed_ref, cot_ref, hid_ref, gate_ref, up_ref, down_ref, resid_ref, out_ref, gate_out, up_out, down_out,
                  hid_in, wide_in, thin_in, own_out, hid_sem, in_sem, out_sem, *scratch):
    reduction = Reduction(*scratch[:-3], split=80)
    gather = TensorGather(own_out, out_ref, *scratch[-3:])
    reduction.greet()
    part = reduction.part
    rows, width, units = resid_ref.shape[0], normed_ref.shape[1], hid_ref.shape[1]
    f32, bf16 = jnp.float32, jnp.bfloat16
    lag = 2
    def hid_load(step): return pltpu.make_async_copy(step_block(hid_ref, step), hid_in.at[step % 2], hid_sem.at[step % 2])
    def loads(block):
        slot = block % 2
        zz, yy, xx = step_target(2 * block)
        at = pl.ds(pl.multiple_of((zz * 2 + yy) * 4 * rows, 4 * rows), 4 * rows)
        return ([pltpu.make_async_copy(src.at[at], wide_in.at[slot, n], in_sem.at[n, slot]) for n, src in enumerate((normed_ref, cot_ref))]
            + [pltpu.make_async_copy(src.at[at], thin_in.at[slot, n], in_sem.at[2 + n, slot]) for n, src in enumerate((hid_ref, gate_ref, up_ref))])
    for one in loads(0): one.start()
    hid_load(0).start()

    def inner(gate_sum, up_sum, down_sum):
        gate_sum[...] = jnp.zeros_like(gate_sum)
        up_sum[...] = jnp.zeros_like(up_sum)
        down_sum[...] = jnp.zeros_like(down_sum)

        def outputs(step):
            slot = step % 2
            hid_load(step).wait()
            @pl.when(step < 15)
            def _(): hid_load(step + 1).start()
            @pl.when(step >= 2)
            def _(): reduction.over_core(step - 2).wait_send()
            hid = hid_in[slot]
            for n in range(width // 512):
                at = pl.ds(n * 512, 512)
                value = nn(hid, down_ref[:, at]).astype(bf16)
                part[slot, 0, :, at] = value[:rows]
                part[slot, 1, :, at] = value[rows:]
            reduction.over_core(step).start()

        def down_gradient(block):
            slot = block % 2
            for one in loads(block): one.wait()
            @pl.when(block < 7)
            def _():
                for one in loads(block + 1): one.start()
            @pl.when(block < 7)
            def _():
                for n in range(units // 256):
                    at = pl.ds(n * 256, 256)
                    down_sum[at, :] += nn(thin_in[slot, 0, :, at].T, wide_in[slot, 1])

        def gate_gradients(block):
            slot = block % 2
            for n in range(width // 256):
                at = pl.ds(n * 256, 256)
                turned = wide_in[slot, 0, :, at].T
                gate_sum[at, :] += nn(turned, thin_in[slot, 1])
                up_sum[at, :] += nn(turned, thin_in[slot, 2])

        @pl.loop(0, 8 + lag)
        def _(block):
            for n, gradients in enumerate((down_gradient, gate_gradients)):
                step = 2 * block + n
                @pl.when(block < 8)
                def _(): outputs(step)
                @pl.when(block >= lag)
                def _(): gradients(block - lag)
                reduction.follow(step)
        kept = [pltpu.make_async_copy(src, dst, out_sem.at[n])
                for n, (src, dst) in enumerate(((gate_sum, gate_out), (up_sum, up_out), (down_sum, down_out)))]
        for one in kept: one.start()
        reduction.finish(16 + 2 * lag)
        own_out[...] = (resid_ref[...] + reduction.mine[reduction.own].astype(f32)).astype(bf16)
        gather.start(); gather.finish()
        reduction.drain()
        for one in kept: one.wait()
    pl.run_scoped(inner, pltpu.VMEM((width, units), f32), pltpu.VMEM((width, units), f32), pltpu.VMEM((units, width), f32))

def run_outputs(normed_all, cot_all, hidden_gated, gate_grad, up_grad, down_flat, resid, collective_id):
    total, width = normed_all.shape; rows = total // 32; units = hidden_gated.shape[1]
    f32, bf16 = jnp.float32, jnp.bfloat16; D = pltpu.SemaphoreType.DMA; V = pltpu.VMEM; S = jax.ShapeDtypeStruct
    anyspec, vspec = pl.BlockSpec(memory_space=pl.ANY), pl.BlockSpec(memory_space=V)
    return pl.pallas_call(output_kernel,
        out_shape=[S((4, rows, width), bf16), S((width, units), f32), S((width, units), f32), S((units, width), f32)],
        in_specs=[anyspec] * 5 + [vspec] * 2, out_specs=[anyspec] * 4,
        scratch_shapes=[V((2, 2 * rows, units), bf16), V((2, 2, 4 * rows, width), bf16), V((2, 3, 4 * rows, units), bf16), V((rows, width), bf16), D((2,)), D((5, 2)), D((3,)),
            *Reduction.scratch(rows, width, bf16, 80), *TensorGather.scratch()],
        compiler_params=pltpu.CompilerParams(collective_id=collective_id, has_side_effects=True, vmem_limit_bytes=62 << 20))(
            normed_all, cot_all, hidden_gated, gate_grad, up_grad, down_flat, resid)


def inverse_rms(values):
    return lax.rsqrt(jnp.mean(values * values, axis=-1, keepdims=True) + EPSILON)

def attend_kernel(x_ref, gain_ref, qkv_ref, cos_ref, sin_ref, head_gain_ref, seg_rows_ref, seg_cols_ref,
                  normed_ref, raw_ref, q_ref, kv_ref, kv_other_ref, full_ref, heads_ref, lse_ref, bias, send_sem, recv_sem):
    z, y, x, c = coords()
    other = (z, 1 - y, 2 * x + c)
    greet([(None, other)])
    f32, bf16 = jnp.float32, jnp.bfloat16
    rows = x_ref.shape[0]; heads = q_ref.shape[1] // HEAD_SIZE; q_width = heads * HEAD_SIZE
    values = x_ref[...].astype(f32)
    normed_ref[...] = (values * inverse_rms(values) * gain_ref[...]).astype(bf16)
    def finish(raw, n):
        normed = raw * inverse_rms(raw) * head_gain_ref[pl.ds(n, 1), :]
        return (normed * cos_ref[...] + pltpu.roll(normed, HEAD_SIZE // 2, 1) * sin_ref[...]).astype(bf16)
    raw_kv = nn(normed_ref[...], qkv_ref[:, pl.ds(q_width, 2 * HEAD_SIZE)])
    raw_ref[:, pl.ds(q_width, HEAD_SIZE)] = raw_kv[:, :HEAD_SIZE]
    kv_ref[:, pl.ds(0, HEAD_SIZE)] = finish(raw_kv[:, :HEAD_SIZE], 1)
    kv_ref[:, pl.ds(HEAD_SIZE, HEAD_SIZE)] = raw_kv[:, HEAD_SIZE:].astype(bf16)
    move = pltpu.make_async_remote_copy(src_ref=kv_ref, dst_ref=kv_other_ref, send_sem=send_sem, recv_sem=recv_sem,
        device_id=other, device_id_type=MESH)
    @pl.when(y == 0)
    def _():
        move.start()
        kv_other_ref[...] = jnp.zeros_like(kv_other_ref)
    @pl.loop(0, heads // 2)
    def _(n):
        at = pl.ds(pl.multiple_of(n * 2 * HEAD_SIZE, 2 * HEAD_SIZE), 2 * HEAD_SIZE)
        raw = nn(normed_ref[...], qkv_ref[:, at])
        raw_ref[:, at] = raw
        for m in range(2):
            one = pl.ds(pl.multiple_of((2 * n + m) * HEAD_SIZE, HEAD_SIZE), HEAD_SIZE)
            q_ref[:, one] = finish(raw[:, m * HEAD_SIZE:(m + 1) * HEAD_SIZE], 0)
    row_id = lax.broadcasted_iota(jnp.int32, (rows, rows), 0)
    col_id = lax.broadcasted_iota(jnp.int32, (rows, rows), 1)
    bias[0] = jnp.where((seg_rows_ref[...] == seg_cols_ref[pl.ds(0, 1), :]) & (col_id <= row_id), 0.0, NEGATIVE)
    bias[1] = jnp.where(seg_rows_ref[...] == seg_cols_ref[pl.ds(1, 1), :], 0.0, NEGATIVE)
    lse_ref[...] = jnp.zeros_like(lse_ref)
    scale = HEAD_SIZE ** -0.5
    lane = lax.broadcasted_iota(jnp.int32, (rows, HEAD_SIZE), 1)
    def head(h, blocks):
        at = pl.ds(pl.multiple_of(h * HEAD_SIZE, HEAD_SIZE), HEAD_SIZE)
        query = q_ref[:, at]
        refs = (kv_ref, kv_other_ref)[:blocks]
        scores = [nt(query, ref[:, pl.ds(0, HEAD_SIZE)]) * scale + bias[n] for n, ref in enumerate(refs)]
        top = functools.reduce(jnp.maximum, [jnp.max(s, axis=1, keepdims=True) for s in scores])
        weights = [jnp.exp(s - top) for s in scores]
        total = sum(jnp.sum(w, axis=1, keepdims=True) for w in weights)
        inverse = 1.0 / total
        full = sum(nn((w * inverse).astype(bf16), ref[:, pl.ds(HEAD_SIZE, HEAD_SIZE)]) for w, ref in zip(weights, refs))
        full_ref[:, at] = full
        heads_ref[:, at] = full.astype(bf16)
        lse_ref[...] = jnp.where(lane == h, top + jnp.log(total), lse_ref[...])
    @pl.when(y == 0)
    def _():
        @pl.loop(0, heads)
        def _(h): head(h, 1)
        move.wait_send()
    @pl.when(y == 1)
    def _():
        move.wait_recv()
        @pl.loop(0, heads)
        def _(h): head(h, 2)

def attend(x, gain, qkv, cos, sin, head_gains, seg_rows, seg_cols, collective_id):
    rows, width = x.shape; q_width = qkv.shape[1] - 2 * HEAD_SIZE
    V = pltpu.VMEM; f32, bf16 = jnp.float32, jnp.bfloat16; S = jax.ShapeDtypeStruct
    vspec = pl.BlockSpec(memory_space=V)
    return pl.pallas_call(attend_kernel,
        out_shape=[S((rows, width), bf16), S((rows, q_width + HEAD_SIZE), f32), S((rows, q_width), bf16), S((rows, 2 * HEAD_SIZE), bf16),
            S((rows, 2 * HEAD_SIZE), bf16), S((rows, q_width), f32), S((rows, q_width), bf16), S((rows, HEAD_SIZE), f32)],
        in_specs=[vspec] * 8, out_specs=[vspec] * 8,
        scratch_shapes=[V((2, rows, rows), f32), pltpu.SemaphoreType.DMA, pltpu.SemaphoreType.DMA],
        compiler_params=pltpu.CompilerParams(collective_id=collective_id, has_side_effects=True, vmem_limit_bytes=48 << 20))(
            x, gain, qkv, cos, sin, head_gains, seg_rows, seg_cols)

def attend_back_kernel(cot_ref, out_w_ref, q_ref, kv_ref, kv_other_ref, raw_ref, full_ref, lse_ref, cos_ref, sin_ref, head_gain_ref,
                       seg_rows_ref, seg_cols_ref, grad_ref, gains_ref, grad_heads, delta, stats, bias, grad_q, grad_kv, kv_send, kv_in, send_sem, recv_sem):
    z, y, x, c = coords()
    other = (z, 1 - y, 2 * x + c)
    greet([(None, other)])
    f32, bf16 = jnp.float32, jnp.bfloat16
    rows = q_ref.shape[0]; heads = q_ref.shape[1] // HEAD_SIZE; q_width = heads * HEAD_SIZE
    scale = HEAD_SIZE ** -0.5
    lane = lax.broadcasted_iota(jnp.int32, (rows, HEAD_SIZE), 1)
    delta[...] = jnp.zeros_like(delta)
    @pl.loop(0, heads // 2)
    def _(n):
        at = pl.ds(pl.multiple_of(n * 2 * HEAD_SIZE, 2 * HEAD_SIZE), 2 * HEAD_SIZE)
        grad = nn(cot_ref[...], out_w_ref[:, at]).astype(bf16)
        grad_heads[:, at] = grad
        product = grad.astype(f32) * full_ref[:, at]
        for m in range(2):
            one = jnp.sum(product[:, m * HEAD_SIZE:(m + 1) * HEAD_SIZE], axis=1, keepdims=True)
            delta[...] = jnp.where(lane == 2 * n + m, one, delta[...])
    stats[0] = lse_ref[...].T
    stats[1] = delta[...].T
    key_id = lax.broadcasted_iota(jnp.int32, (rows, rows), 0)
    query_id = lax.broadcasted_iota(jnp.int32, (rows, rows), 1)
    def block(ref, seg_keys, causal):
        same = seg_keys == seg_cols_ref[pl.ds(0, 1), :]
        bias[...] = jnp.where(same & (key_id <= query_id) if causal else same, 0.0, NEGATIVE)
        grad_kv[...] = jnp.zeros_like(grad_kv)
        key, value = ref[:, pl.ds(0, HEAD_SIZE)], ref[:, pl.ds(HEAD_SIZE, HEAD_SIZE)]
        @pl.loop(0, heads)
        def _(h):
            at = pl.ds(pl.multiple_of(h * HEAD_SIZE, HEAD_SIZE), HEAD_SIZE)
            query, grad = q_ref[:, at], grad_heads[:, at]
            probs = jnp.exp(nt(key, query) * scale + bias[...] - stats[0, pl.ds(h, 1), :])
            grad_scores = (probs * (nt(value, grad) - stats[1, pl.ds(h, 1), :])).astype(bf16)
            grad_kv[:, pl.ds(0, HEAD_SIZE)] += nn(grad_scores, query) * scale
            grad_kv[:, pl.ds(HEAD_SIZE, HEAD_SIZE)] += nn(probs.astype(bf16), grad)
            grad_q[:, at] += lax.dot_general(grad_scores, key, (((0,), (0,)), ((), ())), preferred_element_type=f32) * scale
    grad_q[...] = jnp.zeros_like(grad_q)
    move = pltpu.make_async_remote_copy(src_ref=kv_send, dst_ref=kv_in, send_sem=send_sem, recv_sem=recv_sem, device_id=other, device_id_type=MESH)
    @pl.when(y == 1)
    def _():
        block(kv_other_ref, seg_rows_ref[1], False)
        kv_send[...] = grad_kv[...].astype(bf16)
        move.start()
    block(kv_ref, seg_rows_ref[0], True)
    @pl.when(y == 0)
    def _():
        move.wait_recv()
        grad_kv[...] += kv_in[...].astype(f32)
    def pull(grad, raw, n):
        turned = grad * cos_ref[...] - pltpu.roll(grad, HEAD_SIZE // 2, 1) * sin_ref[...]
        inverse = inverse_rms(raw)
        unit = raw * inverse
        gains_ref[pl.ds(n, 1), :] += jnp.sum(turned * unit, axis=0, keepdims=True)
        scaled = turned * head_gain_ref[pl.ds(n, 1), :]
        return (inverse * (scaled - unit * jnp.mean(scaled * unit, axis=1, keepdims=True))).astype(bf16)
    gains_ref[...] = jnp.zeros_like(gains_ref)
    @pl.loop(0, heads)
    def _(h):
        at = pl.ds(pl.multiple_of(h * HEAD_SIZE, HEAD_SIZE), HEAD_SIZE)
        grad_ref[:, at] = pull(grad_q[:, at], raw_ref[:, at], 0)
    at = pl.ds(q_width, HEAD_SIZE)
    grad_ref[:, at] = pull(grad_kv[:, pl.ds(0, HEAD_SIZE)], raw_ref[:, at], 1)
    grad_ref[:, pl.ds(q_width + HEAD_SIZE, HEAD_SIZE)] = grad_kv[:, pl.ds(HEAD_SIZE, HEAD_SIZE)].astype(bf16)
    @pl.when(y == 1)
    def _(): move.wait_send()

def attend_back(cot, out_w, q, kv, kv_other, raw, full, lse, cos, sin, head_gains, seg_rows, seg_cols, collective_id):
    rows, q_width = q.shape
    V = pltpu.VMEM; f32, bf16 = jnp.float32, jnp.bfloat16; S = jax.ShapeDtypeStruct
    vspec = pl.BlockSpec(memory_space=V)
    return pl.pallas_call(attend_back_kernel,
        out_shape=[S((rows, q_width + 2 * HEAD_SIZE), bf16), S((8, HEAD_SIZE), f32)],
        in_specs=[vspec] * 13, out_specs=[vspec] * 2,
        scratch_shapes=[V((rows, q_width), bf16), V((rows, HEAD_SIZE), f32), V((2, HEAD_SIZE, rows), f32), V((rows, rows), f32), V((rows, q_width), f32),
            V((rows, 2 * HEAD_SIZE), f32), V((rows, 2 * HEAD_SIZE), bf16), V((rows, 2 * HEAD_SIZE), bf16), pltpu.SemaphoreType.DMA, pltpu.SemaphoreType.DMA],
        compiler_params=pltpu.CompilerParams(collective_id=collective_id, has_side_effects=True, vmem_limit_bytes=48 << 20))(
            cot, out_w, q, kv, kv_other, raw, full, lse, cos, sin, head_gains, seg_rows, seg_cols)


def gathered_local(
    hidden_in,
    attn_gain,
    w_query,
    key_weight,
    value_weight,
    w_output,
    query_gain,
    key_gain,
    ffn_gain,
    router,
    gate_weight,
    up_weight,
    down_weight,
    routes,
    segments,
    cotangent,
):
    bf16, f32 = jnp.bfloat16, jnp.float32
    context_size = lax.axis_size(CONTEXT)
    tensor_size = lax.axis_size(TENSOR)
    group_count = lax.axis_size(FSDP) * context_size
    fsdp_rank = lax.axis_index(FSDP)
    context_rank = lax.axis_index(CONTEXT)
    tensor_rank = lax.axis_index(TENSOR)
    group_rank = fsdp_rank * context_size + context_rank
    row_count, width = hidden_in.shape[1:]
    own_count = row_count // tensor_size
    own_start = tensor_rank * own_count
    local_experts, _, hidden_width = gate_weight.shape
    experts_total = router.shape[1]
    first_expert = group_rank * local_experts
    capacity = 9 * row_count * TOPK // (8 * experts_total)
    query_width = w_query.shape[1]

    expert_ids = jnp.arange(experts_total, dtype=jnp.int32)
    chosen = jnp.any(routes[0][..., None] == expert_ids, axis=1)
    kept = chosen & (earlier_counts(chosen) < capacity)
    code = chosen.astype(bf16) + kept.astype(bf16)
    chosen_own = lax.dynamic_slice_in_dim(chosen, own_start, own_count, 0)
    code = code.reshape(tensor_size, own_count, experts_total).transpose(1, 0, 2)

    pieces = (code, router, attn_gain, ffn_gain, query_gain, key_gain, segments)
    small = jnp.concatenate([piece.astype(bf16).reshape(-1) for piece in pieces])
    small = jnp.pad(small, (0, -small.size % 2048)).reshape(-1, 128)
    qkv_weight = jnp.concatenate([w_query, key_weight, value_weight], axis=1)
    pieces_of = [(0, 0, small.shape[0], 0)]
    for array in (1, 2):
        pieces_of += [(array, 0, 112, 0), (array, 112, 96, 0), (array, 208, 48, 1)]
    small, qkv_full, full_output = gather_groups((small, qkv_weight, w_output), tuple(pieces_of), 1)
    grad_out_own = lax.dynamic_slice_in_dim(cotangent[0], own_start, own_count, 0)
    grad_out_own, codes = lax.optimization_barrier((grad_out_own, small))
    grad_out_all = lax.all_gather(grad_out_own, EVERYONE, axis=0, tiled=True)
    small = small.reshape(group_count, -1)
    parts, at = [], code.size
    for piece in pieces[1:]:
        parts.append(small[:, at : at + piece.size])
        at += piece.size
    full_router = parts[0].reshape(width, experts_total)
    gain_attn, gain_ffn, gain_query, gain_key = (
        part.reshape(-1).astype(f32) for part in parts[1:5]
    )
    head_gains = jnp.stack([gain_query, gain_key])
    all_segments = parts[5].astype(jnp.int32)

    own_seg = segments[0]
    first_seg = lax.dynamic_index_in_dim(all_segments, group_rank - context_rank, 0, keepdims=False)
    other_seg = lax.dynamic_index_in_dim(
        all_segments, group_rank + 1 - 2 * context_rank, 0, keepdims=False
    )
    smaller = jnp.sum((own_seg[None, :] < own_seg[:, None]).astype(jnp.int32), axis=1)
    smaller_first = jnp.sum((first_seg[None, :] < own_seg[:, None]).astype(jnp.int32), axis=1)
    positions = jnp.arange(row_count, dtype=jnp.int32) - smaller
    positions = positions + context_rank * (row_count - smaller_first)
    cosine_table, sine_table = rope_tables(positions, HEAD_SIZE)
    turn = jnp.where(jnp.arange(HEAD_SIZE) < HEAD_SIZE // 2, -1.0, 1.0)
    sine_table = sine_table * turn
    seg_rows = jnp.stack([own_seg, other_seg])

    normed_one, raw, query, kv, kv_other, heads_full, heads_low, log_total = attend(
        hidden_in[0],
        gain_attn[None],
        qkv_full,
        cosine_table,
        sine_table,
        head_gains,
        own_seg[:, None],
        seg_rows,
        8,
    )
    input_own = lax.dynamic_slice_in_dim(hidden_in[0], own_start, own_count, 0)
    residual_own, normed_own, normed_all = mix_heads(
        heads_low, full_output, input_own, gain_ffn[None], 3
    )

    units = local_experts * hidden_width
    gate_flat = gate_weight.transpose(1, 0, 2).reshape(width, units)
    up_flat = up_weight.transpose(1, 0, 2).reshape(width, units)
    down_flat = down_weight.reshape(units, width)
    unit_expert = first_expert + jnp.arange(units, dtype=jnp.int32) // hidden_width
    lane_ids = jnp.arange(tensor_size * experts_total, dtype=jnp.int32)
    expand = (lane_ids[:, None] % experts_total == unit_expert[None, :]).astype(bf16)
    column = tensor_rank * experts_total + unit_expert
    place = (column[:, None] == lane_ids[None, :]).astype(bf16)
    router_lanes = jnp.concatenate([full_router] * tensor_size, axis=1)
    grad_resid_own, message, hidden_gated, gate_grad, up_grad = run_experts(
        normed_all,
        grad_out_all,
        codes,
        router_lanes,
        expand,
        place,
        gate_flat,
        up_flat,
        down_flat,
        residual_own,
        normed_own,
        jnp.pad(chosen_own.astype(bf16), ((0, 0), (0, 128 - experts_total))),
        grad_out_own,
        gain_ffn[None],
        4,
    )
    grad_attn = message[:, :own_count, :width].reshape(row_count, width)
    grad_raw, head_gain_grads = attend_back(
        grad_attn,
        full_output,
        query,
        kv,
        kv_other,
        raw,
        heads_full,
        log_total,
        cosine_table,
        sine_table,
        head_gains,
        seg_rows[:, :, None],
        seg_rows,
        9,
    )
    group_logits = message[:, :own_count, width:].reshape(row_count, 128)
    grad_gain_ffn = jnp.sum(message[:, own_count, :width].astype(f32), axis=0)
    normed_group = lax.dynamic_slice_in_dim(normed_all, group_rank * row_count, row_count, 0)
    grad_router = matmul_tn(normed_group, group_logits)
    grad_w_output = matmul_tn(grad_attn, heads_low)
    grad_w_output = lax.psum_scatter(
        grad_w_output.astype(bf16), GROUPS, scatter_dimension=0, tiled=True
    )

    message = pull_inputs(
        grad_raw, qkv_full, hidden_in[0], gain_attn[None], head_gain_grads, grad_resid_own, 6
    )
    input_grad = message[:, :own_count].reshape(row_count, width).astype(f32)
    gain_rows = jnp.sum(message[:, own_count : own_count + 2].astype(f32), axis=0)
    head_gains_grad = jnp.pad(
        gain_rows[1, : 2 * HEAD_SIZE].reshape(2, group_count, -1),
        ((0, 0), (0, 0), (0, (width - HEAD_SIZE) // group_count)),
    ).reshape(2, width)
    columns = jnp.stack([gain_rows[0], head_gains_grad[0], head_gains_grad[1], grad_gain_ffn], axis=1)
    extra = jnp.concatenate([columns, grad_router[:, :experts_total]], axis=1)
    extra = jnp.pad(extra, ((0, 0), (0, 128 - extra.shape[1])))
    grad_qkv = jnp.concatenate([matmul_tn(normed_one, grad_raw), extra], axis=1)
    grad_qkv, hidden_gated = lax.optimization_barrier((grad_qkv.astype(bf16), hidden_gated))
    grad_qkv = lax.psum_scatter(grad_qkv, GROUPS, scatter_dimension=0, tiled=True)
    output, grad_w_gate, grad_w_up, grad_w_down = run_outputs(
        normed_all, grad_out_all, hidden_gated, gate_grad, up_grad, down_flat, residual_own, 10
    )
    own_hidden = lax.dynamic_slice_in_dim(hidden_gated, group_rank * row_count, row_count, 0)
    grad_w_down = grad_w_down + matmul_tn(own_hidden, cotangent[0])

    def by_expert(grad):
        return grad.reshape(width, local_experts, hidden_width).transpose(1, 0, 2)

    grad_w_gate, grad_w_up = by_expert(grad_w_gate), by_expert(grad_w_up)
    output = output.reshape(row_count, width)
    output, grad_w_output = lax.optimization_barrier((output, grad_w_output))
    grad_w_output = grad_w_output.astype(f32)
    grad_qkv, grad_w_output, grad_w_gate, grad_w_up, grad_w_down = lax.optimization_barrier(
        (grad_qkv, grad_w_output, grad_w_gate, grad_w_up, grad_w_down)
    )
    value_at, extra_at = query_width + HEAD_SIZE, query_width + 2 * HEAD_SIZE
    return (
        output[None],
        input_grad[None],
        grad_qkv[:, extra_at].astype(f32),
        grad_qkv[:, :query_width].astype(f32),
        grad_qkv[:, query_width:value_at].astype(f32),
        grad_qkv[:, value_at:extra_at].astype(f32),
        grad_w_output,
        grad_qkv[: query_gain.shape[0], extra_at + 1].astype(f32),
        grad_qkv[: key_gain.shape[0], extra_at + 2].astype(f32),
        grad_qkv[:, extra_at + 3].astype(f32),
        grad_qkv[:, extra_at + 4 : extra_at + 4 + experts_total].astype(f32),
        grad_w_gate,
        grad_w_up,
        grad_w_down.reshape(down_weight.shape),
    )


def local(*arrays):
    sizes = tuple(lax.axis_size(name) for name in EVERYONE)
    return (gathered_local if sizes == (4, 2, 4) and arrays[9].shape[1] == 32 else routed_local)(*arrays)


def solution(mesh):
    in_specs = (
        P(FSDP, CONTEXT, None),
        P(GROUPS),
        P(GROUPS, TENSOR),
        P(GROUPS, TENSOR),
        P(GROUPS, TENSOR),
        P(GROUPS, TENSOR),
        P(GROUPS),
        P(GROUPS),
        P(GROUPS),
        P(GROUPS, None),
        P(GROUPS, None, TENSOR),
        P(GROUPS, None, TENSOR),
        P(GROUPS, TENSOR, None),
        P(FSDP, CONTEXT, None),
        P(FSDP, CONTEXT),
        P(FSDP, CONTEXT, None),
    )
    out_specs = (
        P(FSDP, CONTEXT, None),
        P(FSDP, CONTEXT, None),
        P(GROUPS),
        P(GROUPS, TENSOR),
        P(GROUPS, TENSOR),
        P(GROUPS, TENSOR),
        P(GROUPS, TENSOR),
        P(GROUPS),
        P(GROUPS),
        P(GROUPS),
        P(GROUPS, None),
        P(GROUPS, None, TENSOR),
        P(GROUPS, None, TENSOR),
        P(GROUPS, TENSOR, None),
    )
    return jax.shard_map(local, mesh=mesh, in_specs=in_specs, out_specs=out_specs, check_vma=False)
```
